32 devices in a mesh: dp: 16 (over z, y, core), seq: 2 (over x).
Axes of the slice: x: 2, y: 2, z: 4, core: 2. Of those that a mesh axis runs over, the one named last changes fastest.
Arguments:
- hidden_in: bfloat16 [16, 1024, 768], P('dp', 'seq'), may hold values from -18 to 18
- segment_ids: int32 [16, 1024], P('dp'), may hold values from 0 to 7, as said below
- piece_lengths: int32 [16, 8], P('dp'), may hold values from 0 to 1024, as said below
- time_index: int32 [16, 8], P('dp'), may hold values from 0 to 999
- first_gain: float32 [768], replicated, may hold values from 0.5 to 1.5
- modulation_weight: bfloat16 [128, 4608], replicated, may hold values from -0.5 to 0.5
- modulation_bias: float32 [4608], replicated, may hold values from -4 to 4
- query_key_value_weight: bfloat16 [768, 2304], replicated, may hold values from -0.21875 to 0.21875
- attention_output_matrix: bfloat16 [768, 768], replicated, may hold values from -0.875 to 0.875
- second_gain: float32 [768], replicated, may hold values from 0.5 to 1.5
- widen_weight: bfloat16 [768, 3072], replicated, may hold values from -0.21875 to 0.21875
- expand_bias: float32 [3072], replicated, may hold values from -6 to 6
- narrow_weight: bfloat16 [3072, 768], replicated, may hold values from -0.109375 to 0.109375
- reduce_bias: float32 [768], replicated, may hold values from -6 to 6
- cotangent: bfloat16 [16, 1024, 768], P('dp', 'seq'), may hold values from -6 to 6
Outputs:
- block_out: bfloat16 [16, 1024, 768], P('dp', 'seq')
- input_grad: bfloat16 [16, 1024, 768], P('dp', 'seq')
- first_gain_grad: float32 [768], replicated
- modulation_weight_grad: float32 [128, 4608], P('seq', 'dp')
- modulation_bias_grad: float32 [4608], replicated
- triple_weight_grad: float32 [768, 2304], P('seq', 'dp')
- output_weight_grad: float32 [768, 768], P('seq', 'dp')
- second_gain_grad: float32 [768], replicated
- expand_weight_grad: float32 [768, 3072], P('seq', 'dp')
- expand_bias_grad: float32 [3072], replicated
- reduce_weight_grad: float32 [3072, 768], P('seq', 'dp')
- reduce_bias_grad: float32 [768], replicated
- masked_rms: float32 [3], replicated
The draws below stay inside these ranges and needn't reach their ends.
Inputs may be any that keep to these rules, and one draw needn't show every extreme that they name: `segment_ids`: each slot is cut into equal pieces of 128, 512 or 1024 tokens, the kind drawn for each slot, and a token's segment id is the number of its piece, so ids start at 0 and never fall; the first slot has pieces of 128 and the last one a single piece. piece_lengths[slot, s] counts the valid leading tokens of piece s: more than half of the piece and at most all of it, the first piece of every slot all valid; 0 for numbers beyond the slot's pieces.
All inputs are finite; a program needn't handle non-finite values.
Results may differ from the reference program's by a relative error of at most 0.014.
Values may be sent and summed in bfloat16 or wider, within the bound.
A program may use at most 192 MiB of HBM per device.

```python
import math
import jax
import jax.numpy as jnp
from jax import lax

D = 768
HEADS = 12
HDIM = 64
FF = 3072
COND = 128
SLOT = 1024
MID = 512
SHORT = 128
TSTEPS = 1000
MAXSEQ = 8
SLOTS = 16


def piece_plan(key):
    piece_kind = jax.random.randint(jax.random.fold_in(key, 11), (SLOTS,), 0, 3)
    slot_number = jnp.arange(SLOTS, dtype=jnp.int32)
    piece_kind = jnp.where(slot_number == SLOTS - 1, 2, piece_kind)
    piece_kind = jnp.where(slot_number == 0, 0, piece_kind)
    piece_size = jnp.where(piece_kind == 0, SHORT, jnp.where(piece_kind == 1, MID, SLOT))
    return piece_size.astype(jnp.int32)


def draw_segment_ids(key, part):
    piece_size = piece_plan(key)
    return (jnp.arange(SLOT, dtype=jnp.int32)[None, :] // piece_size[:, None]).astype(jnp.int32)


def draw_piece_lengths(key, part):
    piece_size = piece_plan(key)
    random_bits = jax.random.randint(jax.random.fold_in(key, 12), (SLOTS, MAXSEQ), 0, 1048576)
    lowest = piece_size // 2 + 1
    span_size = piece_size - piece_size // 2
    chosen = lowest[:, None] + random_bits % span_size[:, None]
    piece_number = jnp.arange(MAXSEQ, dtype=jnp.int32)[None, :]
    chosen = jnp.where(piece_number == 0, piece_size[:, None], chosen)
    in_slot = piece_number < (SLOT // piece_size)[:, None]
    return jnp.where(in_slot, chosen, 0).astype(jnp.int32)


def draw_hidden_in(key, part):
    slot_place = jnp.arange(SLOTS).astype(jnp.float32) / max(SLOTS - 1, 1)
    noise = jnp.clip(jax.random.normal(key, (SLOTS, SLOT, D), jnp.float32), -6.0, 6.0)
    rising = 3.0 ** slot_place
    return (noise * rising[:, None, None]).astype(jnp.bfloat16)


def plant(values, rng, least, high):
    longest = values.shape.index(max(values.shape))
    spots = []
    for shift in (0, 1):
        where = [jax.random.randint(jax.random.fold_in(rng, axis), (), 0, length) for axis, length in enumerate(values.shape)]
        where[longest] = (where[longest] + shift) % values.shape[longest]
        spots.append(tuple(where))
    return values.at[spots[0]].set(least).at[spots[1]].set(high)


def block_levels(rng, shape, pieces, low, high):
    factor_of, own = 1.0, jax.random.fold_in(rng, 6)
    for position, blocks in pieces:
        heights = jnp.exp(jax.random.uniform(jax.random.fold_in(own, position), (blocks,), jnp.float32, low / len(pieces), high / len(pieces)))
        factor_of = factor_of * jnp.repeat(heights, shape[position] // blocks).reshape([-1 if axis == position else 1 for axis in range(len(shape))])
    return factor_of


def centred(rng, extent, width, bound, cuts=(), held_as=jnp.bfloat16):
    values = width * jax.random.normal(rng, extent, jnp.float32)
    if cuts:
        values = values * block_levels(rng, extent, cuts, -0.22, 0.18)
    return jnp.clip(values, -bound, bound).astype(held_as)


def setup_inputs(seed: int = 0) -> dict:
    key_list = jax.random.split(jax.random.key(seed), 16)
    return {
        "hidden_in": draw_hidden_in(jax.random.fold_in(key_list[15], 71), 0),
        "segment_ids": draw_segment_ids(jax.random.fold_in(key_list[15], 71), 0),
        "piece_lengths": draw_piece_lengths(jax.random.fold_in(key_list[15], 71), 0),
        "time_index": plant(jax.random.randint(key_list[3], (SLOTS, MAXSEQ), 0, TSTEPS), jax.random.fold_in(key_list[3], 1), 0, TSTEPS - 1).astype(jnp.int32),
        "first_gain": jnp.clip(1.0 + 0.1 * jax.random.normal(key_list[4], (D,), jnp.float32), 0.5, 1.5),
        "modulation_weight": centred(key_list[5], (COND, 6 * D), COND ** -0.5, 0.5),
        "modulation_bias": centred(key_list[6], (6 * D,), 0.3, 4.0, (), jnp.float32),
        "query_key_value_weight": centred(key_list[7], (D, 3 * D), D ** -0.5, 0.21875),
        "attention_output_matrix": centred(key_list[8], (D, D), (D // 16) ** -0.5, 0.875),
        "second_gain": jnp.clip(1.0 + 0.1 * jax.random.normal(key_list[9], (D,), jnp.float32), 0.5, 1.5),
        "widen_weight": centred(key_list[10], (D, FF), D ** -0.5, 0.21875),
        "expand_bias": centred(key_list[11], (FF,), 0.5, 6.0, (), jnp.float32),
        "narrow_weight": centred(key_list[12], (FF, D), FF ** -0.5, 0.109375),
        "reduce_bias": centred(key_list[13], (D,), 0.5, 6.0, (), jnp.float32),
        "cotangent": centred(key_list[14], (SLOTS, SLOT, D), 1.0, 6.0, ((0, 16), (1, 2))),
    }


@jax.custom_vjp
def low(v):
    return lax.optimization_barrier(v.astype(jnp.bfloat16)).astype(jnp.float32)

@jax.custom_vjp
def low_back(v):
    return v

def low_keep(v):
    return (low(v), None)

def low_pass(kept, grad):
    return (grad,)

def back_keep(v):
    return (v, None)

def back_low(kept, grad):
    return (low(grad),)
low.defvjp(low_keep, low_pass)
low_back.defvjp(back_keep, back_low)
highest = lax.Precision.HIGHEST
negative = -1000000000.0

def product(left, right):
    return jnp.dot(left, right, precision=highest, preferred_element_type=jnp.float32)

def layer_norm(values, scaling):
    centered = values - lax.optimization_barrier(jnp.mean(values, axis=-1, keepdims=True))
    spread = lax.optimization_barrier(jnp.mean(centered * centered, axis=-1, keepdims=True))
    return centered * lax.rsqrt(spread + 1e-05) * scaling

def norm_modulate(values, scaling, offset, stretch):
    return layer_norm(values, scaling) * (1.0 + stretch) + offset

def gelu_tanh(values):
    argument = 0.7978845608028654 * (values + 0.044715 * values * values * values)
    return 0.5 * values * (1.0 + jnp.tanh(argument))

def rotate(values, cosine, sine_part):
    halfway = values.shape[-1] // 2
    turned = jnp.concatenate([-values[..., halfway:], values[..., :halfway]], axis=-1)
    return values * cosine + turned * sine_part

def rotary_tables(positions, head_dim):
    freq_index = jnp.arange(head_dim // 2).astype(jnp.float32)
    frequencies = jnp.exp(freq_index * (-2.0 * math.log(10000.0) / head_dim))
    angles = positions[..., None] * frequencies
    angles = jnp.concatenate([angles, angles], axis=-1)
    return (jnp.cos(angles)[..., None, :], jnp.sin(angles)[..., None, :])

def time_embed(time_values, feature_count):
    halfway = feature_count // 2
    freq_index = jnp.arange(halfway).astype(jnp.float32)
    frequencies = jnp.exp(freq_index * (-math.log(10000.0) / halfway))
    angles = time_values.astype(jnp.float32)[..., None] * frequencies
    return jnp.concatenate([jnp.cos(angles), jnp.sin(angles)], axis=-1)

def slot_layout(segments, lengths):
    seg_range = jnp.arange(lengths.shape[-1], dtype=jnp.int32)
    membership = (segments[..., :, None] == seg_range).astype(jnp.float32)
    piece_sizes = lax.optimization_barrier(jnp.sum(membership, axis=-2))
    piece_starts = jnp.cumsum(piece_sizes, axis=-1) - piece_sizes
    token_start = lax.optimization_barrier(jnp.sum(membership * piece_starts[..., None, :], axis=-1))
    positions = jnp.arange(segments.shape[-1]).astype(jnp.float32) - token_start
    valid_limit = lax.optimization_barrier(jnp.sum(membership * lengths.astype(jnp.float32)[..., None, :], axis=-1))
    validity = (positions < valid_limit).astype(jnp.float32)
    return (membership, positions, validity)

def slot_forward(params, hidden, segments, membership, positions, validity, condition):
    first_gain, modulation_weight, modulation_bias, query_key_value_weight, attention_output_matrix, second_gain, widen_weight, expand_bias, narrow_weight, reduce_bias = params
    modulation = product(low(condition), modulation_weight) + modulation_bias
    per_token = product(membership, modulation)
    shift_attn, scale_attn, gate_attn, shift_mlp, scale_mlp, gate_mlp = jnp.split(per_token, 6, axis=-1)
    first_normed_tokens = low(norm_modulate(hidden, first_gain, shift_attn, scale_attn))
    triple = low_back(product(first_normed_tokens, query_key_value_weight))
    query, key_raw, value_raw = jnp.split(triple, 3, axis=-1)
    four_dims = (SLOT, HEADS, HDIM)
    cosine, sine_part = rotary_tables(positions, HDIM)
    query_rot = low(rotate(query.reshape(four_dims), cosine, sine_part))
    key_rot = low(rotate(key_raw.reshape(four_dims), cosine, sine_part))
    value_low = low(value_raw.reshape(four_dims))
    scores = jnp.einsum('qhd,khd->hqk', query_rot, key_rot, precision=highest, preferred_element_type=jnp.float32) * HDIM ** (-0.5)
    scores = low_back(scores)
    key_mask = (segments[:, None] == segments[None, :]) & (validity[None, :] > 0.5)
    scores = jnp.where(key_mask[None], scores, negative)
    row_peak = lax.optimization_barrier(jnp.max(scores, axis=-1, keepdims=True))
    exponent = jnp.exp(scores - row_peak)
    row_total = lax.optimization_barrier(jnp.sum(exponent, axis=-1, keepdims=True))
    probability = exponent / row_total
    attended = jnp.einsum('hqk,khd->qhd', low(probability), value_low, precision=highest, preferred_element_type=jnp.float32)
    attention_result_narrow = low_back(low(attended.reshape(SLOT, D)))
    projected = low_back(product(attention_result_narrow, attention_output_matrix))
    attn_branch = gate_attn * projected
    middle = hidden + attn_branch
    second_normed_tokens = low(norm_modulate(middle, second_gain, shift_mlp, scale_mlp))
    expanded = low_back(product(second_normed_tokens, widen_weight) + expand_bias)
    gelu_activations = low(gelu_tanh(expanded))
    reduced = low_back(product(gelu_activations, narrow_weight) + reduce_bias)
    mlp_branch = gate_mlp * reduced
    block_value = middle + mlp_branch
    masked = validity[:, None]
    stat_terms = jnp.stack([jnp.sum(masked * block_value * block_value), jnp.sum(masked * attn_branch * attn_branch), jnp.sum(masked * mlp_branch * mlp_branch), jnp.sum(validity)])
    return (block_value, stat_terms)

def reference(hidden_in, segment_ids, piece_lengths, time_index, first_gain, modulation_weight, modulation_bias, query_key_value_weight, attention_output_matrix, second_gain, widen_weight, expand_bias, narrow_weight, reduce_bias, cotangent):
    membership, positions, validity = slot_layout(segment_ids, piece_lengths)
    condition = time_embed(time_index, COND)
    params = (first_gain.astype(jnp.float32), modulation_weight.astype(jnp.float32), modulation_bias.astype(jnp.float32), query_key_value_weight.astype(jnp.float32), attention_output_matrix.astype(jnp.float32), second_gain.astype(jnp.float32), widen_weight.astype(jnp.float32), expand_bias.astype(jnp.float32), narrow_weight.astype(jnp.float32), reduce_bias.astype(jnp.float32))

    def whole(hidden, weights):

        def one_slot(inputs):
            hid, seg, mem, pos, val, cond = inputs
            return slot_forward(weights, hid, seg, mem, pos, val, cond)
        values, stats = lax.map(jax.checkpoint(one_slot), (hidden, segment_ids, membership, positions, validity, condition))
        return (values, stats)
    block_value, pullback, stat_terms = jax.vjp(whole, hidden_in.astype(jnp.float32), params, has_aux=True)
    grad_out = cotangent.astype(jnp.float32) * validity[..., None]
    input_grad, weight_grads = pullback(grad_out)
    totals = lax.optimization_barrier(jnp.sum(stat_terms, axis=0))
    masked_rms = jnp.sqrt(totals[:3] / (totals[3] * D))
    return (block_value.astype(jnp.bfloat16), input_grad.astype(jnp.bfloat16), weight_grads[0], weight_grads[1], weight_grads[2], weight_grads[3], weight_grads[4], weight_grads[5], weight_grads[6], weight_grads[7], weight_grads[8], weight_grads[9], masked_rms)
```

```python
import math

import jax
import jax.numpy as jnp
from jax import lax
from jax.experimental import pallas as pl
from jax.experimental.pallas import tpu as pltpu
from jax.sharding import PartitionSpec as P

HEADS = 12


highest = lax.Precision.HIGHEST
negative = -1000000000.0


def layer_norm(values, scaling):
    centered = values - jnp.mean(values, axis=-1, keepdims=True)
    spread = jnp.mean(centered * centered, axis=-1, keepdims=True)
    return centered * lax.rsqrt(spread + 1e-05) * scaling


def norm_modulate(values, scaling, offset, stretch):
    return layer_norm(values, scaling) * (1.0 + stretch) + offset


def gelu_tanh(values):
    argument = 0.7978845608028654 * (values + 0.044715 * values * values * values)
    return 0.5 * values * (1.0 + jnp.tanh(argument))


def rotate(values, cosine, sine_part):
    halfway = values.shape[-1] // 2
    turned = jnp.concatenate([-values[..., halfway:], values[..., :halfway]], axis=-1)
    return values * cosine + turned * sine_part


def rotary_tables(positions, head_dim):
    freq_index = jnp.arange(head_dim // 2).astype(jnp.float32)
    frequencies = jnp.exp(freq_index * (-2.0 * math.log(10000.0) / head_dim))
    angles = positions[..., None] * frequencies
    angles = jnp.concatenate([angles, angles], axis=-1)
    return (jnp.cos(angles)[..., None, :], jnp.sin(angles)[..., None, :])


def time_embed(time_values, feature_count):
    halfway = feature_count // 2
    freq_index = jnp.arange(halfway).astype(jnp.float32)
    frequencies = jnp.exp(freq_index * (-math.log(10000.0) / halfway))
    angles = time_values.astype(jnp.float32)[..., None] * frequencies
    return jnp.concatenate([jnp.cos(angles), jnp.sin(angles)], axis=-1)


def slot_layout(segments, lengths):
    seg_range = jnp.arange(lengths.shape[-1], dtype=jnp.int32)
    membership = (segments[..., :, None] == seg_range).astype(jnp.float32)
    piece_sizes = jnp.sum(membership, axis=-2)
    piece_starts = jnp.cumsum(piece_sizes, axis=-1) - piece_sizes
    token_start = jnp.sum(membership * piece_starts[..., None, :], axis=-1)
    positions = jnp.arange(segments.shape[-1]).astype(jnp.float32) - token_start
    valid_limit = jnp.sum(membership * lengths.astype(jnp.float32)[..., None, :], axis=-1)
    validity = (positions < valid_limit).astype(jnp.float32)
    return (membership, positions, validity)


LANES = 384
GROUP_BITS = 4
MESH_ID = pl.DeviceIdType.MESH
Z2, Z1, Y, CORE, X = 0, 1, 2, 3, 4


def exchange_partner(axis, extra_bits):
    dp, seq = lax.axis_index("dp"), lax.axis_index("seq")
    if axis == X:
        return (dp, 1 - seq)
    return (dp ^ (1 << (GROUP_BITS - 1 - axis + extra_bits)), seq)


def own_bit(axis, extra_bits):
    if axis == X:
        return lax.axis_index("seq")
    return (lax.axis_index("dp") >> (GROUP_BITS - 1 - axis + extra_bits)) & 1


def reduce_tasks(rows):
    streams = (
        (0, 112, (CORE, X, Y, Z1, Z2)),
        (224, 112, (CORE, Y, Z1, X, Z2)),
        (448, 96, (CORE, Z1, X, Y, Z2)),
        (112, 112, (CORE, X, Y, Z1, Z2)),
        (336, 112, (CORE, Y, Z1, X, Z2)),
        (544, 80, (CORE, Z1, X, Y, Z2)),
    )
    return streams


def reduce_kernel(extra_bits, all_bits, parts_ref, small_ref, sum_ref, small_out, acc, got_a, got_b, got_c, got_d, got_e, small_acc, small_got, local_sem, send_sem, recv_sem, small_send, small_recv):
    tasks = reduce_tasks(parts_ref.shape[-2])
    got = (got_a, got_b, got_c, got_d, got_e)
    bits = [own_bit(axis, extra_bits) for axis in range(5)]
    small_partners = [(lax.axis_index("dp"), 1 - lax.axis_index("seq"))] + [
        (lax.axis_index("dp") ^ (1 << bit), lax.axis_index("seq")) for bit in range(all_bits)
    ]
    barrier = pltpu.get_barrier_semaphore()
    for partner in small_partners:
        pl.semaphore_signal(barrier, inc=1, device_id=partner, device_id_type=MESH_ID)
    pl.semaphore_wait(barrier, len(small_partners))

    def region(order, stage, other):
        index = [slice(None)] * 5
        for axis in order[:stage]:
            index[axis] = bits[axis]
        index[order[stage]] = 1 - bits[order[stage]] if other else bits[order[stage]]
        return index

    copies = {}
    local_copies = []
    for number, (first, count, order) in enumerate(tasks):
        keep = pltpu.make_async_copy(
            parts_ref.at[tuple(region(order, 0, False)) + (pl.ds(first, count),)],
            acc.at[:, :, :, :, pl.ds(first, count)],
            local_sem.at[number],
        )
        keep.start()
        local_copies.append(keep)

    def send(number, stage):
        first, count, order = tasks[number]
        index = region(order, stage, True)
        if stage == 0:
            source = parts_ref.at[tuple(index) + (pl.ds(first, count),)]
        else:
            del index[CORE]
            source = acc.at[tuple(index) + (pl.ds(first, count),)]
        target = got[stage].at[(slice(None),) * (4 - stage) + (pl.ds(first, count),)]
        copy = pltpu.make_async_remote_copy(
            source, target, send_sem.at[number, stage], recv_sem.at[number, stage],
            device_id=exchange_partner(order[stage], extra_bits), device_id_type=MESH_ID,
        )
        copy.start()
        copies[number, stage] = copy

    def add(number, stage):
        first, count, order = tasks[number]
        copies[number, stage].wait_recv()
        if stage == 0:
            local_copies[number].wait()
        free = [axis for axis in range(5) if axis not in order[: stage + 1]]

        def one(step, carry):
            index = list(bits)
            got_index = []
            for place, axis in enumerate(free):
                index[axis] = (step >> (len(free) - 1 - place)) & 1
                got_index.append(index[axis])
            del index[CORE]
            rows = pl.ds(first, count)
            mine = acc[tuple(index) + (rows,)].astype(jnp.float32)
            total = mine + got[stage][tuple(got_index) + (rows,)].astype(jnp.float32)
            if stage == 4:
                sum_ref[rows] = total
            else:
                acc[tuple(index) + (rows,)] = total.astype(jnp.bfloat16)
            return carry

        if free:
            lax.fori_loop(0, 2 ** len(free), one, 0)
        else:
            one(0, 0)

    small_copies = []

    def small_send_step(step):
        copy = pltpu.make_async_remote_copy(
            small_acc.at[step], small_got.at[step], small_send.at[step], small_recv.at[step],
            device_id=small_partners[step], device_id_type=MESH_ID,
        )
        copy.start()
        small_copies.append(copy)

    def small_add(step):
        small_copies[step].wait_recv()
        small_acc[step + 1] = small_acc[step] + small_got[step]

    small_acc[0] = small_ref[...]
    for number in range(len(tasks)):
        send(number, 0)
    small_send_step(0)
    for stage in range(1, 5):
        for number in range(len(tasks)):
            add(number, stage - 1)
            send(number, stage)
        small_add(stage - 1)
        small_send_step(stage)
    for number in range(len(tasks)):
        add(number, 4)
    for step in range(4, len(small_partners)):
        small_add(step)
        if step + 1 < len(small_partners):
            small_send_step(step + 1)
    small_out[...] = small_acc[len(small_partners)]
    for copy in copies.values():
        copy.wait_send()
    for copy in small_copies:
        copy.wait_send()


def reduce_everywhere(parts, small):
    dp_size = lax.axis_size("dp")
    all_bits = dp_size.bit_length() - 1
    extra_bits = all_bits - GROUP_BITS
    rows = parts.shape[2]
    parts = parts.reshape((2,) * 5 + parts.shape[2:])
    task_count = len(reduce_tasks(rows))
    steps = all_bits + 1
    bf16 = jnp.bfloat16
    got_shapes = [pltpu.VMEM((2,) * (4 - stage) + (rows, LANES), bf16) for stage in range(5)]
    return pl.pallas_call(
        lambda *refs: reduce_kernel(extra_bits, all_bits, *refs),
        out_shape=(
            jax.ShapeDtypeStruct((rows, LANES), jnp.float32),
            jax.ShapeDtypeStruct(small.shape, jnp.float32),
        ),
        in_specs=[pl.BlockSpec(memory_space=pl.ANY), pl.BlockSpec(memory_space=pltpu.VMEM)],
        out_specs=(pl.BlockSpec(memory_space=pltpu.VMEM), pl.BlockSpec(memory_space=pltpu.VMEM)),
        scratch_shapes=[pltpu.VMEM((2, 2, 2, 2, rows, LANES), bf16)] + got_shapes + [
            pltpu.VMEM((steps + 1,) + small.shape, jnp.float32),
            pltpu.VMEM((steps,) + small.shape, jnp.float32),
            pltpu.SemaphoreType.DMA((task_count,)),
            pltpu.SemaphoreType.DMA((task_count, 5)),
            pltpu.SemaphoreType.DMA((task_count, 5)),
            pltpu.SemaphoreType.DMA((steps,)),
            pltpu.SemaphoreType.DMA((steps,)),
        ],
        compiler_params=pltpu.CompilerParams(
            collective_id=0, has_side_effects=True, vmem_limit_bytes=48 << 20
        ),
    )(parts, small)


def scatter_rest(block, dp_size):
    group = dp_size >> GROUP_BITS
    if group == 1:
        return block
    groups = [[first * group + place for place in range(group)] for first in range(dp_size // group)]
    return lax.psum_scatter(block, "dp", scatter_dimension=0, axis_index_groups=groups, tiled=True)


def local(
    hidden_in,
    segment_ids,
    piece_lengths,
    time_index,
    first_gain,
    modulation_weight,
    modulation_bias,
    query_key_value_weight,
    attention_output_matrix,
    second_gain,
    widen_weight,
    expand_bias,
    narrow_weight,
    reduce_bias,
    cotangent,
):
    slot_count, own_rows, width = hidden_in.shape
    slot_rows = segment_ids.shape[1]
    head_count = HEADS
    head_dim = width // head_count
    score_scale = head_dim ** (-0.5)
    first_row = lax.axis_index("seq") * own_rows
    membership, positions, validity = slot_layout(segment_ids, piece_lengths)
    own_member = lax.dynamic_slice_in_dim(membership, first_row, own_rows, 1)
    own_pos = lax.dynamic_slice_in_dim(positions, first_row, own_rows, 1)
    own_valid = lax.dynamic_slice_in_dim(validity, first_row, own_rows, 1)
    own_segments = lax.dynamic_slice_in_dim(segment_ids, first_row, own_rows, 1)
    allowed = (own_segments[:, :, None] == segment_ids[:, None, :]) & (validity[:, None, :] > 0.5)
    condition = time_embed(time_index, modulation_weight.shape[0]).astype(jnp.bfloat16)
    modulation = (
        jnp.einsum("smc,cf->smf", condition, modulation_weight, preferred_element_type=jnp.float32)
        + modulation_bias
    )
    per_token = jnp.zeros((slot_count, own_rows, modulation.shape[-1]), jnp.float32)
    for segment in range(membership.shape[-1]):
        per_token = (
            per_token
            + own_member[:, :, segment : segment + 1] * modulation[:, segment : segment + 1, :]
        )
    shift_attn, scale_attn, gate_attn, shift_mlp, scale_mlp, gate_mlp = jnp.split(
        per_token, 6, axis=-1
    )
    residual = hidden_in.astype(jnp.float32)
    first_normed_tokens = norm_modulate(residual, first_gain, shift_attn, scale_attn).astype(
        jnp.bfloat16
    )
    triple = jnp.einsum(
        "map,pr->mar",
        first_normed_tokens,
        query_key_value_weight,
        preferred_element_type=jnp.float32,
    )
    query, key_raw, value_raw = jnp.split(triple, 3, axis=-1)
    four_dims = (slot_count, own_rows, head_count, head_dim)
    cosine, sine_part = rotary_tables(own_pos, head_dim)

    def turn(raw_values):
        return rotate(raw_values, cosine, sine_part)

    query_turned, turn_back = jax.vjp(turn, query.reshape(four_dims))
    query_rot = query_turned.astype(jnp.bfloat16)
    key_rot = (
        turn(key_raw.reshape(four_dims)).astype(jnp.bfloat16).reshape(slot_count, own_rows, width)
    )
    value_low = value_raw.astype(jnp.bfloat16)
    all_keys, all_values = (
        lax.all_gather(key_rot, "seq", axis=1, tiled=True),
        lax.all_gather(value_low, "seq", axis=1, tiled=True),
    )
    all_keys = all_keys.reshape(slot_count, slot_rows, head_count, head_dim)
    all_values = all_values.reshape(slot_count, slot_rows, head_count, head_dim)

    def attend(inputs):
        queries, keys, values, key_mask = inputs
        scores = (
            jnp.einsum("qhd,khd->hqk", queries, keys, preferred_element_type=jnp.float32)
            * score_scale
        )
        scores = jnp.where(key_mask[None], scores, negative)
        row_peak = jnp.max(scores, axis=-1, keepdims=True)
        exponent = jnp.exp(scores - row_peak)
        row_total = jnp.sum(exponent, axis=-1, keepdims=True)
        probability = exponent / row_total
        weighted = jnp.einsum(
            "hqk,khd->qhd",
            probability.astype(jnp.bfloat16),
            values,
            preferred_element_type=jnp.float32,
        )
        return (weighted, (row_peak + jnp.log(row_total))[..., 0])

    attended, log_total = lax.map(attend, (query_rot, all_keys, all_values, allowed))
    attention_result_narrow = attended.reshape(slot_count, own_rows, width).astype(jnp.bfloat16)
    projected = jnp.einsum(
        "rkn,nh->rkh",
        attention_result_narrow,
        attention_output_matrix,
        preferred_element_type=jnp.float32,
    )
    attn_branch = gate_attn * projected
    middle = residual + attn_branch
    second_normed_tokens = norm_modulate(middle, second_gain, shift_mlp, scale_mlp).astype(
        jnp.bfloat16
    )
    expanded = (
        jnp.einsum(
            "map,pr->mar", second_normed_tokens, widen_weight, preferred_element_type=jnp.float32
        )
        + expand_bias
    )
    gelu_activations = gelu_tanh(expanded).astype(jnp.bfloat16)
    reduced = (
        jnp.einsum(
            "jpb,bc->jpc", gelu_activations, narrow_weight, preferred_element_type=jnp.float32
        )
        + reduce_bias
    )
    mlp_branch = gate_mlp * reduced
    block_value = middle + mlp_branch
    block_out = block_value.astype(jnp.bfloat16)
    masked = own_valid[..., None]
    stat_terms = jnp.stack(
        [
            jnp.sum(masked * block_value * block_value),
            jnp.sum(masked * attn_branch * attn_branch),
            jnp.sum(masked * mlp_branch * mlp_branch),
            jnp.sum(own_valid),
        ]
    )
    grad_out = cotangent.astype(jnp.float32) * masked
    grad_gate_mlp = grad_out * reduced
    gradient_narrowed = (gate_mlp * grad_out).astype(jnp.bfloat16)
    reduce_weight_grad = jnp.einsum(
        "mhg,mhn->gn", gelu_activations, gradient_narrowed, preferred_element_type=jnp.float32
    )
    reduce_bias_grad = jnp.sum(gradient_narrowed.astype(jnp.float32), axis=(0, 1))
    grad_activated = jnp.einsum(
        "kav,cv->kac", gradient_narrowed, narrow_weight, preferred_element_type=jnp.float32
    )
    gradient_widened = jax.vjp(gelu_tanh, expanded)[1](grad_activated)[0].astype(jnp.bfloat16)
    expand_weight_grad = jnp.einsum(
        "cqe,cqr->er", second_normed_tokens, gradient_widened, preferred_element_type=jnp.float32
    )
    expand_bias_grad = jnp.sum(gradient_widened.astype(jnp.float32), axis=(0, 1))
    grad_normed_two = jnp.einsum(
        "yma,ja->ymj", gradient_widened, widen_weight, preferred_element_type=jnp.float32
    )
    second_back = jax.vjp(norm_modulate, middle, second_gain, shift_mlp, scale_mlp)[1]
    grad_middle_norm, second_gain_grad, grad_shift_mlp, grad_scale_mlp = second_back(
        grad_normed_two
    )
    grad_middle = grad_out + grad_middle_norm
    grad_gate_attn = grad_middle * projected
    gradient_attention_projected = (gate_attn * grad_middle).astype(jnp.bfloat16)
    output_weight_grad = jnp.einsum(
        "grm,gra->ma",
        attention_result_narrow,
        gradient_attention_projected,
        preferred_element_type=jnp.float32,
    )
    grad_attended = (
        jnp.einsum(
            "yzq,rq->yzr",
            gradient_attention_projected,
            attention_output_matrix,
            preferred_element_type=jnp.float32,
        )
        .astype(jnp.bfloat16)
        .reshape(four_dims)
    )

    def attend_back(inputs):
        queries, keys, values, key_mask, log_rows, grad_rows = inputs
        scores = (
            jnp.einsum("qhd,khd->hqk", queries, keys, preferred_element_type=jnp.float32)
            * score_scale
        )
        scores = jnp.where(key_mask[None], scores, negative)
        probability = jnp.exp(scores - log_rows[..., None])
        grad_values = jnp.einsum(
            "hqk,qhd->khd",
            probability.astype(jnp.bfloat16),
            grad_rows,
            preferred_element_type=jnp.float32,
        )
        grad_prob = jnp.einsum(
            "qhd,khd->hqk", grad_rows, values, preferred_element_type=jnp.float32
        )
        row_delta = jnp.sum(grad_prob * probability, axis=-1, keepdims=True)
        grad_scores = (probability * (grad_prob - row_delta)).astype(jnp.bfloat16)
        grad_queries = (
            jnp.einsum("hqk,khd->qhd", grad_scores, keys, preferred_element_type=jnp.float32)
            * score_scale
        )
        grad_keys = (
            jnp.einsum("hqk,qhd->khd", grad_scores, queries, preferred_element_type=jnp.float32)
            * score_scale
        )
        return (
            grad_queries,
            grad_keys.reshape(slot_rows, width),
            grad_values.reshape(slot_rows, width),
        )

    grad_query_rot, grad_key_part, grad_value_part = lax.map(
        attend_back, (query_rot, all_keys, all_values, allowed, log_total, grad_attended)
    )
    grad_key_rot, grad_value = (
        lax.psum_scatter(
            grad_key_part.astype(jnp.bfloat16), "seq", scatter_dimension=1, tiled=True
        ).astype(jnp.float32),
        lax.psum_scatter(
            grad_value_part.astype(jnp.bfloat16), "seq", scatter_dimension=1, tiled=True
        ).astype(jnp.float32),
    )
    grad_query = turn_back(grad_query_rot)[0].reshape(slot_count, own_rows, width)
    grad_key = turn_back(grad_key_rot.reshape(four_dims))[0].reshape(slot_count, own_rows, width)
    gradient_query_key_value = jnp.concatenate([grad_query, grad_key, grad_value], axis=-1).astype(
        jnp.bfloat16
    )
    triple_weight_grad = jnp.einsum(
        "cqe,cqr->er",
        first_normed_tokens,
        gradient_query_key_value,
        preferred_element_type=jnp.float32,
    )
    grad_normed_one = jnp.einsum(
        "yma,ja->ymj",
        gradient_query_key_value,
        query_key_value_weight,
        preferred_element_type=jnp.float32,
    )
    first_back = jax.vjp(norm_modulate, residual, first_gain, shift_attn, scale_attn)[1]
    grad_residual, first_gain_grad, grad_shift_attn, grad_scale_attn = first_back(grad_normed_one)
    input_grad = (grad_middle + grad_residual).astype(jnp.bfloat16)
    grad_tokens = jnp.concatenate(
        [
            grad_shift_attn,
            grad_scale_attn,
            grad_gate_attn,
            grad_shift_mlp,
            grad_scale_mlp,
            grad_gate_mlp,
        ],
        axis=-1,
    )
    grad_modulation = jnp.einsum(
        "slm,slf->smf",
        own_member,
        grad_tokens,
        precision=highest,
        preferred_element_type=jnp.float32,
    )
    modulation_weight_grad = jnp.einsum(
        "smc,smf->cf",
        condition.astype(jnp.float32),
        grad_modulation,
        precision=highest,
        preferred_element_type=jnp.float32,
    )
    modulation_bias_grad = jnp.sum(grad_modulation, axis=(0, 1))
    vectors = [
        first_gain_grad,
        modulation_bias_grad,
        second_gain_grad,
        expand_bias_grad,
        reduce_bias_grad,
        stat_terms,
    ]
    flat_small = jnp.concatenate(vectors)
    small_rows = -(-flat_small.shape[0] // 1024) * 8
    flat_small = jnp.pad(flat_small, (0, small_rows * 128 - flat_small.shape[0]))
    groups = 2**GROUP_BITS
    bf16 = jnp.bfloat16
    expand_part = expand_weight_grad.T.astype(bf16).reshape(groups, -1, 2, LANES).transpose(0, 2, 1, 3)
    reduce_part = reduce_weight_grad.T.astype(bf16).reshape(groups, -1, 2, 4, LANES)
    reduce_part = reduce_part.transpose(0, 2, 3, 1, 4).reshape(groups, 2, -1, LANES)
    output_part = output_weight_grad.T.astype(bf16).reshape(groups, -1, 2, LANES).transpose(0, 2, 1, 3)
    triple_part = triple_weight_grad.T.astype(bf16).reshape(groups, -1, 2, LANES).transpose(0, 2, 1, 3)
    mod_part = modulation_weight_grad.T.astype(bf16).reshape(groups, 6, -1, 2, LANES // 6)
    mod_part = mod_part.transpose(0, 3, 2, 1, 4).reshape(groups, 2, -1, LANES)
    parts = jnp.concatenate([expand_part, reduce_part, output_part, triple_part, mod_part], axis=2)
    block_sum, summed_small = reduce_everywhere(parts, flat_small.reshape(small_rows, 128))
    summed_small = summed_small.reshape(-1)
    small_results = []
    cursor = 0
    for vector in vectors:
        small_results.append(summed_small[cursor : cursor + vector.shape[0]])
        cursor = cursor + vector.shape[0]
    dp_size = lax.axis_size("dp")
    cuts = []
    cursor = 0
    for part in (expand_part, reduce_part, output_part, triple_part, mod_part):
        cuts.append(block_sum[cursor : cursor + part.shape[2]])
        cursor = cursor + part.shape[2]
    expand_block = scatter_rest(cuts[0], dp_size).T
    reduce_block = cuts[1].reshape(4, -1, LANES).transpose(1, 0, 2).reshape(-1, 4 * LANES)
    reduce_block = scatter_rest(reduce_block, dp_size).T
    output_block = scatter_rest(cuts[2], dp_size).T
    triple_block = scatter_rest(cuts[3], dp_size).T
    mod_block = cuts[4].reshape(-1, 6, LANES // 6).transpose(1, 0, 2).reshape(-1, LANES // 6)
    mod_block = scatter_rest(mod_block, dp_size).T
    matrix_parts = (mod_block, triple_block, output_block, expand_block, reduce_block)
    totals = small_results[5]
    masked_rms = jnp.sqrt(totals[:3] / (totals[3] * width))
    return (
        block_out,
        input_grad,
        small_results[0],
        matrix_parts[0],
        small_results[1],
        matrix_parts[1],
        matrix_parts[2],
        small_results[2],
        matrix_parts[3],
        small_results[3],
        matrix_parts[4],
        small_results[4],
        masked_rms,
    )


def solution(mesh):
    in_specs = (
        P("dp", "seq", None),
        P("dp", None),
        P("dp", None),
        P("dp", None),
        P(),
        P(),
        P(),
        P(),
        P(),
        P(),
        P(),
        P(),
        P(),
        P(),
        P("dp", "seq", None),
    )
    out_specs = (
        P("dp", "seq", None),
        P("dp", "seq", None),
        P(),
        P("seq", "dp"),
        P(),
        P("seq", "dp"),
        P("seq", "dp"),
        P(),
        P("seq", "dp"),
        P(),
        P("seq", "dp"),
        P(),
        P(),
    )
    return jax.shard_map(local, mesh=mesh, in_specs=in_specs, out_specs=out_specs, check_vma=False)
```

```python
import functools
import math

import jax
import jax.numpy as jnp
import numpy as np
from jax import lax
from jax.experimental import pallas as pl
from jax.experimental.pallas import tpu as pltpu
from jax.sharding import PartitionSpec as P

HEADS = 12
BLOCK = 128
MAX_SEQUENCES = 8
SEGMENT_LANE = 40
MASKED = -1000000000.0
LANES = 384
GROUP_BITS = 4
MESH_ID = pl.DeviceIdType.MESH
F32, BF16 = jnp.float32, jnp.bfloat16

ROTARY_COS, ROTARY_SIN, BLOCK_COS, BLOCK_SIN = 0, 128, 256, 264
HIGH_COS, HIGH_SIN, LOW_COS, LOW_SIN, TABLE_ROWS = 272, 304, 336, 368, 400

FIRST_GAIN, MOD_BIAS, SECOND_GAIN, EXPAND_BIAS, REDUCE_BIAS, STATS, SMALL_ROWS = 0, 1, 7, 8, 12, 13, 16


def angle_table():
    lane = np.arange(128)
    rotary = np.exp((lane % 32) * (-2.0 * math.log(10000.0) / 64))
    timing = np.exp((lane % 64) * (-math.log(10000.0) / 64))
    steps = np.arange(128)[:, None]
    angles = [
        (np.cos, steps * rotary), (np.sin, steps * rotary),
        (np.cos, steps[:8] * 128 * rotary), (np.sin, steps[:8] * 128 * rotary),
        (np.cos, steps[:32] * 32 * timing), (np.sin, steps[:32] * 32 * timing),
        (np.cos, steps[:32] * timing), (np.sin, steps[:32] * timing),
    ]
    return np.concatenate([fn(angle) for fn, angle in angles]).astype(np.float32)


def dot(left, right):
    return jnp.dot(left, right, preferred_element_type=F32)


def dot_nt(left, right):
    return lax.dot_general(left, right, (((1,), (1,)), ((), ())), preferred_element_type=F32)


def dot_tn(left, right):
    return lax.dot_general(left, right, (((0,), (0,)), ((), ())), preferred_element_type=F32)


def lane_iota(shape):
    return lax.broadcasted_iota(jnp.int32, shape, len(shape) - 1)


def row_iota(shape):
    return lax.broadcasted_iota(jnp.int32, shape, 0)


def block_place(segments, lengths, block):
    segment = segments[0, block * BLOCK]
    before = jnp.int32(0)
    for other in range(segments.shape[1] // BLOCK):
        same = (segments[0, other * BLOCK] == segment) & (other < block)
        before = before + jnp.where(same, 1, 0)
    return segment, before, lengths[0, segment] - before * BLOCK


def rotary_block(table, before):
    cos_row, sin_row = table[pl.ds(ROTARY_COS, 128), :], table[pl.ds(ROTARY_SIN, 128), :]
    cos_block = table[pl.ds(BLOCK_COS + before, 1), :]
    sin_block = table[pl.ds(BLOCK_SIN + before, 1), :]
    cosine = cos_row * cos_block - sin_row * sin_block
    sine = sin_row * cos_block + cos_row * sin_block
    first_half = lane_iota(sine.shape) % 64 < 32
    return cosine, jnp.where(first_half, -sine, sine)


def turn(values, cosine, sine):
    first_half = lane_iota(values.shape) % 64 < 32
    swapped = jnp.where(first_half, pltpu.roll(values, 96, 1), pltpu.roll(values, 32, 1))
    return values * cosine + swapped * sine


def mean_of(values):
    return jnp.mean(values, axis=-1, keepdims=True)


def split_three(values):
    first = values.astype(BF16)
    rest = values - first.astype(F32)
    second = rest.astype(BF16)
    third = (rest - second.astype(F32)).astype(BF16)
    place = lane_iota(values.shape) % 3
    picked = jnp.where(place == 0, first.astype(F32), jnp.where(place == 1, second.astype(F32), third.astype(F32)))
    return picked.astype(BF16)


def forward_kernel(
    segments, lengths, times, hidden, table, first_gain, mod_weight, mod_bias, weight,
    normed, queries, keys, values, attended, query_features, key_features, modulation, condition,
    other_hidden, turned_values, out_t, peak, total, send_sem, recv_sem,
):
    tokens, width = hidden.shape
    blocks = tokens // BLOCK
    seq = lax.axis_index("seq")
    partner = (lax.axis_index("dp"), 1 - seq)
    barrier = pltpu.get_barrier_semaphore()
    pl.semaphore_signal(barrier, inc=1, device_id=partner, device_id_type=MESH_ID)
    pl.semaphore_wait(barrier, 1)
    exchange = pltpu.make_async_remote_copy(
        hidden, other_hidden, send_sem, recv_sem, device_id=partner, device_id_type=MESH_ID
    )
    exchange.start()

    places = []
    for number in range(2 * blocks):
        block = (seq if number < blocks else 1 - seq) * blocks + number % blocks
        places.append(block_place(segments, lengths, block))
        time = times[0, places[number][0]]
        high, low = time // 32, time % 32
        cos_high, sin_high = table[pl.ds(HIGH_COS + high, 1), :], table[pl.ds(HIGH_SIN + high, 1), :]
        cos_low, sin_low = table[pl.ds(LOW_COS + low, 1), :], table[pl.ds(LOW_SIN + low, 1), :]
        cosine = cos_high * cos_low - sin_high * sin_low
        sine = sin_high * cos_low + cos_high * sin_low
        row = jnp.where(lane_iota(cosine.shape) < 64, cosine, sine)
        condition[pl.ds(number, 1), :] = row.astype(BF16).astype(F32)
    modulation[...] = dot(condition[...].astype(BF16), mod_weight[...]) + mod_bias[...]

    lane = lane_iota((BLOCK, 128))
    row = row_iota((BLOCK, 128))

    for part in range(2):
        source = hidden if part == 0 else other_hidden
        if part == 1:
            exchange.wait_recv()
        turns = []
        for number in range(blocks):
            rows = pl.ds(number * BLOCK, BLOCK)
            segment, before, valid_count = places[part * blocks + number]
            turns.append(rotary_block(table, before))
            mine = lane == SEGMENT_LANE + segment
            in_lanes = (lane >= SEGMENT_LANE) & (lane < SEGMENT_LANE + MAX_SEQUENCES)
            blocked = in_lanes & jnp.logical_not(mine & (row < valid_count))
            key_features[part, rows, :] = jnp.where(blocked, MASKED, 0.0).astype(BF16)
            if part == 0:
                query_features[rows, :] = jnp.where(mine, 1.0, 0.0).astype(BF16)
            mod_row = pl.ds(part * blocks + number, 1)
            shift, scale = modulation[mod_row, pl.ds(0, width)], modulation[mod_row, pl.ds(width, width)]
            value = source[rows, :].astype(F32)
            centered = value - mean_of(value)
            spread = mean_of(centered * centered)
            line = centered * lax.rsqrt(spread + 1e-05) * first_gain[...]
            result = (line * (1.0 + scale) + shift).astype(BF16)
            if part == 0:
                normed[rows, :] = result
            else:
                other_hidden[rows, :] = result
        normed_source = normed if part == 0 else other_hidden
        for tile in range(3 * width // LANES):
            which, first = divmod(tile * LANES, width)
            product = dot(normed_source[...], weight[:, pl.ds(tile * LANES, LANES)])
            target = (queries, keys, values)[which]
            for number in range(blocks):
                cosine, sine = turns[number]
                for pair in range(LANES // 128):
                    piece = product[number * BLOCK : (number + 1) * BLOCK, pair * 128 : (pair + 1) * 128]
                    if which < 2:
                        piece = turn(piece, cosine, sine)
                    if which == 0:
                        piece = piece.astype(BF16).astype(F32) * 0.125
                    target[part, pl.ds(number * BLOCK, BLOCK), pl.ds(first + pair * 128, 128)] = piece.astype(BF16)
        turned_values[...] = jnp.transpose(values[part])

        def attend(pair, carry):
            lanes = pl.ds(pl.multiple_of(pair * 128, 128), 128)
            query_pair, key_pair = queries[0, :, lanes], keys[part, :, lanes]
            left = jnp.concatenate([key_pair, key_features[part]], axis=1)
            pair_lane = lane_iota(query_pair.shape)
            for half in range(2):
                head = pair * 2 + half
                head_rows = pl.ds(pl.multiple_of(head * 64, 64), 64)
                one_row = pl.ds(head, 1)
                query = jnp.where((pair_lane < 64) == (half == 0), query_pair, jnp.zeros_like(query_pair))
                scores = dot_nt(left, jnp.concatenate([query, query_features[...]], axis=1))
                top = jnp.max(scores, axis=0, keepdims=True)
                if part == 1:
                    top = jnp.maximum(top, peak[one_row, :])
                weights = jnp.exp(scores - top)
                summed = jnp.sum(weights, axis=0, keepdims=True)
                mixed = dot(turned_values[head_rows, :], weights.astype(BF16))
                if part == 0:
                    out_t[head_rows, :] = mixed
                    total[one_row, :] = summed
                    peak[one_row, :] = top
                else:
                    rescale = jnp.exp(peak[one_row, :] - top)
                    summed = summed + rescale * total[one_row, :]
                    out_t[head_rows, :] = (out_t[head_rows, :] * rescale + mixed) * (1.0 / summed)
                    peak[one_row, :] = top + jnp.log(summed)
            return carry

        lax.fori_loop(0, HEADS // 2, attend, 0)

    attended[...] = jnp.transpose(out_t[...].astype(BF16))
    log_rows = jnp.concatenate(
        [jnp.broadcast_to(peak[pl.ds(head, 1), :], (3, tokens)) for head in range(HEADS)]
        + [jnp.zeros((128 - 3 * HEADS, tokens), F32)], axis=0,
    )
    query_features[...] = query_features[...] + split_three(jnp.transpose(log_rows))
    exchange.wait_send()


def forward(segments, lengths, times, hidden, table, first_gain, mod_weight, mod_bias, weight):
    tokens, width = hidden.shape
    blocks = 2 * tokens // BLOCK
    half = jax.ShapeDtypeStruct((tokens, width), BF16)
    both = jax.ShapeDtypeStruct((2, tokens, width), BF16)
    smem, vmem = pl.BlockSpec(memory_space=pltpu.SMEM), pl.BlockSpec(memory_space=pltpu.VMEM)
    return pl.pallas_call(
        forward_kernel,
        out_shape=(
            half, both, both, both, half,
            jax.ShapeDtypeStruct((tokens, 128), BF16),
            jax.ShapeDtypeStruct((2, tokens, 128), BF16),
            jax.ShapeDtypeStruct((blocks, 6 * width), F32),
            jax.ShapeDtypeStruct((blocks, 128), F32),
        ),
        in_specs=[smem] * 3 + [vmem] * 6,
        out_specs=(vmem,) * 9,
        scratch_shapes=[
            pltpu.VMEM((tokens, width), BF16),
            pltpu.VMEM((width, tokens), BF16),
            pltpu.VMEM((width, tokens), F32),
            pltpu.VMEM((16, tokens), F32),
            pltpu.VMEM((16, tokens), F32),
            pltpu.SemaphoreType.DMA,
            pltpu.SemaphoreType.DMA,
        ],
        compiler_params=pltpu.CompilerParams(
            collective_id=1, has_side_effects=True, vmem_limit_bytes=56 << 20
        ),
    )(segments, lengths, times, hidden, table, first_gain, mod_weight, mod_bias, weight)


TILE = 384


def mlp_kernel(
    segments, lengths, hidden, attended, cotangent, modulation, second_gain, expand_bias, reduce_bias,
    out_weight_hbm, widen_hbm, narrow_hbm,
    block_out, grad_middle, grad_attended, delta_features, mod_grads, small, expand_hbm, reduce_hbm, output_hbm,
    out_weight, widen, narrow, expand_part, reduce_part, output_part,
    projected, middle, normal, spread_row, normed, slope, activated, reduced, grad_low, grad_low_t, grad_normed,
    load_sem, store_sem,
):
    tokens, width = hidden.shape
    hidden_units = widen.shape[1]
    tiles = hidden_units // TILE
    blocks = tokens // BLOCK
    seq = lax.axis_index("seq")
    loads = [
        pltpu.make_async_copy(source, target, load_sem.at[number])
        for number, (source, target) in enumerate(
            ((out_weight_hbm, out_weight), (widen_hbm, widen), (narrow_hbm, narrow))
        )
    ]
    for load in loads:
        load.start()
    row = row_iota((BLOCK, 1))
    keep = []
    for number in range(blocks):
        valid_count = block_place(segments, lengths, seq * blocks + number)[2]
        keep.append(jnp.where(row < valid_count, 1.0, 0.0))

    def mod_part(number, part):
        return modulation[pl.ds(number, 1), pl.ds(part * width, width)]

    loads[0].wait()
    for first in range(0, width, 256):
        lanes = pl.ds(first, 256)
        projected[:, lanes] = dot(attended[...], out_weight[:, lanes])
    branch_sum = jnp.zeros((1, width), F32)
    for number in range(blocks):
        rows = pl.ds(number * BLOCK, BLOCK)
        branch = mod_part(number, 2) * projected[rows, :]
        branch_sum = branch_sum + jnp.sum(keep[number] * branch * branch, axis=0, keepdims=True)
        value = hidden[rows, :].astype(F32) + branch
        middle[rows, :] = value
        centered = value - mean_of(value)
        inverse = lax.rsqrt(mean_of(centered * centered) + 1e-05)
        normal[rows, :] = centered * inverse
        spread_row[rows, :] = jnp.broadcast_to(inverse, (BLOCK, 128))
        line = normal[rows, :] * second_gain[...]
        normed[rows, :] = (line * (1.0 + mod_part(number, 4)) + mod_part(number, 3)).astype(BF16)

    reduced[...] = jnp.zeros_like(reduced)
    loads[1].wait()
    loads[2].wait()

    def ahead(tile):
        lanes = pl.ds(pl.multiple_of(tile * TILE, TILE), TILE)
        u = dot(normed[...], widen[:, lanes]) + expand_bias[:, lanes]
        square = u * u
        tanh = jnp.tanh(u * (0.7978845608028654 + 0.7978845608028654 * 0.044715 * square))
        half_sum = 0.5 + 0.5 * tanh
        active = (u * half_sum).astype(BF16)
        inner = 0.7978845608028654 + 3.0 * 0.7978845608028654 * 0.044715 * square
        slope[:, lanes] = half_sum + (0.5 * u) * (1.0 - tanh * tanh) * inner
        activated[:, lanes] = active
        reduced[...] += dot(active, narrow[lanes, :])

    def ahead_two(step, carry):
        ahead(2 * step)
        ahead(2 * step + 1)
        return carry

    lax.fori_loop(0, tiles // 2, ahead_two, 0)

    value_sum = jnp.zeros((1, width), F32)
    mlp_sum = jnp.zeros((1, width), F32)
    bias_sum = jnp.zeros((1, width), F32)
    for number in range(blocks):
        rows = pl.ds(number * BLOCK, BLOCK)
        gate = mod_part(number, 5)
        full = reduced[rows, :] + reduce_bias[...]
        branch = gate * full
        value = middle[rows, :] + branch
        block_out[rows, :] = value.astype(BF16)
        value_sum = value_sum + jnp.sum(keep[number] * value * value, axis=0, keepdims=True)
        mlp_sum = mlp_sum + jnp.sum(keep[number] * branch * branch, axis=0, keepdims=True)
        grad_out = cotangent[rows, :].astype(F32) * keep[number]
        mod_grads[pl.ds(number, 1), pl.ds(3 * width, width)] = jnp.sum(grad_out * full, axis=0, keepdims=True)
        low = (gate * grad_out).astype(BF16)
        grad_low[rows, :] = low
        bias_sum = bias_sum + jnp.sum(low.astype(F32), axis=0, keepdims=True)
    grad_low_t[...] = jnp.transpose(grad_low[...])
    grad_normed[...] = jnp.zeros_like(grad_normed)
    small[...] = jnp.zeros_like(small)
    small[pl.ds(REDUCE_BIAS, 1), :] = bias_sum

    def stores(tile):
        expand_copy = pltpu.make_async_copy(
            expand_part.at[pl.ds(2 * tile, 2)], expand_hbm.at[pl.ds(2 * tile, 2)], store_sem.at[0, tile]
        )
        reduce_copy = pltpu.make_async_copy(
            reduce_part.at[:, tile // 4, tile % 4], reduce_hbm.at[:, tile // 4, tile % 4], store_sem.at[1, tile]
        )
        return expand_copy, reduce_copy

    def back(tile):
        lanes = pl.ds(pl.multiple_of(tile * TILE, TILE), TILE)
        grad_active = dot_nt(grad_low[...], narrow[lanes, :])
        grad_wide = (grad_active * slope[:, lanes]).astype(BF16)
        slope[pl.ds(0, 1), lanes] = jnp.sum(grad_wide.astype(F32), axis=0, keepdims=True)
        grad_normed[...] += dot_nt(grad_wide, widen[:, lanes])
        expand_t = dot_tn(grad_wide, normed[...]).astype(BF16)
        for group in range(2):
            for side in range(2):
                expand_part[2 * tile + group, side] = expand_t[
                    group * 192 : group * 192 + 192, side * LANES : side * LANES + LANES
                ]
        reduce_t = dot(grad_low_t[...], activated[:, lanes]).astype(BF16)
        reduce_part[:, tile // 4, tile % 4] = reduce_t.reshape(16, 48, TILE)
        for copy in stores(tile):
            copy.start()

    def back_two(step, carry):
        back(2 * step)
        back(2 * step + 1)
        return carry

    lax.fori_loop(0, tiles // 2, back_two, 0)
    for part in range(hidden_units // width):
        small[pl.ds(EXPAND_BIAS + part, 1), :] = slope[pl.ds(0, 1), pl.ds(part * width, width)]

    gain_sum = jnp.zeros((1, width), F32)
    for number in range(blocks):
        rows = pl.ds(number * BLOCK, BLOCK)
        one = pl.ds(number, 1)
        grad = grad_normed[rows, :]
        line = normal[rows, :] * second_gain[...]
        mod_grads[one, pl.ds(width, width)] = jnp.sum(grad, axis=0, keepdims=True)
        mod_grads[one, pl.ds(2 * width, width)] = jnp.sum(grad * line, axis=0, keepdims=True)
        grad_line = grad * (1.0 + mod_part(number, 4))
        gain_sum = gain_sum + jnp.sum(grad_line * normal[rows, :], axis=0, keepdims=True)
        grad_normal = grad_line * second_gain[...]
        along = mean_of(grad_normal * normal[rows, :])
        term = (grad_normal - mean_of(grad_normal) - normal[rows, :] * along) * spread_row[rows, :1]
        total = cotangent[rows, :].astype(F32) * keep[number] + term
        grad_middle[rows, :] = total
        mod_grads[one, pl.ds(0, width)] = jnp.sum(total * projected[rows, :], axis=0, keepdims=True)
        grad_low[rows, :] = (mod_part(number, 2) * total).astype(BF16)
    small[pl.ds(SECOND_GAIN, 1), :] = gain_sum

    for first in range(0, width, TILE):
        output_t = dot_tn(grad_low[:, pl.ds(first, TILE)], attended[...]).astype(BF16)
        for group in range(TILE // 48):
            for side in range(2):
                output_part[first // 48 + group, side] = output_t[
                    group * 48 : group * 48 + 48, side * LANES : side * LANES + LANES
                ]
    output_copy = pltpu.make_async_copy(output_part, output_hbm, load_sem.at[0])
    output_copy.start()
    for first in range(0, width, 256):
        grad_attended[:, pl.ds(first, 256)] = dot_nt(
            grad_low[...], out_weight[pl.ds(first, 256), :]
        ).astype(BF16)
    head_lane = row_iota((width, 128)) // 64 == lane_iota((width, 128)) // 3
    chooser = jnp.where(head_lane & (lane_iota((width, 128)) < 3 * HEADS), 1.0, 0.0).astype(BF16)
    for number in range(blocks):
        rows = pl.ds(number * BLOCK, BLOCK)
        product = grad_attended[rows, :].astype(F32) * attended[rows, :].astype(F32)
        upper = product.astype(BF16)
        lower = (product - upper.astype(F32)).astype(BF16)
        delta_features[rows, :] = split_three(dot(upper, chooser) + dot(lower, chooser))

    lane = lane_iota((1, width))
    counts = jnp.zeros((1, 1), F32)
    for number in range(blocks):
        counts = counts + jnp.sum(keep[number], axis=0, keepdims=True)
    sums = [jnp.sum(term, axis=1, keepdims=True) for term in (value_sum, branch_sum, mlp_sum)] + [counts]
    stats = jnp.zeros((1, width), F32)
    for place, term in enumerate(sums):
        stats = jnp.where(lane == place, term, stats)
    small[pl.ds(STATS, 1), :] = stats

    def drain(tile, carry):
        for copy in stores(tile):
            copy.wait()
        return carry

    lax.fori_loop(0, tiles, drain, 0)
    output_copy.wait()


def mlp(segments, lengths, hidden, attended, cotangent, modulation, second_gain, expand_bias, reduce_bias, out_weight, widen, narrow):
    tokens, width = hidden.shape
    units = widen.shape[1]
    smem, vmem = pl.BlockSpec(memory_space=pltpu.SMEM), pl.BlockSpec(memory_space=pltpu.VMEM)
    hbm = pl.BlockSpec(memory_space=pl.ANY)
    groups = 2**GROUP_BITS
    expand_shape = (groups, 2, units // groups, LANES)
    reduce_shape = (groups, 2, 4, width // groups, LANES)
    output_shape = (groups, 2, width // groups, LANES)
    wide, half = (tokens, units), (tokens, width)
    return pl.pallas_call(
        mlp_kernel,
        out_shape=(
            jax.ShapeDtypeStruct(half, BF16),
            jax.ShapeDtypeStruct(half, F32),
            jax.ShapeDtypeStruct(half, BF16),
            jax.ShapeDtypeStruct((tokens, 128), BF16),
            jax.ShapeDtypeStruct((tokens // BLOCK, 4 * width), F32),
            jax.ShapeDtypeStruct((SMALL_ROWS, width), F32),
            jax.ShapeDtypeStruct(expand_shape, BF16),
            jax.ShapeDtypeStruct(reduce_shape, BF16),
            jax.ShapeDtypeStruct(output_shape, BF16),
        ),
        in_specs=[smem] * 2 + [vmem] * 7 + [hbm] * 3,
        out_specs=(vmem,) * 6 + (hbm,) * 3,
        scratch_shapes=[
            pltpu.VMEM(out_weight.shape, BF16),
            pltpu.VMEM(widen.shape, BF16),
            pltpu.VMEM(narrow.shape, BF16),
            pltpu.VMEM(expand_shape, BF16),
            pltpu.VMEM(reduce_shape, BF16),
            pltpu.VMEM(output_shape, BF16),
            pltpu.VMEM(half, F32),
            pltpu.VMEM(half, F32),
            pltpu.VMEM(half, F32),
            pltpu.VMEM((tokens, 128), F32),
            pltpu.VMEM(half, BF16),
            pltpu.VMEM(wide, F32),
            pltpu.VMEM(wide, BF16),
            pltpu.VMEM(half, F32),
            pltpu.VMEM(half, BF16),
            pltpu.VMEM((width, tokens), BF16),
            pltpu.VMEM(half, F32),
            pltpu.SemaphoreType.DMA((3,)),
            pltpu.SemaphoreType.DMA((2, units // TILE)),
        ],
        compiler_params=pltpu.CompilerParams(vmem_limit_bytes=58 << 20),
    )(segments, lengths, hidden, attended, cotangent, modulation, second_gain, expand_bias, reduce_bias, out_weight, widen, narrow)


def backward_kernel(
    segments, lengths, hidden, normed, queries, keys, values, query_features, key_features, grad_attended, delta_features,
    grad_middle, modulation, mod_grads, small_in, table, first_gain, weight,
    input_grad, small, triple_part, mod_rows,
    other_grad, other_delta, other_features, keys_t, grad_query_t, grad_key, grad_value, grad_triple, grad_normed,
    send_sem, recv_sem,
):
    tokens, width = hidden.shape
    blocks = tokens // BLOCK
    seq = lax.axis_index("seq")
    partner = (lax.axis_index("dp"), 1 - seq)
    barrier = pltpu.get_barrier_semaphore()
    pl.semaphore_signal(barrier, inc=1, device_id=partner, device_id_type=MESH_ID)
    pl.semaphore_wait(barrier, 1)
    exchanges = [
        pltpu.make_async_remote_copy(
            source, target, send_sem.at[number], recv_sem.at[number], device_id=partner, device_id_type=MESH_ID
        )
        for number, (source, target) in enumerate(
            ((grad_attended, other_grad), (delta_features, other_delta), (query_features, other_features))
        )
    ]
    for exchange in exchanges:
        exchange.start()

    for part in range(2):
        keys_t[part] = jnp.transpose(keys[part])

    def own_queries(pair, carry):
        lanes = pl.ds(pl.multiple_of(pair * 128, 128), 128)
        query_pair, grad_pair = queries[0, :, lanes], grad_attended[:, lanes]
        pair_lane = lane_iota(query_pair.shape)
        grad_k = jnp.zeros((tokens, 128), F32)
        grad_v = jnp.zeros((tokens, 128), F32)
        for half in range(2):
            head = pair * 2 + half
            head_rows = pl.ds(pl.multiple_of(head * 64, 64), 64)
            mine = (pair_lane < 64) == (half == 0)
            query = jnp.where(mine, query_pair, jnp.zeros_like(query_pair))
            grad = jnp.where(mine, grad_pair, jnp.zeros_like(grad_pair))
            right_scores = jnp.concatenate([query, query_features[...]], axis=1)
            right_grads = jnp.concatenate([grad, delta_features[...]], axis=1)
            head_lanes = (pair_lane >= 3 * head) & (pair_lane < 3 * head + 3)
            grad_q = jnp.zeros((64, tokens), F32)
            for part in range(2):
                features = jnp.where(head_lanes, jnp.full_like(query_pair, -1.0), key_features[part])
                scores = dot_nt(jnp.concatenate([keys[part, :, lanes], features], axis=1), right_scores)
                weights = jnp.exp(scores)
                grad_weights = dot_nt(jnp.concatenate([values[part, :, lanes], features], axis=1), right_grads)
                grad_scores = (weights * grad_weights).astype(BF16)
                if part == 0:
                    grad_v = grad_v + dot(weights.astype(BF16), grad)
                    grad_k = grad_k + dot(grad_scores, query)
                grad_q = grad_q + dot(keys_t[part, head_rows, :], grad_scores)
            grad_query_t[head_rows, :] = grad_q
        grad_key[:, lanes] = grad_k
        grad_value[:, lanes] = grad_v
        return carry

    lax.fori_loop(0, HEADS // 2, own_queries, 0)
    for exchange in exchanges:
        exchange.wait_recv()

    def other_queries(pair, carry):
        lanes = pl.ds(pl.multiple_of(pair * 128, 128), 128)
        query_pair, grad_pair = queries[1, :, lanes], other_grad[:, lanes]
        pair_lane = lane_iota(query_pair.shape)
        grad_k = grad_key[:, lanes]
        grad_v = grad_value[:, lanes]
        for half in range(2):
            head = pair * 2 + half
            mine = (pair_lane < 64) == (half == 0)
            query = jnp.where(mine, query_pair, jnp.zeros_like(query_pair))
            grad = jnp.where(mine, grad_pair, jnp.zeros_like(grad_pair))
            head_lanes = (pair_lane >= 3 * head) & (pair_lane < 3 * head + 3)
            features = jnp.where(head_lanes, jnp.full_like(query_pair, -1.0), key_features[0])
            scores = dot_nt(
                jnp.concatenate([keys[0, :, lanes], features], axis=1),
                jnp.concatenate([query, other_features[...]], axis=1),
            )
            weights = jnp.exp(scores)
            grad_weights = dot_nt(
                jnp.concatenate([values[0, :, lanes], features], axis=1),
                jnp.concatenate([grad, other_delta[...]], axis=1),
            )
            grad_scores = (weights * grad_weights).astype(BF16)
            grad_v = grad_v + dot(weights.astype(BF16), grad)
            grad_k = grad_k + dot(grad_scores, query)
        grad_key[:, lanes] = grad_k
        grad_value[:, lanes] = grad_v
        return carry

    lax.fori_loop(0, HEADS // 2, other_queries, 0)

    grad_normed[...] = jnp.transpose(grad_query_t[...])
    for number in range(blocks):
        rows = pl.ds(number * BLOCK, BLOCK)
        before = block_place(segments, lengths, seq * blocks + number)[1]
        cosine, sine = rotary_block(table, before)
        for pair in range(HEADS // 2):
            lanes = pl.ds(pair * 128, 128)
            grad_triple[rows, lanes] = (turn(grad_normed[rows, lanes], cosine, -sine) * 0.125).astype(BF16)
            grad_triple[rows, pl.ds(width + pair * 128, 128)] = turn(grad_key[rows, lanes], cosine, -sine).astype(BF16)
        grad_triple[rows, pl.ds(2 * width, width)] = grad_value[rows, :].astype(BF16)

    for part in range(2):
        triple_t = dot_tn(grad_triple[:, pl.ds(part * 1152, 1152)], normed[...]).astype(BF16)
        for group in range(8):
            for side in range(2):
                triple_part[part * 8 + group, side] = triple_t[
                    group * 144 : group * 144 + 144, side * LANES : side * LANES + LANES
                ]
    grad_normed[...] = jnp.zeros_like(grad_normed)
    for first in range(0, 3 * width, width):
        lanes = pl.ds(first, width)
        grad_normed[...] += dot_nt(grad_triple[:, lanes], weight[:, lanes])

    small[...] = small_in[...]
    gain_sum = jnp.zeros((1, width), F32)
    for number in range(blocks):
        rows, one = pl.ds(number * BLOCK, BLOCK), pl.ds(number, 1)
        value = hidden[rows, :].astype(F32)
        centered = value - mean_of(value)
        inverse = lax.rsqrt(mean_of(centered * centered) + 1e-05)
        normal = centered * inverse
        grad = grad_normed[rows, :]
        mod_rows[one, pl.ds(0, width)] = jnp.sum(grad, axis=0, keepdims=True)
        mod_rows[one, pl.ds(width, width)] = jnp.sum(grad * (normal * first_gain[...]), axis=0, keepdims=True)
        mod_rows[one, pl.ds(2 * width, 4 * width)] = mod_grads[one, :]
        grad_line = grad * (1.0 + modulation[one, pl.ds(width, width)])
        gain_sum = gain_sum + jnp.sum(grad_line * normal, axis=0, keepdims=True)
        grad_normal = grad_line * first_gain[...]
        along = mean_of(grad_normal * normal)
        term = (grad_normal - mean_of(grad_normal) - normal * along) * inverse
        input_grad[rows, :] = (grad_middle[rows, :] + term).astype(BF16)
    small[pl.ds(FIRST_GAIN, 1), :] = gain_sum
    for part in range(6):
        small[pl.ds(MOD_BIAS + part, 1), :] = jnp.sum(mod_rows[:, pl.ds(part * width, width)], axis=0, keepdims=True)
    for exchange in exchanges:
        exchange.wait_send()


def backward(*args):
    hidden = args[2]
    tokens, width = hidden.shape
    smem, vmem = pl.BlockSpec(memory_space=pltpu.SMEM), pl.BlockSpec(memory_space=pltpu.VMEM)
    groups = 2**GROUP_BITS
    half = (tokens, width)
    return pl.pallas_call(
        backward_kernel,
        out_shape=(
            jax.ShapeDtypeStruct(half, BF16),
            jax.ShapeDtypeStruct((SMALL_ROWS, width), F32),
            jax.ShapeDtypeStruct((groups, 2, 3 * width // groups, LANES), BF16),
            jax.ShapeDtypeStruct((tokens // BLOCK, 6 * width), F32),
        ),
        in_specs=[smem] * 2 + [vmem] * (len(args) - 2),
        out_specs=(vmem,) * 4,
        scratch_shapes=[
            pltpu.VMEM(half, BF16),
            pltpu.VMEM((tokens, 128), BF16),
            pltpu.VMEM((tokens, 128), BF16),
            pltpu.VMEM((2, width, tokens), BF16),
            pltpu.VMEM((width, tokens), F32),
            pltpu.VMEM(half, F32),
            pltpu.VMEM(half, F32),
            pltpu.VMEM((tokens, 3 * width), BF16),
            pltpu.VMEM(half, F32),
            pltpu.SemaphoreType.DMA((3,)),
            pltpu.SemaphoreType.DMA((3,)),
        ],
        compiler_params=pltpu.CompilerParams(
            collective_id=2, has_side_effects=True, vmem_limit_bytes=58 << 20
        ),
    )(*args)


Z2, Z1, Y, CORE, X = 0, 1, 2, 3, 4


def exchange_partner(axis, extra_bits):
    dp, seq = lax.axis_index("dp"), lax.axis_index("seq")
    if axis == X:
        return (dp, 1 - seq)
    return (dp ^ (1 << (GROUP_BITS - 1 - axis + extra_bits)), seq)


def own_bit(axis, extra_bits):
    if axis == X:
        return lax.axis_index("seq")
    return (lax.axis_index("dp") >> (GROUP_BITS - 1 - axis + extra_bits)) & 1


def reduce_tasks(rows):
    streams = (
        (0, 112, (CORE, X, Y, Z1, Z2)),
        (224, 112, (CORE, Y, Z1, X, Z2)),
        (448, 96, (CORE, Z1, X, Y, Z2)),
        (112, 112, (CORE, X, Y, Z1, Z2)),
        (336, 112, (CORE, Y, Z1, X, Z2)),
        (544, 80, (CORE, Z1, X, Y, Z2)),
    )
    return streams


def reduce_kernel(extra_bits, all_bits, parts_ref, small_ref, sum_ref, small_out, acc, got_a, got_b, got_c, got_d, got_e, small_acc, small_got, local_sem, send_sem, recv_sem, small_send, small_recv):
    tasks = reduce_tasks(parts_ref.shape[-2])
    got = (got_a, got_b, got_c, got_d, got_e)
    bits = [own_bit(axis, extra_bits) for axis in range(5)]
    small_partners = [(lax.axis_index("dp"), 1 - lax.axis_index("seq"))] + [
        (lax.axis_index("dp") ^ (1 << bit), lax.axis_index("seq")) for bit in range(all_bits)
    ]
    barrier = pltpu.get_barrier_semaphore()
    for partner in small_partners:
        pl.semaphore_signal(barrier, inc=1, device_id=partner, device_id_type=MESH_ID)
    pl.semaphore_wait(barrier, len(small_partners))

    def region(order, stage, other):
        index = [slice(None)] * 5
        for axis in order[:stage]:
            index[axis] = bits[axis]
        index[order[stage]] = 1 - bits[order[stage]] if other else bits[order[stage]]
        return index

    copies = {}
    local_copies = []
    for number, (first, count, order) in enumerate(tasks):
        keep = pltpu.make_async_copy(
            parts_ref.at[tuple(region(order, 0, False)) + (pl.ds(first, count),)],
            acc.at[:, :, :, :, pl.ds(first, count)],
            local_sem.at[number],
        )
        keep.start()
        local_copies.append(keep)

    def send(number, stage):
        first, count, order = tasks[number]
        index = region(order, stage, True)
        if stage == 0:
            source = parts_ref.at[tuple(index) + (pl.ds(first, count),)]
        else:
            del index[CORE]
            source = acc.at[tuple(index) + (pl.ds(first, count),)]
        target = got[stage].at[(slice(None),) * (4 - stage) + (pl.ds(first, count),)]
        copy = pltpu.make_async_remote_copy(
            source, target, send_sem.at[number, stage], recv_sem.at[number, stage],
            device_id=exchange_partner(order[stage], extra_bits), device_id_type=MESH_ID,
        )
        copy.start()
        copies[number, stage] = copy

    def add(number, stage):
        first, count, order = tasks[number]
        copies[number, stage].wait_recv()
        if stage == 0:
            local_copies[number].wait()
        free = [axis for axis in range(5) if axis not in order[: stage + 1]]

        def one(step, carry):
            index = list(bits)
            got_index = []
            for place, axis in enumerate(free):
                index[axis] = (step >> (len(free) - 1 - place)) & 1
                got_index.append(index[axis])
            del index[CORE]
            rows = pl.ds(first, count)
            mine = acc[tuple(index) + (rows,)].astype(jnp.float32)
            total = mine + got[stage][tuple(got_index) + (rows,)].astype(jnp.float32)
            if stage == 4:
                sum_ref[rows] = total
            else:
                acc[tuple(index) + (rows,)] = total.astype(jnp.bfloat16)
            return carry

        if free:
            lax.fori_loop(0, 2 ** len(free), one, 0)
        else:
            one(0, 0)

    small_copies = []

    def small_send_step(step):
        copy = pltpu.make_async_remote_copy(
            small_acc.at[step], small_got.at[step], small_send.at[step], small_recv.at[step],
            device_id=small_partners[step], device_id_type=MESH_ID,
        )
        copy.start()
        small_copies.append(copy)

    def small_add(step):
        small_copies[step].wait_recv()
        small_acc[step + 1] = small_acc[step] + small_got[step]

    small_acc[0] = small_ref[...]
    for number in range(len(tasks)):
        send(number, 0)
    small_send_step(0)
    for stage in range(1, 5):
        for number in range(len(tasks)):
            add(number, stage - 1)
            send(number, stage)
        small_add(stage - 1)
        small_send_step(stage)
    for number in range(len(tasks)):
        add(number, 4)
    for step in range(4, len(small_partners)):
        small_add(step)
        if step + 1 < len(small_partners):
            small_send_step(step + 1)
    small_out[...] = small_acc[len(small_partners)]
    for copy in copies.values():
        copy.wait_send()
    for copy in small_copies:
        copy.wait_send()


def reduce_everywhere(parts, small):
    dp_size = lax.axis_size("dp")
    all_bits = dp_size.bit_length() - 1
    extra_bits = all_bits - GROUP_BITS
    rows = parts.shape[2]
    parts = parts.reshape((2,) * 5 + parts.shape[2:])
    task_count = len(reduce_tasks(rows))
    steps = all_bits + 1
    bf16 = jnp.bfloat16
    got_shapes = [pltpu.VMEM((2,) * (4 - stage) + (rows, LANES), bf16) for stage in range(5)]
    return pl.pallas_call(
        lambda *refs: reduce_kernel(extra_bits, all_bits, *refs),
        out_shape=(
            jax.ShapeDtypeStruct((rows, LANES), jnp.float32),
            jax.ShapeDtypeStruct(small.shape, jnp.float32),
        ),
        in_specs=[pl.BlockSpec(memory_space=pl.ANY), pl.BlockSpec(memory_space=pltpu.VMEM)],
        out_specs=(pl.BlockSpec(memory_space=pltpu.VMEM), pl.BlockSpec(memory_space=pltpu.VMEM)),
        scratch_shapes=[pltpu.VMEM((2, 2, 2, 2, rows, LANES), bf16)] + got_shapes + [
            pltpu.VMEM((steps + 1,) + small.shape, jnp.float32),
            pltpu.VMEM((steps,) + small.shape, jnp.float32),
            pltpu.SemaphoreType.DMA((task_count,)),
            pltpu.SemaphoreType.DMA((task_count, 5)),
            pltpu.SemaphoreType.DMA((task_count, 5)),
            pltpu.SemaphoreType.DMA((steps,)),
            pltpu.SemaphoreType.DMA((steps,)),
        ],
        compiler_params=pltpu.CompilerParams(
            collective_id=0, has_side_effects=True, vmem_limit_bytes=48 << 20
        ),
    )(parts, small)


def scatter_rest(block, dp_size):
    group = dp_size >> GROUP_BITS
    if group == 1:
        return block
    groups = [[first * group + place for place in range(group)] for first in range(dp_size // group)]
    return lax.psum_scatter(block, "dp", scatter_dimension=0, axis_index_groups=groups, tiled=True)


def local(
    hidden_in,
    segment_ids,
    piece_lengths,
    time_index,
    first_gain,
    modulation_weight,
    modulation_bias,
    query_key_value_weight,
    attention_output_matrix,
    second_gain,
    widen_weight,
    expand_bias,
    narrow_weight,
    reduce_bias,
    cotangent,
):
    slot_count, own_rows, width = hidden_in.shape
    hidden, cot = hidden_in[0], cotangent[0]
    table = jnp.asarray(angle_table())
    gain_one, gain_two = first_gain[None, :], second_gain[None, :]
    normed, queries, keys, values, attended, query_features, key_features, modulation, condition = forward(
        segment_ids, piece_lengths, time_index, hidden, table, gain_one, modulation_weight,
        modulation_bias[None, :], query_key_value_weight,
    )
    block_out, grad_middle, grad_attended, delta_features, mod_grads, small, expand_part, reduce_part, output_part = mlp(
        segment_ids, piece_lengths, hidden, attended, cot, modulation, gain_two, expand_bias[None, :],
        reduce_bias[None, :], attention_output_matrix, widen_weight, narrow_weight,
    )
    input_grad, small, triple_part, mod_rows = backward(
        segment_ids, piece_lengths, hidden, normed, queries, keys, values, query_features, key_features,
        grad_attended, delta_features, grad_middle, modulation, mod_grads, small, table, gain_one,
        query_key_value_weight,
    )
    groups = 2**GROUP_BITS
    own_condition = condition[: own_rows // BLOCK]
    mod_weight_grad = jnp.einsum("bc,bf->fc", own_condition, mod_rows, precision=lax.Precision.HIGHEST)
    mod_part = mod_weight_grad.astype(BF16).reshape(groups, 6, -1, 2, LANES // 6)
    mod_part = mod_part.transpose(0, 3, 2, 1, 4).reshape(groups, 2, -1, LANES)
    reduce_part = reduce_part.reshape(groups, 2, -1, LANES)
    parts = jnp.concatenate([expand_part, reduce_part, output_part, triple_part, mod_part], axis=2)
    block_sum, small_sum = reduce_everywhere(parts, small)
    dp_size = lax.axis_size("dp")
    cuts = []
    cursor = 0
    for part in (expand_part, reduce_part, output_part, triple_part, mod_part):
        cuts.append(block_sum[cursor : cursor + part.shape[2]])
        cursor = cursor + part.shape[2]
    expand_block = scatter_rest(cuts[0], dp_size).T
    reduce_block = cuts[1].reshape(4, -1, LANES).transpose(1, 0, 2).reshape(-1, 4 * LANES)
    reduce_block = scatter_rest(reduce_block, dp_size).T
    output_block = scatter_rest(cuts[2], dp_size).T
    triple_block = scatter_rest(cuts[3], dp_size).T
    mod_block = cuts[4].reshape(-1, 6, LANES // 6).transpose(1, 0, 2).reshape(-1, LANES // 6)
    mod_block = scatter_rest(mod_block, dp_size).T
    stats = small_sum[STATS]
    return (
        block_out[None],
        input_grad[None],
        small_sum[FIRST_GAIN],
        mod_block,
        small_sum[MOD_BIAS : MOD_BIAS + 6].reshape(-1),
        triple_block,
        output_block,
        small_sum[SECOND_GAIN],
        expand_block,
        small_sum[EXPAND_BIAS : EXPAND_BIAS + 4].reshape(-1),
        reduce_block,
        small_sum[REDUCE_BIAS],
        jnp.sqrt(stats[:3] / (stats[3] * width)),
    )


def solution(mesh):
    in_specs = (
        P("dp", "seq", None),
        P("dp", None),
        P("dp", None),
        P("dp", None),
        P(),
        P(),
        P(),
        P(),
        P(),
        P(),
        P(),
        P(),
        P(),
        P(),
        P("dp", "seq", None),
    )
    out_specs = (
        P("dp", "seq", None),
        P("dp", "seq", None),
        P(),
        P("seq", "dp"),
        P(),
        P("seq", "dp"),
        P("seq", "dp"),
        P(),
        P("seq", "dp"),
        P(),
        P("seq", "dp"),
        P(),
        P(),
    )
    return jax.shard_map(local, mesh=mesh, in_specs=in_specs, out_specs=out_specs, check_vma=False)
```

```python
import functools
import math

import jax
import jax.numpy as jnp
import numpy as np
from jax import lax
from jax.experimental import pallas as pl
from jax.experimental.pallas import tpu as pltpu
from jax.sharding import PartitionSpec as P

HEADS = 12
BLOCK = 128
MAX_SEQUENCES = 8
SEGMENT_LANE = 40
MASKED = -1000000000.0
LANES = 384
GROUP_BITS = 4
MESH_ID = pl.DeviceIdType.MESH
F32, BF16 = jnp.float32, jnp.bfloat16

ROTARY_COS, ROTARY_SIN, BLOCK_COS, BLOCK_SIN = 0, 128, 256, 264
HIGH_COS, HIGH_SIN, LOW_COS, LOW_SIN, TABLE_ROWS = 272, 304, 336, 368, 400

FIRST_GAIN, MOD_BIAS, SECOND_GAIN, EXPAND_BIAS, REDUCE_BIAS, STATS, SMALL_ROWS = 0, 1, 7, 8, 12, 13, 16


def angle_table():
    lane = np.arange(128)
    rotary = np.exp((lane % 32) * (-2.0 * math.log(10000.0) / 64))
    timing = np.exp((lane % 64) * (-math.log(10000.0) / 64))
    steps = np.arange(128)[:, None]
    angles = [
        (np.cos, steps * rotary), (np.sin, steps * rotary),
        (np.cos, steps[:8] * 128 * rotary), (np.sin, steps[:8] * 128 * rotary),
        (np.cos, steps[:32] * 32 * timing), (np.sin, steps[:32] * 32 * timing),
        (np.cos, steps[:32] * timing), (np.sin, steps[:32] * timing),
    ]
    return np.concatenate([fn(angle) for fn, angle in angles]).astype(np.float32)


def dot(left, right):
    return jnp.dot(left, right, preferred_element_type=F32)


def dot_nt(left, right):
    return lax.dot_general(left, right, (((1,), (1,)), ((), ())), preferred_element_type=F32)


def dot_tn(left, right):
    return lax.dot_general(left, right, (((0,), (0,)), ((), ())), preferred_element_type=F32)


def lane_iota(shape):
    return lax.broadcasted_iota(jnp.int32, shape, len(shape) - 1)


def row_iota(shape):
    return lax.broadcasted_iota(jnp.int32, shape, 0)


def block_place(segments, lengths, block):
    segment = segments[0, block * BLOCK]
    before = jnp.int32(0)
    for other in range(segments.shape[1] // BLOCK):
        same = (segments[0, other * BLOCK] == segment) & (other < block)
        before = before + jnp.where(same, 1, 0)
    return segment, before, lengths[0, segment] - before * BLOCK


def rotary_block(table, before):
    cos_row, sin_row = table[pl.ds(ROTARY_COS, 128), :], table[pl.ds(ROTARY_SIN, 128), :]
    cos_block = table[pl.ds(BLOCK_COS + before, 1), :]
    sin_block = table[pl.ds(BLOCK_SIN + before, 1), :]
    cosine = cos_row * cos_block - sin_row * sin_block
    sine = sin_row * cos_block + cos_row * sin_block
    first_half = lane_iota(sine.shape) % 64 < 32
    return cosine, jnp.where(first_half, -sine, sine)


def turn(values, cosine, sine):
    first_half = lane_iota(values.shape) % 64 < 32
    swapped = jnp.where(first_half, pltpu.roll(values, 96, 1), pltpu.roll(values, 32, 1))
    return values * cosine + swapped * sine


def mean_of(values):
    return jnp.mean(values, axis=-1, keepdims=True)


def split_three(values):
    first = values.astype(BF16)
    rest = values - first.astype(F32)
    second = rest.astype(BF16)
    third = (rest - second.astype(F32)).astype(BF16)
    place = lane_iota(values.shape) % 3
    picked = jnp.where(place == 0, first.astype(F32), jnp.where(place == 1, second.astype(F32), third.astype(F32)))
    return picked.astype(BF16)


def forward_kernel(
    segments, lengths, times, hidden, table, first_gain, mod_weight, mod_bias, weight,
    normed, queries, keys, values, attended, query_features, key_features, modulation, condition,
    other_hidden, turned_values, out_t, peak, total, send_sem, recv_sem,
):
    tokens, width = hidden.shape
    blocks = tokens // BLOCK
    seq = lax.axis_index("seq")
    partner = (lax.axis_index("dp"), 1 - seq)
    barrier = pltpu.get_barrier_semaphore()
    pl.semaphore_signal(barrier, inc=1, device_id=partner, device_id_type=MESH_ID)
    pl.semaphore_wait(barrier, 1)
    exchange = pltpu.make_async_remote_copy(
        hidden, other_hidden, send_sem, recv_sem, device_id=partner, device_id_type=MESH_ID
    )
    exchange.start()

    places = []
    for number in range(2 * blocks):
        block = (seq if number < blocks else 1 - seq) * blocks + number % blocks
        places.append(block_place(segments, lengths, block))
        time = times[0, places[number][0]]
        high, low = time // 32, time % 32
        cos_high, sin_high = table[pl.ds(HIGH_COS + high, 1), :], table[pl.ds(HIGH_SIN + high, 1), :]
        cos_low, sin_low = table[pl.ds(LOW_COS + low, 1), :], table[pl.ds(LOW_SIN + low, 1), :]
        cosine = cos_high * cos_low - sin_high * sin_low
        sine = sin_high * cos_low + cos_high * sin_low
        row = jnp.where(lane_iota(cosine.shape) < 64, cosine, sine)
        condition[pl.ds(number, 1), :] = row.astype(BF16).astype(F32)
    modulation[...] = dot(condition[...].astype(BF16), mod_weight[...]) + mod_bias[...]

    lane = lane_iota((BLOCK, 128))
    row = row_iota((BLOCK, 128))

    for part in range(2):
        source = hidden if part == 0 else other_hidden
        if part == 1:
            exchange.wait_recv()
        turns = []
        for number in range(blocks):
            rows = pl.ds(number * BLOCK, BLOCK)
            segment, before, valid_count = places[part * blocks + number]
            turns.append(rotary_block(table, before))
            mine = lane == SEGMENT_LANE + segment
            in_lanes = (lane >= SEGMENT_LANE) & (lane < SEGMENT_LANE + MAX_SEQUENCES)
            blocked = in_lanes & jnp.logical_not(mine & (row < valid_count))
            key_features[part, rows, :] = jnp.where(blocked, MASKED, 0.0).astype(BF16)
            if part == 0:
                query_features[rows, :] = jnp.where(mine, 1.0, 0.0).astype(BF16)
            mod_row = pl.ds(part * blocks + number, 1)
            shift, scale = modulation[mod_row, pl.ds(0, width)], modulation[mod_row, pl.ds(width, width)]
            value = source[rows, :].astype(F32)
            centered = value - mean_of(value)
            spread = mean_of(centered * centered)
            line = centered * lax.rsqrt(spread + 1e-05) * first_gain[...]
            result = (line * (1.0 + scale) + shift).astype(BF16)
            if part == 0:
                normed[rows, :] = result
            else:
                other_hidden[rows, :] = result
        normed_source = normed if part == 0 else other_hidden
        for tile in range(3 * width // LANES):
            which, first = divmod(tile * LANES, width)
            product = dot(normed_source[...], weight[:, pl.ds(tile * LANES, LANES)])
            target = (queries, keys, values)[which]
            for number in range(blocks):
                cosine, sine = turns[number]
                for pair in range(LANES // 128):
                    piece = product[number * BLOCK : (number + 1) * BLOCK, pair * 128 : (pair + 1) * 128]
                    if which < 2:
                        piece = turn(piece, cosine, sine)
                    if which == 0:
                        piece = piece.astype(BF16).astype(F32) * 0.125
                    target[part, pl.ds(number * BLOCK, BLOCK), pl.ds(first + pair * 128, 128)] = piece.astype(BF16)
        turned_values[...] = jnp.transpose(values[part])

        def attend(pair, carry):
            lanes = pl.ds(pl.multiple_of(pair * 128, 128), 128)
            query_pair, key_pair = queries[0, :, lanes], keys[part, :, lanes]
            left = jnp.concatenate([key_pair, key_features[part]], axis=1)
            pair_lane = lane_iota(query_pair.shape)
            for half in range(2):
                head = pair * 2 + half
                head_rows = pl.ds(pl.multiple_of(head * 64, 64), 64)
                one_row = pl.ds(head, 1)
                query = jnp.where((pair_lane < 64) == (half == 0), query_pair, jnp.zeros_like(query_pair))
                scores = dot_nt(left, jnp.concatenate([query, query_features[...]], axis=1))
                top = jnp.max(scores, axis=0, keepdims=True)
                if part == 1:
                    top = jnp.maximum(top, peak[one_row, :])
                weights = jnp.exp(scores - top)
                summed = jnp.sum(weights, axis=0, keepdims=True)
                mixed = dot(turned_values[head_rows, :], weights.astype(BF16))
                if part == 0:
                    out_t[head_rows, :] = mixed
                    total[one_row, :] = summed
                    peak[one_row, :] = top
                else:
                    rescale = jnp.exp(peak[one_row, :] - top)
                    summed = summed + rescale * total[one_row, :]
                    out_t[head_rows, :] = (out_t[head_rows, :] * rescale + mixed) * (1.0 / summed)
                    peak[one_row, :] = top + jnp.log(summed)
            return carry

        lax.fori_loop(0, HEADS // 2, attend, 0)

    attended[...] = jnp.transpose(out_t[...].astype(BF16))
    log_rows = jnp.concatenate(
        [jnp.broadcast_to(peak[pl.ds(head, 1), :], (3, tokens)) for head in range(HEADS)]
        + [jnp.zeros((128 - 3 * HEADS, tokens), F32)], axis=0,
    )
    query_features[...] = query_features[...] + split_three(jnp.transpose(log_rows))
    exchange.wait_send()


def forward(segments, lengths, times, hidden, table, first_gain, mod_weight, mod_bias, weight):
    tokens, width = hidden.shape
    blocks = 2 * tokens // BLOCK
    half = jax.ShapeDtypeStruct((tokens, width), BF16)
    both = jax.ShapeDtypeStruct((2, tokens, width), BF16)
    smem, vmem = pl.BlockSpec(memory_space=pltpu.SMEM), pl.BlockSpec(memory_space=pltpu.VMEM)
    return pl.pallas_call(
        forward_kernel,
        out_shape=(
            half, both, both, both, half,
            jax.ShapeDtypeStruct((tokens, 128), BF16),
            jax.ShapeDtypeStruct((2, tokens, 128), BF16),
            jax.ShapeDtypeStruct((blocks, 6 * width), F32),
            jax.ShapeDtypeStruct((blocks, 128), F32),
        ),
        in_specs=[smem] * 3 + [vmem] * 6,
        out_specs=(vmem,) * 9,
        scratch_shapes=[
            pltpu.VMEM((tokens, width), BF16),
            pltpu.VMEM((width, tokens), BF16),
            pltpu.VMEM((width, tokens), F32),
            pltpu.VMEM((16, tokens), F32),
            pltpu.VMEM((16, tokens), F32),
            pltpu.SemaphoreType.DMA,
            pltpu.SemaphoreType.DMA,
        ],
        compiler_params=pltpu.CompilerParams(
            collective_id=1, has_side_effects=True, vmem_limit_bytes=56 << 20
        ),
    )(segments, lengths, times, hidden, table, first_gain, mod_weight, mod_bias, weight)


TILE = 384


def mlp_kernel(
    segments, lengths, hidden, attended, cotangent, modulation, second_gain, expand_bias, reduce_bias,
    out_weight_hbm, widen_hbm, narrow_hbm,
    block_out, grad_low, normed, normal, spread_row, projected, gate_grads, small, activated_hbm, slope_hbm,
    out_weight, widen, narrow, activated, slope, middle, reduced,
    load_sem, tile_sem, store_sem,
):
    tokens, width = hidden.shape
    tiles = widen.shape[1] // TILE
    blocks = tokens // BLOCK
    seq = lax.axis_index("seq")

    def tile_lanes(tile):
        return pl.ds(pl.multiple_of(tile * TILE, TILE), TILE)

    def tile_loads(tile):
        lanes = tile_lanes(tile)
        return (
            pltpu.make_async_copy(widen_hbm.at[:, lanes], widen.at[:, lanes], tile_sem.at[0, tile]),
            pltpu.make_async_copy(narrow_hbm.at[lanes], narrow.at[lanes], tile_sem.at[1, tile]),
        )

    first_load = pltpu.make_async_copy(out_weight_hbm, out_weight, load_sem)
    first_load.start()
    for tile in range(tiles):
        for load in tile_loads(tile):
            load.start()
    row = row_iota((BLOCK, 1))
    keep = []
    for number in range(blocks):
        valid_count = block_place(segments, lengths, seq * blocks + number)[2]
        keep.append(jnp.where(row < valid_count, 1.0, 0.0))

    def mod_part(number, part):
        return modulation[pl.ds(number, 1), pl.ds(part * width, width)]

    first_load.wait()
    for first in range(0, width, 256):
        lanes = pl.ds(first, 256)
        projected[:, lanes] = dot(attended[...], out_weight[:, lanes])
    branch_sum = jnp.zeros((1, width), F32)
    for number in range(blocks):
        rows = pl.ds(number * BLOCK, BLOCK)
        branch = mod_part(number, 2) * projected[rows, :]
        branch_sum = branch_sum + jnp.sum(keep[number] * branch * branch, axis=0, keepdims=True)
        value = hidden[rows, :].astype(F32) + branch
        middle[rows, :] = value
        centered = value - mean_of(value)
        inverse = lax.rsqrt(mean_of(centered * centered) + 1e-05)
        normal[rows, :] = centered * inverse
        spread_row[rows, :] = jnp.broadcast_to(inverse, (BLOCK, 128))
        line = normal[rows, :] * second_gain[...]
        normed[rows, :] = (line * (1.0 + mod_part(number, 4)) + mod_part(number, 3)).astype(BF16)

    reduced[...] = jnp.zeros_like(reduced)

    def stores(tile):
        return (
            pltpu.make_async_copy(activated.at[tile], activated_hbm.at[tile], store_sem.at[0, tile]),
            pltpu.make_async_copy(slope.at[tile], slope_hbm.at[tile], store_sem.at[1, tile]),
        )

    def ahead(tile):
        lanes = tile_lanes(tile)
        for load in tile_loads(tile):
            load.wait()
        u = dot(normed[...], widen[:, lanes]) + expand_bias[:, lanes]
        square = u * u
        tanh = jnp.tanh(u * (0.7978845608028654 + 0.7978845608028654 * 0.044715 * square))
        half_sum = 0.5 + 0.5 * tanh
        active = (u * half_sum).astype(BF16)
        inner = 0.7978845608028654 + 3.0 * 0.7978845608028654 * 0.044715 * square
        slope[tile] = (half_sum + (0.5 * u) * (1.0 - tanh * tanh) * inner).astype(BF16)
        activated[tile] = active
        reduced[...] += dot(active, narrow[lanes, :])
        for copy in stores(tile):
            copy.start()

    def ahead_two(step, carry):
        ahead(2 * step)
        ahead(2 * step + 1)
        return carry

    lax.fori_loop(0, tiles // 2, ahead_two, 0)

    value_sum = jnp.zeros((1, width), F32)
    mlp_sum = jnp.zeros((1, width), F32)
    bias_sum = jnp.zeros((1, width), F32)
    for number in range(blocks):
        rows = pl.ds(number * BLOCK, BLOCK)
        gate = mod_part(number, 5)
        full = reduced[rows, :] + reduce_bias[...]
        branch = gate * full
        value = middle[rows, :] + branch
        block_out[rows, :] = value.astype(BF16)
        value_sum = value_sum + jnp.sum(keep[number] * value * value, axis=0, keepdims=True)
        mlp_sum = mlp_sum + jnp.sum(keep[number] * branch * branch, axis=0, keepdims=True)
        grad_out = cotangent[rows, :].astype(F32) * keep[number]
        gate_grads[pl.ds(number, 1), :] = jnp.sum(grad_out * full, axis=0, keepdims=True)
        low = (gate * grad_out).astype(BF16)
        grad_low[rows, :] = low
        bias_sum = bias_sum + jnp.sum(low.astype(F32), axis=0, keepdims=True)
    small[...] = jnp.zeros_like(small)
    small[pl.ds(REDUCE_BIAS, 1), :] = bias_sum
    lane = lane_iota((1, width))
    counts = jnp.zeros((1, 1), F32)
    for number in range(blocks):
        counts = counts + jnp.sum(keep[number], axis=0, keepdims=True)
    sums = [jnp.sum(term, axis=1, keepdims=True) for term in (value_sum, branch_sum, mlp_sum)] + [counts]
    stats = jnp.zeros((1, width), F32)
    for place, term in enumerate(sums):
        stats = jnp.where(lane == place, term, stats)
    small[pl.ds(STATS, 1), :] = stats

    def drain(tile, carry):
        for copy in stores(tile):
            copy.wait()
        return carry

    lax.fori_loop(0, tiles, drain, 0)


def mlp(segments, lengths, hidden, attended, cotangent, modulation, second_gain, expand_bias, reduce_bias, out_weight, widen, narrow):
    tokens, width = hidden.shape
    tiles = widen.shape[1] // TILE
    smem, vmem = pl.BlockSpec(memory_space=pltpu.SMEM), pl.BlockSpec(memory_space=pltpu.VMEM)
    hbm = pl.BlockSpec(memory_space=pl.ANY)
    half, by_tile = (tokens, width), (tiles, tokens, TILE)
    return pl.pallas_call(
        mlp_kernel,
        out_shape=(
            jax.ShapeDtypeStruct(half, BF16),
            jax.ShapeDtypeStruct(half, BF16),
            jax.ShapeDtypeStruct(half, BF16),
            jax.ShapeDtypeStruct(half, F32),
            jax.ShapeDtypeStruct((tokens, 128), F32),
            jax.ShapeDtypeStruct(half, F32),
            jax.ShapeDtypeStruct((tokens // BLOCK, width), F32),
            jax.ShapeDtypeStruct((SMALL_ROWS, width), F32),
            jax.ShapeDtypeStruct(by_tile, BF16),
            jax.ShapeDtypeStruct(by_tile, BF16),
        ),
        in_specs=[smem] * 2 + [vmem] * 7 + [hbm] * 3,
        out_specs=(vmem,) * 8 + (hbm,) * 2,
        scratch_shapes=[
            pltpu.VMEM(out_weight.shape, BF16),
            pltpu.VMEM(widen.shape, BF16),
            pltpu.VMEM(narrow.shape, BF16),
            pltpu.VMEM(by_tile, BF16),
            pltpu.VMEM(by_tile, BF16),
            pltpu.VMEM(half, F32),
            pltpu.VMEM(half, F32),
            pltpu.SemaphoreType.DMA,
            pltpu.SemaphoreType.DMA((2, tiles)),
            pltpu.SemaphoreType.DMA((2, tiles)),
        ],
        compiler_params=pltpu.CompilerParams(vmem_limit_bytes=56 << 20),
    )(segments, lengths, hidden, attended, cotangent, modulation, second_gain, expand_bias, reduce_bias, out_weight, widen, narrow)


Z2, Z1, Y, CORE, X = 0, 1, 2, 3, 4


def exchange_partner(axis, extra_bits):
    dp, seq = lax.axis_index("dp"), lax.axis_index("seq")
    if axis == X:
        return (dp, 1 - seq)
    return (dp ^ (1 << (GROUP_BITS - 1 - axis + extra_bits)), seq)


def own_bit(axis, extra_bits):
    if axis == X:
        return lax.axis_index("seq")
    return (lax.axis_index("dp") >> (GROUP_BITS - 1 - axis + extra_bits)) & 1


class Stream:
    def __init__(self, kit, number, part, first, count, fixed, order, got, got_first=0):
        self.kit, self.number, self.part, self.first, self.count = kit, number, part, first, count
        self.fixed, self.order, self.got, self.got_first = fixed, order, got, got_first

    def free(self, stage):
        return [axis for axis in range(5) if axis not in self.fixed and axis not in self.order[: stage + 1]]

    def copy(self, stage):
        bits = self.kit["bits"]
        index = [slice(None)] * 5
        for axis, value in self.fixed.items():
            index[axis] = value
        for axis in self.order[:stage]:
            index[axis] = bits[axis]
        index[self.order[stage]] = 1 - bits[self.order[stage]]
        target = (slice(None),) * len(self.free(stage)) + (pl.ds(self.got_first, self.count),)
        return pltpu.make_async_remote_copy(
            self.part.at[tuple(index) + (pl.ds(self.first, self.count),)],
            self.got[stage].at[target],
            self.kit["send"].at[self.number, stage],
            self.kit["recv"].at[self.number, stage],
            device_id=exchange_partner(self.order[stage], self.kit["extra"]),
            device_id_type=MESH_ID,
        )

    def send(self, stage):
        self.copy(stage).start()

    def add(self, stage, total=None, total_first=0):
        self.copy(stage).wait_recv()
        bits, free = self.kit["bits"], self.free(stage)
        rows, got_rows = pl.ds(self.first, self.count), pl.ds(self.got_first, self.count)

        def one(step, carry):
            index = list(bits)
            for axis, value in self.fixed.items():
                index[axis] = value
            place = []
            for order, axis in enumerate(free):
                index[axis] = (step >> (len(free) - 1 - order)) & 1
                place.append(index[axis])
            mine, theirs = self.part[tuple(index) + (rows,)], self.got[stage][tuple(place) + (got_rows,)]
            if total is None:
                self.part[tuple(index) + (rows,)] = mine + theirs
            else:
                total[pl.ds(total_first, self.count), :] = mine.astype(F32) + theirs.astype(F32)
            return carry

        if free:
            lax.fori_loop(0, 2 ** len(free), one, 0)
        else:
            one(0, 0)

    def done(self):
        for stage in range(len(self.order)):
            self.copy(stage).wait_send()


def backward_kernel(
    extra_bits, all_bits,
    segments, lengths, modulation, gate_grads, small_in, condition, table, first_gain, second_gain,
    narrow_hbm, widen_hbm, out_weight_hbm, activated_hbm, slope_hbm, normed_two_hbm, grad_low_hbm, normal_hbm, spread_hbm,
    projected_hbm, attended_hbm, cotangent_hbm, queries_hbm, keys_hbm, values_hbm, query_features_hbm, key_features_hbm,
    normed_hbm, hidden_hbm, weight_hbm,
    input_grad, sums, mod_out, small_out,
    expand_part, reduce_part, output_part,
    expand_got, reduce_got, one_x, one_z, one_y, one_last, two_z, two_y, two_x, two_last, red_y, red_z, red_w, red_last,
    out_a, out_b, out_c, out_d, out_e, tri_a, tri_b, tri_c, tri_d, tri_e,
    queries, keys, values, query_features, key_features,
    grad_middle, grad_attended, delta_features, other_grad, other_delta, other_features, mod_rows,
    small_acc, small_got, mod_zero, mod_got, mod_one, mod_two, mod_three, mod_four, mod_five,
    cond_zero, cond_got, cond_one, cond_two, cond_three, cond_four, cond_five,
    load_sem, tile_sem, core_send, core_recv, stream_send, stream_recv, swap_send, swap_recv,
    small_send, small_recv, mod_send, mod_recv,
):
    tokens, width = input_grad.shape
    tiles = activated_hbm.shape[0]
    blocks = tokens // BLOCK
    seq = lax.axis_index("seq")
    dp = lax.axis_index("dp")
    bits = [own_bit(axis, extra_bits) for axis in range(5)]
    kit = {"bits": bits, "send": stream_send, "recv": stream_recv, "extra": extra_bits}
    core = bits[CORE]
    own = {axis: bits[axis] for axis in range(5)}

    def others(*axes):
        return {axis: bits[axis] for axis in range(5) if axis not in axes}

    one = [Stream(kit, v, expand_part, 0, 96, {CORE: core, Z2: v}, (X, Z1, Y), (one_x.at[v], one_z.at[v], one_y.at[v])) for v in range(2)]
    two = [Stream(kit, 2 + v, expand_part, 96, 96, {CORE: core, Z2: v}, (Z1, Y, X), (two_z.at[v], two_y.at[v], two_x.at[v])) for v in range(2)]
    red = [Stream(kit, 4 + v, reduce_part, 0, 192, {CORE: core, X: v}, (Y, Z1, Z2), (red_y.at[v], red_z.at[v], red_w.at[v])) for v in range(2)]
    one_merge = Stream(kit, 6, expand_part, 0, 96, others(Z2), (Z2,), (one_last,))
    two_merge = Stream(kit, 7, expand_part, 96, 96, others(Z2), (Z2,), (two_last,))
    red_merge = Stream(kit, 8, reduce_part, 0, 192, others(X), (X,), (red_last,))
    out = Stream(kit, 9, output_part, 0, 48, {}, (CORE, Y, X, Z1, Z2), (out_a, out_b, out_c, out_d, out_e))

    greet = [(dp, 1 - seq)] + [(dp ^ (1 << bit), seq) for bit in range(all_bits)]
    barrier = pltpu.get_barrier_semaphore()
    for partner in greet:
        pl.semaphore_signal(barrier, inc=1, device_id=partner, device_id_type=MESH_ID)

    attention_loads = [
        pltpu.make_async_copy(source, target, load_sem.at[number])
        for number, (source, target) in enumerate(
            ((queries_hbm, queries), (keys_hbm, keys), (values_hbm, values),
             (query_features_hbm, query_features), (key_features_hbm, key_features))
        )
    ]
    row = row_iota((BLOCK, 1))
    keep = []
    for number in range(blocks):
        valid_count = block_place(segments, lengths, seq * blocks + number)[2]
        keep.append(jnp.where(row < valid_count, 1.0, 0.0))

    def mod_part(number, part):
        return modulation[pl.ds(number, 1), pl.ds(part * width, width)]

    def tile_lanes(tile):
        return pl.ds(pl.multiple_of(tile * TILE, TILE), TILE)

    def core_copies(tile):
        at = (tile >> 2, (tile >> 1) & 1, tile & 1)
        rows = pl.ds(pl.multiple_of((tile & 3) * 48, 16), 48)
        everywhere = (slice(None),) * 3
        partner = exchange_partner(CORE, extra_bits)
        return (
            pltpu.make_async_remote_copy(
                expand_part.at[at + (1 - core,)], expand_got.at[at], core_send.at[0, tile], core_recv.at[0, tile],
                device_id=partner, device_id_type=MESH_ID,
            ),
            pltpu.make_async_remote_copy(
                reduce_part.at[everywhere + (1 - core, tile >> 2, rows)], reduce_got.at[everywhere + (tile >> 2, rows)],
                core_send.at[1, tile], core_recv.at[1, tile], device_id=partner, device_id_type=MESH_ID,
            ),
        )

    def core_add(tile):
        at = (tile >> 2, (tile >> 1) & 1, tile & 1)
        rows = pl.ds(pl.multiple_of((tile & 3) * 48, 16), 48)
        for copy in core_copies(tile):
            copy.wait_recv()
        for side in range(2):
            expand_part[at + (core, side)] = expand_part[at + (core, side)] + expand_got[at + (side,)]
        for z2 in range(2):
            for z1 in range(2):
                for y in range(2):
                    index, got = (z2, z1, y, core, tile >> 2, rows), (z2, z1, y, tile >> 2, rows)
                    reduce_part[index] = reduce_part[index] + reduce_got[got]

    def mlp_phase(
        narrow, widen, out_weight, activated, slope, normed_two, grad_low, grad_low_t, normal, spread_row, projected,
        attended, cotangent, bias_row, grad_normed,
    ):
        def tile_loads(tile):
            lanes = tile_lanes(tile)
            pairs = (
                (narrow_hbm.at[lanes], narrow.at[lanes]), (slope_hbm.at[tile], slope.at[tile]),
                (widen_hbm.at[:, lanes], widen.at[:, lanes]), (activated_hbm.at[tile], activated.at[tile]),
            )
            return [pltpu.make_async_copy(source, target, tile_sem.at[place, tile]) for place, (source, target) in enumerate(pairs)]

        loads = [
            pltpu.make_async_copy(source, target, load_sem.at[5 + number])
            for number, (source, target) in enumerate(
                ((grad_low_hbm, grad_low), (normed_two_hbm, normed_two), (normal_hbm, normal), (spread_hbm, spread_row),
                 (projected_hbm, projected), (attended_hbm, attended), (cotangent_hbm, cotangent), (out_weight_hbm, out_weight))
            )
        ]
        for load in loads[:2]:
            load.start()
        for tile in range(tiles):
            for load in tile_loads(tile):
                load.start()
        for load in loads[2:] + attention_loads:
            load.start()
        grad_normed[...] = jnp.zeros_like(grad_normed)
        loads[0].wait()
        grad_low_t[...] = jnp.transpose(grad_low[...])
        loads[1].wait()
        pl.semaphore_wait(barrier, len(greet))

        def back(tile):
            lanes = tile_lanes(tile)
            for load in tile_loads(tile):
                load.wait()
            grad_active = dot_nt(grad_low[...], narrow[lanes, :])
            grad_wide = (grad_active * slope[tile].astype(F32)).astype(BF16)
            bias_row[pl.ds(0, 1), lanes] = jnp.sum(grad_wide.astype(F32), axis=0, keepdims=True)
            grad_normed[...] += dot_nt(grad_wide, widen[:, lanes])
            expand_t = dot_tn(grad_wide, normed_two[...]).astype(BF16)
            at = (tile >> 2, (tile >> 1) & 1, tile & 1)
            for group in range(2):
                for side in range(2):
                    expand_part[at + (group, side)] = expand_t[
                        group * 192 : group * 192 + 192, side * LANES : side * LANES + LANES
                    ]
            reduce_t = dot(grad_low_t[...], activated[tile]).astype(BF16)
            rows = pl.ds(pl.multiple_of((tile & 3) * 48, 16), 48)
            reduce_part[:, :, :, :, tile >> 2, rows] = reduce_t.reshape(2, 2, 2, 2, 48, TILE)
            for copy in core_copies(tile):
                copy.start()

        def back_two(step, carry):
            back(2 * step)

            @pl.when(step > 0)
            def _():
                core_add(2 * step - 1)

            @pl.when(step == 2)
            def _():
                one[0].send(0)
                two[0].send(0)
                red[0].send(0)

            back(2 * step + 1)
            core_add(2 * step)
            return carry

        lax.fori_loop(0, tiles // 2, back_two, 0)
        core_add(tiles - 1)
        one[1].send(0)
        two[1].send(0)
        red[1].send(0)
        small_acc[0] = small_in[...]
        for part in range(tiles * TILE // width):
            small_acc[0, pl.ds(EXPAND_BIAS + part, 1), :] = bias_row[pl.ds(0, 1), pl.ds(part * width, width)]

        for load in loads[2:]:
            load.wait()
        gain_sum = jnp.zeros((1, width), F32)
        for number in range(blocks):
            rows = pl.ds(number * BLOCK, BLOCK)
            here = pl.ds(number, 1)
            grad = grad_normed[rows, :]
            line = normal[rows, :] * second_gain[...]
            mod_rows[here, pl.ds(3 * width, width)] = jnp.sum(grad, axis=0, keepdims=True)
            mod_rows[here, pl.ds(4 * width, width)] = jnp.sum(grad * line, axis=0, keepdims=True)
            mod_rows[here, pl.ds(5 * width, width)] = gate_grads[here, :]
            grad_line = grad * (1.0 + mod_part(number, 4))
            gain_sum = gain_sum + jnp.sum(grad_line * normal[rows, :], axis=0, keepdims=True)
            grad_normal = grad_line * second_gain[...]
            along = mean_of(grad_normal * normal[rows, :])
            term = (grad_normal - mean_of(grad_normal) - normal[rows, :] * along) * spread_row[rows, :1]
            total = cotangent[rows, :].astype(F32) * keep[number] + term
            grad_middle[rows, :] = total
            mod_rows[here, pl.ds(2 * width, width)] = jnp.sum(total * projected[rows, :], axis=0, keepdims=True)
            grad_low[rows, :] = (mod_part(number, 2) * total).astype(BF16)
        small_acc[0, pl.ds(SECOND_GAIN, 1), :] = gain_sum

        for first in range(0, width, 256):
            grad_attended[:, pl.ds(first, 256)] = dot_nt(
                grad_low[...], out_weight[pl.ds(first, 256), :]
            ).astype(BF16)
        head_lane = row_iota((width, 128)) // 64 == lane_iota((width, 128)) // 3
        chooser = jnp.where(head_lane & (lane_iota((width, 128)) < 3 * HEADS), 1.0, 0.0).astype(BF16)
        for number in range(blocks):
            rows = pl.ds(number * BLOCK, BLOCK)
            product = grad_attended[rows, :].astype(F32) * attended[rows, :].astype(F32)
            upper = product.astype(BF16)
            lower = (product - upper.astype(F32)).astype(BF16)
            delta_features[rows, :] = split_three(dot(upper, chooser) + dot(lower, chooser))
        for load in attention_loads:
            load.wait()
        for swap in swaps():
            swap.start()
        for first in range(0, width, TILE):
            output_t = dot_tn(grad_low[:, pl.ds(first, TILE)], attended[...]).astype(BF16)
            for place in range(TILE // 48):
                group = first // 48 + place
                at = (group >> 3, (group >> 2) & 1, (group >> 1) & 1, group & 1)
                for side in range(2):
                    output_part[at + (side,)] = output_t[
                        place * 48 : place * 48 + 48, side * LANES : side * LANES + LANES
                    ]
        out.send(0)

    def swaps():
        partner = (dp, 1 - seq)
        return [
            pltpu.make_async_remote_copy(
                source, target, swap_send.at[number], swap_recv.at[number], device_id=partner, device_id_type=MESH_ID
            )
            for number, (source, target) in enumerate(
                ((grad_attended, other_grad), (delta_features, other_delta), (query_features, other_features))
            )
        ]

    units = tiles * TILE
    pl.run_scoped(
        mlp_phase,
        pltpu.VMEM((units, width), BF16), pltpu.VMEM((width, units), BF16), pltpu.VMEM((width, width), BF16),
        pltpu.VMEM((tiles, tokens, TILE), BF16), pltpu.VMEM((tiles, tokens, TILE), BF16),
        pltpu.VMEM((tokens, width), BF16), pltpu.VMEM((tokens, width), BF16), pltpu.VMEM((width, tokens), BF16),
        pltpu.VMEM((tokens, width), F32), pltpu.VMEM((tokens, 128), F32), pltpu.VMEM((tokens, width), F32),
        pltpu.VMEM((tokens, width), BF16), pltpu.VMEM((tokens, width), BF16), pltpu.VMEM((8, units), F32),
        pltpu.VMEM((tokens, width), F32),
    )

    def step(stream, stage):
        stream.add(stage)
        stream.send(stage + 1)

    def after_all(streams, stage, merge):
        for stream in streams:
            stream.add(stage)
        merge.send(0)

    plan = {
        0: [(step, one[0], 0), (step, two[0], 0)],
        1: [(step, one[1], 0), (step, two[1], 0)],
        2: [(step, red[0], 0)],
        3: [(step, one[0], 1), (step, two[0], 1)],
        4: [(step, one[1], 1), (step, two[1], 1)],
        5: [(step, out, 0)],
        6: [(step, red[1], 0)],
        7: [(step, red[0], 1)],
        8: [(after_all, one, 2, one_merge)],
        9: [(after_all, two, 2, two_merge)],
        10: [(step, red[1], 1), (step, out, 1)],
        11: [],
        12: [(step, out, 2), (after_all, red, 2, red_merge)],
        13: [(one_merge.add, 0, sums, 0), (two_merge.add, 0, sums, 96)],
        14: [(step, out, 3)],
        15: [],
        16: [(red_merge.add, 0, sums, 192)],
        17: [(out.add, 4, sums, 384)],
    }

    def run_plan(pair, first, stride, count):
        for place in range(count):
            actions = plan[first + stride * place]
            if actions:

                @pl.when(pair == place)
                def _(actions=actions):
                    for action in actions:
                        action[0](*action[1:])

    def attention_phase(normed, hidden, weight, keys_t, grad_query_t, grad_key, grad_value, grad_triple, grad_normed, triple_part):
        loads = [
            pltpu.make_async_copy(source, target, load_sem.at[13 + number])
            for number, (source, target) in enumerate(((normed_hbm, normed), (hidden_hbm, hidden), (weight_hbm, weight)))
        ]
        for load in loads:
            load.start()
        for part in range(2):
            keys_t[part] = jnp.transpose(keys[part])

        def own_queries(pair, carry):
            lanes = pl.ds(pl.multiple_of(pair * 128, 128), 128)
            query_pair, grad_pair = queries[0, :, lanes], grad_attended[:, lanes]
            pair_lane = lane_iota(query_pair.shape)
            for half in range(2):
                head = pair * 2 + half
                head_rows = pl.ds(pl.multiple_of(head * 64, 64), 64)
                mine = (pair_lane < 64) == (half == 0)
                query = jnp.where(mine, query_pair, jnp.zeros_like(query_pair))
                grad = jnp.where(mine, grad_pair, jnp.zeros_like(grad_pair))
                right_scores = jnp.concatenate([query, query_features[...]], axis=1)
                right_grads = jnp.concatenate([grad, delta_features[...]], axis=1)
                head_lanes = (pair_lane >= 3 * head) & (pair_lane < 3 * head + 3)
                grad_q = jnp.zeros((64, tokens), F32)
                for part in range(2):
                    features = jnp.where(head_lanes, jnp.full_like(query_pair, -1.0), key_features[part])
                    scores = dot_nt(jnp.concatenate([keys[part, :, lanes], features], axis=1), right_scores)
                    weights = jnp.exp(scores)
                    grad_weights = dot_nt(jnp.concatenate([values[part, :, lanes], features], axis=1), right_grads)
                    grad_scores = (weights * grad_weights).astype(BF16)
                    if part == 0:
                        grad_v = dot(weights.astype(BF16), grad)
                        grad_k = dot(grad_scores, query)
                        if half == 0:
                            grad_value[:, lanes] = grad_v
                            grad_key[:, lanes] = grad_k
                        else:
                            grad_value[:, lanes] += grad_v
                            grad_key[:, lanes] += grad_k
                    grad_q = grad_q + dot(keys_t[part, head_rows, :], grad_scores)
                grad_query_t[head_rows, :] = grad_q
                run_plan(pair, half, 2, HEADS // 2)
            return carry

        lax.fori_loop(0, HEADS // 2, own_queries, 0)
        for swap in swaps():
            swap.wait_recv()

        def other_queries(pair, carry):
            lanes = pl.ds(pl.multiple_of(pair * 128, 128), 128)
            query_pair, grad_pair = queries[1, :, lanes], other_grad[:, lanes]
            pair_lane = lane_iota(query_pair.shape)
            grad_k = grad_key[:, lanes]
            grad_v = grad_value[:, lanes]
            for half in range(2):
                head = pair * 2 + half
                mine = (pair_lane < 64) == (half == 0)
                query = jnp.where(mine, query_pair, jnp.zeros_like(query_pair))
                grad = jnp.where(mine, grad_pair, jnp.zeros_like(grad_pair))
                head_lanes = (pair_lane >= 3 * head) & (pair_lane < 3 * head + 3)
                features = jnp.where(head_lanes, jnp.full_like(query_pair, -1.0), key_features[0])
                scores = dot_nt(
                    jnp.concatenate([keys[0, :, lanes], features], axis=1),
                    jnp.concatenate([query, other_features[...]], axis=1),
                )
                weights = jnp.exp(scores)
                grad_weights = dot_nt(
                    jnp.concatenate([values[0, :, lanes], features], axis=1),
                    jnp.concatenate([grad, other_delta[...]], axis=1),
                )
                grad_scores = (weights * grad_weights).astype(BF16)
                grad_v = grad_v + dot(weights.astype(BF16), grad)
                grad_k = grad_k + dot(grad_scores, query)
            grad_key[:, lanes] = grad_k
            grad_value[:, lanes] = grad_v
            run_plan(pair, 12, 1, HEADS // 2)
            return carry

        lax.fori_loop(0, HEADS // 2, other_queries, 0)

        grad_normed[...] = jnp.transpose(grad_query_t[...])
        for number in range(blocks):
            rows = pl.ds(number * BLOCK, BLOCK)
            before = block_place(segments, lengths, seq * blocks + number)[1]
            cosine, sine = rotary_block(table, before)
            for pair in range(HEADS // 2):
                lanes = pl.ds(pair * 128, 128)
                grad_triple[rows, lanes] = (turn(grad_normed[rows, lanes], cosine, -sine) * 0.125).astype(BF16)
                grad_triple[rows, pl.ds(width + pair * 128, 128)] = turn(grad_key[rows, lanes], cosine, -sine).astype(BF16)
            grad_triple[rows, pl.ds(2 * width, width)] = grad_value[rows, :].astype(BF16)

        for load in loads:
            load.wait()
        for part in range(2):
            triple_t = dot_tn(grad_triple[:, pl.ds(part * 1152, 1152)], normed[...]).astype(BF16)
            for place in range(8):
                at = (part, place >> 2, (place >> 1) & 1, place & 1)
                for side in range(2):
                    triple_part[at + (side,)] = triple_t[
                        place * 144 : place * 144 + 144, side * LANES : side * LANES + LANES
                    ]
        got = (tri_a, tri_b, tri_c, tri_d, tri_e)
        triple = [
            Stream(kit, 10 + number, triple_part, 48 * number, 48, {}, (CORE,) + order, got, 48 * number)
            for number, order in enumerate(((X, Y, Z1, Z2), (Y, Z1, X, Z2), (Z1, X, Y, Z2)))
        ]
        for stream in triple:
            stream.send(0)
        grad_normed[...] = jnp.zeros_like(grad_normed)
        for first in range(0, 3 * width, width):
            lanes = pl.ds(first, width)
            grad_normed[...] += dot_nt(grad_triple[:, lanes], weight[:, lanes])
        for stream in triple:
            step(stream, 0)

        gain_sum = jnp.zeros((1, width), F32)
        for number in range(blocks):
            rows, here = pl.ds(number * BLOCK, BLOCK), pl.ds(number, 1)
            value = hidden[rows, :].astype(F32)
            centered = value - mean_of(value)
            inverse = lax.rsqrt(mean_of(centered * centered) + 1e-05)
            normal = centered * inverse
            grad = grad_normed[rows, :]
            mod_rows[here, pl.ds(0, width)] = jnp.sum(grad, axis=0, keepdims=True)
            mod_rows[here, pl.ds(width, width)] = jnp.sum(grad * (normal * first_gain[...]), axis=0, keepdims=True)
            grad_line = grad * (1.0 + mod_part(number, 1))
            gain_sum = gain_sum + jnp.sum(grad_line * normal, axis=0, keepdims=True)
            grad_normal = grad_line * first_gain[...]
            along = mean_of(grad_normal * normal)
            term = (grad_normal - mean_of(grad_normal) - normal * along) * inverse
            input_grad[rows, :] = (grad_middle[rows, :] + term).astype(BF16)
        small_acc[0, pl.ds(FIRST_GAIN, 1), :] = gain_sum
        for part in range(6):
            small_acc[0, pl.ds(MOD_BIAS + part, 1), :] = jnp.sum(
                mod_rows[:, pl.ds(part * width, width)], axis=0, keepdims=True
            )

        def small_copy(number):
            return pltpu.make_async_remote_copy(
                small_acc.at[number], small_got.at[number], small_send.at[number], small_recv.at[number],
                device_id=greet[(1 + number) % len(greet)], device_id_type=MESH_ID,
            )

        def small_step(number):
            small_copy(number).wait_recv()
            small_acc[number + 1] = small_acc[number] + small_got[number]
            if number + 1 < len(greet):
                small_copy(number + 1).start()

        small_copy(0).start()

        mod_axes = (CORE, Y, Z1, Z2, X)

        def mod_copies(number):
            mods = (mod_zero, mod_one, mod_two, mod_three, mod_four)
            conds = (cond_zero, cond_one, cond_two, cond_three, cond_four)
            if number == 0:
                pairs = ((mod_zero.at[:, :, :, 1 - core], mod_got), (cond_zero, cond_got))
            else:
                later = ((mod_two, cond_two), (mod_three, cond_three), (mod_four, cond_four), (mod_five, cond_five))[number - 1]
                chunks = pl.ds(2 ** (number - 1), 2 ** (number - 1))
                if number == 1:
                    source = mod_one.at[:, :, :, 1 - bits[Y]]
                elif number == 2:
                    source = mod_two.at[:, :, 1 - bits[Z1]]
                elif number == 3:
                    source = mod_three.at[:, 1 - bits[Z2]]
                else:
                    source = mod_four
                pairs = ((source, later[0].at[chunks]), (conds[number], later[1].at[chunks]))
            return [
                pltpu.make_async_remote_copy(
                    source, target, mod_send.at[place, number], mod_recv.at[place, number],
                    device_id=exchange_partner(mod_axes[number], extra_bits), device_id_type=MESH_ID,
                )
                for place, (source, target) in enumerate(pairs)
            ]

        def mod_step(number):
            for copy in mod_copies(number):
                copy.wait_recv()
            if number == 0:
                mod_one[0] = mod_zero[:, :, :, core]
                mod_one[0, :, :, :, pl.ds(4, 4), :] = mod_got[:, :, :, pl.ds(0, 4), :]
                cond_one[0] = cond_zero[...]
                cond_one[0, pl.ds(4, 4), :] = cond_got[pl.ds(0, 4), :]
            if number == 0:
                mod_two[0] = mod_one[0, :, :, bits[Y]]
                cond_two[0] = cond_one[0]
            elif number == 1:
                mod_three[pl.ds(0, 2)] = mod_two[:, :, bits[Z1]]
                cond_three[pl.ds(0, 2)] = cond_two[...]
            elif number == 2:
                mod_four[pl.ds(0, 4)] = mod_three[:, bits[Z2]]
                cond_four[pl.ds(0, 4)] = cond_three[...]
            elif number == 3:
                mod_five[pl.ds(0, 8)] = mod_four[...]
                cond_five[pl.ds(0, 8)] = cond_four[...]
            if number < 4:
                for copy in mod_copies(number + 1):
                    copy.start()

        mod_zero[...] = jnp.zeros_like(mod_zero)
        columns = 6 * width // 16
        for group in range(16):
            at = (group >> 3, (group >> 2) & 1, (group >> 1) & 1, group & 1)
            mod_zero[at + (pl.ds(0, blocks), pl.ds(0, columns))] = mod_rows[:, pl.ds(group * columns, columns)]
        cond_zero[...] = condition[...]
        for copy in mod_copies(0):
            copy.start()

        for number in range(4):
            for stream in triple:
                if number < 3:
                    step(stream, number + 1)
            mod_step(number)
            small_step(number)
        for number, stream in enumerate(triple):
            stream.add(4, sums, 432 + 48 * number)
        mod_step(4)
        chunk_rows = mod_five.shape[0] * mod_five.shape[1]
        gathered = mod_five[...].reshape(chunk_rows, LANES)
        embedded = cond_five[...].reshape(chunk_rows, 128).astype(BF16)
        upper = gathered.astype(BF16)
        lower = (gathered - upper.astype(F32)).astype(BF16)
        mod_out[...] = dot_tn(embedded, upper) + dot_tn(embedded, lower)
        for number in range(4, len(greet)):
            small_step(number)
        small_out[...] = small_acc[len(greet)]
        for stream in triple:
            stream.done()
        for number in range(5):
            for copy in mod_copies(number):
                copy.wait_send()
        for number in range(len(greet)):
            small_copy(number).wait_send()

    pl.run_scoped(
        attention_phase,
        pltpu.VMEM((tokens, width), BF16), pltpu.VMEM((tokens, width), BF16), pltpu.VMEM((width, 3 * width), BF16),
        pltpu.VMEM((2, width, tokens), BF16), pltpu.VMEM((width, tokens), F32), pltpu.VMEM((tokens, width), F32),
        pltpu.VMEM((tokens, width), F32), pltpu.VMEM((tokens, 3 * width), BF16), pltpu.VMEM((tokens, width), F32),
        pltpu.VMEM((2, 2, 2, 2, 2, 144, LANES), BF16),
    )

    for tile in range(tiles):
        for copy in core_copies(tile):
            copy.wait_send()
    for stream in one + two + red + [one_merge, two_merge, red_merge, out]:
        stream.done()
    for swap in swaps():
        swap.wait_send()


def backward(segments, lengths, modulation, gate_grads, small, condition, table, first_gain, second_gain, *arrays):
    tokens, width = arrays[6].shape
    all_bits = lax.axis_size("dp").bit_length() - 1
    extra_bits = all_bits - GROUP_BITS
    steps = all_bits + 1
    smem, vmem = pl.BlockSpec(memory_space=pltpu.SMEM), pl.BlockSpec(memory_space=pltpu.VMEM)
    hbm = pl.BlockSpec(memory_space=pl.ANY)
    tiles = arrays[3].shape[0]

    def rows_of(count, free, lead=()):
        return pltpu.VMEM(lead + (2,) * free + (count, LANES), BF16)

    def half(dtype):
        return pltpu.VMEM((tokens, width), dtype)

    features = pltpu.VMEM((tokens, 128), BF16)
    both = pltpu.VMEM((2, tokens, width), BF16)
    group_rows = [rows_of(count, free) for count in (48, 144) for free in (4, 3, 2, 1, 0)]
    halves = [rows_of(count, free, (2,)) if free >= 0 else rows_of(count, 0) for count in (96, 96, 192) for free in (2, 1, 0, -1)]
    mods = [pltpu.VMEM(shape + (8, LANES), F32) for shape in ((2, 2, 2, 2), (2, 2, 2), (1, 2, 2, 2), (2, 2, 2), (4, 2), (8,), (16,))]
    conds = [pltpu.VMEM(shape + (8, 128), F32) for shape in ((), (), (1,), (2,), (4,), (8,), (16,))]
    dma = pltpu.SemaphoreType.DMA
    return pl.pallas_call(
        functools.partial(backward_kernel, extra_bits, all_bits),
        out_shape=(
            jax.ShapeDtypeStruct((tokens, width), BF16),
            jax.ShapeDtypeStruct((576, LANES), F32),
            jax.ShapeDtypeStruct((128, LANES), F32),
            jax.ShapeDtypeStruct((SMALL_ROWS, width), F32),
        ),
        in_specs=[smem] * 2 + [vmem] * 7 + [hbm] * len(arrays),
        out_specs=(vmem,) * 4,
        scratch_shapes=[rows_of(192, 5), rows_of(192, 5), rows_of(48, 5), rows_of(192, 4), rows_of(192, 4)]
        + halves
        + group_rows
        + [both, both, both, features, pltpu.VMEM((2, tokens, 128), BF16)]
        + [half(F32), half(BF16), features, half(BF16), features, features]
        + [pltpu.VMEM((tokens // BLOCK, 6 * width), F32)]
        + [pltpu.VMEM((steps + 1, SMALL_ROWS, width), F32), pltpu.VMEM((steps, SMALL_ROWS, width), F32)]
        + mods
        + conds
        + [dma((16,)), dma((4, tiles)), dma((2, tiles)), dma((2, tiles)), dma((13, 5)), dma((13, 5)), dma((3,)), dma((3,))]
        + [dma((steps,)), dma((steps,)), dma((2, 5)), dma((2, 5))],
        compiler_params=pltpu.CompilerParams(
            collective_id=2, has_side_effects=True, vmem_limit_bytes=63 << 20
        ),
    )(segments, lengths, modulation, gate_grads, small, condition, table, first_gain, second_gain, *arrays)


def scatter_rest(block, dp_size):
    group = dp_size >> GROUP_BITS
    if group == 1:
        return block
    groups = [[first * group + place for place in range(group)] for first in range(dp_size // group)]
    return lax.psum_scatter(block, "dp", scatter_dimension=0, axis_index_groups=groups, tiled=True)


def local(
    hidden_in,
    segment_ids,
    piece_lengths,
    time_index,
    first_gain,
    modulation_weight,
    modulation_bias,
    query_key_value_weight,
    attention_output_matrix,
    second_gain,
    widen_weight,
    expand_bias,
    narrow_weight,
    reduce_bias,
    cotangent,
):
    slot_count, own_rows, width = hidden_in.shape
    hidden, cot = hidden_in[0], cotangent[0]
    table = jnp.asarray(angle_table())
    gain_one, gain_two = first_gain[None, :], second_gain[None, :]
    normed, queries, keys, values, attended, query_features, key_features, modulation, condition = forward(
        segment_ids, piece_lengths, time_index, hidden, table, gain_one, modulation_weight,
        modulation_bias[None, :], query_key_value_weight,
    )
    block_out, grad_low, normed_two, normal, spread_row, projected, gate_grads, small, activated, slope = mlp(
        segment_ids, piece_lengths, hidden, attended, cot, modulation, gain_two, expand_bias[None, :],
        reduce_bias[None, :], attention_output_matrix, widen_weight, narrow_weight,
    )
    input_grad, block_sum, mod_sum, small_sum = backward(
        segment_ids, piece_lengths, modulation, gate_grads, small, condition, table, gain_one, gain_two,
        narrow_weight, widen_weight, attention_output_matrix, activated, slope, normed_two, grad_low, normal,
        spread_row, projected, attended, cot, queries, keys, values, query_features, key_features, normed, hidden,
        query_key_value_weight,
    )
    dp_size = lax.axis_size("dp")
    expand_block = scatter_rest(block_sum[:192], dp_size).T
    reduce_block = block_sum[192:384].reshape(4, -1, LANES).transpose(1, 0, 2).reshape(-1, 4 * LANES)
    reduce_block = scatter_rest(reduce_block, dp_size).T
    output_block = scatter_rest(block_sum[384:432], dp_size).T
    triple_block = scatter_rest(block_sum[432:576], dp_size).T
    half = mod_sum.shape[0] // 2
    mod_block = lax.dynamic_slice_in_dim(mod_sum, lax.axis_index("seq") * half, half, 0)[:, : 6 * width // 16]
    mod_block = scatter_rest(mod_block.T, dp_size).T
    stats = small_sum[STATS]
    return (
        block_out[None],
        input_grad[None],
        small_sum[FIRST_GAIN],
        mod_block,
        small_sum[MOD_BIAS : MOD_BIAS + 6].reshape(-1),
        triple_block,
        output_block,
        small_sum[SECOND_GAIN],
        expand_block,
        small_sum[EXPAND_BIAS : EXPAND_BIAS + 4].reshape(-1),
        reduce_block,
        small_sum[REDUCE_BIAS],
        jnp.sqrt(stats[:3] / (stats[3] * width)),
    )


def solution(mesh):
    in_specs = (
        P("dp", "seq", None),
        P("dp", None),
        P("dp", None),
        P("dp", None),
        P(),
        P(),
        P(),
        P(),
        P(),
        P(),
        P(),
        P(),
        P(),
        P(),
        P("dp", "seq", None),
    )
    out_specs = (
        P("dp", "seq", None),
        P("dp", "seq", None),
        P(),
        P("seq", "dp"),
        P(),
        P("seq", "dp"),
        P("seq", "dp"),
        P(),
        P("seq", "dp"),
        P(),
        P("seq", "dp"),
        P(),
        P(),
    )
    return jax.shard_map(local, mesh=mesh, in_specs=in_specs, out_specs=out_specs, check_vma=False)
```

```python
import functools
import math

import jax
import jax.numpy as jnp
import numpy as np
from jax import lax
from jax.experimental import pallas as pl
from jax.experimental.pallas import tpu as pltpu
from jax.sharding import PartitionSpec as P

HEADS = 12
BLOCK = 128
MAX_SEQUENCES = 8
SEGMENT_LANE = 40
MASKED = -1000000000.0
LANES = 384
GROUP_BITS = 4
MESH_ID = pl.DeviceIdType.MESH
F32, BF16 = jnp.float32, jnp.bfloat16

ROTARY_COS, ROTARY_SIN, BLOCK_COS, BLOCK_SIN = 0, 128, 256, 264
HIGH_COS, HIGH_SIN, LOW_COS, LOW_SIN, TABLE_ROWS = 272, 304, 336, 368, 400

FIRST_GAIN, MOD_BIAS, SECOND_GAIN, EXPAND_BIAS, REDUCE_BIAS, STATS, SMALL_ROWS = 0, 1, 7, 8, 12, 13, 16


def angle_table():
    lane = np.arange(128)
    rotary = np.exp((lane % 32) * (-2.0 * math.log(10000.0) / 64))
    timing = np.exp((lane % 64) * (-math.log(10000.0) / 64))
    steps = np.arange(128)[:, None]
    angles = [
        (np.cos, steps * rotary), (np.sin, steps * rotary),
        (np.cos, steps[:8] * 128 * rotary), (np.sin, steps[:8] * 128 * rotary),
        (np.cos, steps[:32] * 32 * timing), (np.sin, steps[:32] * 32 * timing),
        (np.cos, steps[:32] * timing), (np.sin, steps[:32] * timing),
    ]
    return np.concatenate([fn(angle) for fn, angle in angles]).astype(np.float32)


def dot(left, right):
    return jnp.dot(left, right, preferred_element_type=F32)


def dot_nt(left, right):
    return lax.dot_general(left, right, (((1,), (1,)), ((), ())), preferred_element_type=F32)


def dot_tn(left, right):
    return lax.dot_general(left, right, (((0,), (0,)), ((), ())), preferred_element_type=F32)


def lane_iota(shape):
    return lax.broadcasted_iota(jnp.int32, shape, len(shape) - 1)


def row_iota(shape):
    return lax.broadcasted_iota(jnp.int32, shape, 0)


def block_place(segments, lengths, block):
    segment = segments[0, block * BLOCK]
    before = jnp.int32(0)
    for other in range(segments.shape[1] // BLOCK):
        same = (segments[0, other * BLOCK] == segment) & (other < block)
        before = before + jnp.where(same, 1, 0)
    return segment, before, lengths[0, segment] - before * BLOCK


def rotary_block(table, before):
    cos_row, sin_row = table[pl.ds(ROTARY_COS, 128), :], table[pl.ds(ROTARY_SIN, 128), :]
    cos_block = table[pl.ds(BLOCK_COS + before, 1), :]
    sin_block = table[pl.ds(BLOCK_SIN + before, 1), :]
    cosine = cos_row * cos_block - sin_row * sin_block
    sine = sin_row * cos_block + cos_row * sin_block
    first_half = lane_iota(sine.shape) % 64 < 32
    return cosine, jnp.where(first_half, -sine, sine)


def turn(values, cosine, sine):
    first_half = lane_iota(values.shape) % 64 < 32
    swapped = jnp.where(first_half, pltpu.roll(values, 96, 1), pltpu.roll(values, 32, 1))
    return values * cosine + swapped * sine


def mean_of(values):
    return jnp.mean(values, axis=-1, keepdims=True)


def split_three(values):
    first = values.astype(BF16)
    rest = values - first.astype(F32)
    second = rest.astype(BF16)
    third = (rest - second.astype(F32)).astype(BF16)
    place = lane_iota(values.shape) % 3
    picked = jnp.where(place == 0, first.astype(F32), jnp.where(place == 1, second.astype(F32), third.astype(F32)))
    return picked.astype(BF16)


def forward_kernel(
    segments, lengths, times, hidden, table, first_gain, mod_weight, mod_bias, weight,
    normed, queries, keys, values, attended, query_features, key_features, modulation, condition,
    other_hidden, turned_values, out_t, peak, total, send_sem, recv_sem,
):
    tokens, width = hidden.shape
    blocks = tokens // BLOCK
    seq = lax.axis_index("seq")
    partner = (lax.axis_index("dp"), 1 - seq)
    barrier = pltpu.get_barrier_semaphore()
    pl.semaphore_signal(barrier, inc=1, device_id=partner, device_id_type=MESH_ID)
    pl.semaphore_wait(barrier, 1)
    exchange = pltpu.make_async_remote_copy(
        hidden, other_hidden, send_sem, recv_sem, device_id=partner, device_id_type=MESH_ID
    )
    exchange.start()

    places = []
    for number in range(2 * blocks):
        block = (seq if number < blocks else 1 - seq) * blocks + number % blocks
        places.append(block_place(segments, lengths, block))
        time = times[0, places[number][0]]
        high, low = time // 32, time % 32
        cos_high, sin_high = table[pl.ds(HIGH_COS + high, 1), :], table[pl.ds(HIGH_SIN + high, 1), :]
        cos_low, sin_low = table[pl.ds(LOW_COS + low, 1), :], table[pl.ds(LOW_SIN + low, 1), :]
        cosine = cos_high * cos_low - sin_high * sin_low
        sine = sin_high * cos_low + cos_high * sin_low
        row = jnp.where(lane_iota(cosine.shape) < 64, cosine, sine)
        condition[pl.ds(number, 1), :] = row.astype(BF16).astype(F32)
    modulation[...] = dot(condition[...].astype(BF16), mod_weight[...]) + mod_bias[...]

    lane = lane_iota((BLOCK, 128))
    row = row_iota((BLOCK, 128))

    for part in range(2):
        source = hidden if part == 0 else other_hidden
        if part == 1:
            exchange.wait_recv()
        turns = []
        for number in range(blocks):
            rows = pl.ds(number * BLOCK, BLOCK)
            segment, before, valid_count = places[part * blocks + number]
            turns.append(rotary_block(table, before))
            mine = lane == SEGMENT_LANE + segment
            in_lanes = (lane >= SEGMENT_LANE) & (lane < SEGMENT_LANE + MAX_SEQUENCES)
            blocked = in_lanes & jnp.logical_not(mine & (row < valid_count))
            key_features[part, rows, :] = jnp.where(blocked, MASKED, 0.0).astype(BF16)
            if part == 0:
                query_features[rows, :] = jnp.where(mine, 1.0, 0.0).astype(BF16)
            mod_row = pl.ds(part * blocks + number, 1)
            shift, scale = modulation[mod_row, pl.ds(0, width)], modulation[mod_row, pl.ds(width, width)]
            value = source[rows, :].astype(F32)
            centered = value - mean_of(value)
            spread = mean_of(centered * centered)
            line = centered * lax.rsqrt(spread + 1e-05) * first_gain[...]
            result = (line * (1.0 + scale) + shift).astype(BF16)
            if part == 0:
                normed[rows, :] = result
            else:
                other_hidden[rows, :] = result
        normed_source = normed if part == 0 else other_hidden
        for tile in range(3 * width // LANES):
            which, first = divmod(tile * LANES, width)
            product = dot(normed_source[...], weight[:, pl.ds(tile * LANES, LANES)])
            target = (queries, keys, values)[which]
            for number in range(blocks):
                cosine, sine = turns[number]
                for pair in range(LANES // 128):
                    piece = product[number * BLOCK : (number + 1) * BLOCK, pair * 128 : (pair + 1) * 128]
                    if which < 2:
                        piece = turn(piece, cosine, sine)
                    if which == 0:
                        piece = piece.astype(BF16).astype(F32) * 0.125
                    target[part, pl.ds(number * BLOCK, BLOCK), pl.ds(first + pair * 128, 128)] = piece.astype(BF16)
        turned_values[...] = jnp.transpose(values[part])

        def attend(pair, carry):
            lanes = pl.ds(pl.multiple_of(pair * 128, 128), 128)
            query_pair, key_pair = queries[0, :, lanes], keys[part, :, lanes]
            left = jnp.concatenate([key_pair, key_features[part]], axis=1)
            pair_lane = lane_iota(query_pair.shape)
            for half in range(2):
                head = pair * 2 + half
                head_rows = pl.ds(pl.multiple_of(head * 64, 64), 64)
                one_row = pl.ds(head, 1)
                query = jnp.where((pair_lane < 64) == (half == 0), query_pair, jnp.zeros_like(query_pair))
                scores = dot_nt(left, jnp.concatenate([query, query_features[...]], axis=1))
                top = jnp.max(scores, axis=0, keepdims=True)
                if part == 1:
                    top = jnp.maximum(top, peak[one_row, :])
                weights = jnp.exp(scores - top)
                summed = jnp.sum(weights, axis=0, keepdims=True)
                mixed = dot(turned_values[head_rows, :], weights.astype(BF16))
                if part == 0:
                    out_t[head_rows, :] = mixed
                    total[one_row, :] = summed
                    peak[one_row, :] = top
                else:
                    rescale = jnp.exp(peak[one_row, :] - top)
                    summed = summed + rescale * total[one_row, :]
                    out_t[head_rows, :] = (out_t[head_rows, :] * rescale + mixed) * (1.0 / summed)
                    peak[one_row, :] = top + jnp.log(summed)
            return carry

        lax.fori_loop(0, HEADS // 2, attend, 0)

    attended[...] = jnp.transpose(out_t[...].astype(BF16))
    log_rows = jnp.concatenate(
        [jnp.broadcast_to(peak[pl.ds(head, 1), :], (3, tokens)) for head in range(HEADS)]
        + [jnp.zeros((128 - 3 * HEADS, tokens), F32)], axis=0,
    )
    query_features[...] = query_features[...] + split_three(jnp.transpose(log_rows))
    exchange.wait_send()


def forward(segments, lengths, times, hidden, table, first_gain, mod_weight, mod_bias, weight):
    tokens, width = hidden.shape
    blocks = 2 * tokens // BLOCK
    half = jax.ShapeDtypeStruct((tokens, width), BF16)
    both = jax.ShapeDtypeStruct((2, tokens, width), BF16)
    smem, vmem = pl.BlockSpec(memory_space=pltpu.SMEM), pl.BlockSpec(memory_space=pltpu.VMEM)
    return pl.pallas_call(
        forward_kernel,
        out_shape=(
            half, both, both, both, half,
            jax.ShapeDtypeStruct((tokens, 128), BF16),
            jax.ShapeDtypeStruct((2, tokens, 128), BF16),
            jax.ShapeDtypeStruct((blocks, 6 * width), F32),
            jax.ShapeDtypeStruct((blocks, 128), F32),
        ),
        in_specs=[smem] * 3 + [vmem] * 6,
        out_specs=(vmem,) * 9,
        scratch_shapes=[
            pltpu.VMEM((tokens, width), BF16),
            pltpu.VMEM((width, tokens), BF16),
            pltpu.VMEM((width, tokens), F32),
            pltpu.VMEM((16, tokens), F32),
            pltpu.VMEM((16, tokens), F32),
            pltpu.SemaphoreType.DMA,
            pltpu.SemaphoreType.DMA,
        ],
        compiler_params=pltpu.CompilerParams(
            collective_id=1, has_side_effects=True, vmem_limit_bytes=56 << 20
        ),
    )(segments, lengths, times, hidden, table, first_gain, mod_weight, mod_bias, weight)


TILE = 384
Z2, Z1, Y, CORE, X = 0, 1, 2, 3, 4


def exchange_partner(axis, extra_bits):
    dp, seq = lax.axis_index("dp"), lax.axis_index("seq")
    if axis == X:
        return (dp, 1 - seq)
    return (dp ^ (1 << (GROUP_BITS - 1 - axis + extra_bits)), seq)


def own_bit(axis, extra_bits):
    if axis == X:
        return lax.axis_index("seq")
    return (lax.axis_index("dp") >> (GROUP_BITS - 1 - axis + extra_bits)) & 1


class Stream:
    def __init__(self, kit, number, part, first, count, fixed, order, got, got_first=0):
        self.kit, self.number, self.part, self.first, self.count = kit, number, part, first, count
        self.fixed, self.order, self.got, self.got_first = fixed, order, got, got_first

    def free(self, stage):
        return [axis for axis in range(5) if axis not in self.fixed and axis not in self.order[: stage + 1]]

    def copy(self, stage):
        bits = self.kit["bits"]
        index = [slice(None)] * 5
        for axis, value in self.fixed.items():
            index[axis] = value
        for axis in self.order[:stage]:
            index[axis] = bits[axis]
        index[self.order[stage]] = 1 - bits[self.order[stage]]
        target = (slice(None),) * len(self.free(stage)) + (pl.ds(self.got_first, self.count),)
        return pltpu.make_async_remote_copy(
            self.part.at[tuple(index) + (pl.ds(self.first, self.count),)],
            self.got[stage].at[target],
            self.kit["send"].at[self.number, stage],
            self.kit["recv"].at[self.number, stage],
            device_id=exchange_partner(self.order[stage], self.kit["extra"]),
            device_id_type=MESH_ID,
        )

    def send(self, stage):
        self.copy(stage).start()

    def add(self, stage, total=None, total_first=0):
        self.copy(stage).wait_recv()
        bits, free = self.kit["bits"], self.free(stage)
        rows, got_rows = pl.ds(self.first, self.count), pl.ds(self.got_first, self.count)

        def one(step, carry):
            index = list(bits)
            for axis, value in self.fixed.items():
                index[axis] = value
            place = []
            for order, axis in enumerate(free):
                index[axis] = (step >> (len(free) - 1 - order)) & 1
                place.append(index[axis])
            mine, theirs = self.part[tuple(index) + (rows,)], self.got[stage][tuple(place) + (got_rows,)]
            if total is None:
                self.part[tuple(index) + (rows,)] = mine + theirs
            else:
                total[pl.ds(total_first, self.count), :] = mine.astype(F32) + theirs.astype(F32)
            return carry

        if free:
            lax.fori_loop(0, 2 ** len(free), one, 0)
        else:
            one(0, 0)

    def done(self):
        for stage in range(len(self.order)):
            self.copy(stage).wait_send()


def backward_kernel(
    extra_bits, all_bits,
    segments, lengths, modulation, condition, table, first_gain, second_gain, expand_bias, reduce_bias,
    narrow_hbm, widen_hbm, out_weight_hbm, attended_hbm, cotangent_hbm, queries_hbm, keys_hbm, values_hbm,
    query_features_hbm, key_features_hbm, normed_hbm, hidden_hbm, weight_hbm,
    block_out, input_grad, sums, mod_out, small_out,
    expand_part, reduce_part, output_part,
    expand_got, reduce_got, wide_a, wide_b, wide_z, wide_last, red_a, red_b, red_c, red_last,
    out_a, out_b, out_c, out_d, out_e, tri_a, tri_b, tri_c, tri_d, tri_e,
    queries, keys, values, query_features, key_features,
    grad_middle, grad_attended, delta_features, other_grad, other_delta, other_features, mod_rows,
    small_acc, small_got, late_acc, late_got, mod_zero, mod_got, mod_one, mod_two, mod_three, mod_four, mod_five,
    cond_zero, cond_got, cond_one, cond_two, cond_three, cond_four, cond_five,
    load_sem, tile_sem, core_send, core_recv, stream_send, stream_recv, swap_send, swap_recv,
    small_send, small_recv, late_send, late_recv, mod_send, mod_recv,
):
    tokens, width = input_grad.shape
    tiles = narrow_hbm.shape[0] // TILE
    blocks = tokens // BLOCK
    seq = lax.axis_index("seq")
    dp = lax.axis_index("dp")
    bits = [own_bit(axis, extra_bits) for axis in range(5)]
    kit = {"bits": bits, "send": stream_send, "recv": stream_recv, "extra": extra_bits}
    core = bits[CORE]

    def others(*axes):
        return {axis: bits[axis] for axis in range(5) if axis not in axes}

    def chosen(**values):
        return {CORE: core, **{{"z2": Z2, "z1": Z1, "x": X}[name]: value for name, value in values.items()}}

    wide = [
        Stream(kit, g, expand_part, 0, 192, chosen(z2=g >> 1, z1=g & 1), (Y, X) if g == 3 else (X, Y), (wide_a.at[g], wide_b.at[g]))
        for g in range(4)
    ]
    red = [
        Stream(
            kit, 4 + g, reduce_part, 96 * (g & 1), 96, chosen(x=g >> 1), (Y, Z1, Z2) if g & 1 else (Z1, Y, Z2),
            (red_a.at[g], red_b.at[g], red_c.at[g]),
        )
        for g in range(4)
    ]
    wide_merge = [Stream(kit, 8 + v, expand_part, 0, 192, {**others(Z1, Z2), Z2: v}, (Z1,), (wide_z.at[v],)) for v in range(2)]
    wide_end = Stream(kit, 10, expand_part, 0, 192, others(Z2), (Z2,), (wide_last,))
    red_end = [Stream(kit, 11 + h, reduce_part, 96 * h, 96, others(X), (X,), (red_last.at[h],)) for h in range(2)]
    out = Stream(kit, 13, output_part, 0, 48, {}, (CORE, Y, X, Z1, Z2), (out_a, out_b, out_c, out_d, out_e))

    greet = [(dp, 1 - seq)] + [(dp ^ (1 << bit), seq) for bit in range(all_bits)]
    barrier = pltpu.get_barrier_semaphore()
    for partner in greet:
        pl.semaphore_signal(barrier, inc=1, device_id=partner, device_id_type=MESH_ID)

    attention_loads = [
        pltpu.make_async_copy(source, target, load_sem.at[number])
        for number, (source, target) in enumerate(
            ((queries_hbm, queries), (keys_hbm, keys), (values_hbm, values),
             (query_features_hbm, query_features), (key_features_hbm, key_features))
        )
    ]
    row = row_iota((BLOCK, 1))
    keep = []
    for number in range(blocks):
        valid_count = block_place(segments, lengths, seq * blocks + number)[2]
        keep.append(jnp.where(row < valid_count, 1.0, 0.0))

    def mod_part(number, part):
        return modulation[pl.ds(number, 1), pl.ds(part * width, width)]

    def tile_lanes(tile):
        return pl.ds(pl.multiple_of(tile * TILE, TILE), TILE)

    def core_copies(tile):
        at = (tile >> 2, (tile >> 1) & 1, tile & 1)
        rows = pl.ds(pl.multiple_of((tile & 3) * 48, 16), 48)
        everywhere = (slice(None),) * 3
        partner = exchange_partner(CORE, extra_bits)
        return (
            pltpu.make_async_remote_copy(
                expand_part.at[at + (1 - core,)], expand_got.at[at], core_send.at[0, tile], core_recv.at[0, tile],
                device_id=partner, device_id_type=MESH_ID,
            ),
            pltpu.make_async_remote_copy(
                reduce_part.at[everywhere + (1 - core, tile >> 2, rows)], reduce_got.at[everywhere + (tile >> 2, rows)],
                core_send.at[1, tile], core_recv.at[1, tile], device_id=partner, device_id_type=MESH_ID,
            ),
        )

    def core_add(tile):
        at = (tile >> 2, (tile >> 1) & 1, tile & 1)
        rows = pl.ds(pl.multiple_of((tile & 3) * 48, 16), 48)
        for copy in core_copies(tile):
            copy.wait_recv()
        for side in range(2):
            expand_part[at + (core, side)] = expand_part[at + (core, side)] + expand_got[at + (side,)]
        for z2 in range(2):
            for z1 in range(2):
                for y in range(2):
                    index, got = (z2, z1, y, core, tile >> 2, rows), (z2, z1, y, tile >> 2, rows)
                    reduce_part[index] = reduce_part[index] + reduce_got[got]

    def step(stream, stage):
        stream.add(stage)
        stream.send(stage + 1)

    def mlp_phase(
        narrow, widen, out_weight, attended, hidden, cotangent, normed_two, grad_low, grad_low_t, normal, spread_row,
        projected, reduced, bias_row, grad_normed,
    ):
        def tile_loads(tile):
            lanes = tile_lanes(tile)
            pairs = ((widen_hbm.at[:, lanes], widen.at[:, lanes]), (narrow_hbm.at[lanes], narrow.at[lanes]))
            return [pltpu.make_async_copy(source, target, tile_sem.at[place, tile]) for place, (source, target) in enumerate(pairs)]

        loads = [
            pltpu.make_async_copy(source, target, load_sem.at[5 + number])
            for number, (source, target) in enumerate(
                ((cotangent_hbm, cotangent), (attended_hbm, attended), (out_weight_hbm, out_weight), (hidden_hbm, hidden))
            )
        ]
        for load in loads:
            load.start()
        for tile in range(tiles):
            for load in tile_loads(tile):
                load.start()
        for load in attention_loads:
            load.start()
        small_acc[0] = jnp.zeros_like(small_acc[0])
        grad_normed[...] = jnp.zeros_like(grad_normed)
        reduced[...] = jnp.zeros_like(reduced)
        loads[0].wait()
        bias_sum = jnp.zeros((1, width), F32)
        for number in range(blocks):
            rows = pl.ds(number * BLOCK, BLOCK)
            low = (mod_part(number, 5) * (cotangent[rows, :].astype(F32) * keep[number])).astype(BF16)
            grad_low[rows, :] = low
            bias_sum = bias_sum + jnp.sum(low.astype(F32), axis=0, keepdims=True)
        small_acc[0, pl.ds(REDUCE_BIAS, 1), :] = bias_sum
        grad_low_t[...] = jnp.transpose(grad_low[...])
        for load in loads[1:]:
            load.wait()
        for first in range(0, width, 256):
            lanes = pl.ds(first, 256)
            projected[:, lanes] = dot(attended[...], out_weight[:, lanes])
        branch_sum = jnp.zeros((1, width), F32)
        for number in range(blocks):
            rows = pl.ds(number * BLOCK, BLOCK)
            branch = mod_part(number, 2) * projected[rows, :]
            branch_sum = branch_sum + jnp.sum(keep[number] * branch * branch, axis=0, keepdims=True)
            value = hidden[rows, :].astype(F32) + branch
            centered = value - mean_of(value)
            inverse = lax.rsqrt(mean_of(centered * centered) + 1e-05)
            normal[rows, :] = centered * inverse
            spread_row[rows, :] = jnp.broadcast_to(inverse, (BLOCK, 128))
            line = normal[rows, :] * second_gain[...]
            normed_two[rows, :] = (line * (1.0 + mod_part(number, 4)) + mod_part(number, 3)).astype(BF16)
        pl.semaphore_wait(barrier, len(greet))

        def through(tile):
            lanes = tile_lanes(tile)
            for load in tile_loads(tile):
                load.wait()
            u = dot(normed_two[...], widen[:, lanes]) + expand_bias[:, lanes]
            grad_active = dot_nt(grad_low[...], narrow[lanes, :])
            square = u * u
            tanh = jnp.tanh(u * (0.7978845608028654 + 0.7978845608028654 * 0.044715 * square))
            half_sum = 0.5 + 0.5 * tanh
            active = (u * half_sum).astype(BF16)
            inner = 0.7978845608028654 + 3.0 * 0.7978845608028654 * 0.044715 * square
            slope = half_sum + (0.5 * u) * (1.0 - tanh * tanh) * inner
            grad_wide = (grad_active * slope).astype(BF16)
            reduced[...] += dot(active, narrow[lanes, :])
            reduce_t = dot(grad_low_t[...], active).astype(BF16)
            rows = pl.ds(pl.multiple_of((tile & 3) * 48, 16), 48)
            reduce_part[:, :, :, :, tile >> 2, rows] = reduce_t.reshape(2, 2, 2, 2, 48, TILE)
            bias_row[pl.ds(0, 1), lanes] = jnp.sum(grad_wide.astype(F32), axis=0, keepdims=True)
            expand_t = dot_tn(grad_wide, normed_two[...]).astype(BF16)
            at = (tile >> 2, (tile >> 1) & 1, tile & 1)
            for group in range(2):
                for side in range(2):
                    expand_part[at + (group, side)] = expand_t[
                        group * 192 : group * 192 + 192, side * LANES : side * LANES + LANES
                    ]
            for copy in core_copies(tile):
                copy.start()
            grad_normed[...] += dot_nt(grad_wide, widen[:, lanes])

        def begin(g):
            wide[g].send(0)
            red[g].send(0)

        def through_two(number, carry):
            through(2 * number)

            @pl.when(number > 0)
            def _():
                core_add(2 * number - 1)

            for g in range(tiles // 2 - 1):

                @pl.when(number == g + 1)
                def _(g=g):
                    begin(g)

            through(2 * number + 1)
            core_add(2 * number)

            @pl.when(number == 2)
            def _():
                step(wide[0], 0)
                step(red[0], 0)

            return carry

        lax.fori_loop(0, tiles // 2, through_two, 0)
        core_add(tiles - 1)
        begin(3)
        step(wide[1], 0)
        step(red[1], 0)
        for part in range(tiles * TILE // width):
            small_acc[0, pl.ds(EXPAND_BIAS + part, 1), :] = bias_row[pl.ds(0, 1), pl.ds(part * width, width)]

        gain_sum = jnp.zeros((1, width), F32)
        value_sum = jnp.zeros((1, width), F32)
        mlp_sum = jnp.zeros((1, width), F32)
        for number in range(blocks):
            rows = pl.ds(number * BLOCK, BLOCK)
            here = pl.ds(number, 1)
            full = reduced[rows, :] + reduce_bias[...]
            branch = mod_part(number, 5) * full
            value = hidden[rows, :].astype(F32) + mod_part(number, 2) * projected[rows, :] + branch
            block_out[rows, :] = value.astype(BF16)
            value_sum = value_sum + jnp.sum(keep[number] * value * value, axis=0, keepdims=True)
            mlp_sum = mlp_sum + jnp.sum(keep[number] * branch * branch, axis=0, keepdims=True)
            grad_out = cotangent[rows, :].astype(F32) * keep[number]
            mod_rows[here, pl.ds(5 * width, width)] = jnp.sum(grad_out * full, axis=0, keepdims=True)
            grad = grad_normed[rows, :]
            line = normal[rows, :] * second_gain[...]
            mod_rows[here, pl.ds(3 * width, width)] = jnp.sum(grad, axis=0, keepdims=True)
            mod_rows[here, pl.ds(4 * width, width)] = jnp.sum(grad * line, axis=0, keepdims=True)
            grad_line = grad * (1.0 + mod_part(number, 4))
            gain_sum = gain_sum + jnp.sum(grad_line * normal[rows, :], axis=0, keepdims=True)
            grad_normal = grad_line * second_gain[...]
            along = mean_of(grad_normal * normal[rows, :])
            term = (grad_normal - mean_of(grad_normal) - normal[rows, :] * along) * spread_row[rows, :1]
            total = grad_out + term
            grad_middle[rows, :] = total
            mod_rows[here, pl.ds(2 * width, width)] = jnp.sum(total * projected[rows, :], axis=0, keepdims=True)
            grad_low[rows, :] = (mod_part(number, 2) * total).astype(BF16)
            if number == 2:
                step(red[2], 0)
        small_acc[0, pl.ds(SECOND_GAIN, 1), :] = gain_sum
        lane = lane_iota((1, width))
        counts = jnp.zeros((1, 1), F32)
        for number in range(blocks):
            counts = counts + jnp.sum(keep[number], axis=0, keepdims=True)
        terms = [jnp.sum(term, axis=1, keepdims=True) for term in (value_sum, branch_sum, mlp_sum)] + [counts]
        stats = jnp.zeros((1, width), F32)
        for place, term in enumerate(terms):
            stats = jnp.where(lane == place, term, stats)
        small_acc[0, pl.ds(STATS, 1), :] = stats
        for part in range(2, 6):
            small_acc[0, pl.ds(MOD_BIAS + part, 1), :] = jnp.sum(
                mod_rows[:, pl.ds(part * width, width)], axis=0, keepdims=True
            )
        small_copy(0).start()
        step(wide[2], 0)
        wide[0].add(1)
        step(red[0], 1)

        for first in range(0, width, 256):
            grad_attended[:, pl.ds(first, 256)] = dot_nt(
                grad_low[...], out_weight[pl.ds(first, 256), :]
            ).astype(BF16)
        head_lane = row_iota((width, 128)) // 64 == lane_iota((width, 128)) // 3
        chooser = jnp.where(head_lane & (lane_iota((width, 128)) < 3 * HEADS), 1.0, 0.0).astype(BF16)
        for number in range(blocks):
            rows = pl.ds(number * BLOCK, BLOCK)
            product = grad_attended[rows, :].astype(F32) * attended[rows, :].astype(F32)
            upper = product.astype(BF16)
            lower = (product - upper.astype(F32)).astype(BF16)
            delta_features[rows, :] = split_three(dot(upper, chooser) + dot(lower, chooser))
        for load in attention_loads:
            load.wait()
        for place in range(HEADS // 2 + 2):
            swap(place).start()
        for first in range(0, width, TILE):
            output_t = dot_tn(grad_low[:, pl.ds(first, TILE)], attended[...]).astype(BF16)
            for place in range(TILE // 48):
                group = first // 48 + place
                at = (group >> 3, (group >> 2) & 1, (group >> 1) & 1, group & 1)
                for side in range(2):
                    output_part[at + (side,)] = output_t[
                        place * 48 : place * 48 + 48, side * LANES : side * LANES + LANES
                    ]
        out.send(0)
        wide[1].add(1)
        wide_merge[0].send(0)
        step(red[1], 1)

    def small_copy(number):
        return pltpu.make_async_remote_copy(
            small_acc.at[number], small_got.at[number], small_send.at[number], small_recv.at[number],
            device_id=greet[(1 + number) % len(greet)], device_id_type=MESH_ID,
        )

    def small_step(number):
        small_copy(number).wait_recv()
        small_acc[number + 1] = small_acc[number] + small_got[number]
        if number + 1 < len(greet):
            small_copy(number + 1).start()

    def swap(place):
        if isinstance(place, int) and place < 2:
            source, target = ((delta_features, other_delta), (query_features, other_features))[place]
        else:
            lanes = pl.ds(pl.multiple_of((place - 2) * 128, 128), 128)
            source, target = grad_attended.at[:, lanes], other_grad.at[:, lanes]
        return pltpu.make_async_remote_copy(
            source, target, swap_send.at[place], swap_recv.at[place], device_id=(dp, 1 - seq), device_id_type=MESH_ID
        )

    units = tiles * TILE
    low_half, wide_half = pltpu.VMEM((tokens, width), BF16), pltpu.VMEM((tokens, width), F32)
    pl.run_scoped(
        mlp_phase,
        pltpu.VMEM((units, width), BF16), pltpu.VMEM((width, units), BF16), pltpu.VMEM((width, width), BF16),
        low_half, low_half, low_half, low_half, low_half, pltpu.VMEM((width, tokens), BF16),
        wide_half, pltpu.VMEM((tokens, 128), F32), wide_half, wide_half, pltpu.VMEM((8, units), F32), wide_half,
    )

    plan = {
        0: [(step, out, 0)],
        1: [],
        2: [(red[0].add, 2), (wide_merge[0].add, 0), (small_step, 0)],
        3: [(step, red[3], 0)],
        4: [(step, wide[3], 0), (small_step, 1)],
        5: [(step, red[2], 1)],
        6: [(wide[2].add, 1), (small_step, 2)],
        7: [(red[1].add, 2), (step, out, 1)],
        8: [(red[2].add, 2), (red_end[0].send, 0), (step, red[3], 1), (small_step, 3)],
        9: [(wide[3].add, 1), (wide_merge[1].send, 0)],
        10: [(red[3].add, 2), (red_end[1].send, 0)],
        11: [(step, out, 2), (small_step, 4)],
        12: [(wide_merge[1].add, 0), (wide_end.send, 0)],
        13: [(step, out, 3)],
        14: [(red_end[0].add, 0, sums, 192), (red_end[1].add, 0, sums, 288)],
        15: [],
        16: [(wide_end.add, 0, sums, 0)],
        17: [(out.add, 4, sums, 384)],
    }

    def run_plan(pair, first, stride, count):
        for place in range(count):
            actions = plan[first + stride * place]
            if actions:

                @pl.when(pair == place)
                def _(actions=actions):
                    for action in actions:
                        action[0](*action[1:])

    def attention_phase(normed, hidden, weight, keys_t, grad_query_t, grad_key, grad_value, grad_triple, grad_normed, triple_part):
        loads = [
            pltpu.make_async_copy(source, target, load_sem.at[9 + number])
            for number, (source, target) in enumerate(((normed_hbm, normed), (hidden_hbm, hidden), (weight_hbm, weight)))
        ]
        for load in loads:
            load.start()
        for part in range(2):
            keys_t[part] = jnp.transpose(keys[part])

        def own_queries(pair, carry):
            lanes = pl.ds(pl.multiple_of(pair * 128, 128), 128)
            query_pair, grad_pair = queries[0, :, lanes], grad_attended[:, lanes]
            pair_lane = lane_iota(query_pair.shape)
            for half in range(2):
                head = pair * 2 + half
                head_rows = pl.ds(pl.multiple_of(head * 64, 64), 64)
                mine = (pair_lane < 64) == (half == 0)
                query = jnp.where(mine, query_pair, jnp.zeros_like(query_pair))
                grad = jnp.where(mine, grad_pair, jnp.zeros_like(grad_pair))
                right_scores = jnp.concatenate([query, query_features[...]], axis=1)
                right_grads = jnp.concatenate([grad, delta_features[...]], axis=1)
                head_lanes = (pair_lane >= 3 * head) & (pair_lane < 3 * head + 3)
                grad_q = jnp.zeros((64, tokens), F32)
                for part in range(2):
                    features = jnp.where(head_lanes, jnp.full_like(query_pair, -1.0), key_features[part])
                    scores = dot_nt(jnp.concatenate([keys[part, :, lanes], features], axis=1), right_scores)
                    weights = jnp.exp(scores)
                    grad_weights = dot_nt(jnp.concatenate([values[part, :, lanes], features], axis=1), right_grads)
                    grad_scores = (weights * grad_weights).astype(BF16)
                    if part == 0:
                        grad_v = dot(weights.astype(BF16), grad)
                        grad_k = dot(grad_scores, query)
                        if half == 0:
                            grad_value[:, lanes] = grad_v
                            grad_key[:, lanes] = grad_k
                        else:
                            grad_value[:, lanes] += grad_v
                            grad_key[:, lanes] += grad_k
                    grad_q = grad_q + dot(keys_t[part, head_rows, :], grad_scores)
                grad_query_t[head_rows, :] = grad_q
                run_plan(pair, half, 2, HEADS // 2)
            return carry

        lax.fori_loop(0, HEADS // 2, own_queries, 0)
        for place in range(2):
            swap(place).wait_recv()

        def other_queries(pair, carry):
            lanes = pl.ds(pl.multiple_of(pair * 128, 128), 128)
            swap(pair + 2).wait_recv()
            query_pair, grad_pair = queries[1, :, lanes], other_grad[:, lanes]
            pair_lane = lane_iota(query_pair.shape)
            grad_k = grad_key[:, lanes]
            grad_v = grad_value[:, lanes]
            for half in range(2):
                head = pair * 2 + half
                mine = (pair_lane < 64) == (half == 0)
                query = jnp.where(mine, query_pair, jnp.zeros_like(query_pair))
                grad = jnp.where(mine, grad_pair, jnp.zeros_like(grad_pair))
                head_lanes = (pair_lane >= 3 * head) & (pair_lane < 3 * head + 3)
                features = jnp.where(head_lanes, jnp.full_like(query_pair, -1.0), key_features[0])
                scores = dot_nt(
                    jnp.concatenate([keys[0, :, lanes], features], axis=1),
                    jnp.concatenate([query, other_features[...]], axis=1),
                )
                weights = jnp.exp(scores)
                grad_weights = dot_nt(
                    jnp.concatenate([values[0, :, lanes], features], axis=1),
                    jnp.concatenate([grad, other_delta[...]], axis=1),
                )
                grad_scores = (weights * grad_weights).astype(BF16)
                grad_v = grad_v + dot(weights.astype(BF16), grad)
                grad_k = grad_k + dot(grad_scores, query)
            grad_key[:, lanes] = grad_k
            grad_value[:, lanes] = grad_v
            run_plan(pair, 12, 1, HEADS // 2)
            return carry

        lax.fori_loop(0, HEADS // 2, other_queries, 0)

        grad_normed[...] = jnp.transpose(grad_query_t[...])
        for number in range(blocks):
            rows = pl.ds(number * BLOCK, BLOCK)
            before = block_place(segments, lengths, seq * blocks + number)[1]
            cosine, sine = rotary_block(table, before)
            for pair in range(HEADS // 2):
                lanes = pl.ds(pair * 128, 128)
                grad_triple[rows, lanes] = (turn(grad_normed[rows, lanes], cosine, -sine) * 0.125).astype(BF16)
                grad_triple[rows, pl.ds(width + pair * 128, 128)] = turn(grad_key[rows, lanes], cosine, -sine).astype(BF16)
            grad_triple[rows, pl.ds(2 * width, width)] = grad_value[rows, :].astype(BF16)

        for load in loads:
            load.wait()
        for part in range(2):
            triple_t = dot_tn(grad_triple[:, pl.ds(part * 1152, 1152)], normed[...]).astype(BF16)
            for place in range(8):
                at = (part, place >> 2, (place >> 1) & 1, place & 1)
                for side in range(2):
                    triple_part[at + (side,)] = triple_t[
                        place * 144 : place * 144 + 144, side * LANES : side * LANES + LANES
                    ]
        got = (tri_a, tri_b, tri_c, tri_d, tri_e)
        triple = [
            Stream(kit, 14 + number, triple_part, 48 * number, 48, {}, (CORE,) + order, got, 48 * number)
            for number, order in enumerate(((X, Y, Z1, Z2), (Y, Z1, X, Z2), (Z1, X, Y, Z2)))
        ]
        for stream in triple:
            stream.send(0)
        grad_normed[...] = jnp.zeros_like(grad_normed)
        for first in range(0, 3 * width, width):
            lanes = pl.ds(first, width)
            grad_normed[...] += dot_nt(grad_triple[:, lanes], weight[:, lanes])
        for stream in triple:
            step(stream, 0)

        gain_sum = jnp.zeros((1, width), F32)
        for number in range(blocks):
            rows, here = pl.ds(number * BLOCK, BLOCK), pl.ds(number, 1)
            value = hidden[rows, :].astype(F32)
            centered = value - mean_of(value)
            inverse = lax.rsqrt(mean_of(centered * centered) + 1e-05)
            normal = centered * inverse
            grad = grad_normed[rows, :]
            mod_rows[here, pl.ds(0, width)] = jnp.sum(grad, axis=0, keepdims=True)
            mod_rows[here, pl.ds(width, width)] = jnp.sum(grad * (normal * first_gain[...]), axis=0, keepdims=True)
            grad_line = grad * (1.0 + mod_part(number, 1))
            gain_sum = gain_sum + jnp.sum(grad_line * normal, axis=0, keepdims=True)
            grad_normal = grad_line * first_gain[...]
            along = mean_of(grad_normal * normal)
            term = (grad_normal - mean_of(grad_normal) - normal * along) * inverse
            input_grad[rows, :] = (grad_middle[rows, :] + term).astype(BF16)
        late_acc[0] = jnp.zeros_like(late_acc[0])
        late_acc[0, pl.ds(0, 1), :] = gain_sum
        for part in range(2):
            late_acc[0, pl.ds(1 + part, 1), :] = jnp.sum(mod_rows[:, pl.ds(part * width, width)], axis=0, keepdims=True)

        def late_copy(number):
            return pltpu.make_async_remote_copy(
                late_acc.at[number], late_got.at[number], late_send.at[number], late_recv.at[number],
                device_id=greet[(1 + number) % len(greet)], device_id_type=MESH_ID,
            )

        def late_step(number):
            late_copy(number).wait_recv()
            late_acc[number + 1] = late_acc[number] + late_got[number]
            if number + 1 < len(greet):
                late_copy(number + 1).start()

        late_copy(0).start()

        mod_axes = (CORE, Y, Z1, Z2, X)

        def mod_copies(number):
            mods = (mod_zero, mod_one, mod_two, mod_three, mod_four)
            conds = (cond_zero, cond_one, cond_two, cond_three, cond_four)
            if number == 0:
                pairs = ((mod_zero.at[:, :, :, 1 - core], mod_got), (cond_zero, cond_got))
            else:
                later = ((mod_two, cond_two), (mod_three, cond_three), (mod_four, cond_four), (mod_five, cond_five))[number - 1]
                chunks = pl.ds(2 ** (number - 1), 2 ** (number - 1))
                if number == 1:
                    source = mod_one.at[:, :, :, 1 - bits[Y]]
                elif number == 2:
                    source = mod_two.at[:, :, 1 - bits[Z1]]
                elif number == 3:
                    source = mod_three.at[:, 1 - bits[Z2]]
                else:
                    source = mod_four
                pairs = ((source, later[0].at[chunks]), (conds[number], later[1].at[chunks]))
            return [
                pltpu.make_async_remote_copy(
                    source, target, mod_send.at[place, number], mod_recv.at[place, number],
                    device_id=exchange_partner(mod_axes[number], extra_bits), device_id_type=MESH_ID,
                )
                for place, (source, target) in enumerate(pairs)
            ]

        def mod_step(number):
            for copy in mod_copies(number):
                copy.wait_recv()
            if number == 0:
                mod_one[0] = mod_zero[:, :, :, core]
                mod_one[0, :, :, :, pl.ds(4, 4), :] = mod_got[:, :, :, pl.ds(0, 4), :]
                cond_one[0] = cond_zero[...]
                cond_one[0, pl.ds(4, 4), :] = cond_got[pl.ds(0, 4), :]
            if number == 0:
                mod_two[0] = mod_one[0, :, :, bits[Y]]
                cond_two[0] = cond_one[0]
            elif number == 1:
                mod_three[pl.ds(0, 2)] = mod_two[:, :, bits[Z1]]
                cond_three[pl.ds(0, 2)] = cond_two[...]
            elif number == 2:
                mod_four[pl.ds(0, 4)] = mod_three[:, bits[Z2]]
                cond_four[pl.ds(0, 4)] = cond_three[...]
            elif number == 3:
                mod_five[pl.ds(0, 8)] = mod_four[...]
                cond_five[pl.ds(0, 8)] = cond_four[...]
            if number < 4:
                for copy in mod_copies(number + 1):
                    copy.start()

        mod_zero[...] = jnp.zeros_like(mod_zero)
        columns = 6 * width // 16
        for group in range(16):
            at = (group >> 3, (group >> 2) & 1, (group >> 1) & 1, group & 1)
            mod_zero[at + (pl.ds(0, blocks), pl.ds(0, columns))] = mod_rows[:, pl.ds(group * columns, columns)]
        cond_zero[...] = condition[...]
        for copy in mod_copies(0):
            copy.start()

        for number in range(4):
            mod_step(number)
            late_step(number)
            if number < 3:
                for stream in triple:
                    step(stream, number + 1)
        for number, stream in enumerate(triple):
            stream.add(4, sums, 432 + 48 * number)
        mod_step(4)
        chunk_rows = mod_five.shape[0] * mod_five.shape[1]
        gathered = mod_five[...].reshape(chunk_rows, LANES)
        embedded = cond_five[...].reshape(chunk_rows, 128).astype(BF16)
        upper = gathered.astype(BF16)
        lower = (gathered - upper.astype(F32)).astype(BF16)
        mod_out[...] = dot_tn(embedded, upper) + dot_tn(embedded, lower)
        for number in range(5, len(greet)):
            small_step(number)
        for number in range(4, len(greet)):
            late_step(number)
        small_out[...] = small_acc[len(greet)]
        small_out[pl.ds(FIRST_GAIN, 1), :] = late_acc[len(greet), pl.ds(0, 1), :]
        small_out[pl.ds(MOD_BIAS, 2), :] = late_acc[len(greet), pl.ds(1, 2), :]
        for stream in triple:
            stream.done()
        for number in range(5):
            for copy in mod_copies(number):
                copy.wait_send()
        for number in range(len(greet)):
            small_copy(number).wait_send()
            late_copy(number).wait_send()

    pl.run_scoped(
        attention_phase,
        pltpu.VMEM((tokens, width), BF16), pltpu.VMEM((tokens, width), BF16), pltpu.VMEM((width, 3 * width), BF16),
        pltpu.VMEM((2, width, tokens), BF16), pltpu.VMEM((width, tokens), F32), pltpu.VMEM((tokens, width), F32),
        pltpu.VMEM((tokens, width), F32), pltpu.VMEM((tokens, 3 * width), BF16), pltpu.VMEM((tokens, width), F32),
        pltpu.VMEM((2, 2, 2, 2, 2, 144, LANES), BF16),
    )

    for tile in range(tiles):
        for copy in core_copies(tile):
            copy.wait_send()
    for stream in wide + red + wide_merge + red_end + [wide_end, out]:
        stream.done()
    for place in range(HEADS // 2 + 2):
        swap(place).wait_send()


def backward(segments, lengths, modulation, condition, table, first_gain, second_gain, expand_bias, reduce_bias, *arrays):
    tokens, width = arrays[3].shape
    all_bits = lax.axis_size("dp").bit_length() - 1
    extra_bits = all_bits - GROUP_BITS
    steps = all_bits + 1
    smem, vmem = pl.BlockSpec(memory_space=pltpu.SMEM), pl.BlockSpec(memory_space=pltpu.VMEM)
    hbm = pl.BlockSpec(memory_space=pl.ANY)
    tiles = arrays[0].shape[0] // TILE

    def rows_of(count, free, lead=()):
        return pltpu.VMEM(lead + (2,) * free + (count, LANES), BF16)

    def half(dtype):
        return pltpu.VMEM((tokens, width), dtype)

    features = pltpu.VMEM((tokens, 128), BF16)
    both = pltpu.VMEM((2, tokens, width), BF16)
    group_rows = [rows_of(count, free) for count in (48, 144) for free in (4, 3, 2, 1, 0)]
    halves = [rows_of(192, 1, (4,)), rows_of(192, 0, (4,)), rows_of(192, 0, (2,)), rows_of(192, 0)]
    halves += [rows_of(96, 2, (4,)), rows_of(96, 1, (4,)), rows_of(96, 0, (4,)), rows_of(96, 0, (2,))]
    mods = [pltpu.VMEM(shape + (8, LANES), F32) for shape in ((2, 2, 2, 2), (2, 2, 2), (1, 2, 2, 2), (2, 2, 2), (4, 2), (8,), (16,))]
    conds = [pltpu.VMEM(shape + (8, 128), F32) for shape in ((), (), (1,), (2,), (4,), (8,), (16,))]
    dma = pltpu.SemaphoreType.DMA
    return pl.pallas_call(
        functools.partial(backward_kernel, extra_bits, all_bits),
        out_shape=(
            jax.ShapeDtypeStruct((tokens, width), BF16),
            jax.ShapeDtypeStruct((tokens, width), BF16),
            jax.ShapeDtypeStruct((576, LANES), F32),
            jax.ShapeDtypeStruct((128, LANES), F32),
            jax.ShapeDtypeStruct((SMALL_ROWS, width), F32),
        ),
        in_specs=[smem] * 2 + [vmem] * 7 + [hbm] * len(arrays),
        out_specs=(vmem,) * 5,
        scratch_shapes=[rows_of(192, 5), rows_of(192, 5), rows_of(48, 5), rows_of(192, 4), rows_of(192, 4)]
        + halves
        + group_rows
        + [both, both, both, features, pltpu.VMEM((2, tokens, 128), BF16)]
        + [half(F32), half(BF16), features, half(BF16), features, features]
        + [pltpu.VMEM((tokens // BLOCK, 6 * width), F32)]
        + [pltpu.VMEM((steps + 1, SMALL_ROWS, width), F32), pltpu.VMEM((steps, SMALL_ROWS, width), F32)]
        + [pltpu.VMEM((steps + 1, 8, width), F32), pltpu.VMEM((steps, 8, width), F32)]
        + mods
        + conds
        + [dma((12,)), dma((2, tiles)), dma((2, tiles)), dma((2, tiles)), dma((17, 5)), dma((17, 5)), dma((8,)), dma((8,))]
        + [dma((steps,)), dma((steps,)), dma((steps,)), dma((steps,)), dma((2, 5)), dma((2, 5))],
        compiler_params=pltpu.CompilerParams(
            collective_id=2, has_side_effects=True, vmem_limit_bytes=63 << 20
        ),
    )(segments, lengths, modulation, condition, table, first_gain, second_gain, expand_bias, reduce_bias, *arrays)


def scatter_rest(block, dp_size):
    group = dp_size >> GROUP_BITS
    if group == 1:
        return block
    groups = [[first * group + place for place in range(group)] for first in range(dp_size // group)]
    return lax.psum_scatter(block, "dp", scatter_dimension=0, axis_index_groups=groups, tiled=True)


def local(
    hidden_in,
    segment_ids,
    piece_lengths,
    time_index,
    first_gain,
    modulation_weight,
    modulation_bias,
    query_key_value_weight,
    attention_output_matrix,
    second_gain,
    widen_weight,
    expand_bias,
    narrow_weight,
    reduce_bias,
    cotangent,
):
    slot_count, own_rows, width = hidden_in.shape
    hidden, cot = hidden_in[0], cotangent[0]
    table = jnp.asarray(angle_table())
    gain_one, gain_two = first_gain[None, :], second_gain[None, :]
    normed, queries, keys, values, attended, query_features, key_features, modulation, condition = forward(
        segment_ids, piece_lengths, time_index, hidden, table, gain_one, modulation_weight,
        modulation_bias[None, :], query_key_value_weight,
    )
    block_out, input_grad, block_sum, mod_sum, small_sum = backward(
        segment_ids, piece_lengths, modulation, condition, table, gain_one, gain_two, expand_bias[None, :],
        reduce_bias[None, :], narrow_weight, widen_weight, attention_output_matrix, attended, cot, queries, keys, values,
        query_features, key_features, normed, hidden, query_key_value_weight,
    )
    dp_size = lax.axis_size("dp")
    expand_block = scatter_rest(block_sum[:192], dp_size).T
    reduce_block = block_sum[192:384].reshape(4, -1, LANES).transpose(1, 0, 2).reshape(-1, 4 * LANES)
    reduce_block = scatter_rest(reduce_block, dp_size).T
    output_block = scatter_rest(block_sum[384:432], dp_size).T
    triple_block = scatter_rest(block_sum[432:576], dp_size).T
    half = mod_sum.shape[0] // 2
    mod_block = lax.dynamic_slice_in_dim(mod_sum, lax.axis_index("seq") * half, half, 0)[:, : 6 * width // 16]
    mod_block = scatter_rest(mod_block.T, dp_size).T
    stats = small_sum[STATS]
    return (
        block_out[None],
        input_grad[None],
        small_sum[FIRST_GAIN],
        mod_block,
        small_sum[MOD_BIAS : MOD_BIAS + 6].reshape(-1),
        triple_block,
        output_block,
        small_sum[SECOND_GAIN],
        expand_block,
        small_sum[EXPAND_BIAS : EXPAND_BIAS + 4].reshape(-1),
        reduce_block,
        small_sum[REDUCE_BIAS],
        jnp.sqrt(stats[:3] / (stats[3] * width)),
    )


def solution(mesh):
    in_specs = (
        P("dp", "seq", None),
        P("dp", None),
        P("dp", None),
        P("dp", None),
        P(),
        P(),
        P(),
        P(),
        P(),
        P(),
        P(),
        P(),
        P(),
        P(),
        P("dp", "seq", None),
    )
    out_specs = (
        P("dp", "seq", None),
        P("dp", "seq", None),
        P(),
        P("seq", "dp"),
        P(),
        P("seq", "dp"),
        P("seq", "dp"),
        P(),
        P("seq", "dp"),
        P(),
        P("seq", "dp"),
        P(),
        P(),
    )
    return jax.shard_map(local, mesh=mesh, in_specs=in_specs, out_specs=out_specs, check_vma=False)
```

```python
import functools
import math

import jax
import jax.numpy as jnp
import numpy as np
from jax import lax
from jax.experimental import pallas as pl
from jax.experimental.pallas import tpu as pltpu
from jax.sharding import PartitionSpec as P

HEADS = 12
BLOCK = 128
MAX_SEQUENCES = 8
SEGMENT_LANE = 40
MASKED = -1000000000.0
LANES = 384
GROUP_BITS = 4
MESH_ID = pl.DeviceIdType.MESH
F32, BF16 = jnp.float32, jnp.bfloat16

ROTARY_COS, ROTARY_SIN, BLOCK_COS, BLOCK_SIN = 0, 128, 256, 264
HIGH_COS, HIGH_SIN, LOW_COS, LOW_SIN, TABLE_ROWS = 272, 304, 336, 368, 400

FIRST_GAIN, MOD_BIAS, SECOND_GAIN, EXPAND_BIAS, REDUCE_BIAS, STATS, SMALL_ROWS = 0, 1, 7, 8, 12, 13, 16


def angle_table():
    lane = np.arange(128)
    rotary = np.exp((lane % 32) * (-2.0 * math.log(10000.0) / 64))
    timing = np.exp((lane % 64) * (-math.log(10000.0) / 64))
    steps = np.arange(128)[:, None]
    angles = [
        (np.cos, steps * rotary), (np.sin, steps * rotary),
        (np.cos, steps[:8] * 128 * rotary), (np.sin, steps[:8] * 128 * rotary),
        (np.cos, steps[:32] * 32 * timing), (np.sin, steps[:32] * 32 * timing),
        (np.cos, steps[:32] * timing), (np.sin, steps[:32] * timing),
    ]
    return np.concatenate([fn(angle) for fn, angle in angles]).astype(np.float32)


def dot(left, right):
    return jnp.dot(left, right, preferred_element_type=F32)


def dot_nt(left, right):
    return lax.dot_general(left, right, (((1,), (1,)), ((), ())), preferred_element_type=F32)


def dot_tn(left, right):
    return lax.dot_general(left, right, (((0,), (0,)), ((), ())), preferred_element_type=F32)


def lane_iota(shape):
    return lax.broadcasted_iota(jnp.int32, shape, len(shape) - 1)


def row_iota(shape):
    return lax.broadcasted_iota(jnp.int32, shape, 0)


def block_place(segments, lengths, block):
    segment = segments[0, block * BLOCK]
    before = jnp.int32(0)
    for other in range(segments.shape[1] // BLOCK):
        same = (segments[0, other * BLOCK] == segment) & (other < block)
        before = before + jnp.where(same, 1, 0)
    return segment, before, lengths[0, segment] - before * BLOCK


def rotary_block(table, before):
    cos_row, sin_row = table[pl.ds(ROTARY_COS, 128), :], table[pl.ds(ROTARY_SIN, 128), :]
    cos_block = table[pl.ds(BLOCK_COS + before, 1), :]
    sin_block = table[pl.ds(BLOCK_SIN + before, 1), :]
    cosine = cos_row * cos_block - sin_row * sin_block
    sine = sin_row * cos_block + cos_row * sin_block
    first_half = lane_iota(sine.shape) % 64 < 32
    return cosine, jnp.where(first_half, -sine, sine)


def turn(values, cosine, sine):
    first_half = lane_iota(values.shape) % 64 < 32
    swapped = jnp.where(first_half, pltpu.roll(values, 96, 1), pltpu.roll(values, 32, 1))
    return values * cosine + swapped * sine


def mean_of(values):
    return jnp.mean(values, axis=-1, keepdims=True)


def split_three(values):
    first = values.astype(BF16)
    rest = values - first.astype(F32)
    second = rest.astype(BF16)
    third = (rest - second.astype(F32)).astype(BF16)
    place = lane_iota(values.shape) % 3
    picked = jnp.where(place == 0, first.astype(F32), jnp.where(place == 1, second.astype(F32), third.astype(F32)))
    return picked.astype(BF16)


def forward_kernel(
    segments, lengths, times, hidden, table, first_gain, mod_weight, mod_bias, weight,
    normed, queries, keys, values, attended, query_features, key_features, modulation, condition,
    other_hidden, turned_values, out_t, peak, total, send_sem, recv_sem,
):
    tokens, width = hidden.shape
    blocks = tokens // BLOCK
    seq = lax.axis_index("seq")
    partner = (lax.axis_index("dp"), 1 - seq)
    barrier = pltpu.get_barrier_semaphore()
    pl.semaphore_signal(barrier, inc=1, device_id=partner, device_id_type=MESH_ID)
    pl.semaphore_wait(barrier, 1)
    exchange = pltpu.make_async_remote_copy(
        hidden, other_hidden, send_sem, recv_sem, device_id=partner, device_id_type=MESH_ID
    )
    exchange.start()

    places = []
    for number in range(2 * blocks):
        block = (seq if number < blocks else 1 - seq) * blocks + number % blocks
        places.append(block_place(segments, lengths, block))
        time = times[0, places[number][0]]
        high, low = time // 32, time % 32
        cos_high, sin_high = table[pl.ds(HIGH_COS + high, 1), :], table[pl.ds(HIGH_SIN + high, 1), :]
        cos_low, sin_low = table[pl.ds(LOW_COS + low, 1), :], table[pl.ds(LOW_SIN + low, 1), :]
        cosine = cos_high * cos_low - sin_high * sin_low
        sine = sin_high * cos_low + cos_high * sin_low
        row = jnp.where(lane_iota(cosine.shape) < 64, cosine, sine)
        condition[pl.ds(number, 1), :] = row.astype(BF16).astype(F32)
    modulation[...] = dot(condition[...].astype(BF16), mod_weight[...]) + mod_bias[...]

    lane = lane_iota((BLOCK, 128))
    row = row_iota((BLOCK, 128))

    for part in range(2):
        source = hidden if part == 0 else other_hidden
        if part == 1:
            exchange.wait_recv()
        turns = []
        for number in range(blocks):
            rows = pl.ds(number * BLOCK, BLOCK)
            segment, before, valid_count = places[part * blocks + number]
            turns.append(rotary_block(table, before))
            mine = lane == SEGMENT_LANE + segment
            in_lanes = (lane >= SEGMENT_LANE) & (lane < SEGMENT_LANE + MAX_SEQUENCES)
            blocked = in_lanes & jnp.logical_not(mine & (row < valid_count))
            key_features[part, rows, :] = jnp.where(blocked, MASKED, 0.0).astype(BF16)
            if part == 0:
                query_features[rows, :] = jnp.where(mine, 1.0, 0.0).astype(BF16)
            mod_row = pl.ds(part * blocks + number, 1)
            shift, scale = modulation[mod_row, pl.ds(0, width)], modulation[mod_row, pl.ds(width, width)]
            value = source[rows, :].astype(F32)
            centered = value - mean_of(value)
            spread = mean_of(centered * centered)
            line = centered * lax.rsqrt(spread + 1e-05) * first_gain[...]
            result = (line * (1.0 + scale) + shift).astype(BF16)
            if part == 0:
                normed[rows, :] = result
            else:
                other_hidden[rows, :] = result
        normed_source = normed if part == 0 else other_hidden
        for tile in range(3 * width // LANES):
            which, first = divmod(tile * LANES, width)
            product = dot(normed_source[...], weight[:, pl.ds(tile * LANES, LANES)])
            target = (queries, keys, values)[which]
            for number in range(blocks):
                cosine, sine = turns[number]
                for pair in range(LANES // 128):
                    piece = product[number * BLOCK : (number + 1) * BLOCK, pair * 128 : (pair + 1) * 128]
                    if which < 2:
                        piece = turn(piece, cosine, sine)
                    if which == 0:
                        piece = piece.astype(BF16).astype(F32) * 0.125
                    target[part, pl.ds(number * BLOCK, BLOCK), pl.ds(first + pair * 128, 128)] = piece.astype(BF16)
        turned_values[...] = jnp.transpose(values[part])

        def attend(pair, carry):
            lanes = pl.ds(pl.multiple_of(pair * 128, 128), 128)
            query_pair, key_pair = queries[0, :, lanes], keys[part, :, lanes]
            left = jnp.concatenate([key_pair, key_features[part]], axis=1)
            pair_lane = lane_iota(query_pair.shape)
            for half in range(2):
                head = pair * 2 + half
                head_rows = pl.ds(pl.multiple_of(head * 64, 64), 64)
                one_row = pl.ds(head, 1)
                query = jnp.where((pair_lane < 64) == (half == 0), query_pair, jnp.zeros_like(query_pair))
                scores = dot_nt(left, jnp.concatenate([query, query_features[...]], axis=1))
                top = jnp.max(scores, axis=0, keepdims=True)
                if part == 1:
                    top = jnp.maximum(top, peak[one_row, :])
                weights = jnp.exp(scores - top)
                summed = jnp.sum(weights, axis=0, keepdims=True)
                mixed = dot(turned_values[head_rows, :], weights.astype(BF16))
                if part == 0:
                    out_t[head_rows, :] = mixed
                    total[one_row, :] = summed
                    peak[one_row, :] = top
                else:
                    rescale = jnp.exp(peak[one_row, :] - top)
                    summed = summed + rescale * total[one_row, :]
                    out_t[head_rows, :] = (out_t[head_rows, :] * rescale + mixed) * (1.0 / summed)
                    peak[one_row, :] = top + jnp.log(summed)
            return carry

        lax.fori_loop(0, HEADS // 2, attend, 0)

    attended[...] = jnp.transpose(out_t[...].astype(BF16))
    log_rows = jnp.concatenate(
        [jnp.broadcast_to(peak[pl.ds(head, 1), :], (3, tokens)) for head in range(HEADS)]
        + [jnp.zeros((128 - 3 * HEADS, tokens), F32)], axis=0,
    )
    query_features[...] = query_features[...] + split_three(jnp.transpose(log_rows))
    exchange.wait_send()


def forward(segments, lengths, times, hidden, table, first_gain, mod_weight, mod_bias, weight):
    tokens, width = hidden.shape
    blocks = 2 * tokens // BLOCK
    half = jax.ShapeDtypeStruct((tokens, width), BF16)
    both = jax.ShapeDtypeStruct((2, tokens, width), BF16)
    smem, vmem = pl.BlockSpec(memory_space=pltpu.SMEM), pl.BlockSpec(memory_space=pltpu.VMEM)
    return pl.pallas_call(
        forward_kernel,
        out_shape=(
            half, both, both, both, half,
            jax.ShapeDtypeStruct((tokens, 128), BF16),
            jax.ShapeDtypeStruct((2, tokens, 128), BF16),
            jax.ShapeDtypeStruct((blocks, 6 * width), F32),
            jax.ShapeDtypeStruct((blocks, 128), F32),
        ),
        in_specs=[smem] * 3 + [vmem] * 6,
        out_specs=(vmem,) * 9,
        scratch_shapes=[
            pltpu.VMEM((tokens, width), BF16),
            pltpu.VMEM((width, tokens), BF16),
            pltpu.VMEM((width, tokens), F32),
            pltpu.VMEM((16, tokens), F32),
            pltpu.VMEM((16, tokens), F32),
            pltpu.SemaphoreType.DMA,
            pltpu.SemaphoreType.DMA,
        ],
        compiler_params=pltpu.CompilerParams(
            collective_id=1, has_side_effects=True, vmem_limit_bytes=56 << 20
        ),
    )(segments, lengths, times, hidden, table, first_gain, mod_weight, mod_bias, weight)


TILE = 384
Z2, Z1, Y, CORE, X = 0, 1, 2, 3, 4


WIDE_ORDERS = ((Y, X), (X, Y), (X, Y), (X, Y))
REDUCE_ORDERS = ((Z1, Y, Z2), (Y, Z1, Z2), (Y, Z2, Z1), (Z2, Y, Z1))
OUTPUT_ORDER = (CORE, X, Y, Z1, Z2)
TRIPLE_ORDERS = ((CORE, Y, X, Z1, Z2), (CORE, Z1, Y, X, Z2), (CORE, X, Y, Z1, Z2))
PLAN = (
    (("T", 6), (("r", 0), ("w", 0),)),
    (("T", 7), (("w", 1),)),
    (("N", 0), (("r", 1),)),
    (("N", 4), (("w", 2),)),
    (("D", 0), (("s", 0), ("r", 2),)),
    (("D", 1), (("r", 0), ("w", 0),)),
    (("A", 1), (("w", 1), ("o", 0),)),
    (("A", 3), (("w", 2), ("w", 3),)),
    (("A", 4), (("r", 3), ("s", 0),)),
    (("A", 6), (("r", 1),)),
    (("A", 7), (("w", 3),)),
    (("A", 9), (("r", 3),)),
    (("A", 10), (("r", 2),)),
    (("E", 0), (("r", 0),)),
    (("B", 0), (("s", 0), ("wm", 0),)),
    (("B", 3), (("r", 1),)),
    (("B", 5), (("wm", 1),)),
    (("C", 0), (("r", 3), ("o", 0),)),
    (("C", 1), (("s", 0), ("r", 2),)),
    (("C", 4), (("q", 0),)),
    (("C", 5), (("q", 1),)),
    (("C", 6), (("re", 1), ("s", 0),)),
    (("F", 0), (("q", 2), ("o", 0), ("we", 0), ("re", 0), ("m", 0), ("q", 0), ("q", 1), ("m", 0), ("o", 0), ("q", 2), ("m", 0), ("q", 1), ("o", 0), ("q", 0), ("q", 2), ("q", 1), ("m", 0), ("q", 0), ("q", 2), ("m", 0), ("q", 1), ("q", 0), ("q", 2),)),
)


def exchange_partner(axis, extra_bits):
    dp, seq = lax.axis_index("dp"), lax.axis_index("seq")
    if axis == X:
        return (dp, 1 - seq)
    return (dp ^ (1 << (GROUP_BITS - 1 - axis + extra_bits)), seq)


def own_bit(axis, extra_bits):
    if axis == X:
        return lax.axis_index("seq")
    return (lax.axis_index("dp") >> (GROUP_BITS - 1 - axis + extra_bits)) & 1


class Stream:
    def __init__(self, kit, number, part, first, count, fixed, order, got, got_first=0, total_first=None):
        self.kit, self.number, self.part, self.first, self.count = kit, number, part, first, count
        self.fixed, self.order, self.got, self.got_first = fixed, order, got, got_first
        self.total_first = total_first

    def free(self, stage):
        return [axis for axis in range(5) if axis not in self.fixed and axis not in self.order[: stage + 1]]

    def copy(self, stage):
        bits = self.kit["bits"]
        index = [slice(None)] * 5
        for axis, value in self.fixed.items():
            index[axis] = value
        for axis in self.order[:stage]:
            index[axis] = bits[axis]
        index[self.order[stage]] = 1 - bits[self.order[stage]]
        target = (slice(None),) * len(self.free(stage)) + (pl.ds(self.got_first, self.count),)
        return pltpu.make_async_remote_copy(
            self.part.at[tuple(index) + (pl.ds(self.first, self.count),)],
            self.got[stage].at[target],
            self.kit["send"].at[self.number, stage],
            self.kit["recv"].at[self.number, stage],
            device_id=exchange_partner(self.order[stage], self.kit["extra"]),
            device_id_type=MESH_ID,
        )

    def send(self, stage):
        self.copy(stage).start()

    def add(self, stage):
        self.copy(stage).wait_recv()
        last = stage == len(self.order) - 1 and self.total_first is not None
        bits, free = self.kit["bits"], self.free(stage)
        rows, got_rows = pl.ds(self.first, self.count), pl.ds(self.got_first, self.count)

        def one(step, carry):
            index = list(bits)
            for axis, value in self.fixed.items():
                index[axis] = value
            place = []
            for order, axis in enumerate(free):
                index[axis] = (step >> (len(free) - 1 - order)) & 1
                place.append(index[axis])
            mine, theirs = self.part[tuple(index) + (rows,)], self.got[stage][tuple(place) + (got_rows,)]
            if last:
                total = mine.astype(F32) + theirs.astype(F32)
                self.kit["sums"][pl.ds(self.total_first, self.count), :] = total
            else:
                self.part[tuple(index) + (rows,)] = mine + theirs
            return carry

        if free:
            lax.fori_loop(0, 2 ** len(free), one, 0)
        else:
            one(0, 0)

    def done(self):
        for stage in range(len(self.order)):
            self.copy(stage).wait_send()


def backward_kernel(
    extra_bits, all_bits,
    segments, lengths, modulation, condition, table, first_gain, second_gain, expand_bias, reduce_bias,
    narrow_hbm, widen_hbm, out_weight_hbm, attended_hbm, cotangent_hbm, queries_hbm, keys_hbm, values_hbm,
    query_features_hbm, key_features_hbm, normed_hbm, hidden_hbm, weight_hbm,
    block_out, input_grad, sums, mod_out, small_out,
    expand_part, reduce_part, output_part,
    expand_got, reduce_got, wide_a, wide_b, wide_z, wide_last, red_a, red_b, red_c, red_last,
    out_a, out_b, out_c, out_d, out_e, tri_a, tri_b, tri_c, tri_d, tri_e,
    queries, keys, values, query_features, key_features,
    grad_middle, grad_attended, delta_features, other_grad, other_delta, other_features, mod_rows,
    small_acc, small_got, late_acc, late_got, mod_got, mod_two, mod_three, mod_four, mod_five,
    cond_zero, cond_got, cond_one, cond_two, cond_three, cond_four, cond_five,
    load_sem, tile_sem, core_send, core_recv, stream_send, stream_recv, swap_send, swap_recv,
    small_send, small_recv, late_send, late_recv, mod_send, mod_recv,
):
    tokens, width = input_grad.shape
    tiles = narrow_hbm.shape[0] // TILE
    blocks = tokens // BLOCK
    seq = lax.axis_index("seq")
    dp = lax.axis_index("dp")
    bits = [own_bit(axis, extra_bits) for axis in range(5)]
    kit = {"bits": bits, "send": stream_send, "recv": stream_recv, "extra": extra_bits, "sums": sums}
    core = bits[CORE]

    def others(*axes):
        return {axis: bits[axis] for axis in range(5) if axis not in axes}

    def chosen(**values):
        return {CORE: core, **{{"z2": Z2, "z1": Z1, "x": X}[name]: value for name, value in values.items()}}

    streams = {}
    for g in range(4):
        streams["w", g] = Stream(
            kit, g, expand_part, 0, 192, chosen(z2=g >> 1, z1=g & 1), WIDE_ORDERS[g], (wide_a.at[g], wide_b.at[g])
        )
        streams["r", g] = Stream(
            kit, 4 + g, reduce_part, 96 * (g & 1), 96, chosen(x=g >> 1), REDUCE_ORDERS[g],
            (red_a.at[g], red_b.at[g], red_c.at[g]),
        )
    for v in range(2):
        streams["wm", v] = Stream(
            kit, 8 + v, expand_part, 0, 192, {**others(Z1, Z2), Z2: v}, (Z1,), (wide_z.at[v],)
        )
        streams["re", v] = Stream(
            kit, 11 + v, reduce_part, 96 * v, 96, others(X), (X,), (red_last.at[v],), total_first=192 + 96 * v
        )
    streams["we", 0] = Stream(kit, 10, expand_part, 0, 192, others(Z2), (Z2,), (wide_last,), total_first=0)
    streams["o", 0] = Stream(
        kit, 13, output_part, 0, 48, {}, OUTPUT_ORDER, (out_a, out_b, out_c, out_d, out_e), total_first=384
    )
    merges = {
        ("wm", 0): (("w", 0), ("w", 1)), ("wm", 1): (("w", 2), ("w", 3)), ("we", 0): (("wm", 0), ("wm", 1)),
        ("re", 0): (("r", 0), ("r", 2)), ("re", 1): (("r", 1), ("r", 3)),
    }
    work, stages, finished = {}, {}, set()
    for slot, names in PLAN:
        todo = work.setdefault(slot, [])
        for name in names:
            stage = stages.get(name, 0)
            stages[name] = stage + 1
            todo.append((True, name, stage))
            if name[0] in ("m", "s"):
                continue
            if stage + 1 < (len(streams[name].order) if name in streams else 5):
                todo.append((False, name, stage + 1))
                continue
            finished.add(name)
            for merged, parts in merges.items():
                if name in parts and finished.issuperset(parts):
                    todo.append((False, merged, 0))

    def perform(slot):
        for is_add, name, stage in work.get(slot, ()):
            if name[0] == "s":
                small_step(stage)
            elif is_add:
                streams[name].add(stage)
            else:
                streams[name].send(stage)

    def perform_at(letter, first, stride, count, index):
        for place in range(count):
            slot = (letter, first + stride * place)
            if work.get(slot):

                @pl.when(index == place)
                def _(slot=slot):
                    perform(slot)

    greet = [(dp, 1 - seq)] + [(dp ^ (1 << bit), seq) for bit in range(all_bits)]
    barrier = pltpu.get_barrier_semaphore()
    for partner in greet:
        pl.semaphore_signal(barrier, inc=1, device_id=partner, device_id_type=MESH_ID)

    attention_loads = [
        pltpu.make_async_copy(source, target, load_sem.at[number])
        for number, (source, target) in enumerate(
            ((queries_hbm, queries), (keys_hbm, keys), (values_hbm, values),
             (query_features_hbm, query_features), (key_features_hbm, key_features))
        )
    ]
    row = row_iota((BLOCK, 1))
    keep = []
    for number in range(blocks):
        valid_count = block_place(segments, lengths, seq * blocks + number)[2]
        keep.append(jnp.where(row < valid_count, 1.0, 0.0))

    def mod_part(number, part):
        return modulation[pl.ds(number, 1), pl.ds(part * width, width)]

    def tile_lanes(tile):
        return pl.ds(pl.multiple_of(tile * TILE, TILE), TILE)

    def core_copies(tile):
        at = (tile >> 2, (tile >> 1) & 1, tile & 1)
        rows = pl.ds(pl.multiple_of((tile & 3) * 48, 16), 48)
        everywhere = (slice(None),) * 3
        partner = exchange_partner(CORE, extra_bits)
        return (
            pltpu.make_async_remote_copy(
                expand_part.at[at + (1 - core,)], expand_got.at[at], core_send.at[0, tile], core_recv.at[0, tile],
                device_id=partner, device_id_type=MESH_ID,
            ),
            pltpu.make_async_remote_copy(
                reduce_part.at[everywhere + (1 - core, tile >> 2, rows)], reduce_got.at[everywhere + (tile >> 2, rows)],
                core_send.at[1, tile], core_recv.at[1, tile], device_id=partner, device_id_type=MESH_ID,
            ),
        )

    def core_add(tile):
        at = (tile >> 2, (tile >> 1) & 1, tile & 1)
        rows = pl.ds(pl.multiple_of((tile & 3) * 48, 16), 48)
        for copy in core_copies(tile):
            copy.wait_recv()
        for side in range(2):
            expand_part[at + (core, side)] = expand_part[at + (core, side)] + expand_got[at + (side,)]
        for z2 in range(2):
            for z1 in range(2):
                for y in range(2):
                    index, got = (z2, z1, y, core, tile >> 2, rows), (z2, z1, y, tile >> 2, rows)
                    reduce_part[index] = reduce_part[index] + reduce_got[got]

    def mlp_phase(
        narrow, widen, out_weight, attended, hidden, cotangent, normed_two, grad_low, grad_low_t,
        projected, reduced, grad_normed,
    ):
        def tile_loads(tile):
            lanes = tile_lanes(tile)
            pairs = ((widen_hbm.at[:, lanes], widen.at[:, lanes]), (narrow_hbm.at[lanes], narrow.at[lanes]))
            return [pltpu.make_async_copy(source, target, tile_sem.at[place, tile]) for place, (source, target) in enumerate(pairs)]

        loads = [
            pltpu.make_async_copy(source, target, load_sem.at[5 + number])
            for number, (source, target) in enumerate(
                ((cotangent_hbm, cotangent), (attended_hbm, attended), (out_weight_hbm, out_weight), (hidden_hbm, hidden))
            )
        ]
        for load in loads:
            load.start()
        for tile in range(tiles):
            for load in tile_loads(tile):
                load.start()
        for load in attention_loads:
            load.start()
        small_acc[0] = jnp.zeros_like(small_acc[0])
        grad_normed[...] = jnp.zeros_like(grad_normed)
        reduced[...] = jnp.zeros_like(reduced)
        loads[0].wait()
        bias_sum = jnp.zeros((1, width), F32)
        for number in range(blocks):
            rows = pl.ds(number * BLOCK, BLOCK)
            low = (mod_part(number, 5) * (cotangent[rows, :].astype(F32) * keep[number])).astype(BF16)
            grad_low[rows, :] = low
            bias_sum = bias_sum + jnp.sum(low.astype(F32), axis=0, keepdims=True)
        small_acc[0, pl.ds(REDUCE_BIAS, 1), :] = bias_sum
        grad_low_t[...] = jnp.transpose(grad_low[...])
        for load in loads[1:]:
            load.wait()
        for first in range(0, width, 256):
            lanes = pl.ds(first, 256)
            projected[:, lanes] = dot(attended[...], out_weight[:, lanes])
        branch_sum = jnp.zeros((1, width), F32)
        for number in range(blocks):
            rows = pl.ds(number * BLOCK, BLOCK)
            branch = mod_part(number, 2) * projected[rows, :]
            branch_sum = branch_sum + jnp.sum(keep[number] * branch * branch, axis=0, keepdims=True)
            value = hidden[rows, :].astype(F32) + branch
            centered = value - mean_of(value)
            inverse = lax.rsqrt(mean_of(centered * centered) + 1e-05)
            line = centered * inverse * second_gain[...]
            normed_two[rows, :] = (line * (1.0 + mod_part(number, 4)) + mod_part(number, 3)).astype(BF16)
        pl.semaphore_wait(barrier, len(greet))

        def through(tile):
            lanes = tile_lanes(tile)
            for load in tile_loads(tile):
                load.wait()
            u = dot(normed_two[...], widen[:, lanes]) + expand_bias[:, lanes]
            grad_active = dot_nt(grad_low[...], narrow[lanes, :])
            square = u * u
            tanh = jnp.tanh(u * (0.7978845608028654 + 0.7978845608028654 * 0.044715 * square))
            half_sum = 0.5 + 0.5 * tanh
            active = (u * half_sum).astype(BF16)
            inner = 0.7978845608028654 + 3.0 * 0.7978845608028654 * 0.044715 * square
            slope = half_sum + (0.5 * u) * (1.0 - tanh * tanh) * inner
            grad_wide = (grad_active * slope).astype(BF16)
            reduced[...] += dot(active, narrow[lanes, :])
            reduce_t = dot(grad_low_t[...], active).astype(BF16)
            rows = pl.ds(pl.multiple_of((tile & 3) * 48, 16), 48)
            reduce_part[:, :, :, :, tile >> 2, rows] = reduce_t.reshape(2, 2, 2, 2, 48, TILE)
            bias_lanes = pl.ds(pl.multiple_of((tile & 1) * TILE, TILE), TILE)
            small_acc[0, pl.ds(EXPAND_BIAS + (tile >> 1), 1), bias_lanes] = jnp.sum(
                grad_wide.astype(F32), axis=0, keepdims=True
            )
            expand_t = dot_tn(grad_wide, normed_two[...]).astype(BF16)
            at = (tile >> 2, (tile >> 1) & 1, tile & 1)
            for group in range(2):
                for side in range(2):
                    expand_part[at + (group, side)] = expand_t[
                        group * 192 : group * 192 + 192, side * LANES : side * LANES + LANES
                    ]
            for copy in core_copies(tile):
                copy.start()
            grad_normed[...] += dot_nt(grad_wide, widen[:, lanes])

        def begin(g):
            streams["w", g].send(0)
            streams["r", g].send(0)

        def through_two(number, carry):
            through(2 * number)

            @pl.when(number > 0)
            def _():
                core_add(2 * number - 1)

            for g in range(tiles // 2 - 1):

                @pl.when(number == g + 1)
                def _(g=g):
                    begin(g)

            perform_at("T", 0, 2, tiles // 2, number)
            through(2 * number + 1)
            core_add(2 * number)
            perform_at("T", 1, 2, tiles // 2, number)
            return carry

        lax.fori_loop(0, tiles // 2, through_two, 0)
        core_add(tiles - 1)
        begin(3)
        gain_sum = jnp.zeros((1, width), F32)
        value_sum = jnp.zeros((1, width), F32)
        mlp_sum = jnp.zeros((1, width), F32)
        for number in range(blocks):
            perform(("N", number))
            rows = pl.ds(number * BLOCK, BLOCK)
            here = pl.ds(number, 1)
            full = reduced[rows, :] + reduce_bias[...]
            branch = mod_part(number, 5) * full
            before = hidden[rows, :].astype(F32) + mod_part(number, 2) * projected[rows, :]
            centered = before - mean_of(before)
            inverse = lax.rsqrt(mean_of(centered * centered) + 1e-05)
            normal = centered * inverse
            value = before + branch
            block_out[rows, :] = value.astype(BF16)
            value_sum = value_sum + jnp.sum(keep[number] * value * value, axis=0, keepdims=True)
            mlp_sum = mlp_sum + jnp.sum(keep[number] * branch * branch, axis=0, keepdims=True)
            grad_out = cotangent[rows, :].astype(F32) * keep[number]
            mod_rows[here, pl.ds(5 * width, width)] = jnp.sum(grad_out * full, axis=0, keepdims=True)
            grad = grad_normed[rows, :]
            line = normal * second_gain[...]
            mod_rows[here, pl.ds(3 * width, width)] = jnp.sum(grad, axis=0, keepdims=True)
            mod_rows[here, pl.ds(4 * width, width)] = jnp.sum(grad * line, axis=0, keepdims=True)
            grad_line = grad * (1.0 + mod_part(number, 4))
            gain_sum = gain_sum + jnp.sum(grad_line * normal, axis=0, keepdims=True)
            grad_normal = grad_line * second_gain[...]
            along = mean_of(grad_normal * normal)
            term = (grad_normal - mean_of(grad_normal) - normal * along) * inverse
            total = grad_out + term
            grad_middle[rows, :] = total
            mod_rows[here, pl.ds(2 * width, width)] = jnp.sum(total * projected[rows, :], axis=0, keepdims=True)
            grad_low[rows, :] = (mod_part(number, 2) * total).astype(BF16)
        small_acc[0, pl.ds(SECOND_GAIN, 1), :] = gain_sum
        lane = lane_iota((1, width))
        counts = jnp.zeros((1, 1), F32)
        for number in range(blocks):
            counts = counts + jnp.sum(keep[number], axis=0, keepdims=True)
        terms = [jnp.sum(term, axis=1, keepdims=True) for term in (value_sum, branch_sum, mlp_sum)] + [counts]
        stats = jnp.zeros((1, width), F32)
        for place, term in enumerate(terms):
            stats = jnp.where(lane == place, term, stats)
        small_acc[0, pl.ds(STATS, 1), :] = stats
        for part in range(2, 6):
            small_acc[0, pl.ds(MOD_BIAS + part, 1), :] = jnp.sum(
                mod_rows[:, pl.ds(part * width, width)], axis=0, keepdims=True
            )
        small_copy(0).start()
        perform(("N", blocks))

        for first in range(0, width, 256):
            grad_attended[:, pl.ds(first, 256)] = dot_nt(
                grad_low[...], out_weight[pl.ds(first, 256), :]
            ).astype(BF16)
        head_lane = row_iota((width, 128)) // 64 == lane_iota((width, 128)) // 3
        chooser = jnp.where(head_lane & (lane_iota((width, 128)) < 3 * HEADS), 1.0, 0.0).astype(BF16)
        for number in range(blocks):
            rows = pl.ds(number * BLOCK, BLOCK)
            product = grad_attended[rows, :].astype(F32) * attended[rows, :].astype(F32)
            upper = product.astype(BF16)
            lower = (product - upper.astype(F32)).astype(BF16)
            delta_features[rows, :] = split_three(dot(upper, chooser) + dot(lower, chooser))
        for load in attention_loads:
            load.wait()
        for place in range(HEADS // 2 + 2):
            swap(place).start()
        perform(("D", 0))
        for first in range(0, width, TILE):
            output_t = dot_tn(grad_low[:, pl.ds(first, TILE)], attended[...]).astype(BF16)
            for place in range(TILE // 48):
                group = first // 48 + place
                at = (group >> 3, (group >> 2) & 1, (group >> 1) & 1, group & 1)
                for side in range(2):
                    output_part[at + (side,)] = output_t[
                        place * 48 : place * 48 + 48, side * LANES : side * LANES + LANES
                    ]
        streams["o", 0].send(0)
        perform(("D", 1))

    def small_copy(number):
        return pltpu.make_async_remote_copy(
            small_acc.at[number], small_got.at[number], small_send.at[number], small_recv.at[number],
            device_id=greet[(1 + number) % len(greet)], device_id_type=MESH_ID,
        )

    def small_step(number):
        small_copy(number).wait_recv()
        small_acc[number + 1] = small_acc[number] + small_got[number]
        if number + 1 < len(greet):
            small_copy(number + 1).start()

    def swap(place):
        if isinstance(place, int) and place < 2:
            source, target = ((delta_features, other_delta), (query_features, other_features))[place]
        else:
            lanes = pl.ds(pl.multiple_of((place - 2) * 128, 128), 128)
            source, target = grad_attended.at[:, lanes], other_grad.at[:, lanes]
        return pltpu.make_async_remote_copy(
            source, target, swap_send.at[place], swap_recv.at[place], device_id=(dp, 1 - seq), device_id_type=MESH_ID
        )

    units = tiles * TILE
    low_half, wide_half = pltpu.VMEM((tokens, width), BF16), pltpu.VMEM((tokens, width), F32)
    pl.run_scoped(
        mlp_phase,
        pltpu.VMEM((units, width), BF16), pltpu.VMEM((width, units), BF16), pltpu.VMEM((width, width), BF16),
        low_half, low_half, low_half, low_half, low_half, pltpu.VMEM((width, tokens), BF16),
        wide_half, wide_half, wide_half,
    )

    def attention_phase(normed, hidden, weight, keys_t, grad_query_t, grad_key, grad_value, grad_triple, grad_normed, triple_part, mod_zero, mod_one):
        loads = [
            pltpu.make_async_copy(source, target, load_sem.at[9 + number])
            for number, (source, target) in enumerate(((normed_hbm, normed), (hidden_hbm, hidden), (weight_hbm, weight)))
        ]
        for load in loads:
            load.start()
        for part in range(2):
            keys_t[part] = jnp.transpose(keys[part])

        def own_queries(pair, carry):
            lanes = pl.ds(pl.multiple_of(pair * 128, 128), 128)
            query_pair, grad_pair = queries[0, :, lanes], grad_attended[:, lanes]
            pair_lane = lane_iota(query_pair.shape)
            for half in range(2):
                head = pair * 2 + half
                head_rows = pl.ds(pl.multiple_of(head * 64, 64), 64)
                mine = (pair_lane < 64) == (half == 0)
                query = jnp.where(mine, query_pair, jnp.zeros_like(query_pair))
                grad = jnp.where(mine, grad_pair, jnp.zeros_like(grad_pair))
                right_scores = jnp.concatenate([query, query_features[...]], axis=1)
                right_grads = jnp.concatenate([grad, delta_features[...]], axis=1)
                head_lanes = (pair_lane >= 3 * head) & (pair_lane < 3 * head + 3)
                grad_q = jnp.zeros((64, tokens), F32)
                for part in range(2):
                    features = jnp.where(head_lanes, jnp.full_like(query_pair, -1.0), key_features[part])
                    scores = dot_nt(jnp.concatenate([keys[part, :, lanes], features], axis=1), right_scores)
                    weights = jnp.exp(scores)
                    grad_weights = dot_nt(jnp.concatenate([values[part, :, lanes], features], axis=1), right_grads)
                    grad_scores = (weights * grad_weights).astype(BF16)
                    if part == 0:
                        grad_v = dot(weights.astype(BF16), grad)
                        grad_k = dot(grad_scores, query)
                        if half == 0:
                            grad_value[:, lanes] = grad_v
                            grad_key[:, lanes] = grad_k
                        else:
                            grad_value[:, lanes] += grad_v
                            grad_key[:, lanes] += grad_k
                    grad_q = grad_q + dot(keys_t[part, head_rows, :], grad_scores)
                grad_query_t[head_rows, :] = grad_q
                perform_at("A", half, 2, HEADS // 2, pair)
            return carry

        lax.fori_loop(0, HEADS // 2, own_queries, 0)
        for load in loads:
            load.wait()
        turns = []
        grad_normed[...] = jnp.transpose(grad_query_t[...])
        for number in range(blocks):
            rows = pl.ds(number * BLOCK, BLOCK)
            before = block_place(segments, lengths, seq * blocks + number)[1]
            cosine, sine = rotary_block(table, before)
            turns.append((cosine, -sine))
            for pair in range(HEADS // 2):
                lanes = pl.ds(pair * 128, 128)
                grad_triple[rows, lanes] = (turn(grad_normed[rows, lanes], cosine, -sine) * 0.125).astype(BF16)

        def third(part):
            triple_t = dot_tn(grad_triple[:, pl.ds(part * width, width)], normed[...]).astype(BF16)
            for place in range(width // 48):
                group, piece = divmod(part * (width // 48) + place, 3)
                at = (group >> 3, (group >> 2) & 1, (group >> 1) & 1, group & 1)
                for side in range(2):
                    triple_part[at + (side, pl.ds(48 * piece, 48))] = triple_t[
                        place * 48 : place * 48 + 48, side * LANES : side * LANES + LANES
                    ]

        third(0)
        grad_normed[...] = dot_nt(grad_triple[:, pl.ds(0, width)], weight[:, pl.ds(0, width)])
        perform(("E", 0))
        for place in range(2):
            swap(place).wait_recv()

        def other_queries(pair, carry):
            lanes = pl.ds(pl.multiple_of(pair * 128, 128), 128)
            swap(pair + 2).wait_recv()
            query_pair, grad_pair = queries[1, :, lanes], other_grad[:, lanes]
            pair_lane = lane_iota(query_pair.shape)
            grad_k = grad_key[:, lanes]
            grad_v = grad_value[:, lanes]
            for half in range(2):
                head = pair * 2 + half
                mine = (pair_lane < 64) == (half == 0)
                query = jnp.where(mine, query_pair, jnp.zeros_like(query_pair))
                grad = jnp.where(mine, grad_pair, jnp.zeros_like(grad_pair))
                head_lanes = (pair_lane >= 3 * head) & (pair_lane < 3 * head + 3)
                features = jnp.where(head_lanes, jnp.full_like(query_pair, -1.0), key_features[0])
                scores = dot_nt(
                    jnp.concatenate([keys[0, :, lanes], features], axis=1),
                    jnp.concatenate([query, other_features[...]], axis=1),
                )
                weights = jnp.exp(scores)
                grad_weights = dot_nt(
                    jnp.concatenate([values[0, :, lanes], features], axis=1),
                    jnp.concatenate([grad, other_delta[...]], axis=1),
                )
                grad_scores = (weights * grad_weights).astype(BF16)
                grad_v = grad_v + dot(weights.astype(BF16), grad)
                grad_k = grad_k + dot(grad_scores, query)
            grad_key[:, lanes] = grad_k
            grad_value[:, lanes] = grad_v
            perform_at("B", 0, 1, HEADS // 2, pair)
            return carry

        lax.fori_loop(0, HEADS // 2, other_queries, 0)

        for number in range(blocks):
            rows = pl.ds(number * BLOCK, BLOCK)
            for pair in range(HEADS // 2):
                lanes = pl.ds(pair * 128, 128)
                grad_triple[rows, pl.ds(width + pair * 128, 128)] = turn(grad_key[rows, lanes], *turns[number]).astype(BF16)
            grad_triple[rows, pl.ds(2 * width, width)] = grad_value[rows, :].astype(BF16)
        third(1)
        third(2)
        triple = [
            Stream(
                kit, 14 + number, triple_part, 48 * number, 48, {}, order, (tri_a, tri_b, tri_c, tri_d, tri_e),
                48 * number, 432 + 48 * number,
            )
            for number, order in enumerate(TRIPLE_ORDERS)
        ]
        for number, stream in enumerate(triple):
            streams["q", number] = stream
            stream.send(0)
        perform(("C", 0))
        for part in range(1, 3):
            lanes = pl.ds(part * width, width)
            grad_normed[...] += dot_nt(grad_triple[:, lanes], weight[:, lanes])
            perform(("C", part))

        gain_sum = jnp.zeros((1, width), F32)
        for number in range(blocks):
            rows, here = pl.ds(number * BLOCK, BLOCK), pl.ds(number, 1)
            value = hidden[rows, :].astype(F32)
            centered = value - mean_of(value)
            inverse = lax.rsqrt(mean_of(centered * centered) + 1e-05)
            normal = centered * inverse
            grad = grad_normed[rows, :]
            mod_rows[here, pl.ds(0, width)] = jnp.sum(grad, axis=0, keepdims=True)
            mod_rows[here, pl.ds(width, width)] = jnp.sum(grad * (normal * first_gain[...]), axis=0, keepdims=True)
            grad_line = grad * (1.0 + mod_part(number, 1))
            gain_sum = gain_sum + jnp.sum(grad_line * normal, axis=0, keepdims=True)
            grad_normal = grad_line * first_gain[...]
            along = mean_of(grad_normal * normal)
            term = (grad_normal - mean_of(grad_normal) - normal * along) * inverse
            input_grad[rows, :] = (grad_middle[rows, :] + term).astype(BF16)
            perform(("C", 3 + number))
        late_acc[0] = jnp.zeros_like(late_acc[0])
        late_acc[0, pl.ds(0, 1), :] = gain_sum
        for part in range(2):
            late_acc[0, pl.ds(1 + part, 1), :] = jnp.sum(mod_rows[:, pl.ds(part * width, width)], axis=0, keepdims=True)

        def late_copy(number):
            return pltpu.make_async_remote_copy(
                late_acc.at[number], late_got.at[number], late_send.at[number], late_recv.at[number],
                device_id=greet[(1 + number) % len(greet)], device_id_type=MESH_ID,
            )

        def late_step(number):
            late_copy(number).wait_recv()
            late_acc[number + 1] = late_acc[number] + late_got[number]
            if number + 1 < len(greet):
                late_copy(number + 1).start()

        late_copy(0).start()

        mod_axes = (CORE, Y, Z1, Z2, X)

        def mod_copies(number):
            mods = (mod_zero, mod_one, mod_two, mod_three, mod_four)
            conds = (cond_zero, cond_one, cond_two, cond_three, cond_four)
            if number == 0:
                pairs = ((mod_zero.at[:, :, :, 1 - core], mod_got), (cond_zero, cond_got))
            else:
                later = ((mod_two, cond_two), (mod_three, cond_three), (mod_four, cond_four), (mod_five, cond_five))[number - 1]
                chunks = pl.ds(2 ** (number - 1), 2 ** (number - 1))
                if number == 1:
                    source = mod_one.at[:, :, :, 1 - bits[Y]]
                elif number == 2:
                    source = mod_two.at[:, :, 1 - bits[Z1]]
                elif number == 3:
                    source = mod_three.at[:, 1 - bits[Z2]]
                else:
                    source = mod_four
                pairs = ((source, later[0].at[chunks]), (conds[number], later[1].at[chunks]))
            return [
                pltpu.make_async_remote_copy(
                    source, target, mod_send.at[place, number], mod_recv.at[place, number],
                    device_id=exchange_partner(mod_axes[number], extra_bits), device_id_type=MESH_ID,
                )
                for place, (source, target) in enumerate(pairs)
            ]

        def mod_step(number):
            for copy in mod_copies(number):
                copy.wait_recv()
            if number == 0:
                mod_one[0] = mod_zero[:, :, :, core]
                mod_one[0, :, :, :, pl.ds(4, 4), :] = mod_got[:, :, :, pl.ds(0, 4), :]
                cond_one[0] = cond_zero[...]
                cond_one[0, pl.ds(4, 4), :] = cond_got[pl.ds(0, 4), :]
            if number == 0:
                mod_two[0] = mod_one[0, :, :, bits[Y]]
                cond_two[0] = cond_one[0]
            elif number == 1:
                mod_three[pl.ds(0, 2)] = mod_two[:, :, bits[Z1]]
                cond_three[pl.ds(0, 2)] = cond_two[...]
            elif number == 2:
                mod_four[pl.ds(0, 4)] = mod_three[:, bits[Z2]]
                cond_four[pl.ds(0, 4)] = cond_three[...]
            elif number == 3:
                mod_five[pl.ds(0, 8)] = mod_four[...]
                cond_five[pl.ds(0, 8)] = cond_four[...]
            if number < 4:
                for copy in mod_copies(number + 1):
                    copy.start()

        mod_zero[...] = jnp.zeros_like(mod_zero)
        columns = 6 * width // 16
        for group in range(16):
            at = (group >> 3, (group >> 2) & 1, (group >> 1) & 1, group & 1)
            mod_zero[at + (pl.ds(0, blocks), pl.ds(0, columns))] = mod_rows[:, pl.ds(group * columns, columns)]
        cond_zero[...] = condition[...]
        for copy in mod_copies(0):
            copy.start()

        for is_add, name, stage in work[("F", 0)]:
            if name[0] == "m":
                mod_step(stage)
                late_step(stage)
            elif name[0] == "s":
                small_step(stage)
            elif is_add:
                streams[name].add(stage)
            else:
                streams[name].send(stage)
        chunk_rows = mod_five.shape[0] * mod_five.shape[1]
        gathered = mod_five[...].reshape(chunk_rows, LANES)
        embedded = cond_five[...].reshape(chunk_rows, 128).astype(BF16)
        upper = gathered.astype(BF16)
        lower = (gathered - upper.astype(F32)).astype(BF16)
        mod_out[...] = dot_tn(embedded, upper) + dot_tn(embedded, lower)
        for number in range(5, len(greet)):
            small_step(number)
        for number in range(5, len(greet)):
            late_step(number)
        small_out[...] = small_acc[len(greet)]
        small_out[pl.ds(FIRST_GAIN, 1), :] = late_acc[len(greet), pl.ds(0, 1), :]
        small_out[pl.ds(MOD_BIAS, 2), :] = late_acc[len(greet), pl.ds(1, 2), :]
        for stream in triple:
            stream.done()
        for number in range(5):
            for copy in mod_copies(number):
                copy.wait_send()
        for number in range(len(greet)):
            small_copy(number).wait_send()
            late_copy(number).wait_send()

    pl.run_scoped(
        attention_phase,
        pltpu.VMEM((tokens, width), BF16), pltpu.VMEM((tokens, width), BF16), pltpu.VMEM((width, 3 * width), BF16),
        pltpu.VMEM((2, width, tokens), BF16), pltpu.VMEM((width, tokens), F32), pltpu.VMEM((tokens, width), F32),
        pltpu.VMEM((tokens, width), F32), pltpu.VMEM((tokens, 3 * width), BF16), pltpu.VMEM((tokens, width), F32),
        pltpu.VMEM((2, 2, 2, 2, 2, 144, LANES), BF16),
        pltpu.VMEM((2, 2, 2, 2, 8, LANES), F32), pltpu.VMEM((1, 2, 2, 2, 8, LANES), F32),
    )

    for tile in range(tiles):
        for copy in core_copies(tile):
            copy.wait_send()
    for name, stream in streams.items():
        if name[0] != "q":
            stream.done()
    for place in range(HEADS // 2 + 2):
        swap(place).wait_send()


def backward(segments, lengths, modulation, condition, table, first_gain, second_gain, expand_bias, reduce_bias, *arrays):
    tokens, width = arrays[3].shape
    all_bits = lax.axis_size("dp").bit_length() - 1
    extra_bits = all_bits - GROUP_BITS
    steps = all_bits + 1
    smem, vmem = pl.BlockSpec(memory_space=pltpu.SMEM), pl.BlockSpec(memory_space=pltpu.VMEM)
    hbm = pl.BlockSpec(memory_space=pl.ANY)
    tiles = arrays[0].shape[0] // TILE

    def rows_of(count, free, lead=()):
        return pltpu.VMEM(lead + (2,) * free + (count, LANES), BF16)

    def half(dtype):
        return pltpu.VMEM((tokens, width), dtype)

    features = pltpu.VMEM((tokens, 128), BF16)
    both = pltpu.VMEM((2, tokens, width), BF16)
    group_rows = [rows_of(count, free) for count in (48, 144) for free in (4, 3, 2, 1, 0)]
    halves = [rows_of(192, 1, (4,)), rows_of(192, 0, (4,)), rows_of(192, 0, (2,)), rows_of(192, 0)]
    halves += [rows_of(96, 2, (4,)), rows_of(96, 1, (4,)), rows_of(96, 0, (4,)), rows_of(96, 0, (2,))]
    mods = [pltpu.VMEM(shape + (8, LANES), F32) for shape in ((2, 2, 2), (2, 2, 2), (4, 2), (8,), (16,))]
    conds = [pltpu.VMEM(shape + (8, 128), F32) for shape in ((), (), (1,), (2,), (4,), (8,), (16,))]
    dma = pltpu.SemaphoreType.DMA
    return pl.pallas_call(
        functools.partial(backward_kernel, extra_bits, all_bits),
        out_shape=(
            jax.ShapeDtypeStruct((tokens, width), BF16),
            jax.ShapeDtypeStruct((tokens, width), BF16),
            jax.ShapeDtypeStruct((576, LANES), F32),
            jax.ShapeDtypeStruct((128, LANES), F32),
            jax.ShapeDtypeStruct((SMALL_ROWS, width), F32),
        ),
        in_specs=[smem] * 2 + [vmem] * 7 + [hbm] * len(arrays),
        out_specs=(vmem,) * 5,
        scratch_shapes=[rows_of(192, 5), rows_of(192, 5), rows_of(48, 5), rows_of(192, 4), rows_of(192, 4)]
        + halves
        + group_rows
        + [both, both, both, features, pltpu.VMEM((2, tokens, 128), BF16)]
        + [half(F32), half(BF16), features, half(BF16), features, features]
        + [pltpu.VMEM((tokens // BLOCK, 6 * width), F32)]
        + [pltpu.VMEM((steps + 1, SMALL_ROWS, width), F32), pltpu.VMEM((steps, SMALL_ROWS, width), F32)]
        + [pltpu.VMEM((steps + 1, 8, width), F32), pltpu.VMEM((steps, 8, width), F32)]
        + mods
        + conds
        + [dma((12,)), dma((2, tiles)), dma((2, tiles)), dma((2, tiles)), dma((17, 5)), dma((17, 5)), dma((8,)), dma((8,))]
        + [dma((steps,)), dma((steps,)), dma((steps,)), dma((steps,)), dma((2, 5)), dma((2, 5))],
        compiler_params=pltpu.CompilerParams(
            collective_id=2, has_side_effects=True, vmem_limit_bytes=63 << 20
        ),
    )(segments, lengths, modulation, condition, table, first_gain, second_gain, expand_bias, reduce_bias, *arrays)


def scatter_rest(block, dp_size):
    group = dp_size >> GROUP_BITS
    if group == 1:
        return block
    groups = [[first * group + place for place in range(group)] for first in range(dp_size // group)]
    return lax.psum_scatter(block, "dp", scatter_dimension=0, axis_index_groups=groups, tiled=True)


def local(
    hidden_in,
    segment_ids,
    piece_lengths,
    time_index,
    first_gain,
    modulation_weight,
    modulation_bias,
    query_key_value_weight,
    attention_output_matrix,
    second_gain,
    widen_weight,
    expand_bias,
    narrow_weight,
    reduce_bias,
    cotangent,
):
    slot_count, own_rows, width = hidden_in.shape
    hidden, cot = hidden_in[0], cotangent[0]
    table = jnp.asarray(angle_table())
    gain_one, gain_two = first_gain[None, :], second_gain[None, :]
    normed, queries, keys, values, attended, query_features, key_features, modulation, condition = forward(
        segment_ids, piece_lengths, time_index, hidden, table, gain_one, modulation_weight,
        modulation_bias[None, :], query_key_value_weight,
    )
    block_out, input_grad, block_sum, mod_sum, small_sum = backward(
        segment_ids, piece_lengths, modulation, condition, table, gain_one, gain_two, expand_bias[None, :],
        reduce_bias[None, :], narrow_weight, widen_weight, attention_output_matrix, attended, cot, queries, keys, values,
        query_features, key_features, normed, hidden, query_key_value_weight,
    )
    dp_size = lax.axis_size("dp")
    expand_block = scatter_rest(block_sum[:192], dp_size).T
    reduce_block = block_sum[192:384].reshape(4, -1, LANES).transpose(1, 0, 2).reshape(-1, 4 * LANES)
    reduce_block = scatter_rest(reduce_block, dp_size).T
    output_block = scatter_rest(block_sum[384:432], dp_size).T
    triple_block = scatter_rest(block_sum[432:576], dp_size).T
    half = mod_sum.shape[0] // 2
    mod_block = lax.dynamic_slice_in_dim(mod_sum, lax.axis_index("seq") * half, half, 0)[:, : 6 * width // 16]
    mod_block = scatter_rest(mod_block.T, dp_size).T
    stats = small_sum[STATS]
    return (
        block_out[None],
        input_grad[None],
        small_sum[FIRST_GAIN],
        mod_block,
        small_sum[MOD_BIAS : MOD_BIAS + 6].reshape(-1),
        triple_block,
        output_block,
        small_sum[SECOND_GAIN],
        expand_block,
        small_sum[EXPAND_BIAS : EXPAND_BIAS + 4].reshape(-1),
        reduce_block,
        small_sum[REDUCE_BIAS],
        jnp.sqrt(stats[:3] / (stats[3] * width)),
    )


def solution(mesh):
    in_specs = (
        P("dp", "seq", None),
        P("dp", None),
        P("dp", None),
        P("dp", None),
        P(),
        P(),
        P(),
        P(),
        P(),
        P(),
        P(),
        P(),
        P(),
        P(),
        P("dp", "seq", None),
    )
    out_specs = (
        P("dp", "seq", None),
        P("dp", "seq", None),
        P(),
        P("seq", "dp"),
        P(),
        P("seq", "dp"),
        P("seq", "dp"),
        P(),
        P("seq", "dp"),
        P(),
        P("seq", "dp"),
        P(),
        P(),
    )
    return jax.shard_map(local, mesh=mesh, in_specs=in_specs, out_specs=out_specs, check_vma=False)
```

```python
import functools
import math

import jax
import jax.numpy as jnp
import numpy as np
from jax import lax
from jax.experimental import pallas as pl
from jax.experimental.pallas import tpu as pltpu
from jax.sharding import PartitionSpec as P

HEADS = 12
BLOCK = 128
MAX_SEQUENCES = 8
SEGMENT_LANE = 40
MASKED = -1000000000.0
LANES = 384
GROUP_BITS = 4
MESH_ID = pl.DeviceIdType.MESH
F32, BF16 = jnp.float32, jnp.bfloat16

ROTARY_COS, ROTARY_SIN, BLOCK_COS, BLOCK_SIN = 0, 128, 256, 264
HIGH_COS, HIGH_SIN, LOW_COS, LOW_SIN, TABLE_ROWS = 272, 304, 336, 368, 400

FIRST_GAIN, MOD_BIAS, SECOND_GAIN, EXPAND_BIAS, REDUCE_BIAS, STATS, SMALL_ROWS = 0, 1, 7, 8, 12, 13, 16


def angle_table():
    lane = np.arange(128)
    rotary = np.exp((lane % 32) * (-2.0 * math.log(10000.0) / 64))
    timing = np.exp((lane % 64) * (-math.log(10000.0) / 64))
    steps = np.arange(128)[:, None]
    angles = [
        (np.cos, steps * rotary), (np.sin, steps * rotary),
        (np.cos, steps[:8] * 128 * rotary), (np.sin, steps[:8] * 128 * rotary),
        (np.cos, steps[:32] * 32 * timing), (np.sin, steps[:32] * 32 * timing),
        (np.cos, steps[:32] * timing), (np.sin, steps[:32] * timing),
    ]
    return np.concatenate([fn(angle) for fn, angle in angles]).astype(np.float32)


def dot(left, right):
    return jnp.dot(left, right, preferred_element_type=F32)


def dot_nt(left, right):
    return lax.dot_general(left, right, (((1,), (1,)), ((), ())), preferred_element_type=F32)


def dot_tn(left, right):
    return lax.dot_general(left, right, (((0,), (0,)), ((), ())), preferred_element_type=F32)


def as_row(vector):
    return vector[...].reshape(1, -1)


def lane_iota(shape):
    return lax.broadcasted_iota(jnp.int32, shape, len(shape) - 1)


def row_iota(shape):
    return lax.broadcasted_iota(jnp.int32, shape, 0)


def block_place(segments, lengths, block):
    segment = segments[0, block * BLOCK]
    before = jnp.int32(0)
    for other in range(segments.shape[1] // BLOCK):
        same = (segments[0, other * BLOCK] == segment) & (other < block)
        before = before + jnp.where(same, 1, 0)
    return segment, before, lengths[0, segment] - before * BLOCK


def rotary_block(table, before):
    cos_row, sin_row = table[pl.ds(ROTARY_COS, 128), :], table[pl.ds(ROTARY_SIN, 128), :]
    cos_block = table[pl.ds(BLOCK_COS + before, 1), :]
    sin_block = table[pl.ds(BLOCK_SIN + before, 1), :]
    cosine = cos_row * cos_block - sin_row * sin_block
    sine = sin_row * cos_block + cos_row * sin_block
    first_half = lane_iota(sine.shape) % 64 < 32
    return cosine, jnp.where(first_half, -sine, sine)


def turn(values, cosine, sine):
    first_half = lane_iota(values.shape) % 64 < 32
    swapped = jnp.where(first_half, pltpu.roll(values, 96, 1), pltpu.roll(values, 32, 1))
    return values * cosine + swapped * sine


def mean_of(values):
    return jnp.mean(values, axis=-1, keepdims=True)


def split_three(values):
    first = values.astype(BF16)
    rest = values - first.astype(F32)
    second = rest.astype(BF16)
    third = (rest - second.astype(F32)).astype(BF16)
    place = lane_iota(values.shape) % 3
    picked = jnp.where(place == 0, first.astype(F32), jnp.where(place == 1, second.astype(F32), third.astype(F32)))
    return picked.astype(BF16)


def forward_kernel(
    segments, lengths, times, hidden, table, first_gain, mod_weight, mod_bias, weight,
    normed, queries, keys, values, attended, query_features, key_features, modulation, condition,
    other_hidden, turned_values, out_t, peak, total, send_sem, recv_sem,
):
    tokens, width = hidden.shape
    blocks = tokens // BLOCK
    seq = lax.axis_index("seq")
    partner = (lax.axis_index("dp"), 1 - seq)
    barrier = pltpu.get_barrier_semaphore()
    pl.semaphore_signal(barrier, inc=1, device_id=partner, device_id_type=MESH_ID)
    pl.semaphore_wait(barrier, 1)
    exchanges = [
        pltpu.make_async_remote_copy(
            hidden.at[pl.ds(place * tokens // 2, tokens // 2)], other_hidden.at[pl.ds(place * tokens // 2, tokens // 2)],
            send_sem.at[place], recv_sem.at[place], device_id=partner, device_id_type=MESH_ID,
        )
        for place in range(2)
    ]
    for exchange in exchanges:
        exchange.start()

    places = []
    for number in range(2 * blocks):
        block = (seq if number < blocks else 1 - seq) * blocks + number % blocks
        places.append(block_place(segments, lengths, block))
        time = times[0, places[number][0]]
        high, low = time // 32, time % 32
        cos_high, sin_high = table[pl.ds(HIGH_COS + high, 1), :], table[pl.ds(HIGH_SIN + high, 1), :]
        cos_low, sin_low = table[pl.ds(LOW_COS + low, 1), :], table[pl.ds(LOW_SIN + low, 1), :]
        cosine = cos_high * cos_low - sin_high * sin_low
        sine = sin_high * cos_low + cos_high * sin_low
        row = jnp.where(lane_iota(cosine.shape) < 64, cosine, sine)
        condition[pl.ds(number, 1), :] = row.astype(BF16).astype(F32)
    modulation[...] = dot(condition[...].astype(BF16), mod_weight[...]) + as_row(mod_bias)

    lane = lane_iota((BLOCK, 128))
    row = row_iota((BLOCK, 128))

    half_blocks = blocks // 2
    sections = ((0, 0, blocks), (1, 0, half_blocks), (1, half_blocks, half_blocks))
    for section, (part, first_block, count) in enumerate(sections):
        source = hidden if part == 0 else other_hidden
        if part == 1:
            exchanges[section - 1].wait_recv()
        section_rows = pl.ds(first_block * BLOCK, count * BLOCK)
        turns = []
        for number in range(first_block, first_block + count):
            rows = pl.ds(number * BLOCK, BLOCK)
            segment, before, valid_count = places[part * blocks + number]
            turns.append(rotary_block(table, before))
            mine = lane == SEGMENT_LANE + segment
            in_lanes = (lane >= SEGMENT_LANE) & (lane < SEGMENT_LANE + MAX_SEQUENCES)
            blocked = in_lanes & jnp.logical_not(mine & (row < valid_count))
            key_features[part, rows, :] = jnp.where(blocked, MASKED, 0.0).astype(BF16)
            if part == 0:
                query_features[rows, :] = jnp.where(mine, 1.0, 0.0).astype(BF16)
            mod_row = pl.ds(part * blocks + number, 1)
            shift, scale = modulation[mod_row, pl.ds(0, width)], modulation[mod_row, pl.ds(width, width)]
            value = source[rows, :].astype(F32)
            centered = value - mean_of(value)
            spread = mean_of(centered * centered)
            line = centered * lax.rsqrt(spread + 1e-05) * as_row(first_gain)
            result = (line * (1.0 + scale) + shift).astype(BF16)
            if part == 0:
                normed[rows, :] = result
            else:
                other_hidden[rows, :] = result
        normed_source = normed if part == 0 else other_hidden
        for tile in range(3 * width // LANES):
            which, first = divmod(tile * LANES, width)
            product = dot(normed_source[section_rows, :], weight[:, pl.ds(tile * LANES, LANES)])
            target = (queries, keys, values)[which]
            for place in range(count):
                cosine, sine = turns[place]
                for pair in range(LANES // 128):
                    piece = product[place * BLOCK : (place + 1) * BLOCK, pair * 128 : (pair + 1) * 128]
                    if which < 2:
                        piece = turn(piece, cosine, sine)
                    if which == 0:
                        piece = piece.astype(BF16).astype(F32) * 0.125
                    rows = pl.ds((first_block + place) * BLOCK, BLOCK)
                    target[part, rows, pl.ds(first + pair * 128, 128)] = piece.astype(BF16)
        turned_rows = pl.ds(0, count * BLOCK)
        turned_values[:, turned_rows] = jnp.transpose(values[part, section_rows, :])

        def attend(pair, carry):
            lanes = pl.ds(pl.multiple_of(pair * 128, 128), 128)
            query_pair, key_pair = queries[0, :, lanes], keys[part, section_rows, lanes]
            left = jnp.concatenate([key_pair, key_features[part, section_rows, :]], axis=1)
            pair_lane = lane_iota(query_pair.shape)
            both = []
            for half in range(2):
                query = jnp.where((pair_lane < 64) == (half == 0), query_pair, jnp.zeros_like(query_pair))
                both.append(dot_nt(left, jnp.concatenate([query, query_features[...]], axis=1)))
            for half, scores in enumerate(both):
                head = pair * 2 + half
                head_rows = pl.ds(pl.multiple_of(head * 64, 64), 64)
                one_row = pl.ds(head, 1)
                top = jnp.max(scores, axis=0, keepdims=True)
                if section > 0:
                    top = jnp.maximum(top, peak[one_row, :])
                weights = jnp.exp(scores - top)
                summed = jnp.sum(weights, axis=0, keepdims=True)
                mixed = dot(turned_values[head_rows, turned_rows], weights.astype(BF16))
                if section > 0:
                    rescale = jnp.exp(peak[one_row, :] - top)
                    summed = summed + rescale * total[one_row, :]
                    mixed = mixed + out_t[head_rows, :] * rescale
                if section < len(sections) - 1:
                    out_t[head_rows, :] = mixed
                    total[one_row, :] = summed
                    peak[one_row, :] = top
                else:
                    out_t[head_rows, :] = mixed * (1.0 / summed)
                    peak[one_row, :] = top + jnp.log(summed)
            return carry

        lax.fori_loop(0, HEADS // 2, attend, 0)

    attended[...] = jnp.transpose(out_t[...].astype(BF16))
    log_rows = jnp.concatenate(
        [jnp.broadcast_to(peak[pl.ds(head, 1), :], (3, tokens)) for head in range(HEADS)]
        + [jnp.zeros((128 - 3 * HEADS, tokens), F32)], axis=0,
    )
    query_features[...] = query_features[...] + split_three(jnp.transpose(log_rows))
    for exchange in exchanges:
        exchange.wait_send()


def forward(segments, lengths, times, hidden, table, first_gain, mod_weight, mod_bias, weight):
    tokens, width = hidden.shape
    blocks = 2 * tokens // BLOCK
    half = jax.ShapeDtypeStruct((tokens, width), BF16)
    both = jax.ShapeDtypeStruct((2, tokens, width), BF16)
    smem, vmem = pl.BlockSpec(memory_space=pltpu.SMEM), pl.BlockSpec(memory_space=pltpu.VMEM)
    return pl.pallas_call(
        forward_kernel,
        out_shape=(
            half, both, both, both, half,
            jax.ShapeDtypeStruct((tokens, 128), BF16),
            jax.ShapeDtypeStruct((2, tokens, 128), BF16),
            jax.ShapeDtypeStruct((blocks, 6 * width), F32),
            jax.ShapeDtypeStruct((blocks, 128), F32),
        ),
        in_specs=[smem] * 3 + [vmem] * 6,
        out_specs=(vmem,) * 9,
        scratch_shapes=[
            pltpu.VMEM((tokens, width), BF16),
            pltpu.VMEM((width, tokens), BF16),
            pltpu.VMEM((width, tokens), F32),
            pltpu.VMEM((16, tokens), F32),
            pltpu.VMEM((16, tokens), F32),
            pltpu.SemaphoreType.DMA((2,)),
            pltpu.SemaphoreType.DMA((2,)),
        ],
        compiler_params=pltpu.CompilerParams(
            collective_id=1, has_side_effects=True, vmem_limit_bytes=56 << 20
        ),
    )(segments, lengths, times, hidden, table, first_gain, mod_weight, mod_bias, weight)


TILE = 384
Z2, Z1, Y, CORE, X = 0, 1, 2, 3, 4


WIDE_ORDERS = ((Y, X), (X, Y), (X, Y), (X, Y))
REDUCE_ORDERS = ((Z1, Y, Z2), (Y, Z1, Z2), (Y, Z2, Z1), (Z2, Y, Z1))
OUTPUT_ORDER = (CORE, X, Y, Z1, Z2)
TRIPLE_ORDERS = ((CORE, Y, X, Z1, Z2), (CORE, Z1, Y, X, Z2), (CORE, X, Y, Z1, Z2))
PLAN = (
    (("T", 6), (("r", 0), ("w", 0),)),
    (("T", 7), (("w", 1),)),
    (("N", 0), (("r", 1),)),
    (("N", 4), (("w", 2),)),
    (("D", 0), (("s", 0), ("r", 2),)),
    (("D", 1), (("r", 0), ("w", 0),)),
    (("A", 1), (("w", 1), ("o", 0),)),
    (("A", 3), (("w", 2), ("w", 3),)),
    (("A", 4), (("r", 3), ("s", 0),)),
    (("A", 6), (("r", 1),)),
    (("A", 7), (("w", 3),)),
    (("A", 9), (("r", 3),)),
    (("A", 10), (("r", 2),)),
    (("E", 0), (("r", 0),)),
    (("B", 0), (("s", 0), ("wm", 0),)),
    (("B", 3), (("r", 1),)),
    (("B", 5), (("wm", 1),)),
    (("C", 0), (("r", 3), ("o", 0),)),
    (("C", 1), (("s", 0), ("r", 2),)),
    (("C", 4), (("q", 0),)),
    (("C", 5), (("q", 1),)),
    (("C", 6), (("re", 1), ("s", 0),)),
    (("F", 0), (("q", 2), ("o", 0), ("we", 0), ("re", 0), ("m", 0), ("q", 0), ("q", 1), ("m", 0), ("o", 0), ("q", 2), ("m", 0), ("q", 1), ("o", 0), ("q", 0), ("q", 2), ("q", 1), ("m", 0), ("q", 0), ("q", 2), ("m", 0), ("q", 1), ("q", 0), ("q", 2),)),
)


def exchange_partner(axis, extra_bits):
    dp, seq = lax.axis_index("dp"), lax.axis_index("seq")
    if axis == X:
        return (dp, 1 - seq)
    return (dp ^ (1 << (GROUP_BITS - 1 - axis + extra_bits)), seq)


def own_bit(axis, extra_bits):
    if axis == X:
        return lax.axis_index("seq")
    return (lax.axis_index("dp") >> (GROUP_BITS - 1 - axis + extra_bits)) & 1


class Stream:
    def __init__(self, kit, number, part, first, count, fixed, order, got, got_first=0, total_first=None):
        self.kit, self.number, self.part, self.first, self.count = kit, number, part, first, count
        self.fixed, self.order, self.got, self.got_first = fixed, order, got, got_first
        self.total_first = total_first

    def free(self, stage):
        return [axis for axis in range(5) if axis not in self.fixed and axis not in self.order[: stage + 1]]

    def copy(self, stage):
        bits = self.kit["bits"]
        index = [slice(None)] * 5
        for axis, value in self.fixed.items():
            index[axis] = value
        for axis in self.order[:stage]:
            index[axis] = bits[axis]
        index[self.order[stage]] = 1 - bits[self.order[stage]]
        target = (slice(None),) * len(self.free(stage)) + (pl.ds(self.got_first, self.count),)
        return pltpu.make_async_remote_copy(
            self.part.at[tuple(index) + (pl.ds(self.first, self.count),)],
            self.got[stage].at[target],
            self.kit["send"].at[self.number, stage],
            self.kit["recv"].at[self.number, stage],
            device_id=exchange_partner(self.order[stage], self.kit["extra"]),
            device_id_type=MESH_ID,
        )

    def send(self, stage):
        self.copy(stage).start()

    def add(self, stage):
        self.copy(stage).wait_recv()
        last = stage == len(self.order) - 1 and self.total_first is not None
        bits, free = self.kit["bits"], self.free(stage)
        rows, got_rows = pl.ds(self.first, self.count), pl.ds(self.got_first, self.count)

        def one(step, carry):
            index = list(bits)
            for axis, value in self.fixed.items():
                index[axis] = value
            place = []
            for order, axis in enumerate(free):
                index[axis] = (step >> (len(free) - 1 - order)) & 1
                place.append(index[axis])
            mine, theirs = self.part[tuple(index) + (rows,)], self.got[stage][tuple(place) + (got_rows,)]
            if last:
                total = mine.astype(F32) + theirs.astype(F32)
                self.kit["sums"][pl.ds(self.total_first, self.count), :] = total
            else:
                self.part[tuple(index) + (rows,)] = mine + theirs
            return carry

        if free:
            lax.fori_loop(0, 2 ** len(free), one, 0)
        else:
            one(0, 0)

    def done(self):
        for stage in range(len(self.order)):
            self.copy(stage).wait_send()


def backward_kernel(
    extra_bits, all_bits,
    segments, lengths, modulation, condition, table, first_gain, second_gain, expand_bias, reduce_bias,
    narrow_hbm, widen_hbm, out_weight_hbm, attended_hbm, cotangent_hbm, queries_hbm, keys_hbm, values_hbm,
    query_features_hbm, key_features_hbm, normed_hbm, hidden_hbm, weight_hbm,
    block_out, input_grad, sums, mod_out, small_out,
    expand_part, reduce_part, output_part,
    expand_got, reduce_got, wide_a, wide_b, wide_z, wide_last, red_a, red_b, red_c, red_last,
    out_a, out_b, out_c, out_d, out_e, tri_a, tri_b, tri_c, tri_d, tri_e,
    queries, keys, values, query_features, key_features,
    grad_middle, grad_attended, delta_features, other_grad, other_delta, other_features, mod_rows,
    small_acc, small_got, late_acc, late_got, mod_got, mod_two, mod_three, mod_four, mod_five,
    cond_zero, cond_got, cond_one, cond_two, cond_three, cond_four, cond_five,
    load_sem, tile_sem, core_send, core_recv, stream_send, stream_recv, swap_send, swap_recv,
    small_send, small_recv, late_send, late_recv, mod_send, mod_recv,
):
    tokens, width = input_grad.shape
    tiles = narrow_hbm.shape[0] // TILE
    blocks = tokens // BLOCK
    seq = lax.axis_index("seq")
    dp = lax.axis_index("dp")
    bits = [own_bit(axis, extra_bits) for axis in range(5)]
    kit = {"bits": bits, "send": stream_send, "recv": stream_recv, "extra": extra_bits, "sums": sums}
    core = bits[CORE]

    def others(*axes):
        return {axis: bits[axis] for axis in range(5) if axis not in axes}

    def chosen(**values):
        return {CORE: core, **{{"z2": Z2, "z1": Z1, "x": X}[name]: value for name, value in values.items()}}

    streams = {}
    for g in range(4):
        streams["w", g] = Stream(
            kit, g, expand_part, 0, 192, chosen(z2=g >> 1, z1=g & 1), WIDE_ORDERS[g], (wide_a.at[g], wide_b.at[g])
        )
        streams["r", g] = Stream(
            kit, 4 + g, reduce_part, 96 * (g & 1), 96, chosen(x=g >> 1), REDUCE_ORDERS[g],
            (red_a.at[g], red_b.at[g], red_c.at[g]),
        )
    for v in range(2):
        streams["wm", v] = Stream(
            kit, 8 + v, expand_part, 0, 192, {**others(Z1, Z2), Z2: v}, (Z1,), (wide_z.at[v],)
        )
        streams["re", v] = Stream(
            kit, 11 + v, reduce_part, 96 * v, 96, others(X), (X,), (red_last.at[v],), total_first=192 + 96 * v
        )
    streams["we", 0] = Stream(kit, 10, expand_part, 0, 192, others(Z2), (Z2,), (wide_last,), total_first=0)
    streams["o", 0] = Stream(
        kit, 13, output_part, 0, 48, {}, OUTPUT_ORDER, (out_a, out_b, out_c, out_d, out_e), total_first=384
    )
    merges = {
        ("wm", 0): (("w", 0), ("w", 1)), ("wm", 1): (("w", 2), ("w", 3)), ("we", 0): (("wm", 0), ("wm", 1)),
        ("re", 0): (("r", 0), ("r", 2)), ("re", 1): (("r", 1), ("r", 3)),
    }
    work, stages, finished = {}, {}, set()
    for slot, names in PLAN:
        todo = work.setdefault(slot, [])
        for name in names:
            stage = stages.get(name, 0)
            stages[name] = stage + 1
            todo.append((True, name, stage))
            if name[0] in ("m", "s"):
                continue
            if stage + 1 < (len(streams[name].order) if name in streams else 5):
                todo.append((False, name, stage + 1))
                continue
            finished.add(name)
            for merged, parts in merges.items():
                if name in parts and finished.issuperset(parts):
                    todo.append((False, merged, 0))

    def perform(slot):
        for is_add, name, stage in work.get(slot, ()):
            if name[0] == "s":
                small_step(stage)
            elif is_add:
                streams[name].add(stage)
            else:
                streams[name].send(stage)

    def perform_at(letter, first, stride, count, index):
        for place in range(count):
            slot = (letter, first + stride * place)
            if work.get(slot):

                @pl.when(index == place)
                def _(slot=slot):
                    perform(slot)

    greet = [(dp, 1 - seq)] + [(dp ^ (1 << bit), seq) for bit in range(all_bits)]
    barrier = pltpu.get_barrier_semaphore()
    for partner in greet:
        pl.semaphore_signal(barrier, inc=1, device_id=partner, device_id_type=MESH_ID)

    attention_loads = [
        pltpu.make_async_copy(source, target, load_sem.at[number])
        for number, (source, target) in enumerate(
            ((queries_hbm, queries), (keys_hbm, keys), (values_hbm, values),
             (query_features_hbm, query_features), (key_features_hbm, key_features))
        )
    ]
    row = row_iota((BLOCK, 1))
    keep = []
    for number in range(blocks):
        valid_count = block_place(segments, lengths, seq * blocks + number)[2]
        keep.append(jnp.where(row < valid_count, 1.0, 0.0))

    def mod_part(number, part):
        return modulation[pl.ds(number, 1), pl.ds(part * width, width)]

    def tile_lanes(tile):
        return pl.ds(pl.multiple_of(tile * TILE, TILE), TILE)

    def core_copies(tile):
        at = (tile >> 2, (tile >> 1) & 1, tile & 1)
        rows = pl.ds(pl.multiple_of((tile & 3) * 48, 16), 48)
        everywhere = (slice(None),) * 3
        partner = exchange_partner(CORE, extra_bits)
        return (
            pltpu.make_async_remote_copy(
                expand_part.at[at + (1 - core,)], expand_got.at[at], core_send.at[0, tile], core_recv.at[0, tile],
                device_id=partner, device_id_type=MESH_ID,
            ),
            pltpu.make_async_remote_copy(
                reduce_part.at[everywhere + (1 - core, tile >> 2, rows)], reduce_got.at[everywhere + (tile >> 2, rows)],
                core_send.at[1, tile], core_recv.at[1, tile], device_id=partner, device_id_type=MESH_ID,
            ),
        )

    def core_add(tile):
        at = (tile >> 2, (tile >> 1) & 1, tile & 1)
        rows = pl.ds(pl.multiple_of((tile & 3) * 48, 16), 48)
        for copy in core_copies(tile):
            copy.wait_recv()
        for side in range(2):
            expand_part[at + (core, side)] = expand_part[at + (core, side)] + expand_got[at + (side,)]
        for z2 in range(2):
            for z1 in range(2):
                for y in range(2):
                    index, got = (z2, z1, y, core, tile >> 2, rows), (z2, z1, y, tile >> 2, rows)
                    reduce_part[index] = reduce_part[index] + reduce_got[got]

    def mlp_phase(
        narrow, widen, out_weight, attended, hidden, cotangent, normed_two, grad_low, grad_low_t,
        projected, reduced, grad_normed,
    ):
        def tile_loads(tile):
            lanes = tile_lanes(tile)
            pairs = ((widen_hbm.at[:, lanes], widen.at[:, lanes]), (narrow_hbm.at[lanes], narrow.at[lanes]))
            return [pltpu.make_async_copy(source, target, tile_sem.at[place, tile]) for place, (source, target) in enumerate(pairs)]

        loads = [
            pltpu.make_async_copy(source, target, load_sem.at[5 + number])
            for number, (source, target) in enumerate(
                ((cotangent_hbm, cotangent), (attended_hbm, attended), (out_weight_hbm, out_weight), (hidden_hbm, hidden))
            )
        ]
        for load in loads:
            load.start()
        for tile in range(tiles):
            for load in tile_loads(tile):
                load.start()
        for load in attention_loads:
            load.start()
        small_acc[0] = jnp.zeros_like(small_acc[0])
        grad_normed[...] = jnp.zeros_like(grad_normed)
        reduced[...] = jnp.zeros_like(reduced)
        loads[0].wait()
        bias_sum = jnp.zeros((1, width), F32)
        for number in range(blocks):
            rows = pl.ds(number * BLOCK, BLOCK)
            low = (mod_part(number, 5) * (cotangent[rows, :].astype(F32) * keep[number])).astype(BF16)
            grad_low[rows, :] = low
            bias_sum = bias_sum + jnp.sum(low.astype(F32), axis=0, keepdims=True)
        small_acc[0, pl.ds(REDUCE_BIAS, 1), :] = bias_sum
        grad_low_t[...] = jnp.transpose(grad_low[...])
        for load in loads[1:]:
            load.wait()
        for first in range(0, width, 256):
            lanes = pl.ds(first, 256)
            projected[:, lanes] = dot(attended[...], out_weight[:, lanes])
        branch_sum = jnp.zeros((1, width), F32)
        for number in range(blocks):
            rows = pl.ds(number * BLOCK, BLOCK)
            branch = mod_part(number, 2) * projected[rows, :]
            branch_sum = branch_sum + jnp.sum(keep[number] * branch * branch, axis=0, keepdims=True)
            value = hidden[rows, :].astype(F32) + branch
            centered = value - mean_of(value)
            inverse = lax.rsqrt(mean_of(centered * centered) + 1e-05)
            line = centered * inverse * as_row(second_gain)
            normed_two[rows, :] = (line * (1.0 + mod_part(number, 4)) + mod_part(number, 3)).astype(BF16)
        pl.semaphore_wait(barrier, len(greet))

        def through(tile):
            lanes = tile_lanes(tile)
            for load in tile_loads(tile):
                load.wait()
            u = dot(normed_two[...], widen[:, lanes]) + expand_bias[lanes].reshape(1, TILE)
            grad_active = dot_nt(grad_low[...], narrow[lanes, :])
            square = u * u
            tanh = jnp.tanh(u * (0.7978845608028654 + 0.7978845608028654 * 0.044715 * square))
            half_sum = 0.5 + 0.5 * tanh
            active = (u * half_sum).astype(BF16)
            inner = 0.7978845608028654 + 3.0 * 0.7978845608028654 * 0.044715 * square
            slope = half_sum + (0.5 * u) * (1.0 - tanh * tanh) * inner
            grad_wide = (grad_active * slope).astype(BF16)
            reduced[...] += dot(active, narrow[lanes, :])
            reduce_t = dot(grad_low_t[...], active).astype(BF16)
            rows = pl.ds(pl.multiple_of((tile & 3) * 48, 16), 48)
            reduce_part[:, :, :, :, tile >> 2, rows] = reduce_t.reshape(2, 2, 2, 2, 48, TILE)
            bias_lanes = pl.ds(pl.multiple_of((tile & 1) * TILE, TILE), TILE)
            small_acc[0, pl.ds(EXPAND_BIAS + (tile >> 1), 1), bias_lanes] = jnp.sum(
                grad_wide.astype(F32), axis=0, keepdims=True
            )
            expand_t = dot_tn(grad_wide, normed_two[...]).astype(BF16)
            at = (tile >> 2, (tile >> 1) & 1, tile & 1)
            for group in range(2):
                for side in range(2):
                    expand_part[at + (group, side)] = expand_t[
                        group * 192 : group * 192 + 192, side * LANES : side * LANES + LANES
                    ]
            for copy in core_copies(tile):
                copy.start()
            grad_normed[...] += dot_nt(grad_wide, widen[:, lanes])

        def begin(g):
            streams["w", g].send(0)
            streams["r", g].send(0)

        def through_two(number, carry):
            through(2 * number)

            @pl.when(number > 0)
            def _():
                core_add(2 * number - 1)

            for g in range(tiles // 2 - 1):

                @pl.when(number == g + 1)
                def _(g=g):
                    begin(g)

            perform_at("T", 0, 2, tiles // 2, number)
            through(2 * number + 1)
            core_add(2 * number)
            perform_at("T", 1, 2, tiles // 2, number)
            return carry

        lax.fori_loop(0, tiles // 2, through_two, 0)
        core_add(tiles - 1)
        begin(3)
        gain_sum = jnp.zeros((1, width), F32)
        value_sum = jnp.zeros((1, width), F32)
        mlp_sum = jnp.zeros((1, width), F32)
        for number in range(blocks):
            perform(("N", number))
            rows = pl.ds(number * BLOCK, BLOCK)
            here = pl.ds(number, 1)
            full = reduced[rows, :] + as_row(reduce_bias)
            branch = mod_part(number, 5) * full
            before = hidden[rows, :].astype(F32) + mod_part(number, 2) * projected[rows, :]
            centered = before - mean_of(before)
            inverse = lax.rsqrt(mean_of(centered * centered) + 1e-05)
            normal = centered * inverse
            value = before + branch
            block_out[rows, :] = value.astype(BF16)
            value_sum = value_sum + jnp.sum(keep[number] * value * value, axis=0, keepdims=True)
            mlp_sum = mlp_sum + jnp.sum(keep[number] * branch * branch, axis=0, keepdims=True)
            grad_out = cotangent[rows, :].astype(F32) * keep[number]
            mod_rows[here, pl.ds(5 * width, width)] = jnp.sum(grad_out * full, axis=0, keepdims=True)
            grad = grad_normed[rows, :]
            line = normal * as_row(second_gain)
            mod_rows[here, pl.ds(3 * width, width)] = jnp.sum(grad, axis=0, keepdims=True)
            mod_rows[here, pl.ds(4 * width, width)] = jnp.sum(grad * line, axis=0, keepdims=True)
            grad_line = grad * (1.0 + mod_part(number, 4))
            gain_sum = gain_sum + jnp.sum(grad_line * normal, axis=0, keepdims=True)
            grad_normal = grad_line * as_row(second_gain)
            along = mean_of(grad_normal * normal)
            term = (grad_normal - mean_of(grad_normal) - normal * along) * inverse
            total = grad_out + term
            grad_middle[rows, :] = total
            mod_rows[here, pl.ds(2 * width, width)] = jnp.sum(total * projected[rows, :], axis=0, keepdims=True)
            grad_low[rows, :] = (mod_part(number, 2) * total).astype(BF16)
        small_acc[0, pl.ds(SECOND_GAIN, 1), :] = gain_sum
        lane = lane_iota((1, width))
        counts = jnp.zeros((1, 1), F32)
        for number in range(blocks):
            counts = counts + jnp.sum(keep[number], axis=0, keepdims=True)
        terms = [jnp.sum(term, axis=1, keepdims=True) for term in (value_sum, branch_sum, mlp_sum)] + [counts]
        stats = jnp.zeros((1, width), F32)
        for place, term in enumerate(terms):
            stats = jnp.where(lane == place, term, stats)
        small_acc[0, pl.ds(STATS, 1), :] = stats
        for part in range(2, 6):
            small_acc[0, pl.ds(MOD_BIAS + part, 1), :] = jnp.sum(
                mod_rows[:, pl.ds(part * width, width)], axis=0, keepdims=True
            )
        small_copy(0).start()
        perform(("N", blocks))

        for first in range(0, width, 256):
            grad_attended[:, pl.ds(first, 256)] = dot_nt(
                grad_low[...], out_weight[pl.ds(first, 256), :]
            ).astype(BF16)
        head_lane = row_iota((width, 128)) // 64 == lane_iota((width, 128)) // 3
        chooser = jnp.where(head_lane & (lane_iota((width, 128)) < 3 * HEADS), 1.0, 0.0).astype(BF16)
        for number in range(blocks):
            rows = pl.ds(number * BLOCK, BLOCK)
            product = grad_attended[rows, :].astype(F32) * attended[rows, :].astype(F32)
            upper = product.astype(BF16)
            lower = (product - upper.astype(F32)).astype(BF16)
            delta_features[rows, :] = split_three(dot(upper, chooser) + dot(lower, chooser))
        for load in attention_loads:
            load.wait()
        for place in range(HEADS // 2 + 2):
            swap(place).start()
        perform(("D", 0))
        for first in range(0, width, TILE):
            output_t = dot_tn(grad_low[:, pl.ds(first, TILE)], attended[...]).astype(BF16)
            for place in range(TILE // 48):
                group = first // 48 + place
                at = (group >> 3, (group >> 2) & 1, (group >> 1) & 1, group & 1)
                for side in range(2):
                    output_part[at + (side,)] = output_t[
                        place * 48 : place * 48 + 48, side * LANES : side * LANES + LANES
                    ]
        streams["o", 0].send(0)
        perform(("D", 1))

    def small_copy(number):
        return pltpu.make_async_remote_copy(
            small_acc.at[number], small_got.at[number], small_send.at[number], small_recv.at[number],
            device_id=greet[(1 + number) % len(greet)], device_id_type=MESH_ID,
        )

    def small_step(number):
        small_copy(number).wait_recv()
        small_acc[number + 1] = small_acc[number] + small_got[number]
        if number + 1 < len(greet):
            small_copy(number + 1).start()

    def swap(place):
        if isinstance(place, int) and place < 2:
            source, target = ((delta_features, other_delta), (query_features, other_features))[place]
        else:
            lanes = pl.ds(pl.multiple_of((place - 2) * 128, 128), 128)
            source, target = grad_attended.at[:, lanes], other_grad.at[:, lanes]
        return pltpu.make_async_remote_copy(
            source, target, swap_send.at[place], swap_recv.at[place], device_id=(dp, 1 - seq), device_id_type=MESH_ID
        )

    units = tiles * TILE
    low_half, wide_half = pltpu.VMEM((tokens, width), BF16), pltpu.VMEM((tokens, width), F32)
    pl.run_scoped(
        mlp_phase,
        pltpu.VMEM((units, width), BF16), pltpu.VMEM((width, units), BF16), pltpu.VMEM((width, width), BF16),
        low_half, low_half, low_half, low_half, low_half, pltpu.VMEM((width, tokens), BF16),
        wide_half, wide_half, wide_half,
    )

    def attention_phase(normed, hidden, weight, keys_t, grad_query_t, grad_key, grad_value, grad_triple, grad_normed, triple_part, mod_zero, mod_one):
        loads = [
            pltpu.make_async_copy(source, target, load_sem.at[9 + number])
            for number, (source, target) in enumerate(((normed_hbm, normed), (hidden_hbm, hidden), (weight_hbm, weight)))
        ]
        for load in loads:
            load.start()
        for part in range(2):
            keys_t[part] = jnp.transpose(keys[part])

        def own_queries(pair, carry):
            lanes = pl.ds(pl.multiple_of(pair * 128, 128), 128)
            query_pair, grad_pair = queries[0, :, lanes], grad_attended[:, lanes]
            pair_lane = lane_iota(query_pair.shape)
            for half in range(2):
                head = pair * 2 + half
                head_rows = pl.ds(pl.multiple_of(head * 64, 64), 64)
                mine = (pair_lane < 64) == (half == 0)
                query = jnp.where(mine, query_pair, jnp.zeros_like(query_pair))
                grad = jnp.where(mine, grad_pair, jnp.zeros_like(grad_pair))
                right_scores = jnp.concatenate([query, query_features[...]], axis=1)
                right_grads = jnp.concatenate([grad, delta_features[...]], axis=1)
                head_lanes = (pair_lane >= 3 * head) & (pair_lane < 3 * head + 3)
                grad_q = jnp.zeros((64, tokens), F32)
                for part in range(2):
                    features = jnp.where(head_lanes, jnp.full_like(query_pair, -1.0), key_features[part])
                    scores = dot_nt(jnp.concatenate([keys[part, :, lanes], features], axis=1), right_scores)
                    weights = jnp.exp(scores)
                    grad_weights = dot_nt(jnp.concatenate([values[part, :, lanes], features], axis=1), right_grads)
                    grad_scores = (weights * grad_weights).astype(BF16)
                    if part == 0:
                        grad_v = dot(weights.astype(BF16), grad)
                        grad_k = dot(grad_scores, query)
                        if half == 0:
                            grad_value[:, lanes] = grad_v
                            grad_key[:, lanes] = grad_k
                        else:
                            grad_value[:, lanes] += grad_v
                            grad_key[:, lanes] += grad_k
                    grad_q = grad_q + dot(keys_t[part, head_rows, :], grad_scores)
                grad_query_t[head_rows, :] = grad_q
                perform_at("A", half, 2, HEADS // 2, pair)
            return carry

        lax.fori_loop(0, HEADS // 2, own_queries, 0)
        for load in loads:
            load.wait()
        turns = []
        grad_normed[...] = jnp.transpose(grad_query_t[...])
        for number in range(blocks):
            rows = pl.ds(number * BLOCK, BLOCK)
            before = block_place(segments, lengths, seq * blocks + number)[1]
            cosine, sine = rotary_block(table, before)
            turns.append((cosine, -sine))
            for pair in range(HEADS // 2):
                lanes = pl.ds(pair * 128, 128)
                grad_triple[rows, lanes] = (turn(grad_normed[rows, lanes], cosine, -sine) * 0.125).astype(BF16)

        def third(part):
            triple_t = dot_tn(grad_triple[:, pl.ds(part * width, width)], normed[...]).astype(BF16)
            for place in range(width // 48):
                group, piece = divmod(part * (width // 48) + place, 3)
                at = (group >> 3, (group >> 2) & 1, (group >> 1) & 1, group & 1)
                for side in range(2):
                    triple_part[at + (side, pl.ds(48 * piece, 48))] = triple_t[
                        place * 48 : place * 48 + 48, side * LANES : side * LANES + LANES
                    ]

        third(0)
        grad_normed[...] = dot_nt(grad_triple[:, pl.ds(0, width)], weight[:, pl.ds(0, width)])
        perform(("E", 0))
        for place in range(2):
            swap(place).wait_recv()

        def other_queries(pair, carry):
            lanes = pl.ds(pl.multiple_of(pair * 128, 128), 128)
            swap(pair + 2).wait_recv()
            query_pair, grad_pair = queries[1, :, lanes], other_grad[:, lanes]
            pair_lane = lane_iota(query_pair.shape)
            grad_k = grad_key[:, lanes]
            grad_v = grad_value[:, lanes]
            for half in range(2):
                head = pair * 2 + half
                mine = (pair_lane < 64) == (half == 0)
                query = jnp.where(mine, query_pair, jnp.zeros_like(query_pair))
                grad = jnp.where(mine, grad_pair, jnp.zeros_like(grad_pair))
                head_lanes = (pair_lane >= 3 * head) & (pair_lane < 3 * head + 3)
                features = jnp.where(head_lanes, jnp.full_like(query_pair, -1.0), key_features[0])
                scores = dot_nt(
                    jnp.concatenate([keys[0, :, lanes], features], axis=1),
                    jnp.concatenate([query, other_features[...]], axis=1),
                )
                weights = jnp.exp(scores)
                grad_weights = dot_nt(
                    jnp.concatenate([values[0, :, lanes], features], axis=1),
                    jnp.concatenate([grad, other_delta[...]], axis=1),
                )
                grad_scores = (weights * grad_weights).astype(BF16)
                grad_v = grad_v + dot(weights.astype(BF16), grad)
                grad_k = grad_k + dot(grad_scores, query)
            grad_key[:, lanes] = grad_k
            grad_value[:, lanes] = grad_v
            perform_at("B", 0, 1, HEADS // 2, pair)
            return carry

        lax.fori_loop(0, HEADS // 2, other_queries, 0)

        for number in range(blocks):
            rows = pl.ds(number * BLOCK, BLOCK)
            for pair in range(HEADS // 2):
                lanes = pl.ds(pair * 128, 128)
                grad_triple[rows, pl.ds(width + pair * 128, 128)] = turn(grad_key[rows, lanes], *turns[number]).astype(BF16)
            grad_triple[rows, pl.ds(2 * width, width)] = grad_value[rows, :].astype(BF16)
        third(1)
        third(2)
        triple = [
            Stream(
                kit, 14 + number, triple_part, 48 * number, 48, {}, order, (tri_a, tri_b, tri_c, tri_d, tri_e),
                48 * number, 432 + 48 * number,
            )
            for number, order in enumerate(TRIPLE_ORDERS)
        ]
        for number, stream in enumerate(triple):
            streams["q", number] = stream
            stream.send(0)
        perform(("C", 0))
        for part in range(1, 3):
            lanes = pl.ds(part * width, width)
            grad_normed[...] += dot_nt(grad_triple[:, lanes], weight[:, lanes])
            perform(("C", part))

        gain_sum = jnp.zeros((1, width), F32)
        for number in range(blocks):
            rows, here = pl.ds(number * BLOCK, BLOCK), pl.ds(number, 1)
            value = hidden[rows, :].astype(F32)
            centered = value - mean_of(value)
            inverse = lax.rsqrt(mean_of(centered * centered) + 1e-05)
            normal = centered * inverse
            grad = grad_normed[rows, :]
            mod_rows[here, pl.ds(0, width)] = jnp.sum(grad, axis=0, keepdims=True)
            mod_rows[here, pl.ds(width, width)] = jnp.sum(grad * (normal * as_row(first_gain)), axis=0, keepdims=True)
            grad_line = grad * (1.0 + mod_part(number, 1))
            gain_sum = gain_sum + jnp.sum(grad_line * normal, axis=0, keepdims=True)
            grad_normal = grad_line * as_row(first_gain)
            along = mean_of(grad_normal * normal)
            term = (grad_normal - mean_of(grad_normal) - normal * along) * inverse
            input_grad[rows, :] = (grad_middle[rows, :] + term).astype(BF16)
            perform(("C", 3 + number))
        late_acc[0] = jnp.zeros_like(late_acc[0])
        late_acc[0, pl.ds(0, 1), :] = gain_sum
        for part in range(2):
            late_acc[0, pl.ds(1 + part, 1), :] = jnp.sum(mod_rows[:, pl.ds(part * width, width)], axis=0, keepdims=True)

        def late_copy(number):
            return pltpu.make_async_remote_copy(
                late_acc.at[number], late_got.at[number], late_send.at[number], late_recv.at[number],
                device_id=greet[(1 + number) % len(greet)], device_id_type=MESH_ID,
            )

        def late_step(number):
            late_copy(number).wait_recv()
            late_acc[number + 1] = late_acc[number] + late_got[number]
            if number + 1 < len(greet):
                late_copy(number + 1).start()

        late_copy(0).start()

        mod_axes = (CORE, Y, Z1, Z2, X)

        def mod_copies(number):
            mods = (mod_zero, mod_one, mod_two, mod_three, mod_four)
            conds = (cond_zero, cond_one, cond_two, cond_three, cond_four)
            if number == 0:
                pairs = ((mod_zero.at[:, :, :, 1 - core], mod_got), (cond_zero, cond_got))
            else:
                later = ((mod_two, cond_two), (mod_three, cond_three), (mod_four, cond_four), (mod_five, cond_five))[number - 1]
                chunks = pl.ds(2 ** (number - 1), 2 ** (number - 1))
                if number == 1:
                    source = mod_one.at[:, :, :, 1 - bits[Y]]
                elif number == 2:
                    source = mod_two.at[:, :, 1 - bits[Z1]]
                elif number == 3:
                    source = mod_three.at[:, 1 - bits[Z2]]
                else:
                    source = mod_four
                pairs = ((source, later[0].at[chunks]), (conds[number], later[1].at[chunks]))
            return [
                pltpu.make_async_remote_copy(
                    source, target, mod_send.at[place, number], mod_recv.at[place, number],
                    device_id=exchange_partner(mod_axes[number], extra_bits), device_id_type=MESH_ID,
                )
                for place, (source, target) in enumerate(pairs)
            ]

        def mod_step(number):
            for copy in mod_copies(number):
                copy.wait_recv()
            if number == 0:
                mod_one[0] = mod_zero[:, :, :, core]
                mod_one[0, :, :, :, pl.ds(4, 4), :] = mod_got[:, :, :, pl.ds(0, 4), :]
                cond_one[0] = cond_zero[...]
                cond_one[0, pl.ds(4, 4), :] = cond_got[pl.ds(0, 4), :]
            if number == 0:
                mod_two[0] = mod_one[0, :, :, bits[Y]]
                cond_two[0] = cond_one[0]
            elif number == 1:
                mod_three[pl.ds(0, 2)] = mod_two[:, :, bits[Z1]]
                cond_three[pl.ds(0, 2)] = cond_two[...]
            elif number == 2:
                mod_four[pl.ds(0, 4)] = mod_three[:, bits[Z2]]
                cond_four[pl.ds(0, 4)] = cond_three[...]
            elif number == 3:
                mod_five[pl.ds(0, 8)] = mod_four[...]
                cond_five[pl.ds(0, 8)] = cond_four[...]
            if number < 4:
                for copy in mod_copies(number + 1):
                    copy.start()

        mod_zero[...] = jnp.zeros_like(mod_zero)
        columns = 6 * width // 16
        for group in range(16):
            at = (group >> 3, (group >> 2) & 1, (group >> 1) & 1, group & 1)
            mod_zero[at + (pl.ds(0, blocks), pl.ds(0, columns))] = mod_rows[:, pl.ds(group * columns, columns)]
        cond_zero[...] = condition[...]
        for copy in mod_copies(0):
            copy.start()

        for is_add, name, stage in work[("F", 0)]:
            if name[0] == "m":
                mod_step(stage)
                late_step(stage)
            elif name[0] == "s":
                small_step(stage)
            elif is_add:
                streams[name].add(stage)
            else:
                streams[name].send(stage)
        chunk_rows = mod_five.shape[0] * mod_five.shape[1]
        gathered = mod_five[...].reshape(chunk_rows, LANES)
        embedded = cond_five[...].reshape(chunk_rows, 128).astype(BF16)
        upper = gathered.astype(BF16)
        lower = (gathered - upper.astype(F32)).astype(BF16)
        mod_out[...] = dot_tn(embedded, upper) + dot_tn(embedded, lower)
        for number in range(5, len(greet)):
            small_step(number)
        for number in range(5, len(greet)):
            late_step(number)
        small_out[...] = small_acc[len(greet)]
        small_out[pl.ds(FIRST_GAIN, 1), :] = late_acc[len(greet), pl.ds(0, 1), :]
        small_out[pl.ds(MOD_BIAS, 2), :] = late_acc[len(greet), pl.ds(1, 2), :]
        for stream in triple:
            stream.done()
        for number in range(5):
            for copy in mod_copies(number):
                copy.wait_send()
        for number in range(len(greet)):
            small_copy(number).wait_send()
            late_copy(number).wait_send()

    pl.run_scoped(
        attention_phase,
        pltpu.VMEM((tokens, width), BF16), pltpu.VMEM((tokens, width), BF16), pltpu.VMEM((width, 3 * width), BF16),
        pltpu.VMEM((2, width, tokens), BF16), pltpu.VMEM((width, tokens), F32), pltpu.VMEM((tokens, width), F32),
        pltpu.VMEM((tokens, width), F32), pltpu.VMEM((tokens, 3 * width), BF16), pltpu.VMEM((tokens, width), F32),
        pltpu.VMEM((2, 2, 2, 2, 2, 144, LANES), BF16),
        pltpu.VMEM((2, 2, 2, 2, 8, LANES), F32), pltpu.VMEM((1, 2, 2, 2, 8, LANES), F32),
    )

    for tile in range(tiles):
        for copy in core_copies(tile):
            copy.wait_send()
    for name, stream in streams.items():
        if name[0] != "q":
            stream.done()
    for place in range(HEADS // 2 + 2):
        swap(place).wait_send()


def backward(segments, lengths, modulation, condition, table, first_gain, second_gain, expand_bias, reduce_bias, *arrays):
    tokens, width = arrays[3].shape
    all_bits = lax.axis_size("dp").bit_length() - 1
    extra_bits = all_bits - GROUP_BITS
    steps = all_bits + 1
    smem, vmem = pl.BlockSpec(memory_space=pltpu.SMEM), pl.BlockSpec(memory_space=pltpu.VMEM)
    hbm = pl.BlockSpec(memory_space=pl.ANY)
    tiles = arrays[0].shape[0] // TILE

    def rows_of(count, free, lead=()):
        return pltpu.VMEM(lead + (2,) * free + (count, LANES), BF16)

    def half(dtype):
        return pltpu.VMEM((tokens, width), dtype)

    features = pltpu.VMEM((tokens, 128), BF16)
    both = pltpu.VMEM((2, tokens, width), BF16)
    group_rows = [rows_of(count, free) for count in (48, 144) for free in (4, 3, 2, 1, 0)]
    halves = [rows_of(192, 1, (4,)), rows_of(192, 0, (4,)), rows_of(192, 0, (2,)), rows_of(192, 0)]
    halves += [rows_of(96, 2, (4,)), rows_of(96, 1, (4,)), rows_of(96, 0, (4,)), rows_of(96, 0, (2,))]
    mods = [pltpu.VMEM(shape + (8, LANES), F32) for shape in ((2, 2, 2), (2, 2, 2), (4, 2), (8,), (16,))]
    conds = [pltpu.VMEM(shape + (8, 128), F32) for shape in ((), (), (1,), (2,), (4,), (8,), (16,))]
    dma = pltpu.SemaphoreType.DMA
    return pl.pallas_call(
        functools.partial(backward_kernel, extra_bits, all_bits),
        out_shape=(
            jax.ShapeDtypeStruct((tokens, width), BF16),
            jax.ShapeDtypeStruct((tokens, width), BF16),
            jax.ShapeDtypeStruct((576, LANES), F32),
            jax.ShapeDtypeStruct((128, LANES), F32),
            jax.ShapeDtypeStruct((SMALL_ROWS, width), F32),
        ),
        in_specs=[smem] * 2 + [vmem] * 7 + [hbm] * len(arrays),
        out_specs=(vmem,) * 5,
        scratch_shapes=[rows_of(192, 5), rows_of(192, 5), rows_of(48, 5), rows_of(192, 4), rows_of(192, 4)]
        + halves
        + group_rows
        + [both, both, both, features, pltpu.VMEM((2, tokens, 128), BF16)]
        + [half(F32), half(BF16), features, half(BF16), features, features]
        + [pltpu.VMEM((tokens // BLOCK, 6 * width), F32)]
        + [pltpu.VMEM((steps + 1, SMALL_ROWS, width), F32), pltpu.VMEM((steps, SMALL_ROWS, width), F32)]
        + [pltpu.VMEM((steps + 1, 8, width), F32), pltpu.VMEM((steps, 8, width), F32)]
        + mods
        + conds
        + [dma((12,)), dma((2, tiles)), dma((2, tiles)), dma((2, tiles)), dma((17, 5)), dma((17, 5)), dma((8,)), dma((8,))]
        + [dma((steps,)), dma((steps,)), dma((steps,)), dma((steps,)), dma((2, 5)), dma((2, 5))],
        compiler_params=pltpu.CompilerParams(
            collective_id=2, has_side_effects=True, vmem_limit_bytes=63 << 20
        ),
    )(segments, lengths, modulation, condition, table, first_gain, second_gain, expand_bias, reduce_bias, *arrays)


def scatter_rest(block, dp_size):
    group = dp_size >> GROUP_BITS
    if group == 1:
        return block
    groups = [[first * group + place for place in range(group)] for first in range(dp_size // group)]
    return lax.psum_scatter(block, "dp", scatter_dimension=0, axis_index_groups=groups, tiled=True)


def finish_kernel(
    block_in, grad_in, sums, mod_sum, small,
    block_out, input_grad, first_gain, mod_block, mod_bias, triple_block, output_block, second_gain, expand_block,
    expand_bias, reduce_block, reduce_bias, masked_rms,
):
    width = first_gain.shape[0]
    block_out[...] = block_in[...]
    input_grad[...] = grad_in[...]
    expand_block[...] = sums[pl.ds(0, 192), :]
    for chunk in range(4):
        reduce_block[:, pl.ds(chunk * LANES, LANES)] = sums[pl.ds(192 + 48 * chunk, 48), :]
    output_block[...] = sums[pl.ds(384, 48), :]
    triple_block[...] = sums[pl.ds(432, 144), :]
    half = mod_sum.shape[0] // 2
    first_row = pl.multiple_of(lax.axis_index("seq") * half, half)
    mod_block[...] = mod_sum[pl.ds(first_row, half), pl.ds(0, mod_block.shape[1])]
    for target, first in (
        (first_gain, FIRST_GAIN), (mod_bias, MOD_BIAS), (second_gain, SECOND_GAIN), (expand_bias, EXPAND_BIAS),
        (reduce_bias, REDUCE_BIAS),
    ):
        for part in range(target.shape[0] // width):
            target[pl.ds(part * width, width)] = small[first + part, :]
    count = jnp.sum(jnp.where(lane_iota((1, width)) == 3, small[pl.ds(STATS, 1), :], 0.0))
    masked_rms[...] = jnp.sqrt(small[pl.ds(STATS, 1), pl.ds(0, 128)] / (count * width))


def finish(block_out, input_grad, sums, mod_sum, small):
    width = small.shape[1]
    vmem = pl.BlockSpec(memory_space=pltpu.VMEM)
    shapes = (
        (width,), (mod_sum.shape[0] // 2, 6 * width // 16), (6 * width,), (144, LANES), (48, LANES), (width,), (192, LANES),
        (4 * width,), (48, 4 * LANES), (width,), (1, 128),
    )
    block_out, input_grad, *rest = pl.pallas_call(
        finish_kernel,
        out_shape=(
            jax.ShapeDtypeStruct(block_out.shape, block_out.dtype),
            jax.ShapeDtypeStruct(input_grad.shape, input_grad.dtype),
        )
        + tuple(jax.ShapeDtypeStruct(shape, F32) for shape in shapes),
        in_specs=[vmem] * 5,
        out_specs=(vmem,) * (2 + len(shapes)),
    )(block_out, input_grad, sums, mod_sum, small)
    for place in (3, 4, 6, 8):
        rest[place] = rest[place].T
    return (block_out, input_grad, *rest[:-1], rest[-1][0, :3])


def local(
    hidden_in,
    segment_ids,
    piece_lengths,
    time_index,
    first_gain,
    modulation_weight,
    modulation_bias,
    query_key_value_weight,
    attention_output_matrix,
    second_gain,
    widen_weight,
    expand_bias,
    narrow_weight,
    reduce_bias,
    cotangent,
):
    slot_count, own_rows, width = hidden_in.shape
    hidden, cot = hidden_in[0], cotangent[0]
    table = jnp.asarray(angle_table())
    gain_one, gain_two = first_gain, second_gain
    normed, queries, keys, values, attended, query_features, key_features, modulation, condition = forward(
        segment_ids, piece_lengths, time_index, hidden, table, gain_one, modulation_weight,
        modulation_bias, query_key_value_weight,
    )
    block_out, input_grad, block_sum, mod_sum, small_sum = backward(
        segment_ids, piece_lengths, modulation, condition, table, gain_one, gain_two, expand_bias,
        reduce_bias, narrow_weight, widen_weight, attention_output_matrix, attended, cot, queries, keys, values,
        query_features, key_features, normed, hidden, query_key_value_weight,
    )
    dp_size = lax.axis_size("dp")
    if dp_size == 2**GROUP_BITS:
        block_out, input_grad, *rest = finish(block_out, input_grad, block_sum, mod_sum, small_sum)
        return (block_out[None], input_grad[None], *rest)
    expand_block = scatter_rest(block_sum[:192], dp_size).T
    reduce_block = block_sum[192:384].reshape(4, -1, LANES).transpose(1, 0, 2).reshape(-1, 4 * LANES)
    reduce_block = scatter_rest(reduce_block, dp_size).T
    output_block = scatter_rest(block_sum[384:432], dp_size).T
    triple_block = scatter_rest(block_sum[432:576], dp_size).T
    half = mod_sum.shape[0] // 2
    mod_block = lax.dynamic_slice_in_dim(mod_sum, lax.axis_index("seq") * half, half, 0)[:, : 6 * width // 16]
    mod_block = scatter_rest(mod_block.T, dp_size).T
    stats = small_sum[STATS]
    return (
        block_out[None],
        input_grad[None],
        small_sum[FIRST_GAIN],
        mod_block,
        small_sum[MOD_BIAS : MOD_BIAS + 6].reshape(-1),
        triple_block,
        output_block,
        small_sum[SECOND_GAIN],
        expand_block,
        small_sum[EXPAND_BIAS : EXPAND_BIAS + 4].reshape(-1),
        reduce_block,
        small_sum[REDUCE_BIAS],
        jnp.sqrt(stats[:3] / (stats[3] * width)),
    )


def solution(mesh):
    in_specs = (
        P("dp", "seq", None),
        P("dp", None),
        P("dp", None),
        P("dp", None),
        P(),
        P(),
        P(),
        P(),
        P(),
        P(),
        P(),
        P(),
        P(),
        P(),
        P("dp", "seq", None),
    )
    out_specs = (
        P("dp", "seq", None),
        P("dp", "seq", None),
        P(),
        P("seq", "dp"),
        P(),
        P("seq", "dp"),
        P("seq", "dp"),
        P(),
        P("seq", "dp"),
        P(),
        P("seq", "dp"),
        P(),
        P(),
    )
    return jax.shard_map(local, mesh=mesh, in_specs=in_specs, out_specs=out_specs, check_vma=False)
```

```python
import functools
import math

import jax
import jax.numpy as jnp
import numpy as np
from jax import lax
from jax.experimental import pallas as pl
from jax.experimental.pallas import tpu as pltpu
from jax.sharding import PartitionSpec as P

HEADS = 12
BLOCK = 128
MAX_SEQUENCES = 8
SEGMENT_LANE = 40
MASKED = -1000000000.0
LANES = 384
GROUP_BITS = 4
MESH_ID = pl.DeviceIdType.MESH
F32, BF16 = jnp.float32, jnp.bfloat16

ROTARY_COS, ROTARY_SIN, BLOCK_COS, BLOCK_SIN = 0, 128, 256, 264
HIGH_COS, HIGH_SIN, LOW_COS, LOW_SIN, TABLE_ROWS = 272, 304, 336, 368, 400

FIRST_GAIN, MOD_BIAS, SECOND_GAIN, EXPAND_BIAS, REDUCE_BIAS, STATS, SMALL_ROWS = 0, 1, 7, 8, 12, 13, 16


def angle_table():
    lane = np.arange(128)
    rotary = np.exp((lane % 32) * (-2.0 * math.log(10000.0) / 64))
    timing = np.exp((lane % 64) * (-math.log(10000.0) / 64))
    steps = np.arange(128)[:, None]
    angles = [
        (np.cos, steps * rotary), (np.sin, steps * rotary),
        (np.cos, steps[:8] * 128 * rotary), (np.sin, steps[:8] * 128 * rotary),
        (np.cos, steps[:32] * 32 * timing), (np.sin, steps[:32] * 32 * timing),
        (np.cos, steps[:32] * timing), (np.sin, steps[:32] * timing),
    ]
    return np.concatenate([fn(angle) for fn, angle in angles]).astype(np.float32)


def dot(left, right):
    return jnp.dot(left, right, preferred_element_type=F32)


def dot_nt(left, right):
    return lax.dot_general(left, right, (((1,), (1,)), ((), ())), preferred_element_type=F32)


def dot_tn(left, right):
    return lax.dot_general(left, right, (((0,), (0,)), ((), ())), preferred_element_type=F32)


def as_row(vector):
    return vector[...].reshape(1, -1)


def lane_iota(shape):
    return lax.broadcasted_iota(jnp.int32, shape, len(shape) - 1)


def row_iota(shape):
    return lax.broadcasted_iota(jnp.int32, shape, 0)


def block_place(segments, lengths, block):
    segment = segments[0, block * BLOCK]
    before = jnp.int32(0)
    for other in range(segments.shape[1] // BLOCK):
        same = (segments[0, other * BLOCK] == segment) & (other < block)
        before = before + jnp.where(same, 1, 0)
    return segment, before, lengths[0, segment] - before * BLOCK


def rotary_block(table, before):
    cos_row, sin_row = table[pl.ds(ROTARY_COS, 128), :], table[pl.ds(ROTARY_SIN, 128), :]
    cos_block = table[pl.ds(BLOCK_COS + before, 1), :]
    sin_block = table[pl.ds(BLOCK_SIN + before, 1), :]
    cosine = cos_row * cos_block - sin_row * sin_block
    sine = sin_row * cos_block + cos_row * sin_block
    first_half = lane_iota(sine.shape) % 64 < 32
    return cosine, jnp.where(first_half, -sine, sine)


def turn(values, cosine, sine):
    first_half = lane_iota(values.shape) % 64 < 32
    swapped = jnp.where(first_half, pltpu.roll(values, 96, 1), pltpu.roll(values, 32, 1))
    return values * cosine + swapped * sine


def mean_of(values):
    return jnp.mean(values, axis=-1, keepdims=True)


def split_three(values):
    first = values.astype(BF16)
    rest = values - first.astype(F32)
    second = rest.astype(BF16)
    third = (rest - second.astype(F32)).astype(BF16)
    place = lane_iota(values.shape) % 3
    picked = jnp.where(place == 0, first.astype(F32), jnp.where(place == 1, second.astype(F32), third.astype(F32)))
    return picked.astype(BF16)


def forward_kernel(
    segments, lengths, times, hidden, table, first_gain, mod_weight, mod_bias, weight,
    normed, queries, keys, values, attended, query_features, key_features, modulation, condition,
    other_hidden, turned_values, out_t, peak, total, send_sem, recv_sem,
):
    tokens, width = hidden.shape
    blocks = tokens // BLOCK
    seq = lax.axis_index("seq")
    partner = (lax.axis_index("dp"), 1 - seq)
    barrier = pltpu.get_barrier_semaphore()
    pl.semaphore_signal(barrier, inc=1, device_id=partner, device_id_type=MESH_ID)
    pl.semaphore_wait(barrier, 1)
    exchanges = [
        pltpu.make_async_remote_copy(
            hidden.at[pl.ds(place * tokens // 2, tokens // 2)], other_hidden.at[pl.ds(place * tokens // 2, tokens // 2)],
            send_sem.at[place], recv_sem.at[place], device_id=partner, device_id_type=MESH_ID,
        )
        for place in range(2)
    ]
    for exchange in exchanges:
        exchange.start()

    places = []
    for number in range(2 * blocks):
        block = (seq if number < blocks else 1 - seq) * blocks + number % blocks
        places.append(block_place(segments, lengths, block))
        time = times[0, places[number][0]]
        high, low = time // 32, time % 32
        cos_high, sin_high = table[pl.ds(HIGH_COS + high, 1), :], table[pl.ds(HIGH_SIN + high, 1), :]
        cos_low, sin_low = table[pl.ds(LOW_COS + low, 1), :], table[pl.ds(LOW_SIN + low, 1), :]
        cosine = cos_high * cos_low - sin_high * sin_low
        sine = sin_high * cos_low + cos_high * sin_low
        row = jnp.where(lane_iota(cosine.shape) < 64, cosine, sine)
        condition[pl.ds(number, 1), :] = row.astype(BF16).astype(F32)
    modulation[...] = dot(condition[...].astype(BF16), mod_weight[...]) + as_row(mod_bias)

    lane = lane_iota((BLOCK, 128))
    row = row_iota((BLOCK, 128))

    half_blocks = blocks // 2
    sections = ((0, 0, blocks), (1, 0, half_blocks), (1, half_blocks, half_blocks))
    for section, (part, first_block, count) in enumerate(sections):
        source = hidden if part == 0 else other_hidden
        if part == 1:
            exchanges[section - 1].wait_recv()
        section_rows = pl.ds(first_block * BLOCK, count * BLOCK)
        turns = []
        for number in range(first_block, first_block + count):
            rows = pl.ds(number * BLOCK, BLOCK)
            segment, before, valid_count = places[part * blocks + number]
            turns.append(rotary_block(table, before))
            mine = lane == SEGMENT_LANE + segment
            in_lanes = (lane >= SEGMENT_LANE) & (lane < SEGMENT_LANE + MAX_SEQUENCES)
            blocked = in_lanes & jnp.logical_not(mine & (row < valid_count))
            key_features[part, rows, :] = jnp.where(blocked, MASKED, 0.0).astype(BF16)
            if part == 0:
                query_features[rows, :] = jnp.where(mine, 1.0, 0.0).astype(BF16)
            mod_row = pl.ds(part * blocks + number, 1)
            shift, scale = modulation[mod_row, pl.ds(0, width)], modulation[mod_row, pl.ds(width, width)]
            value = source[rows, :].astype(F32)
            centered = value - mean_of(value)
            spread = mean_of(centered * centered)
            line = centered * lax.rsqrt(spread + 1e-05) * as_row(first_gain)
            result = (line * (1.0 + scale) + shift).astype(BF16)
            if part == 0:
                normed[rows, :] = result
            else:
                other_hidden[rows, :] = result
        normed_source = normed if part == 0 else other_hidden
        for tile in range(3 * width // LANES):
            which, first = divmod(tile * LANES, width)
            product = dot(normed_source[section_rows, :], weight[:, pl.ds(tile * LANES, LANES)])
            target = (queries, keys, values)[which]
            for place in range(count):
                cosine, sine = turns[place]
                for pair in range(LANES // 128):
                    piece = product[place * BLOCK : (place + 1) * BLOCK, pair * 128 : (pair + 1) * 128]
                    if which < 2:
                        piece = turn(piece, cosine, sine)
                    if which == 0:
                        piece = piece.astype(BF16).astype(F32) * 0.125
                    rows = pl.ds((first_block + place) * BLOCK, BLOCK)
                    target[part, rows, pl.ds(first + pair * 128, 128)] = piece.astype(BF16)
        turned_rows = pl.ds(0, count * BLOCK)
        turned_values[:, turned_rows] = jnp.transpose(values[part, section_rows, :])

        def attend(pair, carry):
            lanes = pl.ds(pl.multiple_of(pair * 128, 128), 128)
            query_pair, key_pair = queries[0, :, lanes], keys[part, section_rows, lanes]
            left = jnp.concatenate([key_pair, key_features[part, section_rows, :]], axis=1)
            pair_lane = lane_iota(query_pair.shape)
            both = []
            for half in range(2):
                query = jnp.where((pair_lane < 64) == (half == 0), query_pair, jnp.zeros_like(query_pair))
                both.append(dot_nt(left, jnp.concatenate([query, query_features[...]], axis=1)))
            for half, scores in enumerate(both):
                head = pair * 2 + half
                head_rows = pl.ds(pl.multiple_of(head * 64, 64), 64)
                one_row = pl.ds(head, 1)
                top = jnp.max(scores, axis=0, keepdims=True)
                if section > 0:
                    top = jnp.maximum(top, peak[one_row, :])
                weights = jnp.exp(scores - top)
                summed = jnp.sum(weights, axis=0, keepdims=True)
                mixed = dot(turned_values[head_rows, turned_rows], weights.astype(BF16))
                if section > 0:
                    rescale = jnp.exp(peak[one_row, :] - top)
                    summed = summed + rescale * total[one_row, :]
                    mixed = mixed + out_t[head_rows, :] * rescale
                if section < len(sections) - 1:
                    out_t[head_rows, :] = mixed
                    total[one_row, :] = summed
                    peak[one_row, :] = top
                else:
                    out_t[head_rows, :] = mixed * (1.0 / summed)
                    peak[one_row, :] = top + jnp.log(summed)
            return carry

        lax.fori_loop(0, HEADS // 2, attend, 0)

    attended[...] = jnp.transpose(out_t[...].astype(BF16))
    log_rows = jnp.concatenate(
        [jnp.broadcast_to(peak[pl.ds(head, 1), :], (3, tokens)) for head in range(HEADS)]
        + [jnp.zeros((128 - 3 * HEADS, tokens), F32)], axis=0,
    )
    query_features[...] = query_features[...] + split_three(jnp.transpose(log_rows))
    for exchange in exchanges:
        exchange.wait_send()


def forward(segments, lengths, times, hidden, table, first_gain, mod_weight, mod_bias, weight):
    tokens, width = hidden.shape
    blocks = 2 * tokens // BLOCK
    half = jax.ShapeDtypeStruct((tokens, width), BF16)
    both = jax.ShapeDtypeStruct((2, tokens, width), BF16)
    smem, vmem = pl.BlockSpec(memory_space=pltpu.SMEM), pl.BlockSpec(memory_space=pltpu.VMEM)
    return pl.pallas_call(
        forward_kernel,
        out_shape=(
            half, both, both, both, half,
            jax.ShapeDtypeStruct((tokens, 128), BF16),
            jax.ShapeDtypeStruct((2, tokens, 128), BF16),
            jax.ShapeDtypeStruct((blocks, 6 * width), F32),
            jax.ShapeDtypeStruct((blocks, 128), F32),
        ),
        in_specs=[smem] * 3 + [vmem] * 6,
        out_specs=(vmem,) * 9,
        scratch_shapes=[
            pltpu.VMEM((tokens, width), BF16),
            pltpu.VMEM((width, tokens), BF16),
            pltpu.VMEM((width, tokens), F32),
            pltpu.VMEM((16, tokens), F32),
            pltpu.VMEM((16, tokens), F32),
            pltpu.SemaphoreType.DMA((2,)),
            pltpu.SemaphoreType.DMA((2,)),
        ],
        compiler_params=pltpu.CompilerParams(
            collective_id=1, has_side_effects=True, vmem_limit_bytes=56 << 20
        ),
    )(segments, lengths, times, hidden, table, first_gain, mod_weight, mod_bias, weight)


TILE = 384
Z2, Z1, Y, CORE, X = 0, 1, 2, 3, 4


WIDE_ORDERS = ((X, Y), (Y, X), (X, Y), (Y, X))
REDUCE_ORDERS = ((Z1, Z2, Y), (Z1, Y, Z2), (Y, Z1, Z2), (Z1, Y, Z2))
OUTPUT_ORDER = (CORE, Z1, Y, X, Z2)
TRIPLE_ORDERS = ((Y, X, Z1, Z2), (Z1, X, Y, Z2), (X, Y, Z1, Z2))
PLAN = (
    (("T", 6), (("r", 0), ("w", 0),)),
    (("N", 0), (("w", 1), ("r", 1),)),
    (("D", 1), (("w", 2),)),
    (("D", 2), (("r", 2),)),
    (("A", 0), (("s", 0), ("r", 0),)),
    (("A", 1), (("w", 1), ("w", 0),)),
    (("A", 2), (("o", 0),)),
    (("A", 4), (("r", 3),)),
    (("A", 5), (("w", 3),)),
    (("A", 6), (("r", 2),)),
    (("A", 8), (("r", 1), ("wm", 0),)),
    (("A", 10), (("w", 2),)),
    (("A", 11), (("s", 0),)),
    (("E", 0), (("o", 0), ("r", 0),)),
    (("B", 0), (("r", 3),)),
    (("B", 2), (("r", 2),)),
    (("B", 4), (("o", 0), ("w", 3),)),
    (("B", 5), (("s", 0), ("r", 1),)),
    (("C", 0), (("o", 0), ("r", 3),)),
    (("C", 1), (("re", 0),)),
    (("C", 2), (("wm", 1),)),
    (("C", 3), (("s", 0),)),
    (("C", 4), (("re", 1),)),
    (("C", 5), (("o", 0),)),
    (("F", 0), (("m", 0), ("we", 0), ("q", 0), ("q", 2), ("s", 0), ("m", 0), ("q", 1), ("q", 0), ("q", 2), ("m", 0), ("q", 0), ("q", 1), ("q", 2), ("q", 1), ("m", 0), ("q", 0), ("q", 2), ("q", 1), ("m", 0),)),
)


def exchange_partner(axis, extra_bits):
    dp, seq = lax.axis_index("dp"), lax.axis_index("seq")
    if axis == X:
        return (dp, 1 - seq)
    return (dp ^ (1 << (GROUP_BITS - 1 - axis + extra_bits)), seq)


def own_bit(axis, extra_bits):
    if axis == X:
        return lax.axis_index("seq")
    return (lax.axis_index("dp") >> (GROUP_BITS - 1 - axis + extra_bits)) & 1


class Stream:
    def __init__(self, kit, number, part, first, count, fixed, order, got, got_first=0, total_first=None):
        self.kit, self.number, self.part, self.first, self.count = kit, number, part, first, count
        self.fixed, self.order, self.got, self.got_first = fixed, order, got, got_first
        self.total_first = total_first

    def free(self, stage):
        return [axis for axis in range(5) if axis not in self.fixed and axis not in self.order[: stage + 1]]

    def copy(self, stage):
        bits = self.kit["bits"]
        index = [slice(None)] * 5
        for axis, value in self.fixed.items():
            index[axis] = value
        for axis in self.order[:stage]:
            index[axis] = bits[axis]
        index[self.order[stage]] = 1 - bits[self.order[stage]]
        target = (slice(None),) * len(self.free(stage)) + (pl.ds(self.got_first, self.count),)
        return pltpu.make_async_remote_copy(
            self.part.at[tuple(index) + (pl.ds(self.first, self.count),)],
            self.got[stage].at[target],
            self.kit["send"].at[self.number, stage],
            self.kit["recv"].at[self.number, stage],
            device_id=exchange_partner(self.order[stage], self.kit["extra"]),
            device_id_type=MESH_ID,
        )

    def send(self, stage):
        self.copy(stage).start()

    def add(self, stage):
        self.copy(stage).wait_recv()
        last = stage == len(self.order) - 1 and self.total_first is not None
        bits, free = self.kit["bits"], self.free(stage)
        rows, got_rows = pl.ds(self.first, self.count), pl.ds(self.got_first, self.count)

        def one(step, carry):
            index = list(bits)
            for axis, value in self.fixed.items():
                index[axis] = value
            place = []
            for order, axis in enumerate(free):
                index[axis] = (step >> (len(free) - 1 - order)) & 1
                place.append(index[axis])
            mine, theirs = self.part[tuple(index) + (rows,)], self.got[stage][tuple(place) + (got_rows,)]
            if last:
                total = mine.astype(F32) + theirs.astype(F32)
                self.kit["sums"][pl.ds(self.total_first, self.count), :] = total
            else:
                self.part[tuple(index) + (rows,)] = mine + theirs
            return carry

        if free:
            lax.fori_loop(0, 2 ** len(free), one, 0)
        else:
            one(0, 0)

    def done(self):
        for stage in range(len(self.order)):
            self.copy(stage).wait_send()


def backward_kernel(
    extra_bits, all_bits,
    segments, lengths, modulation, condition, table, first_gain, second_gain, expand_bias, reduce_bias,
    narrow_hbm, widen_hbm, out_weight_hbm, attended_hbm, cotangent_hbm, queries_hbm, keys_hbm, values_hbm,
    query_features_hbm, key_features_hbm, normed_hbm, hidden_hbm, weight_hbm,
    block_out, input_grad, sums, mod_out, small_out,
    expand_part, reduce_part, output_part,
    expand_got, reduce_got, wide_a, wide_b, wide_z, wide_last, red_a, red_b, red_c, red_last,
    out_a, out_b, out_c, out_d, out_e, tri_a, tri_b, tri_c, tri_d, tri_e,
    queries, keys, values, query_features, key_features,
    grad_middle, grad_attended, delta_features, other_grad, other_delta, other_features, mod_rows,
    small_acc, small_got, late_acc, late_got, mod_got, mod_two, mod_three, mod_four, mod_five,
    cond_zero, cond_got, cond_one, cond_two, cond_three, cond_four, cond_five,
    load_sem, tile_sem, core_send, core_recv, stream_send, stream_recv, swap_send, swap_recv,
    small_send, small_recv, late_send, late_recv, mod_send, mod_recv, triple_send, triple_recv,
):
    tokens, width = input_grad.shape
    tiles = narrow_hbm.shape[0] // TILE
    blocks = tokens // BLOCK
    seq = lax.axis_index("seq")
    dp = lax.axis_index("dp")
    bits = [own_bit(axis, extra_bits) for axis in range(5)]
    kit = {"bits": bits, "send": stream_send, "recv": stream_recv, "extra": extra_bits, "sums": sums}
    core = bits[CORE]

    def others(*axes):
        return {axis: bits[axis] for axis in range(5) if axis not in axes}

    def chosen(**values):
        return {CORE: core, **{{"z2": Z2, "z1": Z1, "x": X}[name]: value for name, value in values.items()}}

    streams = {}
    for g in range(4):
        streams["w", g] = Stream(
            kit, g, expand_part, 0, 192, chosen(z2=g >> 1, z1=g & 1), WIDE_ORDERS[g], (wide_a.at[g], wide_b.at[g])
        )
        streams["r", g] = Stream(
            kit, 4 + g, reduce_part, 96 * (g & 1), 96, chosen(x=g >> 1), REDUCE_ORDERS[g],
            (red_a.at[g], red_b.at[g], red_c.at[g]),
        )
    for v in range(2):
        streams["wm", v] = Stream(
            kit, 8 + v, expand_part, 0, 192, {**others(Z1, Z2), Z2: v}, (Z1,), (wide_z.at[v],)
        )
        streams["re", v] = Stream(
            kit, 11 + v, reduce_part, 96 * v, 96, others(X), (X,), (red_last.at[v],), total_first=192 + 96 * v
        )
    streams["we", 0] = Stream(kit, 10, expand_part, 0, 192, others(Z2), (Z2,), (wide_last,), total_first=0)
    streams["o", 0] = Stream(
        kit, 13, output_part, 0, 48, {}, OUTPUT_ORDER, (out_a, out_b, out_c, out_d, out_e), total_first=384
    )
    merges = {
        ("wm", 0): (("w", 0), ("w", 1)), ("wm", 1): (("w", 2), ("w", 3)), ("we", 0): (("wm", 0), ("wm", 1)),
        ("re", 0): (("r", 0), ("r", 2)), ("re", 1): (("r", 1), ("r", 3)),
    }
    work, stages, finished = {}, {}, set()
    for slot, names in PLAN:
        todo = work.setdefault(slot, [])
        for name in names:
            stage = stages.get(name, 0)
            stages[name] = stage + 1
            todo.append((True, name, stage))
            if name[0] in ("m", "s"):
                continue
            if stage + 1 < (len(streams[name].order) if name in streams else 4):
                todo.append((False, name, stage + 1))
                continue
            finished.add(name)
            for merged, parts in merges.items():
                if name in parts and finished.issuperset(parts):
                    todo.append((False, merged, 0))

    def perform(slot):
        for is_add, name, stage in work.get(slot, ()):
            if name[0] == "s":
                small_step(stage)
            elif is_add:
                streams[name].add(stage)
            else:
                streams[name].send(stage)

    def perform_at(letter, first, stride, count, index):
        for place in range(count):
            slot = (letter, first + stride * place)
            if work.get(slot):

                @pl.when(index == place)
                def _(slot=slot):
                    perform(slot)

    greet = [(dp, 1 - seq)] + [(dp ^ (1 << bit), seq) for bit in range(all_bits)]
    barrier = pltpu.get_barrier_semaphore()
    for partner in greet:
        pl.semaphore_signal(barrier, inc=1, device_id=partner, device_id_type=MESH_ID)

    attention_loads = [
        pltpu.make_async_copy(source, target, load_sem.at[number])
        for number, (source, target) in enumerate(
            ((queries_hbm, queries), (keys_hbm, keys), (values_hbm, values),
             (query_features_hbm, query_features), (key_features_hbm, key_features))
        )
    ]
    row = row_iota((BLOCK, 1))
    keep = []
    for number in range(blocks):
        valid_count = block_place(segments, lengths, seq * blocks + number)[2]
        keep.append(jnp.where(row < valid_count, 1.0, 0.0))

    def mod_part(number, part):
        return modulation[pl.ds(number, 1), pl.ds(part * width, width)]

    def tile_lanes(tile):
        return pl.ds(pl.multiple_of(tile * TILE, TILE), TILE)

    def core_copies(tile):
        at = (tile >> 2, (tile >> 1) & 1, tile & 1)
        rows = pl.ds(pl.multiple_of((tile & 3) * 48, 16), 48)
        everywhere = (slice(None),) * 3
        partner = exchange_partner(CORE, extra_bits)
        return (
            pltpu.make_async_remote_copy(
                expand_part.at[at + (1 - core,)], expand_got.at[at], core_send.at[0, tile], core_recv.at[0, tile],
                device_id=partner, device_id_type=MESH_ID,
            ),
            pltpu.make_async_remote_copy(
                reduce_part.at[everywhere + (1 - core, tile >> 2, rows)], reduce_got.at[everywhere + (tile >> 2, rows)],
                core_send.at[1, tile], core_recv.at[1, tile], device_id=partner, device_id_type=MESH_ID,
            ),
        )

    def core_add(tile):
        at = (tile >> 2, (tile >> 1) & 1, tile & 1)
        rows = pl.ds(pl.multiple_of((tile & 3) * 48, 16), 48)
        for copy in core_copies(tile):
            copy.wait_recv()
        for side in range(2):
            expand_part[at + (core, side)] = expand_part[at + (core, side)] + expand_got[at + (side,)]
        for z2 in range(2):
            for z1 in range(2):
                for y in range(2):
                    index, got = (z2, z1, y, core, tile >> 2, rows), (z2, z1, y, tile >> 2, rows)
                    reduce_part[index] = reduce_part[index] + reduce_got[got]

    def mlp_phase(
        narrow, widen, out_weight, attended, hidden, cotangent, normed_two, grad_low, grad_low_t,
        projected, reduced, grad_normed,
    ):
        def tile_loads(tile):
            lanes = tile_lanes(tile)
            pairs = ((widen_hbm.at[:, lanes], widen.at[:, lanes]), (narrow_hbm.at[lanes], narrow.at[lanes]))
            return [pltpu.make_async_copy(source, target, tile_sem.at[place, tile]) for place, (source, target) in enumerate(pairs)]

        loads = [
            pltpu.make_async_copy(source, target, load_sem.at[5 + number])
            for number, (source, target) in enumerate(
                ((cotangent_hbm, cotangent), (attended_hbm, attended), (out_weight_hbm, out_weight), (hidden_hbm, hidden))
            )
        ]
        for load in loads:
            load.start()
        for tile in range(tiles):
            for load in tile_loads(tile):
                load.start()
        for load in attention_loads:
            load.start()
        small_acc[0] = jnp.zeros_like(small_acc[0])
        grad_normed[...] = jnp.zeros_like(grad_normed)
        reduced[...] = jnp.zeros_like(reduced)
        loads[0].wait()
        bias_sum = jnp.zeros((1, width), F32)
        for number in range(blocks):
            rows = pl.ds(number * BLOCK, BLOCK)
            low = (mod_part(number, 5) * (cotangent[rows, :].astype(F32) * keep[number])).astype(BF16)
            grad_low[rows, :] = low
            bias_sum = bias_sum + jnp.sum(low.astype(F32), axis=0, keepdims=True)
        small_acc[0, pl.ds(REDUCE_BIAS, 1), :] = bias_sum
        grad_low_t[...] = jnp.transpose(grad_low[...])
        for load in loads[1:]:
            load.wait()
        for first in range(0, width, 256):
            lanes = pl.ds(first, 256)
            projected[:, lanes] = dot(attended[...], out_weight[:, lanes])
        branch_sum = jnp.zeros((1, width), F32)
        for number in range(blocks):
            rows = pl.ds(number * BLOCK, BLOCK)
            branch = mod_part(number, 2) * projected[rows, :]
            branch_sum = branch_sum + jnp.sum(keep[number] * branch * branch, axis=0, keepdims=True)
            value = hidden[rows, :].astype(F32) + branch
            centered = value - mean_of(value)
            inverse = lax.rsqrt(mean_of(centered * centered) + 1e-05)
            line = centered * inverse * as_row(second_gain)
            normed_two[rows, :] = (line * (1.0 + mod_part(number, 4)) + mod_part(number, 3)).astype(BF16)
        pl.semaphore_wait(barrier, len(greet))

        def through(tile):
            lanes = tile_lanes(tile)
            for load in tile_loads(tile):
                load.wait()
            u = dot(normed_two[...], widen[:, lanes]) + expand_bias[lanes].reshape(1, TILE)
            grad_active = dot_nt(grad_low[...], narrow[lanes, :])
            square = u * u
            tanh = jnp.tanh(u * (0.7978845608028654 + 0.7978845608028654 * 0.044715 * square))
            half_sum = 0.5 + 0.5 * tanh
            active = (u * half_sum).astype(BF16)
            inner = 0.7978845608028654 + 3.0 * 0.7978845608028654 * 0.044715 * square
            slope = half_sum + (0.5 * u) * (1.0 - tanh * tanh) * inner
            grad_wide = (grad_active * slope).astype(BF16)
            reduced[...] += dot(active, narrow[lanes, :])
            reduce_t = dot(grad_low_t[...], active).astype(BF16)
            rows = pl.ds(pl.multiple_of((tile & 3) * 48, 16), 48)
            reduce_part[:, :, :, :, tile >> 2, rows] = reduce_t.reshape(2, 2, 2, 2, 48, TILE)
            bias_lanes = pl.ds(pl.multiple_of((tile & 1) * TILE, TILE), TILE)
            small_acc[0, pl.ds(EXPAND_BIAS + (tile >> 1), 1), bias_lanes] = jnp.sum(
                grad_wide.astype(F32), axis=0, keepdims=True
            )
            expand_t = dot_tn(grad_wide, normed_two[...]).astype(BF16)
            at = (tile >> 2, (tile >> 1) & 1, tile & 1)
            for group in range(2):
                for side in range(2):
                    expand_part[at + (group, side)] = expand_t[
                        group * 192 : group * 192 + 192, side * LANES : side * LANES + LANES
                    ]
            for copy in core_copies(tile):
                copy.start()
            grad_normed[...] += dot_nt(grad_wide, widen[:, lanes])

        def begin(g):
            streams["w", g].send(0)
            streams["r", g].send(0)

        def through_two(number, carry):
            through(2 * number)

            @pl.when(number > 0)
            def _():
                core_add(2 * number - 1)

            for g in range(tiles // 2 - 1):

                @pl.when(number == g + 1)
                def _(g=g):
                    begin(g)

            perform_at("T", 0, 2, tiles // 2, number)
            through(2 * number + 1)
            core_add(2 * number)
            perform_at("T", 1, 2, tiles // 2, number)
            return carry

        lax.fori_loop(0, tiles // 2, through_two, 0)
        core_add(tiles - 1)
        begin(3)
        gain_sum = jnp.zeros((1, width), F32)
        for number in range(blocks):
            perform(("N", number))
            rows = pl.ds(number * BLOCK, BLOCK)
            here = pl.ds(number, 1)
            before = hidden[rows, :].astype(F32) + mod_part(number, 2) * projected[rows, :]
            centered = before - mean_of(before)
            inverse = lax.rsqrt(mean_of(centered * centered) + 1e-05)
            normal = centered * inverse
            grad = grad_normed[rows, :]
            line = normal * as_row(second_gain)
            mod_rows[here, pl.ds(3 * width, width)] = jnp.sum(grad, axis=0, keepdims=True)
            mod_rows[here, pl.ds(4 * width, width)] = jnp.sum(grad * line, axis=0, keepdims=True)
            grad_line = grad * (1.0 + mod_part(number, 4))
            gain_sum = gain_sum + jnp.sum(grad_line * normal, axis=0, keepdims=True)
            grad_normal = grad_line * as_row(second_gain)
            along = mean_of(grad_normal * normal)
            term = (grad_normal - mean_of(grad_normal) - normal * along) * inverse
            total = cotangent[rows, :].astype(F32) * keep[number] + term
            grad_middle[rows, :] = total
            grad_low[rows, :] = (mod_part(number, 2) * total).astype(BF16)
        small_acc[0, pl.ds(SECOND_GAIN, 1), :] = gain_sum
        perform(("N", blocks))

        for first in range(0, width, 256):
            grad_attended[:, pl.ds(first, 256)] = dot_nt(
                grad_low[...], out_weight[pl.ds(first, 256), :]
            ).astype(BF16)
        head_lane = row_iota((width, 128)) // 64 == lane_iota((width, 128)) // 3
        chooser = jnp.where(head_lane & (lane_iota((width, 128)) < 3 * HEADS), 1.0, 0.0).astype(BF16)
        for number in range(blocks):
            rows = pl.ds(number * BLOCK, BLOCK)
            product = grad_attended[rows, :].astype(F32) * attended[rows, :].astype(F32)
            upper = product.astype(BF16)
            lower = (product - upper.astype(F32)).astype(BF16)
            delta_features[rows, :] = split_three(dot(upper, chooser) + dot(lower, chooser))
        for load in attention_loads:
            load.wait()
        for place in range(HEADS // 2 + 2):
            swap(place).start()
        perform(("D", 0))
        value_sum = jnp.zeros((1, width), F32)
        mlp_sum = jnp.zeros((1, width), F32)
        for number in range(blocks):
            rows = pl.ds(number * BLOCK, BLOCK)
            here = pl.ds(number, 1)
            full = reduced[rows, :] + as_row(reduce_bias)
            branch = mod_part(number, 5) * full
            value = hidden[rows, :].astype(F32) + mod_part(number, 2) * projected[rows, :] + branch
            block_out[rows, :] = value.astype(BF16)
            value_sum = value_sum + jnp.sum(keep[number] * value * value, axis=0, keepdims=True)
            mlp_sum = mlp_sum + jnp.sum(keep[number] * branch * branch, axis=0, keepdims=True)
            grad_out = cotangent[rows, :].astype(F32) * keep[number]
            mod_rows[here, pl.ds(5 * width, width)] = jnp.sum(grad_out * full, axis=0, keepdims=True)
            mod_rows[here, pl.ds(2 * width, width)] = jnp.sum(
                grad_middle[rows, :] * projected[rows, :], axis=0, keepdims=True
            )
        lane = lane_iota((1, width))
        counts = jnp.zeros((1, 1), F32)
        for number in range(blocks):
            counts = counts + jnp.sum(keep[number], axis=0, keepdims=True)
        terms = [jnp.sum(term, axis=1, keepdims=True) for term in (value_sum, branch_sum, mlp_sum)] + [counts]
        stats = jnp.zeros((1, width), F32)
        for place, term in enumerate(terms):
            stats = jnp.where(lane == place, term, stats)
        small_acc[0, pl.ds(STATS, 1), :] = stats
        for part in range(2, 6):
            small_acc[0, pl.ds(MOD_BIAS + part, 1), :] = jnp.sum(
                mod_rows[:, pl.ds(part * width, width)], axis=0, keepdims=True
            )
        small_copy(0).start()
        perform(("D", 1))
        for first in range(0, width, TILE):
            output_t = dot_tn(grad_low[:, pl.ds(first, TILE)], attended[...]).astype(BF16)
            for place in range(TILE // 48):
                group = first // 48 + place
                at = (group >> 3, (group >> 2) & 1, (group >> 1) & 1, group & 1)
                for side in range(2):
                    output_part[at + (side,)] = output_t[
                        place * 48 : place * 48 + 48, side * LANES : side * LANES + LANES
                    ]
        streams["o", 0].send(0)
        perform(("D", 2))

    def small_copy(number):
        return pltpu.make_async_remote_copy(
            small_acc.at[number], small_got.at[number], small_send.at[number], small_recv.at[number],
            device_id=greet[(1 + number) % len(greet)], device_id_type=MESH_ID,
        )

    def small_step(number):
        small_copy(number).wait_recv()
        small_acc[number + 1] = small_acc[number] + small_got[number]
        if number + 1 < len(greet):
            small_copy(number + 1).start()

    def swap(place):
        if isinstance(place, int) and place < 2:
            source, target = ((delta_features, other_delta), (query_features, other_features))[place]
        else:
            lanes = pl.ds(pl.multiple_of((place - 2) * 128, 128), 128)
            source, target = grad_attended.at[:, lanes], other_grad.at[:, lanes]
        return pltpu.make_async_remote_copy(
            source, target, swap_send.at[place], swap_recv.at[place], device_id=(dp, 1 - seq), device_id_type=MESH_ID
        )

    units = tiles * TILE
    low_half, wide_half = pltpu.VMEM((tokens, width), BF16), pltpu.VMEM((tokens, width), F32)
    pl.run_scoped(
        mlp_phase,
        pltpu.VMEM((units, width), BF16), pltpu.VMEM((width, units), BF16), pltpu.VMEM((width, width), BF16),
        low_half, low_half, low_half, low_half, low_half, pltpu.VMEM((width, tokens), BF16),
        wide_half, wide_half, wide_half,
    )

    def attention_phase(normed, hidden, weight, keys_t, grad_query_t, grad_key, grad_value, grad_triple, grad_normed, triple_part, mod_zero, mod_one):
        loads = [
            pltpu.make_async_copy(source, target, load_sem.at[9 + number])
            for number, (source, target) in enumerate(((normed_hbm, normed), (hidden_hbm, hidden), (weight_hbm, weight)))
        ]
        for load in loads:
            load.start()
        for part in range(2):
            keys_t[part] = jnp.transpose(keys[part])

        def own_queries(pair, carry):
            lanes = pl.ds(pl.multiple_of(pair * 128, 128), 128)
            query_pair, grad_pair = queries[0, :, lanes], grad_attended[:, lanes]
            pair_lane = lane_iota(query_pair.shape)
            for half in range(2):
                head = pair * 2 + half
                head_rows = pl.ds(pl.multiple_of(head * 64, 64), 64)
                mine = (pair_lane < 64) == (half == 0)
                query = jnp.where(mine, query_pair, jnp.zeros_like(query_pair))
                grad = jnp.where(mine, grad_pair, jnp.zeros_like(grad_pair))
                right_scores = jnp.concatenate([query, query_features[...]], axis=1)
                right_grads = jnp.concatenate([grad, delta_features[...]], axis=1)
                head_lanes = (pair_lane >= 3 * head) & (pair_lane < 3 * head + 3)
                grad_q = jnp.zeros((64, tokens), F32)
                for part in range(2):
                    features = jnp.where(head_lanes, jnp.full_like(query_pair, -1.0), key_features[part])
                    scores = dot_nt(jnp.concatenate([keys[part, :, lanes], features], axis=1), right_scores)
                    weights = jnp.exp(scores)
                    grad_weights = dot_nt(jnp.concatenate([values[part, :, lanes], features], axis=1), right_grads)
                    grad_scores = (weights * grad_weights).astype(BF16)
                    if part == 0:
                        grad_v = dot(weights.astype(BF16), grad)
                        grad_k = dot(grad_scores, query)
                        if half == 0:
                            grad_value[:, lanes] = grad_v
                            grad_key[:, lanes] = grad_k
                        else:
                            grad_value[:, lanes] += grad_v
                            grad_key[:, lanes] += grad_k
                    grad_q = grad_q + dot(keys_t[part, head_rows, :], grad_scores)
                grad_query_t[head_rows, :] = grad_q
                perform_at("A", half, 2, HEADS // 2, pair)
            return carry

        lax.fori_loop(0, HEADS // 2, own_queries, 0)
        for load in loads:
            load.wait()
        turns = []
        grad_normed[...] = jnp.transpose(grad_query_t[...])
        for number in range(blocks):
            rows = pl.ds(number * BLOCK, BLOCK)
            before = block_place(segments, lengths, seq * blocks + number)[1]
            cosine, sine = rotary_block(table, before)
            turns.append((cosine, -sine))
            for pair in range(HEADS // 2):
                lanes = pl.ds(pair * 128, 128)
                grad_triple[rows, lanes] = (turn(grad_normed[rows, lanes], cosine, -sine) * 0.125).astype(BF16)

        def third(part):
            triple_t = dot_tn(grad_triple[:, pl.ds(part * width, width)], normed[...]).astype(BF16)
            for place in range(width // 48):
                group, piece = divmod(part * (width // 48) + place, 3)
                at = (group >> 3, (group >> 2) & 1, (group >> 1) & 1, group & 1)
                for side in range(2):
                    triple_part[at + (side, pl.ds(48 * piece, 48))] = triple_t[
                        place * 48 : place * 48 + 48, side * LANES : side * LANES + LANES
                    ]

        def triple_core(number):
            index = ((0, 0), (0, 1), (1,))[number]
            full = (slice(None),) * (3 - len(index))
            return pltpu.make_async_remote_copy(
                triple_part.at[index + full + (1 - core,)], tri_a.at[index],
                triple_send.at[number], triple_recv.at[number],
                device_id=exchange_partner(CORE, extra_bits), device_id_type=MESH_ID,
            )

        def triple_add(number):
            triple_core(number).wait_recv()
            for z1 in (number,) if number < 2 else range(2):
                for y in range(2):
                    for side in range(2):
                        got = (number // 2, z1, y)
                        triple_part[got + (core, side)] = triple_part[got + (core, side)] + tri_a[got + (side,)]

        third(0)
        triple_core(0).start()
        grad_normed[...] = dot_nt(grad_triple[:, pl.ds(0, width)], weight[:, pl.ds(0, width)])
        perform(("E", 0))
        for place in range(2):
            swap(place).wait_recv()

        def other_queries(pair, carry):
            lanes = pl.ds(pl.multiple_of(pair * 128, 128), 128)
            swap(pair + 2).wait_recv()
            query_pair, grad_pair = queries[1, :, lanes], other_grad[:, lanes]
            pair_lane = lane_iota(query_pair.shape)
            grad_k = grad_key[:, lanes]
            grad_v = grad_value[:, lanes]
            for half in range(2):
                head = pair * 2 + half
                mine = (pair_lane < 64) == (half == 0)
                query = jnp.where(mine, query_pair, jnp.zeros_like(query_pair))
                grad = jnp.where(mine, grad_pair, jnp.zeros_like(grad_pair))
                head_lanes = (pair_lane >= 3 * head) & (pair_lane < 3 * head + 3)
                features = jnp.where(head_lanes, jnp.full_like(query_pair, -1.0), key_features[0])
                scores = dot_nt(
                    jnp.concatenate([keys[0, :, lanes], features], axis=1),
                    jnp.concatenate([query, other_features[...]], axis=1),
                )
                weights = jnp.exp(scores)
                grad_weights = dot_nt(
                    jnp.concatenate([values[0, :, lanes], features], axis=1),
                    jnp.concatenate([grad, other_delta[...]], axis=1),
                )
                grad_scores = (weights * grad_weights).astype(BF16)
                grad_v = grad_v + dot(weights.astype(BF16), grad)
                grad_k = grad_k + dot(grad_scores, query)
            grad_key[:, lanes] = grad_k
            grad_value[:, lanes] = grad_v
            perform_at("B", 0, 1, HEADS // 2, pair)
            return carry

        lax.fori_loop(0, HEADS // 2, other_queries, 0)

        for number in range(blocks):
            rows = pl.ds(number * BLOCK, BLOCK)
            for pair in range(HEADS // 2):
                lanes = pl.ds(pair * 128, 128)
                grad_triple[rows, pl.ds(width + pair * 128, 128)] = turn(grad_key[rows, lanes], *turns[number]).astype(BF16)
            grad_triple[rows, pl.ds(2 * width, width)] = grad_value[rows, :].astype(BF16)
        third(1)
        triple_core(1).start()
        triple_add(0)
        third(2)
        triple_core(2).start()
        triple_add(1)
        triple = [
            Stream(
                kit, 14 + number, triple_part, 48 * number, 48, {CORE: core}, order, (tri_b, tri_c, tri_d, tri_e),
                48 * number, 432 + 48 * number,
            )
            for number, order in enumerate(TRIPLE_ORDERS)
        ]
        perform(("C", 0))
        for part in range(1, 3):
            lanes = pl.ds(part * width, width)
            grad_normed[...] += dot_nt(grad_triple[:, lanes], weight[:, lanes])
            perform(("C", part))
        triple_add(2)
        for number, stream in enumerate(triple):
            streams["q", number] = stream
            stream.send(0)

        gain_sum = jnp.zeros((1, width), F32)
        for number in range(blocks):
            rows, here = pl.ds(number * BLOCK, BLOCK), pl.ds(number, 1)
            value = hidden[rows, :].astype(F32)
            centered = value - mean_of(value)
            inverse = lax.rsqrt(mean_of(centered * centered) + 1e-05)
            normal = centered * inverse
            grad = grad_normed[rows, :]
            mod_rows[here, pl.ds(0, width)] = jnp.sum(grad, axis=0, keepdims=True)
            mod_rows[here, pl.ds(width, width)] = jnp.sum(grad * (normal * as_row(first_gain)), axis=0, keepdims=True)
            grad_line = grad * (1.0 + mod_part(number, 1))
            gain_sum = gain_sum + jnp.sum(grad_line * normal, axis=0, keepdims=True)
            grad_normal = grad_line * as_row(first_gain)
            along = mean_of(grad_normal * normal)
            term = (grad_normal - mean_of(grad_normal) - normal * along) * inverse
            input_grad[rows, :] = (grad_middle[rows, :] + term).astype(BF16)
            perform(("C", 3 + number))
        late_acc[0] = jnp.zeros_like(late_acc[0])
        late_acc[0, pl.ds(0, 1), :] = gain_sum
        for part in range(2):
            late_acc[0, pl.ds(1 + part, 1), :] = jnp.sum(mod_rows[:, pl.ds(part * width, width)], axis=0, keepdims=True)

        def late_copy(number):
            return pltpu.make_async_remote_copy(
                late_acc.at[number], late_got.at[number], late_send.at[number], late_recv.at[number],
                device_id=greet[(1 + number) % len(greet)], device_id_type=MESH_ID,
            )

        def late_step(number):
            late_copy(number).wait_recv()
            late_acc[number + 1] = late_acc[number] + late_got[number]
            if number + 1 < len(greet):
                late_copy(number + 1).start()

        late_copy(0).start()

        mod_axes = (CORE, Y, Z1, Z2, X)

        def mod_copies(number):
            mods = (mod_zero, mod_one, mod_two, mod_three, mod_four)
            conds = (cond_zero, cond_one, cond_two, cond_three, cond_four)
            if number == 0:
                pairs = ((mod_zero.at[:, :, :, 1 - core], mod_got), (cond_zero, cond_got))
            else:
                later = ((mod_two, cond_two), (mod_three, cond_three), (mod_four, cond_four), (mod_five, cond_five))[number - 1]
                chunks = pl.ds(2 ** (number - 1), 2 ** (number - 1))
                if number == 1:
                    source = mod_one.at[:, :, :, 1 - bits[Y]]
                elif number == 2:
                    source = mod_two.at[:, :, 1 - bits[Z1]]
                elif number == 3:
                    source = mod_three.at[:, 1 - bits[Z2]]
                else:
                    source = mod_four
                pairs = ((source, later[0].at[chunks]), (conds[number], later[1].at[chunks]))
            return [
                pltpu.make_async_remote_copy(
                    source, target, mod_send.at[place, number], mod_recv.at[place, number],
                    device_id=exchange_partner(mod_axes[number], extra_bits), device_id_type=MESH_ID,
                )
                for place, (source, target) in enumerate(pairs)
            ]

        def mod_step(number):
            for copy in mod_copies(number):
                copy.wait_recv()
            if number == 0:
                mod_one[0] = mod_zero[:, :, :, core]
                mod_one[0, :, :, :, pl.ds(4, 4), :] = mod_got[:, :, :, pl.ds(0, 4), :]
                cond_one[0] = cond_zero[...]
                cond_one[0, pl.ds(4, 4), :] = cond_got[pl.ds(0, 4), :]
            if number == 0:
                mod_two[0] = mod_one[0, :, :, bits[Y]]
                cond_two[0] = cond_one[0]
            elif number == 1:
                mod_three[pl.ds(0, 2)] = mod_two[:, :, bits[Z1]]
                cond_three[pl.ds(0, 2)] = cond_two[...]
            elif number == 2:
                mod_four[pl.ds(0, 4)] = mod_three[:, bits[Z2]]
                cond_four[pl.ds(0, 4)] = cond_three[...]
            elif number == 3:
                mod_five[pl.ds(0, 8)] = mod_four[...]
                cond_five[pl.ds(0, 8)] = cond_four[...]
            if number < 4:
                for copy in mod_copies(number + 1):
                    copy.start()

        mod_zero[...] = jnp.zeros_like(mod_zero)
        columns = 6 * width // 16
        for group in range(16):
            at = (group >> 3, (group >> 2) & 1, (group >> 1) & 1, group & 1)
            mod_zero[at + (pl.ds(0, blocks), pl.ds(0, columns))] = mod_rows[:, pl.ds(group * columns, columns)]
        cond_zero[...] = condition[...]
        for copy in mod_copies(0):
            copy.start()

        for is_add, name, stage in work[("F", 0)]:
            if name[0] == "m":
                mod_step(stage)
                late_step(stage)
            elif name[0] == "s":
                small_step(stage)
            elif is_add:
                streams[name].add(stage)
            else:
                streams[name].send(stage)
        chunk_rows = mod_five.shape[0] * mod_five.shape[1]
        gathered = mod_five[...].reshape(chunk_rows, LANES)
        embedded = cond_five[...].reshape(chunk_rows, 128).astype(BF16)
        upper = gathered.astype(BF16)
        lower = (gathered - upper.astype(F32)).astype(BF16)
        mod_out[...] = dot_tn(embedded, upper) + dot_tn(embedded, lower)
        for number in range(5, len(greet)):
            small_step(number)
        for number in range(5, len(greet)):
            late_step(number)
        small_out[...] = small_acc[len(greet)]
        small_out[pl.ds(FIRST_GAIN, 1), :] = late_acc[len(greet), pl.ds(0, 1), :]
        small_out[pl.ds(MOD_BIAS, 2), :] = late_acc[len(greet), pl.ds(1, 2), :]
        for stream in triple:
            stream.done()
        for number in range(3):
            triple_core(number).wait_send()
        for number in range(5):
            for copy in mod_copies(number):
                copy.wait_send()
        for number in range(len(greet)):
            small_copy(number).wait_send()
            late_copy(number).wait_send()

    pl.run_scoped(
        attention_phase,
        pltpu.VMEM((tokens, width), BF16), pltpu.VMEM((tokens, width), BF16), pltpu.VMEM((width, 3 * width), BF16),
        pltpu.VMEM((2, width, tokens), BF16), pltpu.VMEM((width, tokens), F32), pltpu.VMEM((tokens, width), F32),
        pltpu.VMEM((tokens, width), F32), pltpu.VMEM((tokens, 3 * width), BF16), pltpu.VMEM((tokens, width), F32),
        pltpu.VMEM((2, 2, 2, 2, 2, 144, LANES), BF16),
        pltpu.VMEM((2, 2, 2, 2, 8, LANES), F32), pltpu.VMEM((1, 2, 2, 2, 8, LANES), F32),
    )

    for tile in range(tiles):
        for copy in core_copies(tile):
            copy.wait_send()
    for name, stream in streams.items():
        if name[0] != "q":
            stream.done()
    for place in range(HEADS // 2 + 2):
        swap(place).wait_send()


def backward(segments, lengths, modulation, condition, table, first_gain, second_gain, expand_bias, reduce_bias, *arrays):
    tokens, width = arrays[3].shape
    all_bits = lax.axis_size("dp").bit_length() - 1
    extra_bits = all_bits - GROUP_BITS
    steps = all_bits + 1
    smem, vmem = pl.BlockSpec(memory_space=pltpu.SMEM), pl.BlockSpec(memory_space=pltpu.VMEM)
    hbm = pl.BlockSpec(memory_space=pl.ANY)
    tiles = arrays[0].shape[0] // TILE

    def rows_of(count, free, lead=()):
        return pltpu.VMEM(lead + (2,) * free + (count, LANES), BF16)

    def half(dtype):
        return pltpu.VMEM((tokens, width), dtype)

    features = pltpu.VMEM((tokens, 128), BF16)
    both = pltpu.VMEM((2, tokens, width), BF16)
    group_rows = [rows_of(count, free) for count in (48, 144) for free in (4, 3, 2, 1, 0)]
    halves = [rows_of(192, 1, (4,)), rows_of(192, 0, (4,)), rows_of(192, 0, (2,)), rows_of(192, 0)]
    halves += [rows_of(96, 2, (4,)), rows_of(96, 1, (4,)), rows_of(96, 0, (4,)), rows_of(96, 0, (2,))]
    mods = [pltpu.VMEM(shape + (8, LANES), F32) for shape in ((2, 2, 2), (2, 2, 2), (4, 2), (8,), (16,))]
    conds = [pltpu.VMEM(shape + (8, 128), F32) for shape in ((), (), (1,), (2,), (4,), (8,), (16,))]
    dma = pltpu.SemaphoreType.DMA
    return pl.pallas_call(
        functools.partial(backward_kernel, extra_bits, all_bits),
        out_shape=(
            jax.ShapeDtypeStruct((tokens, width), BF16),
            jax.ShapeDtypeStruct((tokens, width), BF16),
            jax.ShapeDtypeStruct((576, LANES), F32),
            jax.ShapeDtypeStruct((128, LANES), F32),
            jax.ShapeDtypeStruct((SMALL_ROWS, width), F32),
        ),
        in_specs=[smem] * 2 + [vmem] * 7 + [hbm] * len(arrays),
        out_specs=(vmem,) * 5,
        scratch_shapes=[rows_of(192, 5), rows_of(192, 5), rows_of(48, 5), rows_of(192, 4), rows_of(192, 4)]
        + halves
        + group_rows
        + [both, both, both, features, pltpu.VMEM((2, tokens, 128), BF16)]
        + [half(F32), half(BF16), features, half(BF16), features, features]
        + [pltpu.VMEM((tokens // BLOCK, 6 * width), F32)]
        + [pltpu.VMEM((steps + 1, SMALL_ROWS, width), F32), pltpu.VMEM((steps, SMALL_ROWS, width), F32)]
        + [pltpu.VMEM((steps + 1, 8, width), F32), pltpu.VMEM((steps, 8, width), F32)]
        + mods
        + conds
        + [dma((12,)), dma((2, tiles)), dma((2, tiles)), dma((2, tiles)), dma((17, 5)), dma((17, 5)), dma((8,)), dma((8,))]
        + [dma((steps,)), dma((steps,)), dma((steps,)), dma((steps,)), dma((2, 5)), dma((2, 5)), dma((3,)), dma((3,))],
        compiler_params=pltpu.CompilerParams(
            collective_id=2, has_side_effects=True, vmem_limit_bytes=63 << 20
        ),
    )(segments, lengths, modulation, condition, table, first_gain, second_gain, expand_bias, reduce_bias, *arrays)


def scatter_rest(block, dp_size):
    group = dp_size >> GROUP_BITS
    if group == 1:
        return block
    groups = [[first * group + place for place in range(group)] for first in range(dp_size // group)]
    return lax.psum_scatter(block, "dp", scatter_dimension=0, axis_index_groups=groups, tiled=True)


def finish_kernel(
    block_in, grad_in, sums, mod_sum, small,
    block_out, input_grad, first_gain, mod_block, mod_bias, triple_block, output_block, second_gain, expand_block,
    expand_bias, reduce_block, reduce_bias, masked_rms,
):
    width = first_gain.shape[0]
    block_out[...] = block_in[...]
    input_grad[...] = grad_in[...]
    expand_block[...] = sums[pl.ds(0, 192), :]
    for chunk in range(4):
        reduce_block[:, pl.ds(chunk * LANES, LANES)] = sums[pl.ds(192 + 48 * chunk, 48), :]
    output_block[...] = sums[pl.ds(384, 48), :]
    triple_block[...] = sums[pl.ds(432, 144), :]
    half = mod_sum.shape[0] // 2
    first_row = pl.multiple_of(lax.axis_index("seq") * half, half)
    mod_block[...] = mod_sum[pl.ds(first_row, half), pl.ds(0, mod_block.shape[1])]
    for target, first in (
        (first_gain, FIRST_GAIN), (mod_bias, MOD_BIAS), (second_gain, SECOND_GAIN), (expand_bias, EXPAND_BIAS),
        (reduce_bias, REDUCE_BIAS),
    ):
        for part in range(target.shape[0] // width):
            target[pl.ds(part * width, width)] = small[first + part, :]
    count = jnp.sum(jnp.where(lane_iota((1, width)) == 3, small[pl.ds(STATS, 1), :], 0.0))
    masked_rms[...] = jnp.sqrt(small[STATS, pl.ds(0, 128)] / (count * width))[:3]


def finish(block_out, input_grad, sums, mod_sum, small):
    width = small.shape[1]
    vmem = pl.BlockSpec(memory_space=pltpu.VMEM)
    shapes = (
        (width,), (mod_sum.shape[0] // 2, 6 * width // 16), (6 * width,), (144, LANES), (48, LANES), (width,), (192, LANES),
        (4 * width,), (48, 4 * LANES), (width,), (3,),
    )
    block_out, input_grad, *rest = pl.pallas_call(
        finish_kernel,
        out_shape=(
            jax.ShapeDtypeStruct(block_out.shape, block_out.dtype),
            jax.ShapeDtypeStruct(input_grad.shape, input_grad.dtype),
        )
        + tuple(jax.ShapeDtypeStruct(shape, F32) for shape in shapes),
        in_specs=[vmem] * 5,
        out_specs=(vmem,) * (2 + len(shapes)),
    )(block_out, input_grad, sums, mod_sum, small)
    for place in (3, 4, 6, 8):
        rest[place] = rest[place].T
    return (block_out, input_grad, *rest)


def local(
    hidden_in,
    segment_ids,
    piece_lengths,
    time_index,
    first_gain,
    modulation_weight,
    modulation_bias,
    query_key_value_weight,
    attention_output_matrix,
    second_gain,
    widen_weight,
    expand_bias,
    narrow_weight,
    reduce_bias,
    cotangent,
):
    slot_count, own_rows, width = hidden_in.shape
    hidden, cot = hidden_in[0], cotangent[0]
    table = jnp.asarray(angle_table())
    gain_one, gain_two = first_gain, second_gain
    normed, queries, keys, values, attended, query_features, key_features, modulation, condition = forward(
        segment_ids, piece_lengths, time_index, hidden, table, gain_one, modulation_weight,
        modulation_bias, query_key_value_weight,
    )
    block_out, input_grad, block_sum, mod_sum, small_sum = backward(
        segment_ids, piece_lengths, modulation, condition, table, gain_one, gain_two, expand_bias,
        reduce_bias, narrow_weight, widen_weight, attention_output_matrix, attended, cot, queries, keys, values,
        query_features, key_features, normed, hidden, query_key_value_weight,
    )
    dp_size = lax.axis_size("dp")
    if dp_size == 2**GROUP_BITS:
        block_out, input_grad, *rest = finish(block_out, input_grad, block_sum, mod_sum, small_sum)
        return (block_out[None], input_grad[None], *rest)
    expand_block = scatter_rest(block_sum[:192], dp_size).T
    reduce_block = block_sum[192:384].reshape(4, -1, LANES).transpose(1, 0, 2).reshape(-1, 4 * LANES)
    reduce_block = scatter_rest(reduce_block, dp_size).T
    output_block = scatter_rest(block_sum[384:432], dp_size).T
    triple_block = scatter_rest(block_sum[432:576], dp_size).T
    half = mod_sum.shape[0] // 2
    mod_block = lax.dynamic_slice_in_dim(mod_sum, lax.axis_index("seq") * half, half, 0)[:, : 6 * width // 16]
    mod_block = scatter_rest(mod_block.T, dp_size).T
    stats = small_sum[STATS]
    return (
        block_out[None],
        input_grad[None],
        small_sum[FIRST_GAIN],
        mod_block,
        small_sum[MOD_BIAS : MOD_BIAS + 6].reshape(-1),
        triple_block,
        output_block,
        small_sum[SECOND_GAIN],
        expand_block,
        small_sum[EXPAND_BIAS : EXPAND_BIAS + 4].reshape(-1),
        reduce_block,
        small_sum[REDUCE_BIAS],
        jnp.sqrt(stats[:3] / (stats[3] * width)),
    )


def solution(mesh):
    in_specs = (
        P("dp", "seq", None),
        P("dp", None),
        P("dp", None),
        P("dp", None),
        P(),
        P(),
        P(),
        P(),
        P(),
        P(),
        P(),
        P(),
        P(),
        P(),
        P("dp", "seq", None),
    )
    out_specs = (
        P("dp", "seq", None),
        P("dp", "seq", None),
        P(),
        P("seq", "dp"),
        P(),
        P("seq", "dp"),
        P("seq", "dp"),
        P(),
        P("seq", "dp"),
        P(),
        P("seq", "dp"),
        P(),
        P(),
    )
    return jax.shard_map(local, mesh=mesh, in_specs=in_specs, out_specs=out_specs, check_vma=False)
```

```python
import functools
import math

import jax
import jax.numpy as jnp
import numpy as np
from jax import lax
from jax.experimental import pallas as pl
from jax.experimental.pallas import tpu as pltpu
from jax.sharding import PartitionSpec as P

HEADS = 12
BLOCK = 128
MAX_SEQUENCES = 8
SEGMENT_LANE = 40
MASKED = -1000000000.0
LANES = 384
GROUP_BITS = 4
MESH_ID = pl.DeviceIdType.MESH
F32, BF16 = jnp.float32, jnp.bfloat16

ROTARY_COS, ROTARY_SIN, BLOCK_COS, BLOCK_SIN = 0, 128, 256, 264
HIGH_COS, HIGH_SIN, LOW_COS, LOW_SIN, TABLE_ROWS = 272, 304, 336, 368, 400

FIRST_GAIN, MOD_BIAS, SECOND_GAIN, EXPAND_BIAS, REDUCE_BIAS, STATS, SMALL_ROWS = 0, 1, 7, 8, 12, 13, 16


def angle_table():
    lane = np.arange(128)
    rotary = np.exp((lane % 32) * (-2.0 * math.log(10000.0) / 64))
    timing = np.exp((lane % 64) * (-math.log(10000.0) / 64))
    steps = np.arange(128)[:, None]
    angles = [
        (np.cos, steps * rotary), (np.sin, steps * rotary),
        (np.cos, steps[:8] * 128 * rotary), (np.sin, steps[:8] * 128 * rotary),
        (np.cos, steps[:32] * 32 * timing), (np.sin, steps[:32] * 32 * timing),
        (np.cos, steps[:32] * timing), (np.sin, steps[:32] * timing),
    ]
    return np.concatenate([fn(angle) for fn, angle in angles]).astype(np.float32)


def dot(left, right):
    return jnp.dot(left, right, preferred_element_type=F32)


def dot_nt(left, right):
    return lax.dot_general(left, right, (((1,), (1,)), ((), ())), preferred_element_type=F32)


def dot_tn(left, right):
    return lax.dot_general(left, right, (((0,), (0,)), ((), ())), preferred_element_type=F32)


def as_row(vector):
    return vector[...].reshape(1, -1)


def lane_iota(shape):
    return lax.broadcasted_iota(jnp.int32, shape, len(shape) - 1)


def row_iota(shape):
    return lax.broadcasted_iota(jnp.int32, shape, 0)


def block_place(segments, lengths, block):
    segment = segments[0, block * BLOCK]
    before = jnp.int32(0)
    for other in range(segments.shape[1] // BLOCK):
        same = (segments[0, other * BLOCK] == segment) & (other < block)
        before = before + jnp.where(same, 1, 0)
    return segment, before, lengths[0, segment] - before * BLOCK


def rotary_block(table, before):
    cos_row, sin_row = table[pl.ds(ROTARY_COS, 128), :], table[pl.ds(ROTARY_SIN, 128), :]
    cos_block = table[pl.ds(BLOCK_COS + before, 1), :]
    sin_block = table[pl.ds(BLOCK_SIN + before, 1), :]
    cosine = cos_row * cos_block - sin_row * sin_block
    sine = sin_row * cos_block + cos_row * sin_block
    first_half = lane_iota(sine.shape) % 64 < 32
    return cosine, jnp.where(first_half, -sine, sine)


def turn(values, cosine, sine):
    first_half = lane_iota(values.shape) % 64 < 32
    swapped = jnp.where(first_half, pltpu.roll(values, 96, 1), pltpu.roll(values, 32, 1))
    return values * cosine + swapped * sine


def mean_of(values):
    return jnp.mean(values, axis=-1, keepdims=True)


def split_three(values):
    first = values.astype(BF16)
    rest = values - first.astype(F32)
    second = rest.astype(BF16)
    third = (rest - second.astype(F32)).astype(BF16)
    place = lane_iota(values.shape) % 3
    picked = jnp.where(place == 0, first.astype(F32), jnp.where(place == 1, second.astype(F32), third.astype(F32)))
    return picked.astype(BF16)


def forward_kernel(
    segments, lengths, times, hidden, table, first_gain, mod_weight_hbm, mod_bias, weight_hbm,
    normed_hbm, queries_hbm, keys_hbm, values_hbm, attended, query_features, key_features, modulation, condition,
    mod_weight, weight, normed, queries, keys, values,
    other_hidden, turned_values, out_t, peak, total, send_sem, recv_sem, load_sem, store_sem,
):
    tokens, width = hidden.shape
    blocks = tokens // BLOCK
    seq = lax.axis_index("seq")
    partner = (lax.axis_index("dp"), 1 - seq)
    mod_load = pltpu.make_async_copy(mod_weight_hbm, mod_weight, load_sem.at[0])
    weight_load = pltpu.make_async_copy(weight_hbm, weight, load_sem.at[1])
    mod_load.start()
    weight_load.start()
    stores = []
    barrier = pltpu.get_barrier_semaphore()
    pl.semaphore_signal(barrier, inc=1, device_id=partner, device_id_type=MESH_ID)
    pl.semaphore_wait(barrier, 1)
    exchanges = [
        pltpu.make_async_remote_copy(
            hidden.at[pl.ds(place * tokens // 2, tokens // 2)], other_hidden.at[pl.ds(place * tokens // 2, tokens // 2)],
            send_sem.at[place], recv_sem.at[place], device_id=partner, device_id_type=MESH_ID,
        )
        for place in range(2)
    ]
    for exchange in exchanges:
        exchange.start()

    places = []
    for number in range(2 * blocks):
        block = (seq if number < blocks else 1 - seq) * blocks + number % blocks
        places.append(block_place(segments, lengths, block))
        time = times[0, places[number][0]]
        high, low = time // 32, time % 32
        cos_high, sin_high = table[pl.ds(HIGH_COS + high, 1), :], table[pl.ds(HIGH_SIN + high, 1), :]
        cos_low, sin_low = table[pl.ds(LOW_COS + low, 1), :], table[pl.ds(LOW_SIN + low, 1), :]
        cosine = cos_high * cos_low - sin_high * sin_low
        sine = sin_high * cos_low + cos_high * sin_low
        row = jnp.where(lane_iota(cosine.shape) < 64, cosine, sine)
        condition[pl.ds(number, 1), :] = row.astype(BF16).astype(F32)
    mod_load.wait()
    modulation[...] = dot(condition[...].astype(BF16), mod_weight[...]) + as_row(mod_bias)

    lane = lane_iota((BLOCK, 128))
    row = row_iota((BLOCK, 128))

    half_blocks = blocks // 2
    sections = ((0, 0, blocks), (1, 0, half_blocks), (1, half_blocks, half_blocks))
    for section, (part, first_block, count) in enumerate(sections):
        source = hidden if part == 0 else other_hidden
        if part == 1:
            exchanges[section - 1].wait_recv()
        section_rows = pl.ds(first_block * BLOCK, count * BLOCK)
        turns = []
        for number in range(first_block, first_block + count):
            rows = pl.ds(number * BLOCK, BLOCK)
            segment, before, valid_count = places[part * blocks + number]
            turns.append(rotary_block(table, before))
            mine = lane == SEGMENT_LANE + segment
            in_lanes = (lane >= SEGMENT_LANE) & (lane < SEGMENT_LANE + MAX_SEQUENCES)
            blocked = in_lanes & jnp.logical_not(mine & (row < valid_count))
            key_features[part, rows, :] = jnp.where(blocked, MASKED, 0.0).astype(BF16)
            if part == 0:
                query_features[rows, :] = jnp.where(mine, 1.0, 0.0).astype(BF16)
            mod_row = pl.ds(part * blocks + number, 1)
            shift, scale = modulation[mod_row, pl.ds(0, width)], modulation[mod_row, pl.ds(width, width)]
            value = source[rows, :].astype(F32)
            centered = value - mean_of(value)
            spread = mean_of(centered * centered)
            line = centered * lax.rsqrt(spread + 1e-05) * as_row(first_gain)
            result = (line * (1.0 + scale) + shift).astype(BF16)
            if part == 0:
                normed[rows, :] = result
            else:
                other_hidden[rows, :] = result
        normed_source = normed if part == 0 else other_hidden
        if section == 0:
            weight_load.wait()
            stores.append(pltpu.make_async_copy(normed, normed_hbm, store_sem.at[3, 0]))
            stores[-1].start()
        for tile in range(3 * width // LANES):
            which, first = divmod(tile * LANES, width)
            product = dot(normed_source[section_rows, :], weight[:, pl.ds(tile * LANES, LANES)])
            target = (queries, keys, values)[which]
            for place in range(count):
                cosine, sine = turns[place]
                for pair in range(LANES // 128):
                    piece = product[place * BLOCK : (place + 1) * BLOCK, pair * 128 : (pair + 1) * 128]
                    if which < 2:
                        piece = turn(piece, cosine, sine)
                    if which == 0:
                        piece = piece.astype(BF16).astype(F32) * 0.125
                    rows = pl.ds((first_block + place) * BLOCK, BLOCK)
                    target[part, rows, pl.ds(first + pair * 128, 128)] = piece.astype(BF16)
        for place, (source, target) in enumerate(((queries, queries_hbm), (keys, keys_hbm), (values, values_hbm))):
            copy = pltpu.make_async_copy(
                source.at[part, section_rows], target.at[part, section_rows], store_sem.at[place, section]
            )
            copy.start()
            stores.append(copy)
        turned_rows = pl.ds(0, count * BLOCK)
        turned_values[:, turned_rows] = jnp.transpose(values[part, section_rows, :])

        def attend(pair, carry):
            lanes = pl.ds(pl.multiple_of(pair * 128, 128), 128)
            query_pair, key_pair = queries[0, :, lanes], keys[part, section_rows, lanes]
            left = jnp.concatenate([key_pair, key_features[part, section_rows, :]], axis=1)
            pair_lane = lane_iota(query_pair.shape)
            both = []
            for half in range(2):
                query = jnp.where((pair_lane < 64) == (half == 0), query_pair, jnp.zeros_like(query_pair))
                both.append(dot_nt(left, jnp.concatenate([query, query_features[...]], axis=1)))
            for half, scores in enumerate(both):
                head = pair * 2 + half
                head_rows = pl.ds(pl.multiple_of(head * 64, 64), 64)
                one_row = pl.ds(head, 1)
                top = jnp.max(scores, axis=0, keepdims=True)
                if section > 0:
                    top = jnp.maximum(top, peak[one_row, :])
                weights = jnp.exp(scores - top)
                summed = jnp.sum(weights, axis=0, keepdims=True)
                mixed = dot(turned_values[head_rows, turned_rows], weights.astype(BF16))
                if section > 0:
                    rescale = jnp.exp(peak[one_row, :] - top)
                    summed = summed + rescale * total[one_row, :]
                    mixed = mixed + out_t[head_rows, :] * rescale
                if section < len(sections) - 1:
                    out_t[head_rows, :] = mixed
                    total[one_row, :] = summed
                    peak[one_row, :] = top
                else:
                    out_t[head_rows, :] = mixed * (1.0 / summed)
                    peak[one_row, :] = top + jnp.log(summed)
            return carry

        lax.fori_loop(0, HEADS // 2, attend, 0)

    attended[...] = jnp.transpose(out_t[...].astype(BF16))
    log_rows = jnp.concatenate(
        [jnp.broadcast_to(peak[pl.ds(head, 1), :], (3, tokens)) for head in range(HEADS)]
        + [jnp.zeros((128 - 3 * HEADS, tokens), F32)], axis=0,
    )
    query_features[...] = query_features[...] + split_three(jnp.transpose(log_rows))
    for copy in stores:
        copy.wait()
    for exchange in exchanges:
        exchange.wait_send()


def forward(segments, lengths, times, hidden, table, first_gain, mod_weight, mod_bias, weight):
    tokens, width = hidden.shape
    blocks = 2 * tokens // BLOCK
    half = jax.ShapeDtypeStruct((tokens, width), BF16)
    both = jax.ShapeDtypeStruct((2, tokens, width), BF16)
    smem, vmem = pl.BlockSpec(memory_space=pltpu.SMEM), pl.BlockSpec(memory_space=pltpu.VMEM)
    hbm = pl.BlockSpec(memory_space=pl.ANY)
    return pl.pallas_call(
        forward_kernel,
        out_shape=(
            half, both, both, both, half,
            jax.ShapeDtypeStruct((tokens, 128), BF16),
            jax.ShapeDtypeStruct((2, tokens, 128), BF16),
            jax.ShapeDtypeStruct((blocks, 6 * width), F32),
            jax.ShapeDtypeStruct((blocks, 128), F32),
        ),
        in_specs=[smem] * 3 + [vmem] * 3 + [hbm, vmem, hbm],
        out_specs=(hbm,) * 4 + (vmem,) * 5,
        scratch_shapes=[
            pltpu.VMEM(mod_weight.shape, BF16),
            pltpu.VMEM(weight.shape, BF16),
            pltpu.VMEM((tokens, width), BF16),
            pltpu.VMEM((2, tokens, width), BF16),
            pltpu.VMEM((2, tokens, width), BF16),
            pltpu.VMEM((2, tokens, width), BF16),
            pltpu.VMEM((tokens, width), BF16),
            pltpu.VMEM((width, tokens), BF16),
            pltpu.VMEM((width, tokens), F32),
            pltpu.VMEM((16, tokens), F32),
            pltpu.VMEM((16, tokens), F32),
            pltpu.SemaphoreType.DMA((2,)),
            pltpu.SemaphoreType.DMA((2,)),
            pltpu.SemaphoreType.DMA((2,)),
            pltpu.SemaphoreType.DMA((4, 3)),
        ],
        compiler_params=pltpu.CompilerParams(
            collective_id=1, has_side_effects=True, vmem_limit_bytes=56 << 20
        ),
    )(segments, lengths, times, hidden, table, first_gain, mod_weight, mod_bias, weight)


TILE = 384
Z2, Z1, Y, CORE, X = 0, 1, 2, 3, 4


WIDE_ORDERS = ((X, Y), (Y, X), (X, Y), (Y, X))
REDUCE_ORDERS = ((Z1, Z2, Y), (Z1, Y, Z2), (Y, Z1, Z2), (Z1, Y, Z2))
OUTPUT_ORDER = (CORE, Z1, Y, X, Z2)
TRIPLE_ORDERS = ((Y, X, Z1, Z2), (Z1, X, Y, Z2), (X, Y, Z1, Z2))
PLAN = (
    (("T", 6), (("r", 0), ("w", 0),)),
    (("N", 0), (("w", 1), ("r", 1),)),
    (("D", 1), (("w", 2),)),
    (("D", 2), (("r", 2),)),
    (("A", 0), (("s", 0), ("r", 0),)),
    (("A", 1), (("w", 1), ("w", 0),)),
    (("A", 2), (("o", 0),)),
    (("A", 4), (("r", 3),)),
    (("A", 5), (("w", 3),)),
    (("A", 6), (("r", 2),)),
    (("A", 8), (("r", 1), ("wm", 0),)),
    (("A", 10), (("w", 2),)),
    (("A", 11), (("s", 0),)),
    (("E", 0), (("o", 0), ("r", 0),)),
    (("B", 0), (("r", 3),)),
    (("B", 2), (("r", 2),)),
    (("B", 4), (("o", 0), ("w", 3),)),
    (("B", 5), (("s", 0), ("r", 1),)),
    (("C", 0), (("o", 0), ("r", 3),)),
    (("C", 1), (("re", 0),)),
    (("C", 2), (("wm", 1),)),
    (("C", 3), (("s", 0),)),
    (("C", 4), (("re", 1),)),
    (("C", 5), (("o", 0),)),
    (("F", 0), (("m", 0), ("we", 0), ("q", 0), ("q", 2), ("s", 0), ("m", 0), ("q", 1), ("q", 0), ("q", 2), ("m", 0), ("q", 0), ("q", 1), ("q", 2), ("q", 1), ("m", 0), ("q", 0), ("q", 2), ("q", 1), ("m", 0),)),
)


def exchange_partner(axis, extra_bits):
    dp, seq = lax.axis_index("dp"), lax.axis_index("seq")
    if axis == X:
        return (dp, 1 - seq)
    return (dp ^ (1 << (GROUP_BITS - 1 - axis + extra_bits)), seq)


def own_bit(axis, extra_bits):
    if axis == X:
        return lax.axis_index("seq")
    return (lax.axis_index("dp") >> (GROUP_BITS - 1 - axis + extra_bits)) & 1


class Stream:
    def __init__(self, kit, number, part, first, count, fixed, order, got, got_first=0, total_first=None):
        self.kit, self.number, self.part, self.first, self.count = kit, number, part, first, count
        self.fixed, self.order, self.got, self.got_first = fixed, order, got, got_first
        self.total_first = total_first

    def free(self, stage):
        return [axis for axis in range(5) if axis not in self.fixed and axis not in self.order[: stage + 1]]

    def copy(self, stage):
        bits = self.kit["bits"]
        index = [slice(None)] * 5
        for axis, value in self.fixed.items():
            index[axis] = value
        for axis in self.order[:stage]:
            index[axis] = bits[axis]
        index[self.order[stage]] = 1 - bits[self.order[stage]]
        target = (slice(None),) * len(self.free(stage)) + (pl.ds(self.got_first, self.count),)
        return pltpu.make_async_remote_copy(
            self.part.at[tuple(index) + (pl.ds(self.first, self.count),)],
            self.got[stage].at[target],
            self.kit["send"].at[self.number, stage],
            self.kit["recv"].at[self.number, stage],
            device_id=exchange_partner(self.order[stage], self.kit["extra"]),
            device_id_type=MESH_ID,
        )

    def send(self, stage):
        self.copy(stage).start()

    def add(self, stage):
        self.copy(stage).wait_recv()
        last = stage == len(self.order) - 1 and self.total_first is not None
        bits, free = self.kit["bits"], self.free(stage)
        rows, got_rows = pl.ds(self.first, self.count), pl.ds(self.got_first, self.count)

        def one(step, carry):
            index = list(bits)
            for axis, value in self.fixed.items():
                index[axis] = value
            place = []
            for order, axis in enumerate(free):
                index[axis] = (step >> (len(free) - 1 - order)) & 1
                place.append(index[axis])
            mine, theirs = self.part[tuple(index) + (rows,)], self.got[stage][tuple(place) + (got_rows,)]
            if last:
                total = mine.astype(F32) + theirs.astype(F32)
                self.kit["sums"][pl.ds(self.total_first, self.count), :] = total
            else:
                self.part[tuple(index) + (rows,)] = mine + theirs
            return carry

        if free:
            lax.fori_loop(0, 2 ** len(free), one, 0)
        else:
            one(0, 0)

    def done(self):
        for stage in range(len(self.order)):
            self.copy(stage).wait_send()


def backward_kernel(
    extra_bits, all_bits,
    segments, lengths, modulation, condition, table, first_gain, second_gain, expand_bias, reduce_bias,
    narrow_hbm, widen_hbm, out_weight_hbm, attended_hbm, cotangent_hbm, queries_hbm, keys_hbm, values_hbm,
    query_features_hbm, key_features_hbm, normed_hbm, hidden_hbm, weight_hbm,
    block_out, input_grad, sums, mod_out, small_out,
    expand_part, reduce_part, output_part,
    expand_got, reduce_got, wide_a, wide_b, wide_z, wide_last, red_a, red_b, red_c, red_last,
    out_a, out_b, out_c, out_d, out_e, tri_a, tri_b, tri_c, tri_d, tri_e,
    queries, keys, values, query_features, key_features,
    grad_middle, grad_attended, delta_features, other_grad, other_delta, other_features, mod_rows,
    small_acc, small_got, late_acc, late_got, mod_got, mod_two, mod_three, mod_four, mod_five,
    cond_zero, cond_got, cond_one, cond_two, cond_three, cond_four, cond_five,
    load_sem, tile_sem, core_send, core_recv, stream_send, stream_recv, swap_send, swap_recv,
    small_send, small_recv, late_send, late_recv, mod_send, mod_recv, triple_send, triple_recv,
):
    tokens, width = input_grad.shape
    tiles = narrow_hbm.shape[0] // TILE
    blocks = tokens // BLOCK
    seq = lax.axis_index("seq")
    dp = lax.axis_index("dp")
    bits = [own_bit(axis, extra_bits) for axis in range(5)]
    kit = {"bits": bits, "send": stream_send, "recv": stream_recv, "extra": extra_bits, "sums": sums}
    core = bits[CORE]

    def others(*axes):
        return {axis: bits[axis] for axis in range(5) if axis not in axes}

    def chosen(**values):
        return {CORE: core, **{{"z2": Z2, "z1": Z1, "x": X}[name]: value for name, value in values.items()}}

    streams = {}
    for g in range(4):
        streams["w", g] = Stream(
            kit, g, expand_part, 0, 192, chosen(z2=g >> 1, z1=g & 1), WIDE_ORDERS[g], (wide_a.at[g], wide_b.at[g])
        )
        streams["r", g] = Stream(
            kit, 4 + g, reduce_part, 96 * (g & 1), 96, chosen(x=g >> 1), REDUCE_ORDERS[g],
            (red_a.at[g], red_b.at[g], red_c.at[g]),
        )
    for v in range(2):
        streams["wm", v] = Stream(
            kit, 8 + v, expand_part, 0, 192, {**others(Z1, Z2), Z2: v}, (Z1,), (wide_z.at[v],)
        )
        streams["re", v] = Stream(
            kit, 11 + v, reduce_part, 96 * v, 96, others(X), (X,), (red_last.at[v],), total_first=192 + 96 * v
        )
    streams["we", 0] = Stream(kit, 10, expand_part, 0, 192, others(Z2), (Z2,), (wide_last,), total_first=0)
    streams["o", 0] = Stream(
        kit, 13, output_part, 0, 48, {}, OUTPUT_ORDER, (out_a, out_b, out_c, out_d, out_e), total_first=384
    )
    merges = {
        ("wm", 0): (("w", 0), ("w", 1)), ("wm", 1): (("w", 2), ("w", 3)), ("we", 0): (("wm", 0), ("wm", 1)),
        ("re", 0): (("r", 0), ("r", 2)), ("re", 1): (("r", 1), ("r", 3)),
    }
    work, stages, finished = {}, {}, set()
    for slot, names in PLAN:
        todo = work.setdefault(slot, [])
        for name in names:
            stage = stages.get(name, 0)
            stages[name] = stage + 1
            todo.append((True, name, stage))
            if name[0] in ("m", "s"):
                continue
            if stage + 1 < (len(streams[name].order) if name in streams else 4):
                todo.append((False, name, stage + 1))
                continue
            finished.add(name)
            for merged, parts in merges.items():
                if name in parts and finished.issuperset(parts):
                    todo.append((False, merged, 0))

    def perform(slot):
        for is_add, name, stage in work.get(slot, ()):
            if name[0] == "s":
                small_step(stage)
            elif is_add:
                streams[name].add(stage)
            else:
                streams[name].send(stage)

    def perform_at(letter, first, stride, count, index):
        for place in range(count):
            slot = (letter, first + stride * place)
            if work.get(slot):

                @pl.when(index == place)
                def _(slot=slot):
                    perform(slot)

    greet = [(dp, 1 - seq)] + [(dp ^ (1 << bit), seq) for bit in range(all_bits)]
    barrier = pltpu.get_barrier_semaphore()
    for partner in greet:
        pl.semaphore_signal(barrier, inc=1, device_id=partner, device_id_type=MESH_ID)

    attention_loads = [
        pltpu.make_async_copy(source, target, load_sem.at[number])
        for number, (source, target) in enumerate(
            ((queries_hbm, queries), (keys_hbm, keys), (values_hbm, values),
             (query_features_hbm, query_features), (key_features_hbm, key_features))
        )
    ]
    row = row_iota((BLOCK, 1))
    keep = []
    for number in range(blocks):
        valid_count = block_place(segments, lengths, seq * blocks + number)[2]
        keep.append(jnp.where(row < valid_count, 1.0, 0.0))

    def mod_part(number, part):
        return modulation[pl.ds(number, 1), pl.ds(part * width, width)]

    def tile_lanes(tile):
        return pl.ds(pl.multiple_of(tile * TILE, TILE), TILE)

    def core_copies(tile):
        at = (tile >> 2, (tile >> 1) & 1, tile & 1)
        rows = pl.ds(pl.multiple_of((tile & 3) * 48, 16), 48)
        everywhere = (slice(None),) * 3
        partner = exchange_partner(CORE, extra_bits)
        return (
            pltpu.make_async_remote_copy(
                expand_part.at[at + (1 - core,)], expand_got.at[at], core_send.at[0, tile], core_recv.at[0, tile],
                device_id=partner, device_id_type=MESH_ID,
            ),
            pltpu.make_async_remote_copy(
                reduce_part.at[everywhere + (1 - core, tile >> 2, rows)], reduce_got.at[everywhere + (tile >> 2, rows)],
                core_send.at[1, tile], core_recv.at[1, tile], device_id=partner, device_id_type=MESH_ID,
            ),
        )

    def core_add(tile):
        at = (tile >> 2, (tile >> 1) & 1, tile & 1)
        rows = pl.ds(pl.multiple_of((tile & 3) * 48, 16), 48)
        for copy in core_copies(tile):
            copy.wait_recv()
        for side in range(2):
            expand_part[at + (core, side)] = expand_part[at + (core, side)] + expand_got[at + (side,)]
        for z2 in range(2):
            for z1 in range(2):
                for y in range(2):
                    index, got = (z2, z1, y, core, tile >> 2, rows), (z2, z1, y, tile >> 2, rows)
                    reduce_part[index] = reduce_part[index] + reduce_got[got]

    def mlp_phase(
        narrow, widen, out_weight, attended, hidden, cotangent, normed_two, grad_low, grad_low_t,
        projected, reduced, grad_normed,
    ):
        def tile_loads(tile):
            lanes = tile_lanes(tile)
            pairs = ((widen_hbm.at[:, lanes], widen.at[:, lanes]), (narrow_hbm.at[lanes], narrow.at[lanes]))
            return [pltpu.make_async_copy(source, target, tile_sem.at[place, tile]) for place, (source, target) in enumerate(pairs)]

        loads = [
            pltpu.make_async_copy(source, target, load_sem.at[5 + number])
            for number, (source, target) in enumerate(
                ((cotangent_hbm, cotangent), (attended_hbm, attended), (out_weight_hbm, out_weight), (hidden_hbm, hidden))
            )
        ]
        for load in loads:
            load.start()
        for tile in range(tiles):
            for load in tile_loads(tile):
                load.start()
        for load in attention_loads:
            load.start()
        small_acc[0] = jnp.zeros_like(small_acc[0])
        grad_normed[...] = jnp.zeros_like(grad_normed)
        reduced[...] = jnp.zeros_like(reduced)
        loads[0].wait()
        bias_sum = jnp.zeros((1, width), F32)
        for number in range(blocks):
            rows = pl.ds(number * BLOCK, BLOCK)
            low = (mod_part(number, 5) * (cotangent[rows, :].astype(F32) * keep[number])).astype(BF16)
            grad_low[rows, :] = low
            bias_sum = bias_sum + jnp.sum(low.astype(F32), axis=0, keepdims=True)
        small_acc[0, pl.ds(REDUCE_BIAS, 1), :] = bias_sum
        grad_low_t[...] = jnp.transpose(grad_low[...])
        for load in loads[1:]:
            load.wait()
        for first in range(0, width, 256):
            lanes = pl.ds(first, 256)
            projected[:, lanes] = dot(attended[...], out_weight[:, lanes])
        branch_sum = jnp.zeros((1, width), F32)
        for number in range(blocks):
            rows = pl.ds(number * BLOCK, BLOCK)
            branch = mod_part(number, 2) * projected[rows, :]
            branch_sum = branch_sum + jnp.sum(keep[number] * branch * branch, axis=0, keepdims=True)
            value = hidden[rows, :].astype(F32) + branch
            centered = value - mean_of(value)
            inverse = lax.rsqrt(mean_of(centered * centered) + 1e-05)
            line = centered * inverse * as_row(second_gain)
            normed_two[rows, :] = (line * (1.0 + mod_part(number, 4)) + mod_part(number, 3)).astype(BF16)
        pl.semaphore_wait(barrier, len(greet))

        def through(tile):
            lanes = tile_lanes(tile)
            for load in tile_loads(tile):
                load.wait()
            u = dot(normed_two[...], widen[:, lanes]) + expand_bias[lanes].reshape(1, TILE)
            grad_active = dot_nt(grad_low[...], narrow[lanes, :])
            square = u * u
            tanh = jnp.tanh(u * (0.7978845608028654 + 0.7978845608028654 * 0.044715 * square))
            half_sum = 0.5 + 0.5 * tanh
            active = (u * half_sum).astype(BF16)
            inner = 0.7978845608028654 + 3.0 * 0.7978845608028654 * 0.044715 * square
            slope = half_sum + (0.5 * u) * (1.0 - tanh * tanh) * inner
            grad_wide = (grad_active * slope).astype(BF16)
            reduced[...] += dot(active, narrow[lanes, :])
            reduce_t = dot(grad_low_t[...], active).astype(BF16)
            rows = pl.ds(pl.multiple_of((tile & 3) * 48, 16), 48)
            reduce_part[:, :, :, :, tile >> 2, rows] = reduce_t.reshape(2, 2, 2, 2, 48, TILE)
            bias_lanes = pl.ds(pl.multiple_of((tile & 1) * TILE, TILE), TILE)
            small_acc[0, pl.ds(EXPAND_BIAS + (tile >> 1), 1), bias_lanes] = jnp.sum(
                grad_wide.astype(F32), axis=0, keepdims=True
            )
            expand_t = dot_tn(grad_wide, normed_two[...]).astype(BF16)
            at = (tile >> 2, (tile >> 1) & 1, tile & 1)
            for group in range(2):
                for side in range(2):
                    expand_part[at + (group, side)] = expand_t[
                        group * 192 : group * 192 + 192, side * LANES : side * LANES + LANES
                    ]
            for copy in core_copies(tile):
                copy.start()
            grad_normed[...] += dot_nt(grad_wide, widen[:, lanes])

        def begin(g):
            streams["w", g].send(0)
            streams["r", g].send(0)

        def through_two(number, carry):
            through(2 * number)

            @pl.when(number > 0)
            def _():
                core_add(2 * number - 1)

            for g in range(tiles // 2 - 1):

                @pl.when(number == g + 1)
                def _(g=g):
                    begin(g)

            perform_at("T", 0, 2, tiles // 2, number)
            through(2 * number + 1)
            core_add(2 * number)
            perform_at("T", 1, 2, tiles // 2, number)
            return carry

        lax.fori_loop(0, tiles // 2, through_two, 0)
        core_add(tiles - 1)
        begin(3)
        gain_sum = jnp.zeros((1, width), F32)
        for number in range(blocks):
            perform(("N", number))
            rows = pl.ds(number * BLOCK, BLOCK)
            here = pl.ds(number, 1)
            before = hidden[rows, :].astype(F32) + mod_part(number, 2) * projected[rows, :]
            centered = before - mean_of(before)
            inverse = lax.rsqrt(mean_of(centered * centered) + 1e-05)
            normal = centered * inverse
            grad = grad_normed[rows, :]
            line = normal * as_row(second_gain)
            mod_rows[here, pl.ds(3 * width, width)] = jnp.sum(grad, axis=0, keepdims=True)
            mod_rows[here, pl.ds(4 * width, width)] = jnp.sum(grad * line, axis=0, keepdims=True)
            grad_line = grad * (1.0 + mod_part(number, 4))
            gain_sum = gain_sum + jnp.sum(grad_line * normal, axis=0, keepdims=True)
            grad_normal = grad_line * as_row(second_gain)
            along = mean_of(grad_normal * normal)
            term = (grad_normal - mean_of(grad_normal) - normal * along) * inverse
            total = cotangent[rows, :].astype(F32) * keep[number] + term
            grad_middle[rows, :] = total
            grad_low[rows, :] = (mod_part(number, 2) * total).astype(BF16)
        small_acc[0, pl.ds(SECOND_GAIN, 1), :] = gain_sum
        perform(("N", blocks))

        for first in range(0, width, 256):
            grad_attended[:, pl.ds(first, 256)] = dot_nt(
                grad_low[...], out_weight[pl.ds(first, 256), :]
            ).astype(BF16)
        head_lane = row_iota((width, 128)) // 64 == lane_iota((width, 128)) // 3
        chooser = jnp.where(head_lane & (lane_iota((width, 128)) < 3 * HEADS), 1.0, 0.0).astype(BF16)
        for number in range(blocks):
            rows = pl.ds(number * BLOCK, BLOCK)
            product = grad_attended[rows, :].astype(F32) * attended[rows, :].astype(F32)
            upper = product.astype(BF16)
            lower = (product - upper.astype(F32)).astype(BF16)
            delta_features[rows, :] = split_three(dot(upper, chooser) + dot(lower, chooser))
        for load in attention_loads:
            load.wait()
        for place in range(HEADS // 2 + 2):
            swap(place).start()
        perform(("D", 0))
        value_sum = jnp.zeros((1, width), F32)
        mlp_sum = jnp.zeros((1, width), F32)
        for number in range(blocks):
            rows = pl.ds(number * BLOCK, BLOCK)
            here = pl.ds(number, 1)
            full = reduced[rows, :] + as_row(reduce_bias)
            branch = mod_part(number, 5) * full
            value = hidden[rows, :].astype(F32) + mod_part(number, 2) * projected[rows, :] + branch
            block_out[rows, :] = value.astype(BF16)
            value_sum = value_sum + jnp.sum(keep[number] * value * value, axis=0, keepdims=True)
            mlp_sum = mlp_sum + jnp.sum(keep[number] * branch * branch, axis=0, keepdims=True)
            grad_out = cotangent[rows, :].astype(F32) * keep[number]
            mod_rows[here, pl.ds(5 * width, width)] = jnp.sum(grad_out * full, axis=0, keepdims=True)
            mod_rows[here, pl.ds(2 * width, width)] = jnp.sum(
                grad_middle[rows, :] * projected[rows, :], axis=0, keepdims=True
            )
        lane = lane_iota((1, width))
        counts = jnp.zeros((1, 1), F32)
        for number in range(blocks):
            counts = counts + jnp.sum(keep[number], axis=0, keepdims=True)
        terms = [jnp.sum(term, axis=1, keepdims=True) for term in (value_sum, branch_sum, mlp_sum)] + [counts]
        stats = jnp.zeros((1, width), F32)
        for place, term in enumerate(terms):
            stats = jnp.where(lane == place, term, stats)
        small_acc[0, pl.ds(STATS, 1), :] = stats
        for part in range(2, 6):
            small_acc[0, pl.ds(MOD_BIAS + part, 1), :] = jnp.sum(
                mod_rows[:, pl.ds(part * width, width)], axis=0, keepdims=True
            )
        small_copy(0).start()
        perform(("D", 1))
        for first in range(0, width, TILE):
            output_t = dot_tn(grad_low[:, pl.ds(first, TILE)], attended[...]).astype(BF16)
            for place in range(TILE // 48):
                group = first // 48 + place
                at = (group >> 3, (group >> 2) & 1, (group >> 1) & 1, group & 1)
                for side in range(2):
                    output_part[at + (side,)] = output_t[
                        place * 48 : place * 48 + 48, side * LANES : side * LANES + LANES
                    ]
        streams["o", 0].send(0)
        perform(("D", 2))

    def small_copy(number):
        return pltpu.make_async_remote_copy(
            small_acc.at[number], small_got.at[number], small_send.at[number], small_recv.at[number],
            device_id=greet[(1 + number) % len(greet)], device_id_type=MESH_ID,
        )

    def small_step(number):
        small_copy(number).wait_recv()
        small_acc[number + 1] = small_acc[number] + small_got[number]
        if number + 1 < len(greet):
            small_copy(number + 1).start()

    def swap(place):
        if isinstance(place, int) and place < 2:
            source, target = ((delta_features, other_delta), (query_features, other_features))[place]
        else:
            lanes = pl.ds(pl.multiple_of((place - 2) * 128, 128), 128)
            source, target = grad_attended.at[:, lanes], other_grad.at[:, lanes]
        return pltpu.make_async_remote_copy(
            source, target, swap_send.at[place], swap_recv.at[place], device_id=(dp, 1 - seq), device_id_type=MESH_ID
        )

    units = tiles * TILE
    low_half, wide_half = pltpu.VMEM((tokens, width), BF16), pltpu.VMEM((tokens, width), F32)
    pl.run_scoped(
        mlp_phase,
        pltpu.VMEM((units, width), BF16), pltpu.VMEM((width, units), BF16), pltpu.VMEM((width, width), BF16),
        low_half, low_half, low_half, low_half, low_half, pltpu.VMEM((width, tokens), BF16),
        wide_half, wide_half, wide_half,
    )

    def attention_phase(normed, hidden, weight, keys_t, grad_query_t, grad_key, grad_value, grad_triple, grad_normed, triple_part, mod_zero, mod_one):
        loads = [
            pltpu.make_async_copy(source, target, load_sem.at[9 + number])
            for number, (source, target) in enumerate(((normed_hbm, normed), (hidden_hbm, hidden), (weight_hbm, weight)))
        ]
        for load in loads:
            load.start()
        for part in range(2):
            keys_t[part] = jnp.transpose(keys[part])

        def own_queries(pair, carry):
            lanes = pl.ds(pl.multiple_of(pair * 128, 128), 128)
            query_pair, grad_pair = queries[0, :, lanes], grad_attended[:, lanes]
            pair_lane = lane_iota(query_pair.shape)
            for half in range(2):
                head = pair * 2 + half
                head_rows = pl.ds(pl.multiple_of(head * 64, 64), 64)
                mine = (pair_lane < 64) == (half == 0)
                query = jnp.where(mine, query_pair, jnp.zeros_like(query_pair))
                grad = jnp.where(mine, grad_pair, jnp.zeros_like(grad_pair))
                right_scores = jnp.concatenate([query, query_features[...]], axis=1)
                right_grads = jnp.concatenate([grad, delta_features[...]], axis=1)
                head_lanes = (pair_lane >= 3 * head) & (pair_lane < 3 * head + 3)
                grad_q = jnp.zeros((64, tokens), F32)
                for part in range(2):
                    features = jnp.where(head_lanes, jnp.full_like(query_pair, -1.0), key_features[part])
                    scores = dot_nt(jnp.concatenate([keys[part, :, lanes], features], axis=1), right_scores)
                    weights = jnp.exp(scores)
                    grad_weights = dot_nt(jnp.concatenate([values[part, :, lanes], features], axis=1), right_grads)
                    grad_scores = (weights * grad_weights).astype(BF16)
                    if part == 0:
                        grad_v = dot(weights.astype(BF16), grad)
                        grad_k = dot(grad_scores, query)
                        if half == 0:
                            grad_value[:, lanes] = grad_v
                            grad_key[:, lanes] = grad_k
                        else:
                            grad_value[:, lanes] += grad_v
                            grad_key[:, lanes] += grad_k
                    grad_q = grad_q + dot(keys_t[part, head_rows, :], grad_scores)
                grad_query_t[head_rows, :] = grad_q
                perform_at("A", half, 2, HEADS // 2, pair)
            return carry

        lax.fori_loop(0, HEADS // 2, own_queries, 0)
        for load in loads:
            load.wait()
        turns = []
        grad_normed[...] = jnp.transpose(grad_query_t[...])
        for number in range(blocks):
            rows = pl.ds(number * BLOCK, BLOCK)
            before = block_place(segments, lengths, seq * blocks + number)[1]
            cosine, sine = rotary_block(table, before)
            turns.append((cosine, -sine))
            for pair in range(HEADS // 2):
                lanes = pl.ds(pair * 128, 128)
                grad_triple[rows, lanes] = (turn(grad_normed[rows, lanes], cosine, -sine) * 0.125).astype(BF16)

        def third(part):
            triple_t = dot_tn(grad_triple[:, pl.ds(part * width, width)], normed[...]).astype(BF16)
            for place in range(width // 48):
                group, piece = divmod(part * (width // 48) + place, 3)
                at = (group >> 3, (group >> 2) & 1, (group >> 1) & 1, group & 1)
                for side in range(2):
                    triple_part[at + (side, pl.ds(48 * piece, 48))] = triple_t[
                        place * 48 : place * 48 + 48, side * LANES : side * LANES + LANES
                    ]

        def triple_core(number):
            index = ((0, 0), (0, 1), (1,))[number]
            full = (slice(None),) * (3 - len(index))
            return pltpu.make_async_remote_copy(
                triple_part.at[index + full + (1 - core,)], tri_a.at[index],
                triple_send.at[number], triple_recv.at[number],
                device_id=exchange_partner(CORE, extra_bits), device_id_type=MESH_ID,
            )

        def triple_add(number):
            triple_core(number).wait_recv()
            for z1 in (number,) if number < 2 else range(2):
                for y in range(2):
                    for side in range(2):
                        got = (number // 2, z1, y)
                        triple_part[got + (core, side)] = triple_part[got + (core, side)] + tri_a[got + (side,)]

        third(0)
        triple_core(0).start()
        grad_normed[...] = dot_nt(grad_triple[:, pl.ds(0, width)], weight[:, pl.ds(0, width)])
        perform(("E", 0))
        for place in range(2):
            swap(place).wait_recv()

        def other_queries(pair, carry):
            lanes = pl.ds(pl.multiple_of(pair * 128, 128), 128)
            swap(pair + 2).wait_recv()
            query_pair, grad_pair = queries[1, :, lanes], other_grad[:, lanes]
            pair_lane = lane_iota(query_pair.shape)
            grad_k = grad_key[:, lanes]
            grad_v = grad_value[:, lanes]
            for half in range(2):
                head = pair * 2 + half
                mine = (pair_lane < 64) == (half == 0)
                query = jnp.where(mine, query_pair, jnp.zeros_like(query_pair))
                grad = jnp.where(mine, grad_pair, jnp.zeros_like(grad_pair))
                head_lanes = (pair_lane >= 3 * head) & (pair_lane < 3 * head + 3)
                features = jnp.where(head_lanes, jnp.full_like(query_pair, -1.0), key_features[0])
                scores = dot_nt(
                    jnp.concatenate([keys[0, :, lanes], features], axis=1),
                    jnp.concatenate([query, other_features[...]], axis=1),
                )
                weights = jnp.exp(scores)
                grad_weights = dot_nt(
                    jnp.concatenate([values[0, :, lanes], features], axis=1),
                    jnp.concatenate([grad, other_delta[...]], axis=1),
                )
                grad_scores = (weights * grad_weights).astype(BF16)
                grad_v = grad_v + dot(weights.astype(BF16), grad)
                grad_k = grad_k + dot(grad_scores, query)
            grad_key[:, lanes] = grad_k
            grad_value[:, lanes] = grad_v
            perform_at("B", 0, 1, HEADS // 2, pair)
            return carry

        lax.fori_loop(0, HEADS // 2, other_queries, 0)

        for number in range(blocks):
            rows = pl.ds(number * BLOCK, BLOCK)
            for pair in range(HEADS // 2):
                lanes = pl.ds(pair * 128, 128)
                grad_triple[rows, pl.ds(width + pair * 128, 128)] = turn(grad_key[rows, lanes], *turns[number]).astype(BF16)
            grad_triple[rows, pl.ds(2 * width, width)] = grad_value[rows, :].astype(BF16)
        third(1)
        triple_core(1).start()
        triple_add(0)
        third(2)
        triple_core(2).start()
        triple_add(1)
        triple = [
            Stream(
                kit, 14 + number, triple_part, 48 * number, 48, {CORE: core}, order, (tri_b, tri_c, tri_d, tri_e),
                48 * number, 432 + 48 * number,
            )
            for number, order in enumerate(TRIPLE_ORDERS)
        ]
        perform(("C", 0))
        for part in range(1, 3):
            lanes = pl.ds(part * width, width)
            grad_normed[...] += dot_nt(grad_triple[:, lanes], weight[:, lanes])
            perform(("C", part))
        triple_add(2)
        for number, stream in enumerate(triple):
            streams["q", number] = stream
            stream.send(0)

        gain_sum = jnp.zeros((1, width), F32)
        for number in range(blocks):
            rows, here = pl.ds(number * BLOCK, BLOCK), pl.ds(number, 1)
            value = hidden[rows, :].astype(F32)
            centered = value - mean_of(value)
            inverse = lax.rsqrt(mean_of(centered * centered) + 1e-05)
            normal = centered * inverse
            grad = grad_normed[rows, :]
            mod_rows[here, pl.ds(0, width)] = jnp.sum(grad, axis=0, keepdims=True)
            mod_rows[here, pl.ds(width, width)] = jnp.sum(grad * (normal * as_row(first_gain)), axis=0, keepdims=True)
            grad_line = grad * (1.0 + mod_part(number, 1))
            gain_sum = gain_sum + jnp.sum(grad_line * normal, axis=0, keepdims=True)
            grad_normal = grad_line * as_row(first_gain)
            along = mean_of(grad_normal * normal)
            term = (grad_normal - mean_of(grad_normal) - normal * along) * inverse
            input_grad[rows, :] = (grad_middle[rows, :] + term).astype(BF16)
            perform(("C", 3 + number))
        late_acc[0] = jnp.zeros_like(late_acc[0])
        late_acc[0, pl.ds(0, 1), :] = gain_sum
        for part in range(2):
            late_acc[0, pl.ds(1 + part, 1), :] = jnp.sum(mod_rows[:, pl.ds(part * width, width)], axis=0, keepdims=True)

        def late_copy(number):
            return pltpu.make_async_remote_copy(
                late_acc.at[number], late_got.at[number], late_send.at[number], late_recv.at[number],
                device_id=greet[(1 + number) % len(greet)], device_id_type=MESH_ID,
            )

        def late_step(number):
            late_copy(number).wait_recv()
            late_acc[number + 1] = late_acc[number] + late_got[number]
            if number + 1 < len(greet):
                late_copy(number + 1).start()

        late_copy(0).start()

        mod_axes = (CORE, Y, Z1, Z2, X)

        def mod_copies(number):
            mods = (mod_zero, mod_one, mod_two, mod_three, mod_four)
            conds = (cond_zero, cond_one, cond_two, cond_three, cond_four)
            if number == 0:
                pairs = ((mod_zero.at[:, :, :, 1 - core], mod_got), (cond_zero, cond_got))
            else:
                later = ((mod_two, cond_two), (mod_three, cond_three), (mod_four, cond_four), (mod_five, cond_five))[number - 1]
                chunks = pl.ds(2 ** (number - 1), 2 ** (number - 1))
                if number == 1:
                    source = mod_one.at[:, :, :, 1 - bits[Y]]
                elif number == 2:
                    source = mod_two.at[:, :, 1 - bits[Z1]]
                elif number == 3:
                    source = mod_three.at[:, 1 - bits[Z2]]
                else:
                    source = mod_four
                pairs = ((source, later[0].at[chunks]), (conds[number], later[1].at[chunks]))
            return [
                pltpu.make_async_remote_copy(
                    source, target, mod_send.at[place, number], mod_recv.at[place, number],
                    device_id=exchange_partner(mod_axes[number], extra_bits), device_id_type=MESH_ID,
                )
                for place, (source, target) in enumerate(pairs)
            ]

        def mod_step(number):
            for copy in mod_copies(number):
                copy.wait_recv()
            if number == 0:
                mod_one[0] = mod_zero[:, :, :, core]
                mod_one[0, :, :, :, pl.ds(4, 4), :] = mod_got[:, :, :, pl.ds(0, 4), :]
                cond_one[0] = cond_zero[...]
                cond_one[0, pl.ds(4, 4), :] = cond_got[pl.ds(0, 4), :]
            if number == 0:
                mod_two[0] = mod_one[0, :, :, bits[Y]]
                cond_two[0] = cond_one[0]
            elif number == 1:
                mod_three[pl.ds(0, 2)] = mod_two[:, :, bits[Z1]]
                cond_three[pl.ds(0, 2)] = cond_two[...]
            elif number == 2:
                mod_four[pl.ds(0, 4)] = mod_three[:, bits[Z2]]
                cond_four[pl.ds(0, 4)] = cond_three[...]
            elif number == 3:
                mod_five[pl.ds(0, 8)] = mod_four[...]
                cond_five[pl.ds(0, 8)] = cond_four[...]
            if number < 4:
                for copy in mod_copies(number + 1):
                    copy.start()

        mod_zero[...] = jnp.zeros_like(mod_zero)
        columns = 6 * width // 16
        for group in range(16):
            at = (group >> 3, (group >> 2) & 1, (group >> 1) & 1, group & 1)
            mod_zero[at + (pl.ds(0, blocks), pl.ds(0, columns))] = mod_rows[:, pl.ds(group * columns, columns)]
        cond_zero[...] = condition[...]
        for copy in mod_copies(0):
            copy.start()

        for is_add, name, stage in work[("F", 0)]:
            if name[0] == "m":
                mod_step(stage)
                late_step(stage)
            elif name[0] == "s":
                small_step(stage)
            elif is_add:
                streams[name].add(stage)
            else:
                streams[name].send(stage)
        chunk_rows = mod_five.shape[0] * mod_five.shape[1]
        gathered = mod_five[...].reshape(chunk_rows, LANES)
        embedded = cond_five[...].reshape(chunk_rows, 128).astype(BF16)
        upper = gathered.astype(BF16)
        lower = (gathered - upper.astype(F32)).astype(BF16)
        mod_out[...] = dot_tn(embedded, upper) + dot_tn(embedded, lower)
        for number in range(5, len(greet)):
            small_step(number)
        for number in range(5, len(greet)):
            late_step(number)
        small_out[...] = small_acc[len(greet)]
        small_out[pl.ds(FIRST_GAIN, 1), :] = late_acc[len(greet), pl.ds(0, 1), :]
        small_out[pl.ds(MOD_BIAS, 2), :] = late_acc[len(greet), pl.ds(1, 2), :]
        for stream in triple:
            stream.done()
        for number in range(3):
            triple_core(number).wait_send()
        for number in range(5):
            for copy in mod_copies(number):
                copy.wait_send()
        for number in range(len(greet)):
            small_copy(number).wait_send()
            late_copy(number).wait_send()

    pl.run_scoped(
        attention_phase,
        pltpu.VMEM((tokens, width), BF16), pltpu.VMEM((tokens, width), BF16), pltpu.VMEM((width, 3 * width), BF16),
        pltpu.VMEM((2, width, tokens), BF16), pltpu.VMEM((width, tokens), F32), pltpu.VMEM((tokens, width), F32),
        pltpu.VMEM((tokens, width), F32), pltpu.VMEM((tokens, 3 * width), BF16), pltpu.VMEM((tokens, width), F32),
        pltpu.VMEM((2, 2, 2, 2, 2, 144, LANES), BF16),
        pltpu.VMEM((2, 2, 2, 2, 8, LANES), F32), pltpu.VMEM((1, 2, 2, 2, 8, LANES), F32),
    )

    for tile in range(tiles):
        for copy in core_copies(tile):
            copy.wait_send()
    for name, stream in streams.items():
        if name[0] != "q":
            stream.done()
    for place in range(HEADS // 2 + 2):
        swap(place).wait_send()


def backward(segments, lengths, modulation, condition, table, first_gain, second_gain, expand_bias, reduce_bias, *arrays):
    tokens, width = arrays[3].shape
    all_bits = lax.axis_size("dp").bit_length() - 1
    extra_bits = all_bits - GROUP_BITS
    steps = all_bits + 1
    smem, vmem = pl.BlockSpec(memory_space=pltpu.SMEM), pl.BlockSpec(memory_space=pltpu.VMEM)
    hbm = pl.BlockSpec(memory_space=pl.ANY)
    tiles = arrays[0].shape[0] // TILE

    def rows_of(count, free, lead=()):
        return pltpu.VMEM(lead + (2,) * free + (count, LANES), BF16)

    def half(dtype):
        return pltpu.VMEM((tokens, width), dtype)

    features = pltpu.VMEM((tokens, 128), BF16)
    both = pltpu.VMEM((2, tokens, width), BF16)
    group_rows = [rows_of(count, free) for count in (48, 144) for free in (4, 3, 2, 1, 0)]
    halves = [rows_of(192, 1, (4,)), rows_of(192, 0, (4,)), rows_of(192, 0, (2,)), rows_of(192, 0)]
    halves += [rows_of(96, 2, (4,)), rows_of(96, 1, (4,)), rows_of(96, 0, (4,)), rows_of(96, 0, (2,))]
    mods = [pltpu.VMEM(shape + (8, LANES), F32) for shape in ((2, 2, 2), (2, 2, 2), (4, 2), (8,), (16,))]
    conds = [pltpu.VMEM(shape + (8, 128), F32) for shape in ((), (), (1,), (2,), (4,), (8,), (16,))]
    dma = pltpu.SemaphoreType.DMA
    return pl.pallas_call(
        functools.partial(backward_kernel, extra_bits, all_bits),
        out_shape=(
            jax.ShapeDtypeStruct((tokens, width), BF16),
            jax.ShapeDtypeStruct((tokens, width), BF16),
            jax.ShapeDtypeStruct((576, LANES), F32),
            jax.ShapeDtypeStruct((128, LANES), F32),
            jax.ShapeDtypeStruct((SMALL_ROWS, width), F32),
        ),
        in_specs=[smem] * 2 + [vmem] * 7 + [hbm] * len(arrays),
        out_specs=(vmem,) * 5,
        scratch_shapes=[rows_of(192, 5), rows_of(192, 5), rows_of(48, 5), rows_of(192, 4), rows_of(192, 4)]
        + halves
        + group_rows
        + [both, both, both, features, pltpu.VMEM((2, tokens, 128), BF16)]
        + [half(F32), half(BF16), features, half(BF16), features, features]
        + [pltpu.VMEM((tokens // BLOCK, 6 * width), F32)]
        + [pltpu.VMEM((steps + 1, SMALL_ROWS, width), F32), pltpu.VMEM((steps, SMALL_ROWS, width), F32)]
        + [pltpu.VMEM((steps + 1, 8, width), F32), pltpu.VMEM((steps, 8, width), F32)]
        + mods
        + conds
        + [dma((12,)), dma((2, tiles)), dma((2, tiles)), dma((2, tiles)), dma((17, 5)), dma((17, 5)), dma((8,)), dma((8,))]
        + [dma((steps,)), dma((steps,)), dma((steps,)), dma((steps,)), dma((2, 5)), dma((2, 5)), dma((3,)), dma((3,))],
        compiler_params=pltpu.CompilerParams(
            collective_id=2, has_side_effects=True, vmem_limit_bytes=63 << 20
        ),
    )(segments, lengths, modulation, condition, table, first_gain, second_gain, expand_bias, reduce_bias, *arrays)


def scatter_rest(block, dp_size):
    group = dp_size >> GROUP_BITS
    if group == 1:
        return block
    groups = [[first * group + place for place in range(group)] for first in range(dp_size // group)]
    return lax.psum_scatter(block, "dp", scatter_dimension=0, axis_index_groups=groups, tiled=True)


def finish_kernel(
    block_in, grad_in, sums, mod_sum, small,
    block_out, input_grad, first_gain, mod_block, mod_bias, triple_block, output_block, second_gain, expand_block,
    expand_bias, reduce_block, reduce_bias, masked_rms,
):
    width = first_gain.shape[0]
    block_out[...] = block_in[...]
    input_grad[...] = grad_in[...]
    expand_block[...] = sums[pl.ds(0, 192), :]
    for chunk in range(4):
        reduce_block[:, pl.ds(chunk * LANES, LANES)] = sums[pl.ds(192 + 48 * chunk, 48), :]
    output_block[...] = sums[pl.ds(384, 48), :]
    triple_block[...] = sums[pl.ds(432, 144), :]
    half = mod_sum.shape[0] // 2
    first_row = pl.multiple_of(lax.axis_index("seq") * half, half)
    mod_block[...] = mod_sum[pl.ds(first_row, half), pl.ds(0, mod_block.shape[1])]
    for target, first in (
        (first_gain, FIRST_GAIN), (mod_bias, MOD_BIAS), (second_gain, SECOND_GAIN), (expand_bias, EXPAND_BIAS),
        (reduce_bias, REDUCE_BIAS),
    ):
        for part in range(target.shape[0] // width):
            target[pl.ds(part * width, width)] = small[first + part, :]
    count = jnp.sum(jnp.where(lane_iota((1, width)) == 3, small[pl.ds(STATS, 1), :], 0.0))
    masked_rms[...] = jnp.sqrt(small[STATS, pl.ds(0, 128)] / (count * width))[:3]


def finish(block_out, input_grad, sums, mod_sum, small):
    width = small.shape[1]
    vmem = pl.BlockSpec(memory_space=pltpu.VMEM)
    shapes = (
        (width,), (mod_sum.shape[0] // 2, 6 * width // 16), (6 * width,), (144, LANES), (48, LANES), (width,), (192, LANES),
        (4 * width,), (48, 4 * LANES), (width,), (3,),
    )
    block_out, input_grad, *rest = pl.pallas_call(
        finish_kernel,
        out_shape=(
            jax.ShapeDtypeStruct(block_out.shape, block_out.dtype),
            jax.ShapeDtypeStruct(input_grad.shape, input_grad.dtype),
        )
        + tuple(jax.ShapeDtypeStruct(shape, F32) for shape in shapes),
        in_specs=[vmem] * 5,
        out_specs=(vmem,) * (2 + len(shapes)),
    )(block_out, input_grad, sums, mod_sum, small)
    for place in (3, 4, 6, 8):
        rest[place] = rest[place].T
    return (block_out, input_grad, *rest)


def local(
    hidden_in,
    segment_ids,
    piece_lengths,
    time_index,
    first_gain,
    modulation_weight,
    modulation_bias,
    query_key_value_weight,
    attention_output_matrix,
    second_gain,
    widen_weight,
    expand_bias,
    narrow_weight,
    reduce_bias,
    cotangent,
):
    slot_count, own_rows, width = hidden_in.shape
    hidden, cot = hidden_in[0], cotangent[0]
    table = jnp.asarray(angle_table())
    gain_one, gain_two = first_gain, second_gain
    normed, queries, keys, values, attended, query_features, key_features, modulation, condition = forward(
        segment_ids, piece_lengths, time_index, hidden, table, gain_one, modulation_weight,
        modulation_bias, query_key_value_weight,
    )
    block_out, input_grad, block_sum, mod_sum, small_sum = backward(
        segment_ids, piece_lengths, modulation, condition, table, gain_one, gain_two, expand_bias,
        reduce_bias, narrow_weight, widen_weight, attention_output_matrix, attended, cot, queries, keys, values,
        query_features, key_features, normed, hidden, query_key_value_weight,
    )
    dp_size = lax.axis_size("dp")
    if dp_size == 2**GROUP_BITS:
        block_out, input_grad, *rest = finish(block_out, input_grad, block_sum, mod_sum, small_sum)
        return (block_out[None], input_grad[None], *rest)
    expand_block = scatter_rest(block_sum[:192], dp_size).T
    reduce_block = block_sum[192:384].reshape(4, -1, LANES).transpose(1, 0, 2).reshape(-1, 4 * LANES)
    reduce_block = scatter_rest(reduce_block, dp_size).T
    output_block = scatter_rest(block_sum[384:432], dp_size).T
    triple_block = scatter_rest(block_sum[432:576], dp_size).T
    half = mod_sum.shape[0] // 2
    mod_block = lax.dynamic_slice_in_dim(mod_sum, lax.axis_index("seq") * half, half, 0)[:, : 6 * width // 16]
    mod_block = scatter_rest(mod_block.T, dp_size).T
    stats = small_sum[STATS]
    return (
        block_out[None],
        input_grad[None],
        small_sum[FIRST_GAIN],
        mod_block,
        small_sum[MOD_BIAS : MOD_BIAS + 6].reshape(-1),
        triple_block,
        output_block,
        small_sum[SECOND_GAIN],
        expand_block,
        small_sum[EXPAND_BIAS : EXPAND_BIAS + 4].reshape(-1),
        reduce_block,
        small_sum[REDUCE_BIAS],
        jnp.sqrt(stats[:3] / (stats[3] * width)),
    )


def solution(mesh):
    in_specs = (
        P("dp", "seq", None),
        P("dp", None),
        P("dp", None),
        P("dp", None),
        P(),
        P(),
        P(),
        P(),
        P(),
        P(),
        P(),
        P(),
        P(),
        P(),
        P("dp", "seq", None),
    )
    out_specs = (
        P("dp", "seq", None),
        P("dp", "seq", None),
        P(),
        P("seq", "dp"),
        P(),
        P("seq", "dp"),
        P("seq", "dp"),
        P(),
        P("seq", "dp"),
        P(),
        P("seq", "dp"),
        P(),
        P(),
    )
    return jax.shard_map(local, mesh=mesh, in_specs=in_specs, out_specs=out_specs, check_vma=False)
```

```python
import functools
import math

import jax
import jax.numpy as jnp
import numpy as np
from jax import lax
from jax.experimental import pallas as pl
from jax.experimental.pallas import tpu as pltpu
from jax.sharding import PartitionSpec as P

HEADS = 12
BLOCK = 128
MAX_SEQUENCES = 8
SEGMENT_LANE = 40
MASKED = -1000000000.0
LANES = 384
GROUP_BITS = 4
MESH_ID = pl.DeviceIdType.MESH
F32, BF16 = jnp.float32, jnp.bfloat16

ROTARY_COS, ROTARY_SIN, BLOCK_COS, BLOCK_SIN = 0, 128, 256, 264
HIGH_COS, HIGH_SIN, LOW_COS, LOW_SIN, TABLE_ROWS = 272, 304, 336, 368, 400

FIRST_GAIN, MOD_BIAS, SECOND_GAIN, EXPAND_BIAS, REDUCE_BIAS, STATS, SMALL_ROWS = 0, 1, 7, 8, 12, 13, 16


def angle_table():
    lane = np.arange(128)
    rotary = np.exp((lane % 32) * (-2.0 * math.log(10000.0) / 64))
    timing = np.exp((lane % 64) * (-math.log(10000.0) / 64))
    steps = np.arange(128)[:, None]
    angles = [
        (np.cos, steps * rotary), (np.sin, steps * rotary),
        (np.cos, steps[:8] * 128 * rotary), (np.sin, steps[:8] * 128 * rotary),
        (np.cos, steps[:32] * 32 * timing), (np.sin, steps[:32] * 32 * timing),
        (np.cos, steps[:32] * timing), (np.sin, steps[:32] * timing),
    ]
    return np.concatenate([fn(angle) for fn, angle in angles]).astype(np.float32)


def dot(left, right):
    return jnp.dot(left, right, preferred_element_type=F32)


def dot_nt(left, right):
    return lax.dot_general(left, right, (((1,), (1,)), ((), ())), preferred_element_type=F32)


def dot_tn(left, right):
    return lax.dot_general(left, right, (((0,), (0,)), ((), ())), preferred_element_type=F32)


def as_row(vector):
    return vector[...].reshape(1, -1)


def lane_iota(shape):
    return lax.broadcasted_iota(jnp.int32, shape, len(shape) - 1)


def row_iota(shape):
    return lax.broadcasted_iota(jnp.int32, shape, 0)


def block_place(segments, lengths, block):
    segment = segments[0, block * BLOCK]
    before = jnp.int32(0)
    for other in range(segments.shape[1] // BLOCK):
        same = (segments[0, other * BLOCK] == segment) & (other < block)
        before = before + jnp.where(same, 1, 0)
    return segment, before, lengths[0, segment] - before * BLOCK


def rotary_block(table, before):
    cos_row, sin_row = table[pl.ds(ROTARY_COS, 128), :], table[pl.ds(ROTARY_SIN, 128), :]
    cos_block = table[pl.ds(BLOCK_COS + before, 1), :]
    sin_block = table[pl.ds(BLOCK_SIN + before, 1), :]
    cosine = cos_row * cos_block - sin_row * sin_block
    sine = sin_row * cos_block + cos_row * sin_block
    first_half = lane_iota(sine.shape) % 64 < 32
    return cosine, jnp.where(first_half, -sine, sine)


def turn(values, cosine, sine):
    first_half = lane_iota(values.shape) % 64 < 32
    swapped = jnp.where(first_half, pltpu.roll(values, 96, 1), pltpu.roll(values, 32, 1))
    return values * cosine + swapped * sine


def mean_of(values):
    return jnp.mean(values, axis=-1, keepdims=True)


def split_three(values):
    first = values.astype(BF16)
    rest = values - first.astype(F32)
    second = rest.astype(BF16)
    third = (rest - second.astype(F32)).astype(BF16)
    place = lane_iota(values.shape) % 3
    picked = jnp.where(place == 0, first.astype(F32), jnp.where(place == 1, second.astype(F32), third.astype(F32)))
    return picked.astype(BF16)


def forward_kernel(
    segments, lengths, times, hidden, table, first_gain, mod_weight_hbm, mod_bias, weight_hbm,
    normed_hbm, queries_hbm, keys_hbm, values_hbm, attended, query_features, key_features, modulation, condition,
    mod_weight, weight, normed, queries, keys, values,
    other_hidden, turned_values, out_t, peak, total, send_sem, recv_sem, load_sem, store_sem,
):
    tokens, width = hidden.shape
    blocks = tokens // BLOCK
    seq = lax.axis_index("seq")
    partner = (lax.axis_index("dp"), 1 - seq)
    mod_load = pltpu.make_async_copy(mod_weight_hbm, mod_weight, load_sem.at[0])
    weight_load = pltpu.make_async_copy(weight_hbm, weight, load_sem.at[1])
    mod_load.start()
    weight_load.start()
    stores = []
    barrier = pltpu.get_barrier_semaphore()
    pl.semaphore_signal(barrier, inc=1, device_id=partner, device_id_type=MESH_ID)
    pl.semaphore_wait(barrier, 1)
    exchanges = [
        pltpu.make_async_remote_copy(
            hidden.at[pl.ds(place * tokens // 2, tokens // 2)], other_hidden.at[pl.ds(place * tokens // 2, tokens // 2)],
            send_sem.at[place], recv_sem.at[place], device_id=partner, device_id_type=MESH_ID,
        )
        for place in range(2)
    ]
    for exchange in exchanges:
        exchange.start()

    places = []
    for number in range(2 * blocks):
        block = (seq if number < blocks else 1 - seq) * blocks + number % blocks
        places.append(block_place(segments, lengths, block))
        time = times[0, places[number][0]]
        high, low = time // 32, time % 32
        cos_high, sin_high = table[pl.ds(HIGH_COS + high, 1), :], table[pl.ds(HIGH_SIN + high, 1), :]
        cos_low, sin_low = table[pl.ds(LOW_COS + low, 1), :], table[pl.ds(LOW_SIN + low, 1), :]
        cosine = cos_high * cos_low - sin_high * sin_low
        sine = sin_high * cos_low + cos_high * sin_low
        row = jnp.where(lane_iota(cosine.shape) < 64, cosine, sine)
        condition[pl.ds(number, 1), :] = row.astype(BF16).astype(F32)
    mod_load.wait()
    modulation[...] = dot(condition[...].astype(BF16), mod_weight[...]) + as_row(mod_bias)

    lane = lane_iota((BLOCK, 128))
    row = row_iota((BLOCK, 128))

    half_blocks = blocks // 2
    sections = ((0, 0, blocks), (1, 0, half_blocks), (1, half_blocks, half_blocks))
    for section, (part, first_block, count) in enumerate(sections):
        source = hidden if part == 0 else other_hidden
        if part == 1:
            exchanges[section - 1].wait_recv()
        section_rows = pl.ds(first_block * BLOCK, count * BLOCK)
        turns = []
        for number in range(first_block, first_block + count):
            rows = pl.ds(number * BLOCK, BLOCK)
            segment, before, valid_count = places[part * blocks + number]
            turns.append(rotary_block(table, before))
            mine = lane == SEGMENT_LANE + segment
            in_lanes = (lane >= SEGMENT_LANE) & (lane < SEGMENT_LANE + MAX_SEQUENCES)
            blocked = in_lanes & jnp.logical_not(mine & (row < valid_count))
            key_features[part, rows, :] = jnp.where(blocked, MASKED, 0.0).astype(BF16)
            if part == 0:
                query_features[rows, :] = jnp.where(mine, 1.0, 0.0).astype(BF16)
            mod_row = pl.ds(part * blocks + number, 1)
            shift, scale = modulation[mod_row, pl.ds(0, width)], modulation[mod_row, pl.ds(width, width)]
            value = source[rows, :].astype(F32)
            centered = value - mean_of(value)
            spread = mean_of(centered * centered)
            line = centered * lax.rsqrt(spread + 1e-05) * as_row(first_gain)
            result = (line * (1.0 + scale) + shift).astype(BF16)
            if part == 0:
                normed[rows, :] = result
            else:
                other_hidden[rows, :] = result
        normed_source = normed if part == 0 else other_hidden
        if section == 0:
            weight_load.wait()
            stores.append(pltpu.make_async_copy(normed, normed_hbm, store_sem.at[3, 0]))
            stores[-1].start()
        for tile in range(3 * width // LANES):
            which, first = divmod(tile * LANES, width)
            product = dot(normed_source[section_rows, :], weight[:, pl.ds(tile * LANES, LANES)])
            target = (queries, keys, values)[which]
            for place in range(count):
                cosine, sine = turns[place]
                for pair in range(LANES // 128):
                    piece = product[place * BLOCK : (place + 1) * BLOCK, pair * 128 : (pair + 1) * 128]
                    if which < 2:
                        piece = turn(piece, cosine, sine)
                    if which == 0:
                        piece = piece.astype(BF16).astype(F32) * 0.125
                    rows = pl.ds((first_block + place) * BLOCK, BLOCK)
                    target[part, rows, pl.ds(first + pair * 128, 128)] = piece.astype(BF16)
        for place, (source, target) in enumerate(((queries, queries_hbm), (keys, keys_hbm), (values, values_hbm))):
            copy = pltpu.make_async_copy(
                source.at[part, section_rows], target.at[part, section_rows], store_sem.at[place, section]
            )
            copy.start()
            stores.append(copy)
        turned_rows = pl.ds(0, count * BLOCK)
        turned_values[:, turned_rows] = jnp.transpose(values[part, section_rows, :])

        def attend_two(step, carry):
            for place in range(2):
                attend(2 * step + place, carry)
            return carry

        def attend(pair, carry):
            lanes = pl.ds(pl.multiple_of(pair * 128, 128), 128)
            query_pair, key_pair = queries[0, :, lanes], keys[part, section_rows, lanes]
            left = jnp.concatenate([key_pair, key_features[part, section_rows, :]], axis=1)
            pair_lane = lane_iota(query_pair.shape)
            both = []
            for half in range(2):
                query = jnp.where((pair_lane < 64) == (half == 0), query_pair, jnp.zeros_like(query_pair))
                both.append(dot_nt(left, jnp.concatenate([query, query_features[...]], axis=1)))
            for half, scores in enumerate(both):
                head = pair * 2 + half
                head_rows = pl.ds(pl.multiple_of(head * 64, 64), 64)
                one_row = pl.ds(head, 1)
                top = jnp.max(scores, axis=0, keepdims=True)
                if section > 0:
                    top = jnp.maximum(top, peak[one_row, :])
                weights = jnp.exp(scores - top)
                summed = jnp.sum(weights, axis=0, keepdims=True)
                mixed = dot(turned_values[head_rows, turned_rows], weights.astype(BF16))
                if section > 0:
                    rescale = jnp.exp(peak[one_row, :] - top)
                    summed = summed + rescale * total[one_row, :]
                    mixed = mixed + out_t[head_rows, :] * rescale
                if section < len(sections) - 1:
                    out_t[head_rows, :] = mixed
                    total[one_row, :] = summed
                    peak[one_row, :] = top
                else:
                    out_t[head_rows, :] = mixed * (1.0 / summed)
                    peak[one_row, :] = top + jnp.log(summed)
            return carry

        lax.fori_loop(0, HEADS // 4, attend_two, 0)

    attended[...] = jnp.transpose(out_t[...].astype(BF16))
    log_rows = jnp.concatenate(
        [jnp.broadcast_to(peak[pl.ds(head, 1), :], (3, tokens)) for head in range(HEADS)]
        + [jnp.zeros((128 - 3 * HEADS, tokens), F32)], axis=0,
    )
    query_features[...] = query_features[...] + split_three(jnp.transpose(log_rows))
    for copy in stores:
        copy.wait()
    for exchange in exchanges:
        exchange.wait_send()


def forward(segments, lengths, times, hidden, table, first_gain, mod_weight, mod_bias, weight):
    tokens, width = hidden.shape
    blocks = 2 * tokens // BLOCK
    half = jax.ShapeDtypeStruct((tokens, width), BF16)
    both = jax.ShapeDtypeStruct((2, tokens, width), BF16)
    smem, vmem = pl.BlockSpec(memory_space=pltpu.SMEM), pl.BlockSpec(memory_space=pltpu.VMEM)
    hbm = pl.BlockSpec(memory_space=pl.ANY)
    return pl.pallas_call(
        forward_kernel,
        out_shape=(
            half, both, both, both, half,
            jax.ShapeDtypeStruct((tokens, 128), BF16),
            jax.ShapeDtypeStruct((2, tokens, 128), BF16),
            jax.ShapeDtypeStruct((blocks, 6 * width), F32),
            jax.ShapeDtypeStruct((blocks, 128), F32),
        ),
        in_specs=[smem] * 3 + [vmem] * 3 + [hbm, vmem, hbm],
        out_specs=(hbm,) * 4 + (vmem,) * 5,
        scratch_shapes=[
            pltpu.VMEM(mod_weight.shape, BF16),
            pltpu.VMEM(weight.shape, BF16),
            pltpu.VMEM((tokens, width), BF16),
            pltpu.VMEM((2, tokens, width), BF16),
            pltpu.VMEM((2, tokens, width), BF16),
            pltpu.VMEM((2, tokens, width), BF16),
            pltpu.VMEM((tokens, width), BF16),
            pltpu.VMEM((width, tokens), BF16),
            pltpu.VMEM((width, tokens), F32),
            pltpu.VMEM((16, tokens), F32),
            pltpu.VMEM((16, tokens), F32),
            pltpu.SemaphoreType.DMA((2,)),
            pltpu.SemaphoreType.DMA((2,)),
            pltpu.SemaphoreType.DMA((2,)),
            pltpu.SemaphoreType.DMA((4, 3)),
        ],
        compiler_params=pltpu.CompilerParams(
            collective_id=1, has_side_effects=True, vmem_limit_bytes=56 << 20
        ),
    )(segments, lengths, times, hidden, table, first_gain, mod_weight, mod_bias, weight)


TILE = 384
Z2, Z1, Y, CORE, X = 0, 1, 2, 3, 4


WIDE_ORDERS = ((X, Y), (Y, X), (X, Y), (Y, X))
REDUCE_ORDERS = ((Z1, Z2, Y), (Z1, Y, Z2), (Y, Z1, Z2), (Z1, Y, Z2))
OUTPUT_ORDER = (CORE, Z1, Y, X, Z2)
TRIPLE_ORDERS = ((Y, X, Z1, Z2), (Z1, X, Y, Z2), (X, Y, Z1, Z2))
PLAN = (
    (("T", 6), (("r", 0), ("w", 0),)),
    (("N", 0), (("w", 1), ("r", 1),)),
    (("D", 1), (("w", 2),)),
    (("D", 2), (("r", 2),)),
    (("A", 0), (("s", 0), ("r", 0),)),
    (("A", 1), (("w", 1), ("w", 0),)),
    (("A", 2), (("o", 0),)),
    (("A", 4), (("r", 3),)),
    (("A", 5), (("w", 3),)),
    (("A", 6), (("r", 2),)),
    (("A", 8), (("r", 1), ("wm", 0),)),
    (("A", 10), (("w", 2),)),
    (("A", 11), (("s", 0),)),
    (("E", 0), (("o", 0), ("r", 0),)),
    (("B", 0), (("r", 3),)),
    (("B", 2), (("r", 2),)),
    (("B", 4), (("o", 0), ("w", 3),)),
    (("B", 5), (("s", 0), ("r", 1),)),
    (("C", 0), (("o", 0), ("r", 3),)),
    (("C", 1), (("re", 0),)),
    (("C", 2), (("wm", 1),)),
    (("C", 3), (("s", 0),)),
    (("C", 4), (("re", 1),)),
    (("C", 5), (("o", 0),)),
    (("F", 0), (("m", 0), ("we", 0), ("q", 0), ("q", 2), ("s", 0), ("m", 0), ("q", 1), ("q", 0), ("q", 2), ("m", 0), ("q", 0), ("q", 1), ("q", 2), ("q", 1), ("m", 0), ("q", 0), ("q", 2), ("q", 1), ("m", 0),)),
)


def exchange_partner(axis, extra_bits):
    dp, seq = lax.axis_index("dp"), lax.axis_index("seq")
    if axis == X:
        return (dp, 1 - seq)
    return (dp ^ (1 << (GROUP_BITS - 1 - axis + extra_bits)), seq)


def own_bit(axis, extra_bits):
    if axis == X:
        return lax.axis_index("seq")
    return (lax.axis_index("dp") >> (GROUP_BITS - 1 - axis + extra_bits)) & 1


class Stream:
    def __init__(self, kit, number, part, first, count, fixed, order, got, got_first=0, total_first=None):
        self.kit, self.number, self.part, self.first, self.count = kit, number, part, first, count
        self.fixed, self.order, self.got, self.got_first = fixed, order, got, got_first
        self.total_first = total_first

    def free(self, stage):
        return [axis for axis in range(5) if axis not in self.fixed and axis not in self.order[: stage + 1]]

    def copy(self, stage):
        bits = self.kit["bits"]
        index = [slice(None)] * 5
        for axis, value in self.fixed.items():
            index[axis] = value
        for axis in self.order[:stage]:
            index[axis] = bits[axis]
        index[self.order[stage]] = 1 - bits[self.order[stage]]
        target = (slice(None),) * len(self.free(stage)) + (pl.ds(self.got_first, self.count),)
        return pltpu.make_async_remote_copy(
            self.part.at[tuple(index) + (pl.ds(self.first, self.count),)],
            self.got[stage].at[target],
            self.kit["send"].at[self.number, stage],
            self.kit["recv"].at[self.number, stage],
            device_id=exchange_partner(self.order[stage], self.kit["extra"]),
            device_id_type=MESH_ID,
        )

    def send(self, stage):
        self.copy(stage).start()

    def add(self, stage):
        self.copy(stage).wait_recv()
        last = stage == len(self.order) - 1 and self.total_first is not None
        bits, free = self.kit["bits"], self.free(stage)
        rows, got_rows = pl.ds(self.first, self.count), pl.ds(self.got_first, self.count)

        def one(step, carry):
            index = list(bits)
            for axis, value in self.fixed.items():
                index[axis] = value
            place = []
            for order, axis in enumerate(free):
                index[axis] = (step >> (len(free) - 1 - order)) & 1
                place.append(index[axis])
            mine, theirs = self.part[tuple(index) + (rows,)], self.got[stage][tuple(place) + (got_rows,)]
            if last:
                total = mine.astype(F32) + theirs.astype(F32)
                self.kit["sums"][pl.ds(self.total_first, self.count), :] = total
            else:
                self.part[tuple(index) + (rows,)] = mine + theirs
            return carry

        if free:
            lax.fori_loop(0, 2 ** len(free), one, 0)
        else:
            one(0, 0)

    def done(self):
        for stage in range(len(self.order)):
            self.copy(stage).wait_send()


def backward_kernel(
    extra_bits, all_bits,
    segments, lengths, modulation, condition, table, first_gain, second_gain, expand_bias, reduce_bias,
    narrow_hbm, widen_hbm, out_weight_hbm, attended_hbm, cotangent_hbm, queries_hbm, keys_hbm, values_hbm,
    query_features_hbm, key_features_hbm, normed_hbm, hidden_hbm, weight_hbm,
    block_out, input_grad, sums, mod_out, small_out,
    expand_part, reduce_part, output_part,
    expand_got, reduce_got, wide_a, wide_b, wide_z, wide_last, red_a, red_b, red_c, red_last,
    out_a, out_b, out_c, out_d, out_e, tri_a, tri_b, tri_c, tri_d, tri_e,
    queries, keys, values, query_features, key_features,
    grad_middle, grad_attended, delta_features, other_grad, other_delta, other_features, mod_rows,
    small_acc, small_got, late_acc, late_got, mod_got, mod_two, mod_three, mod_four, mod_five,
    cond_zero, cond_got, cond_one, cond_two, cond_three, cond_four, cond_five,
    load_sem, tile_sem, core_send, core_recv, stream_send, stream_recv, swap_send, swap_recv,
    small_send, small_recv, late_send, late_recv, mod_send, mod_recv, triple_send, triple_recv,
):
    tokens, width = input_grad.shape
    tiles = narrow_hbm.shape[0] // TILE
    blocks = tokens // BLOCK
    seq = lax.axis_index("seq")
    dp = lax.axis_index("dp")
    bits = [own_bit(axis, extra_bits) for axis in range(5)]
    kit = {"bits": bits, "send": stream_send, "recv": stream_recv, "extra": extra_bits, "sums": sums}
    core = bits[CORE]

    def others(*axes):
        return {axis: bits[axis] for axis in range(5) if axis not in axes}

    def chosen(**values):
        return {CORE: core, **{{"z2": Z2, "z1": Z1, "x": X}[name]: value for name, value in values.items()}}

    streams = {}
    for g in range(4):
        streams["w", g] = Stream(
            kit, g, expand_part, 0, 192, chosen(z2=g >> 1, z1=g & 1), WIDE_ORDERS[g], (wide_a.at[g], wide_b.at[g])
        )
        streams["r", g] = Stream(
            kit, 4 + g, reduce_part, 96 * (g & 1), 96, chosen(x=g >> 1), REDUCE_ORDERS[g],
            (red_a.at[g], red_b.at[g], red_c.at[g]),
        )
    for v in range(2):
        streams["wm", v] = Stream(
            kit, 8 + v, expand_part, 0, 192, {**others(Z1, Z2), Z2: v}, (Z1,), (wide_z.at[v],)
        )
        streams["re", v] = Stream(
            kit, 11 + v, reduce_part, 96 * v, 96, others(X), (X,), (red_last.at[v],), total_first=192 + 96 * v
        )
    streams["we", 0] = Stream(kit, 10, expand_part, 0, 192, others(Z2), (Z2,), (wide_last,), total_first=0)
    streams["o", 0] = Stream(
        kit, 13, output_part, 0, 48, {}, OUTPUT_ORDER, (out_a, out_b, out_c, out_d, out_e), total_first=384
    )
    merges = {
        ("wm", 0): (("w", 0), ("w", 1)), ("wm", 1): (("w", 2), ("w", 3)), ("we", 0): (("wm", 0), ("wm", 1)),
        ("re", 0): (("r", 0), ("r", 2)), ("re", 1): (("r", 1), ("r", 3)),
    }
    work, stages, finished = {}, {}, set()
    for slot, names in PLAN:
        todo = work.setdefault(slot, [])
        for name in names:
            stage = stages.get(name, 0)
            stages[name] = stage + 1
            todo.append((True, name, stage))
            if name[0] in ("m", "s"):
                continue
            if stage + 1 < (len(streams[name].order) if name in streams else 4):
                todo.append((False, name, stage + 1))
                continue
            finished.add(name)
            for merged, parts in merges.items():
                if name in parts and finished.issuperset(parts):
                    todo.append((False, merged, 0))

    def perform(slot):
        for is_add, name, stage in work.get(slot, ()):
            if name[0] == "s":
                small_step(stage)
            elif is_add:
                streams[name].add(stage)
            else:
                streams[name].send(stage)

    def perform_at(letter, first, stride, count, index):
        for place in range(count):
            slot = (letter, first + stride * place)
            if work.get(slot):

                @pl.when(index == place)
                def _(slot=slot):
                    perform(slot)

    greet = [(dp, 1 - seq)] + [(dp ^ (1 << bit), seq) for bit in range(all_bits)]
    barrier = pltpu.get_barrier_semaphore()
    for partner in greet:
        pl.semaphore_signal(barrier, inc=1, device_id=partner, device_id_type=MESH_ID)

    attention_loads = [
        pltpu.make_async_copy(source, target, load_sem.at[number])
        for number, (source, target) in enumerate(
            ((queries_hbm, queries), (keys_hbm, keys), (values_hbm, values),
             (query_features_hbm, query_features), (key_features_hbm, key_features))
        )
    ]
    row = row_iota((BLOCK, 1))
    keep = []
    for number in range(blocks):
        valid_count = block_place(segments, lengths, seq * blocks + number)[2]
        keep.append(jnp.where(row < valid_count, 1.0, 0.0))

    def mod_part(number, part):
        return modulation[pl.ds(number, 1), pl.ds(part * width, width)]

    def tile_lanes(tile):
        return pl.ds(pl.multiple_of(tile * TILE, TILE), TILE)

    def core_copies(tile):
        at = (tile >> 2, (tile >> 1) & 1, tile & 1)
        rows = pl.ds(pl.multiple_of((tile & 3) * 48, 16), 48)
        everywhere = (slice(None),) * 3
        partner = exchange_partner(CORE, extra_bits)
        return (
            pltpu.make_async_remote_copy(
                expand_part.at[at + (1 - core,)], expand_got.at[at], core_send.at[0, tile], core_recv.at[0, tile],
                device_id=partner, device_id_type=MESH_ID,
            ),
            pltpu.make_async_remote_copy(
                reduce_part.at[everywhere + (1 - core, tile >> 2, rows)], reduce_got.at[everywhere + (tile >> 2, rows)],
                core_send.at[1, tile], core_recv.at[1, tile], device_id=partner, device_id_type=MESH_ID,
            ),
        )

    def core_add(tile):
        at = (tile >> 2, (tile >> 1) & 1, tile & 1)
        rows = pl.ds(pl.multiple_of((tile & 3) * 48, 16), 48)
        for copy in core_copies(tile):
            copy.wait_recv()
        for side in range(2):
            expand_part[at + (core, side)] = expand_part[at + (core, side)] + expand_got[at + (side,)]
        for z2 in range(2):
            for z1 in range(2):
                for y in range(2):
                    index, got = (z2, z1, y, core, tile >> 2, rows), (z2, z1, y, tile >> 2, rows)
                    reduce_part[index] = reduce_part[index] + reduce_got[got]

    def mlp_phase(
        narrow, widen, out_weight, attended, hidden, cotangent, normed_two, grad_low, grad_low_t,
        projected, reduced, grad_normed,
    ):
        def tile_loads(tile):
            lanes = tile_lanes(tile)
            pairs = ((widen_hbm.at[:, lanes], widen.at[:, lanes]), (narrow_hbm.at[lanes], narrow.at[lanes]))
            return [pltpu.make_async_copy(source, target, tile_sem.at[place, tile]) for place, (source, target) in enumerate(pairs)]

        loads = [
            pltpu.make_async_copy(source, target, load_sem.at[5 + number])
            for number, (source, target) in enumerate(
                ((cotangent_hbm, cotangent), (attended_hbm, attended), (out_weight_hbm, out_weight), (hidden_hbm, hidden))
            )
        ]
        for load in loads:
            load.start()
        for tile in range(tiles):
            for load in tile_loads(tile):
                load.start()
        for load in attention_loads:
            load.start()
        small_acc[0] = jnp.zeros_like(small_acc[0])
        grad_normed[...] = jnp.zeros_like(grad_normed)
        reduced[...] = jnp.zeros_like(reduced)
        loads[0].wait()
        bias_sum = jnp.zeros((1, width), F32)
        for number in range(blocks):
            rows = pl.ds(number * BLOCK, BLOCK)
            low = (mod_part(number, 5) * (cotangent[rows, :].astype(F32) * keep[number])).astype(BF16)
            grad_low[rows, :] = low
            bias_sum = bias_sum + jnp.sum(low.astype(F32), axis=0, keepdims=True)
        small_acc[0, pl.ds(REDUCE_BIAS, 1), :] = bias_sum
        grad_low_t[...] = jnp.transpose(grad_low[...])
        for load in loads[1:]:
            load.wait()
        for first in range(0, width, 256):
            lanes = pl.ds(first, 256)
            projected[:, lanes] = dot(attended[...], out_weight[:, lanes])
        branch_sum = jnp.zeros((1, width), F32)
        for number in range(blocks):
            rows = pl.ds(number * BLOCK, BLOCK)
            branch = mod_part(number, 2) * projected[rows, :]
            branch_sum = branch_sum + jnp.sum(keep[number] * branch * branch, axis=0, keepdims=True)
            value = hidden[rows, :].astype(F32) + branch
            centered = value - mean_of(value)
            inverse = lax.rsqrt(mean_of(centered * centered) + 1e-05)
            line = centered * inverse * as_row(second_gain)
            normed_two[rows, :] = (line * (1.0 + mod_part(number, 4)) + mod_part(number, 3)).astype(BF16)
        pl.semaphore_wait(barrier, len(greet))

        def through(tile):
            lanes = tile_lanes(tile)
            for load in tile_loads(tile):
                load.wait()
            u = dot(normed_two[...], widen[:, lanes]) + expand_bias[lanes].reshape(1, TILE)
            grad_active = dot_nt(grad_low[...], narrow[lanes, :])
            square = u * u
            tanh = jnp.tanh(u * (0.7978845608028654 + 0.7978845608028654 * 0.044715 * square))
            half_sum = 0.5 + 0.5 * tanh
            active = (u * half_sum).astype(BF16)
            inner = 0.7978845608028654 + 3.0 * 0.7978845608028654 * 0.044715 * square
            slope = half_sum + (0.5 * u) * (1.0 - tanh * tanh) * inner
            grad_wide = (grad_active * slope).astype(BF16)
            reduced[...] += dot(active, narrow[lanes, :])
            reduce_t = dot(grad_low_t[...], active).astype(BF16)
            rows = pl.ds(pl.multiple_of((tile & 3) * 48, 16), 48)
            reduce_part[:, :, :, :, tile >> 2, rows] = reduce_t.reshape(2, 2, 2, 2, 48, TILE)
            bias_lanes = pl.ds(pl.multiple_of((tile & 1) * TILE, TILE), TILE)
            small_acc[0, pl.ds(EXPAND_BIAS + (tile >> 1), 1), bias_lanes] = jnp.sum(
                grad_wide.astype(F32), axis=0, keepdims=True
            )
            expand_t = dot_tn(grad_wide, normed_two[...]).astype(BF16)
            at = (tile >> 2, (tile >> 1) & 1, tile & 1)
            for group in range(2):
                for side in range(2):
                    expand_part[at + (group, side)] = expand_t[
                        group * 192 : group * 192 + 192, side * LANES : side * LANES + LANES
                    ]
            for copy in core_copies(tile):
                copy.start()
            grad_normed[...] += dot_nt(grad_wide, widen[:, lanes])

        def begin(g):
            streams["w", g].send(0)
            streams["r", g].send(0)

        def through_two(number, carry):
            through(2 * number)

            @pl.when(number > 0)
            def _():
                core_add(2 * number - 1)

            for g in range(tiles // 2 - 1):

                @pl.when(number == g + 1)
                def _(g=g):
                    begin(g)

            perform_at("T", 0, 2, tiles // 2, number)
            through(2 * number + 1)
            core_add(2 * number)
            perform_at("T", 1, 2, tiles // 2, number)
            return carry

        lax.fori_loop(0, tiles // 2, through_two, 0)
        core_add(tiles - 1)
        begin(3)
        gain_sum = jnp.zeros((1, width), F32)
        for number in range(blocks):
            perform(("N", number))
            rows = pl.ds(number * BLOCK, BLOCK)
            here = pl.ds(number, 1)
            before = hidden[rows, :].astype(F32) + mod_part(number, 2) * projected[rows, :]
            centered = before - mean_of(before)
            inverse = lax.rsqrt(mean_of(centered * centered) + 1e-05)
            normal = centered * inverse
            grad = grad_normed[rows, :]
            line = normal * as_row(second_gain)
            mod_rows[here, pl.ds(3 * width, width)] = jnp.sum(grad, axis=0, keepdims=True)
            mod_rows[here, pl.ds(4 * width, width)] = jnp.sum(grad * line, axis=0, keepdims=True)
            grad_line = grad * (1.0 + mod_part(number, 4))
            gain_sum = gain_sum + jnp.sum(grad_line * normal, axis=0, keepdims=True)
            grad_normal = grad_line * as_row(second_gain)
            along = mean_of(grad_normal * normal)
            term = (grad_normal - mean_of(grad_normal) - normal * along) * inverse
            total = cotangent[rows, :].astype(F32) * keep[number] + term
            grad_middle[rows, :] = total
            grad_low[rows, :] = (mod_part(number, 2) * total).astype(BF16)
        small_acc[0, pl.ds(SECOND_GAIN, 1), :] = gain_sum
        perform(("N", blocks))

        for first in range(0, width, 256):
            grad_attended[:, pl.ds(first, 256)] = dot_nt(
                grad_low[...], out_weight[pl.ds(first, 256), :]
            ).astype(BF16)
        head_lane = row_iota((width, 128)) // 64 == lane_iota((width, 128)) // 3
        chooser = jnp.where(head_lane & (lane_iota((width, 128)) < 3 * HEADS), 1.0, 0.0).astype(BF16)
        for number in range(blocks):
            rows = pl.ds(number * BLOCK, BLOCK)
            product = grad_attended[rows, :].astype(F32) * attended[rows, :].astype(F32)
            upper = product.astype(BF16)
            lower = (product - upper.astype(F32)).astype(BF16)
            delta_features[rows, :] = split_three(dot(upper, chooser) + dot(lower, chooser))
        for load in attention_loads:
            load.wait()
        for place in range(HEADS // 2 + 2):
            swap(place).start()
        perform(("D", 0))
        value_sum = jnp.zeros((1, width), F32)
        mlp_sum = jnp.zeros((1, width), F32)
        for number in range(blocks):
            rows = pl.ds(number * BLOCK, BLOCK)
            here = pl.ds(number, 1)
            full = reduced[rows, :] + as_row(reduce_bias)
            branch = mod_part(number, 5) * full
            value = hidden[rows, :].astype(F32) + mod_part(number, 2) * projected[rows, :] + branch
            block_out[rows, :] = value.astype(BF16)
            value_sum = value_sum + jnp.sum(keep[number] * value * value, axis=0, keepdims=True)
            mlp_sum = mlp_sum + jnp.sum(keep[number] * branch * branch, axis=0, keepdims=True)
            grad_out = cotangent[rows, :].astype(F32) * keep[number]
            mod_rows[here, pl.ds(5 * width, width)] = jnp.sum(grad_out * full, axis=0, keepdims=True)
            mod_rows[here, pl.ds(2 * width, width)] = jnp.sum(
                grad_middle[rows, :] * projected[rows, :], axis=0, keepdims=True
            )
        lane = lane_iota((1, width))
        counts = jnp.zeros((1, 1), F32)
        for number in range(blocks):
            counts = counts + jnp.sum(keep[number], axis=0, keepdims=True)
        terms = [jnp.sum(term, axis=1, keepdims=True) for term in (value_sum, branch_sum, mlp_sum)] + [counts]
        stats = jnp.zeros((1, width), F32)
        for place, term in enumerate(terms):
            stats = jnp.where(lane == place, term, stats)
        small_acc[0, pl.ds(STATS, 1), :] = stats
        for part in range(2, 6):
            small_acc[0, pl.ds(MOD_BIAS + part, 1), :] = jnp.sum(
                mod_rows[:, pl.ds(part * width, width)], axis=0, keepdims=True
            )
        small_copy(0).start()
        perform(("D", 1))
        for first in range(0, width, TILE):
            output_t = dot_tn(grad_low[:, pl.ds(first, TILE)], attended[...]).astype(BF16)
            for place in range(TILE // 48):
                group = first // 48 + place
                at = (group >> 3, (group >> 2) & 1, (group >> 1) & 1, group & 1)
                for side in range(2):
                    output_part[at + (side,)] = output_t[
                        place * 48 : place * 48 + 48, side * LANES : side * LANES + LANES
                    ]
        streams["o", 0].send(0)
        perform(("D", 2))

    def small_copy(number):
        return pltpu.make_async_remote_copy(
            small_acc.at[number], small_got.at[number], small_send.at[number], small_recv.at[number],
            device_id=greet[(1 + number) % len(greet)], device_id_type=MESH_ID,
        )

    def small_step(number):
        small_copy(number).wait_recv()
        small_acc[number + 1] = small_acc[number] + small_got[number]
        if number + 1 < len(greet):
            small_copy(number + 1).start()

    def swap(place):
        if isinstance(place, int) and place < 2:
            source, target = ((delta_features, other_delta), (query_features, other_features))[place]
        else:
            lanes = pl.ds(pl.multiple_of((place - 2) * 128, 128), 128)
            source, target = grad_attended.at[:, lanes], other_grad.at[:, lanes]
        return pltpu.make_async_remote_copy(
            source, target, swap_send.at[place], swap_recv.at[place], device_id=(dp, 1 - seq), device_id_type=MESH_ID
        )

    units = tiles * TILE
    low_half, wide_half = pltpu.VMEM((tokens, width), BF16), pltpu.VMEM((tokens, width), F32)
    pl.run_scoped(
        mlp_phase,
        pltpu.VMEM((units, width), BF16), pltpu.VMEM((width, units), BF16), pltpu.VMEM((width, width), BF16),
        low_half, low_half, low_half, low_half, low_half, pltpu.VMEM((width, tokens), BF16),
        wide_half, wide_half, wide_half,
    )

    def attention_phase(normed, hidden, weight, keys_t, grad_query_t, grad_key, grad_value, grad_triple, grad_normed, triple_part, mod_zero, mod_one):
        loads = [
            pltpu.make_async_copy(source, target, load_sem.at[9 + number])
            for number, (source, target) in enumerate(((normed_hbm, normed), (hidden_hbm, hidden), (weight_hbm, weight)))
        ]
        for load in loads:
            load.start()
        for part in range(2):
            keys_t[part] = jnp.transpose(keys[part])

        def own_queries(pair, carry):
            lanes = pl.ds(pl.multiple_of(pair * 128, 128), 128)
            query_pair, grad_pair = queries[0, :, lanes], grad_attended[:, lanes]
            pair_lane = lane_iota(query_pair.shape)
            for half in range(2):
                head = pair * 2 + half
                head_rows = pl.ds(pl.multiple_of(head * 64, 64), 64)
                mine = (pair_lane < 64) == (half == 0)
                query = jnp.where(mine, query_pair, jnp.zeros_like(query_pair))
                grad = jnp.where(mine, grad_pair, jnp.zeros_like(grad_pair))
                right_scores = jnp.concatenate([query, query_features[...]], axis=1)
                right_grads = jnp.concatenate([grad, delta_features[...]], axis=1)
                head_lanes = (pair_lane >= 3 * head) & (pair_lane < 3 * head + 3)
                grad_q = jnp.zeros((64, tokens), F32)
                for part in range(2):
                    features = jnp.where(head_lanes, jnp.full_like(query_pair, -1.0), key_features[part])
                    scores = dot_nt(jnp.concatenate([keys[part, :, lanes], features], axis=1), right_scores)
                    weights = jnp.exp(scores)
                    grad_weights = dot_nt(jnp.concatenate([values[part, :, lanes], features], axis=1), right_grads)
                    grad_scores = (weights * grad_weights).astype(BF16)
                    if part == 0:
                        grad_v = dot(weights.astype(BF16), grad)
                        grad_k = dot(grad_scores, query)
                        if half == 0:
                            grad_value[:, lanes] = grad_v
                            grad_key[:, lanes] = grad_k
                        else:
                            grad_value[:, lanes] += grad_v
                            grad_key[:, lanes] += grad_k
                    grad_q = grad_q + dot(keys_t[part, head_rows, :], grad_scores)
                grad_query_t[head_rows, :] = grad_q
                perform_at("A", half, 2, HEADS // 2, pair)
            return carry

        lax.fori_loop(0, HEADS // 2, own_queries, 0)
        for load in loads:
            load.wait()
        turns = []
        grad_normed[...] = jnp.transpose(grad_query_t[...])
        for number in range(blocks):
            rows = pl.ds(number * BLOCK, BLOCK)
            before = block_place(segments, lengths, seq * blocks + number)[1]
            cosine, sine = rotary_block(table, before)
            turns.append((cosine, -sine))
            for pair in range(HEADS // 2):
                lanes = pl.ds(pair * 128, 128)
                grad_triple[rows, lanes] = (turn(grad_normed[rows, lanes], cosine, -sine) * 0.125).astype(BF16)

        def third(part):
            triple_t = dot_tn(grad_triple[:, pl.ds(part * width, width)], normed[...]).astype(BF16)
            for place in range(width // 48):
                group, piece = divmod(part * (width // 48) + place, 3)
                at = (group >> 3, (group >> 2) & 1, (group >> 1) & 1, group & 1)
                for side in range(2):
                    triple_part[at + (side, pl.ds(48 * piece, 48))] = triple_t[
                        place * 48 : place * 48 + 48, side * LANES : side * LANES + LANES
                    ]

        def triple_core(number):
            index = ((0, 0), (0, 1), (1,))[number]
            full = (slice(None),) * (3 - len(index))
            return pltpu.make_async_remote_copy(
                triple_part.at[index + full + (1 - core,)], tri_a.at[index],
                triple_send.at[number], triple_recv.at[number],
                device_id=exchange_partner(CORE, extra_bits), device_id_type=MESH_ID,
            )

        def triple_add(number):
            triple_core(number).wait_recv()
            for z1 in (number,) if number < 2 else range(2):
                for y in range(2):
                    for side in range(2):
                        got = (number // 2, z1, y)
                        triple_part[got + (core, side)] = triple_part[got + (core, side)] + tri_a[got + (side,)]

        third(0)
        triple_core(0).start()
        grad_normed[...] = dot_nt(grad_triple[:, pl.ds(0, width)], weight[:, pl.ds(0, width)])
        perform(("E", 0))
        for place in range(2):
            swap(place).wait_recv()

        def other_queries(pair, carry):
            lanes = pl.ds(pl.multiple_of(pair * 128, 128), 128)
            swap(pair + 2).wait_recv()
            query_pair, grad_pair = queries[1, :, lanes], other_grad[:, lanes]
            pair_lane = lane_iota(query_pair.shape)
            grad_k = grad_key[:, lanes]
            grad_v = grad_value[:, lanes]
            for half in range(2):
                head = pair * 2 + half
                mine = (pair_lane < 64) == (half == 0)
                query = jnp.where(mine, query_pair, jnp.zeros_like(query_pair))
                grad = jnp.where(mine, grad_pair, jnp.zeros_like(grad_pair))
                head_lanes = (pair_lane >= 3 * head) & (pair_lane < 3 * head + 3)
                features = jnp.where(head_lanes, jnp.full_like(query_pair, -1.0), key_features[0])
                scores = dot_nt(
                    jnp.concatenate([keys[0, :, lanes], features], axis=1),
                    jnp.concatenate([query, other_features[...]], axis=1),
                )
                weights = jnp.exp(scores)
                grad_weights = dot_nt(
                    jnp.concatenate([values[0, :, lanes], features], axis=1),
                    jnp.concatenate([grad, other_delta[...]], axis=1),
                )
                grad_scores = (weights * grad_weights).astype(BF16)
                grad_v = grad_v + dot(weights.astype(BF16), grad)
                grad_k = grad_k + dot(grad_scores, query)
            grad_key[:, lanes] = grad_k
            grad_value[:, lanes] = grad_v
            perform_at("B", 0, 1, HEADS // 2, pair)
            return carry

        lax.fori_loop(0, HEADS // 2, other_queries, 0)

        for number in range(blocks):
            rows = pl.ds(number * BLOCK, BLOCK)
            for pair in range(HEADS // 2):
                lanes = pl.ds(pair * 128, 128)
                grad_triple[rows, pl.ds(width + pair * 128, 128)] = turn(grad_key[rows, lanes], *turns[number]).astype(BF16)
            grad_triple[rows, pl.ds(2 * width, width)] = grad_value[rows, :].astype(BF16)
        third(1)
        triple_core(1).start()
        triple_add(0)
        third(2)
        triple_core(2).start()
        triple_add(1)
        triple = [
            Stream(
                kit, 14 + number, triple_part, 48 * number, 48, {CORE: core}, order, (tri_b, tri_c, tri_d, tri_e),
                48 * number, 432 + 48 * number,
            )
            for number, order in enumerate(TRIPLE_ORDERS)
        ]
        perform(("C", 0))
        for part in range(1, 3):
            lanes = pl.ds(part * width, width)
            grad_normed[...] += dot_nt(grad_triple[:, lanes], weight[:, lanes])
            perform(("C", part))
        triple_add(2)
        for number, stream in enumerate(triple):
            streams["q", number] = stream
            stream.send(0)

        gain_sum = jnp.zeros((1, width), F32)
        for number in range(blocks):
            rows, here = pl.ds(number * BLOCK, BLOCK), pl.ds(number, 1)
            value = hidden[rows, :].astype(F32)
            centered = value - mean_of(value)
            inverse = lax.rsqrt(mean_of(centered * centered) + 1e-05)
            normal = centered * inverse
            grad = grad_normed[rows, :]
            mod_rows[here, pl.ds(0, width)] = jnp.sum(grad, axis=0, keepdims=True)
            mod_rows[here, pl.ds(width, width)] = jnp.sum(grad * (normal * as_row(first_gain)), axis=0, keepdims=True)
            grad_line = grad * (1.0 + mod_part(number, 1))
            gain_sum = gain_sum + jnp.sum(grad_line * normal, axis=0, keepdims=True)
            grad_normal = grad_line * as_row(first_gain)
            along = mean_of(grad_normal * normal)
            term = (grad_normal - mean_of(grad_normal) - normal * along) * inverse
            input_grad[rows, :] = (grad_middle[rows, :] + term).astype(BF16)
            perform(("C", 3 + number))
        late_acc[0] = jnp.zeros_like(late_acc[0])
        late_acc[0, pl.ds(0, 1), :] = gain_sum
        for part in range(2):
            late_acc[0, pl.ds(1 + part, 1), :] = jnp.sum(mod_rows[:, pl.ds(part * width, width)], axis=0, keepdims=True)

        def late_copy(number):
            return pltpu.make_async_remote_copy(
                late_acc.at[number], late_got.at[number], late_send.at[number], late_recv.at[number],
                device_id=greet[(1 + number) % len(greet)], device_id_type=MESH_ID,
            )

        def late_step(number):
            late_copy(number).wait_recv()
            late_acc[number + 1] = late_acc[number] + late_got[number]
            if number + 1 < len(greet):
                late_copy(number + 1).start()

        late_copy(0).start()

        mod_axes = (CORE, Y, Z1, Z2, X)

        def mod_copies(number):
            mods = (mod_zero, mod_one, mod_two, mod_three, mod_four)
            conds = (cond_zero, cond_one, cond_two, cond_three, cond_four)
            if number == 0:
                pairs = ((mod_zero.at[:, :, :, 1 - core], mod_got), (cond_zero, cond_got))
            else:
                later = ((mod_two, cond_two), (mod_three, cond_three), (mod_four, cond_four), (mod_five, cond_five))[number - 1]
                chunks = pl.ds(2 ** (number - 1), 2 ** (number - 1))
                if number == 1:
                    source = mod_one.at[:, :, :, 1 - bits[Y]]
                elif number == 2:
                    source = mod_two.at[:, :, 1 - bits[Z1]]
                elif number == 3:
                    source = mod_three.at[:, 1 - bits[Z2]]
                else:
                    source = mod_four
                pairs = ((source, later[0].at[chunks]), (conds[number], later[1].at[chunks]))
            return [
                pltpu.make_async_remote_copy(
                    source, target, mod_send.at[place, number], mod_recv.at[place, number],
                    device_id=exchange_partner(mod_axes[number], extra_bits), device_id_type=MESH_ID,
                )
                for place, (source, target) in enumerate(pairs)
            ]

        def mod_step(number):
            for copy in mod_copies(number):
                copy.wait_recv()
            if number == 0:
                mod_one[0] = mod_zero[:, :, :, core]
                mod_one[0, :, :, :, pl.ds(4, 4), :] = mod_got[:, :, :, pl.ds(0, 4), :]
                cond_one[0] = cond_zero[...]
                cond_one[0, pl.ds(4, 4), :] = cond_got[pl.ds(0, 4), :]
            if number == 0:
                mod_two[0] = mod_one[0, :, :, bits[Y]]
                cond_two[0] = cond_one[0]
            elif number == 1:
                mod_three[pl.ds(0, 2)] = mod_two[:, :, bits[Z1]]
                cond_three[pl.ds(0, 2)] = cond_two[...]
            elif number == 2:
                mod_four[pl.ds(0, 4)] = mod_three[:, bits[Z2]]
                cond_four[pl.ds(0, 4)] = cond_three[...]
            elif number == 3:
                mod_five[pl.ds(0, 8)] = mod_four[...]
                cond_five[pl.ds(0, 8)] = cond_four[...]
            if number < 4:
                for copy in mod_copies(number + 1):
                    copy.start()

        mod_zero[...] = jnp.zeros_like(mod_zero)
        columns = 6 * width // 16
        for group in range(16):
            at = (group >> 3, (group >> 2) & 1, (group >> 1) & 1, group & 1)
            mod_zero[at + (pl.ds(0, blocks), pl.ds(0, columns))] = mod_rows[:, pl.ds(group * columns, columns)]
        cond_zero[...] = condition[...]
        for copy in mod_copies(0):
            copy.start()

        for is_add, name, stage in work[("F", 0)]:
            if name[0] == "m":
                mod_step(stage)
                late_step(stage)
            elif name[0] == "s":
                small_step(stage)
            elif is_add:
                streams[name].add(stage)
            else:
                streams[name].send(stage)
        chunk_rows = mod_five.shape[0] * mod_five.shape[1]
        gathered = mod_five[...].reshape(chunk_rows, LANES)
        embedded = cond_five[...].reshape(chunk_rows, 128).astype(BF16)
        upper = gathered.astype(BF16)
        lower = (gathered - upper.astype(F32)).astype(BF16)
        mod_out[...] = dot_tn(embedded, upper) + dot_tn(embedded, lower)
        for number in range(5, len(greet)):
            small_step(number)
        for number in range(5, len(greet)):
            late_step(number)
        small_out[...] = small_acc[len(greet)]
        small_out[pl.ds(FIRST_GAIN, 1), :] = late_acc[len(greet), pl.ds(0, 1), :]
        small_out[pl.ds(MOD_BIAS, 2), :] = late_acc[len(greet), pl.ds(1, 2), :]
        for stream in triple:
            stream.done()
        for number in range(3):
            triple_core(number).wait_send()
        for number in range(5):
            for copy in mod_copies(number):
                copy.wait_send()
        for number in range(len(greet)):
            small_copy(number).wait_send()
            late_copy(number).wait_send()

    pl.run_scoped(
        attention_phase,
        pltpu.VMEM((tokens, width), BF16), pltpu.VMEM((tokens, width), BF16), pltpu.VMEM((width, 3 * width), BF16),
        pltpu.VMEM((2, width, tokens), BF16), pltpu.VMEM((width, tokens), F32), pltpu.VMEM((tokens, width), F32),
        pltpu.VMEM((tokens, width), F32), pltpu.VMEM((tokens, 3 * width), BF16), pltpu.VMEM((tokens, width), F32),
        pltpu.VMEM((2, 2, 2, 2, 2, 144, LANES), BF16),
        pltpu.VMEM((2, 2, 2, 2, 8, LANES), F32), pltpu.VMEM((1, 2, 2, 2, 8, LANES), F32),
    )

    for tile in range(tiles):
        for copy in core_copies(tile):
            copy.wait_send()
    for name, stream in streams.items():
        if name[0] != "q":
            stream.done()
    for place in range(HEADS // 2 + 2):
        swap(place).wait_send()


def backward(segments, lengths, modulation, condition, table, first_gain, second_gain, expand_bias, reduce_bias, *arrays):
    tokens, width = arrays[3].shape
    all_bits = lax.axis_size("dp").bit_length() - 1
    extra_bits = all_bits - GROUP_BITS
    steps = all_bits + 1
    smem, vmem = pl.BlockSpec(memory_space=pltpu.SMEM), pl.BlockSpec(memory_space=pltpu.VMEM)
    hbm = pl.BlockSpec(memory_space=pl.ANY)
    tiles = arrays[0].shape[0] // TILE

    def rows_of(count, free, lead=()):
        return pltpu.VMEM(lead + (2,) * free + (count, LANES), BF16)

    def half(dtype):
        return pltpu.VMEM((tokens, width), dtype)

    features = pltpu.VMEM((tokens, 128), BF16)
    both = pltpu.VMEM((2, tokens, width), BF16)
    group_rows = [rows_of(count, free) for count in (48, 144) for free in (4, 3, 2, 1, 0)]
    halves = [rows_of(192, 1, (4,)), rows_of(192, 0, (4,)), rows_of(192, 0, (2,)), rows_of(192, 0)]
    halves += [rows_of(96, 2, (4,)), rows_of(96, 1, (4,)), rows_of(96, 0, (4,)), rows_of(96, 0, (2,))]
    mods = [pltpu.VMEM(shape + (8, LANES), F32) for shape in ((2, 2, 2), (2, 2, 2), (4, 2), (8,), (16,))]
    conds = [pltpu.VMEM(shape + (8, 128), F32) for shape in ((), (), (1,), (2,), (4,), (8,), (16,))]
    dma = pltpu.SemaphoreType.DMA
    return pl.pallas_call(
        functools.partial(backward_kernel, extra_bits, all_bits),
        out_shape=(
            jax.ShapeDtypeStruct((tokens, width), BF16),
            jax.ShapeDtypeStruct((tokens, width), BF16),
            jax.ShapeDtypeStruct((576, LANES), F32),
            jax.ShapeDtypeStruct((128, LANES), F32),
            jax.ShapeDtypeStruct((SMALL_ROWS, width), F32),
        ),
        in_specs=[smem] * 2 + [vmem] * 7 + [hbm] * len(arrays),
        out_specs=(vmem,) * 5,
        scratch_shapes=[rows_of(192, 5), rows_of(192, 5), rows_of(48, 5), rows_of(192, 4), rows_of(192, 4)]
        + halves
        + group_rows
        + [both, both, both, features, pltpu.VMEM((2, tokens, 128), BF16)]
        + [half(F32), half(BF16), features, half(BF16), features, features]
        + [pltpu.VMEM((tokens // BLOCK, 6 * width), F32)]
        + [pltpu.VMEM((steps + 1, SMALL_ROWS, width), F32), pltpu.VMEM((steps, SMALL_ROWS, width), F32)]
        + [pltpu.VMEM((steps + 1, 8, width), F32), pltpu.VMEM((steps, 8, width), F32)]
        + mods
        + conds
        + [dma((12,)), dma((2, tiles)), dma((2, tiles)), dma((2, tiles)), dma((17, 5)), dma((17, 5)), dma((8,)), dma((8,))]
        + [dma((steps,)), dma((steps,)), dma((steps,)), dma((steps,)), dma((2, 5)), dma((2, 5)), dma((3,)), dma((3,))],
        compiler_params=pltpu.CompilerParams(
            collective_id=2, has_side_effects=True, vmem_limit_bytes=63 << 20
        ),
    )(segments, lengths, modulation, condition, table, first_gain, second_gain, expand_bias, reduce_bias, *arrays)


def scatter_rest(block, dp_size):
    group = dp_size >> GROUP_BITS
    if group == 1:
        return block
    groups = [[first * group + place for place in range(group)] for first in range(dp_size // group)]
    return lax.psum_scatter(block, "dp", scatter_dimension=0, axis_index_groups=groups, tiled=True)


def finish_kernel(
    block_in, grad_in, sums, mod_sum, small,
    block_out, input_grad, first_gain, mod_block, mod_bias, triple_block, output_block, second_gain, expand_block,
    expand_bias, reduce_block, reduce_bias, masked_rms,
):
    width = first_gain.shape[0]
    block_out[...] = block_in[...]
    input_grad[...] = grad_in[...]
    expand_block[...] = sums[pl.ds(0, 192), :]
    for chunk in range(4):
        reduce_block[:, pl.ds(chunk * LANES, LANES)] = sums[pl.ds(192 + 48 * chunk, 48), :]
    output_block[...] = sums[pl.ds(384, 48), :]
    triple_block[...] = sums[pl.ds(432, 144), :]
    half = mod_sum.shape[0] // 2
    first_row = pl.multiple_of(lax.axis_index("seq") * half, half)
    mod_block[...] = mod_sum[pl.ds(first_row, half), pl.ds(0, mod_block.shape[1])]
    for target, first in (
        (first_gain, FIRST_GAIN), (mod_bias, MOD_BIAS), (second_gain, SECOND_GAIN), (expand_bias, EXPAND_BIAS),
        (reduce_bias, REDUCE_BIAS),
    ):
        for part in range(target.shape[0] // width):
            target[pl.ds(part * width, width)] = small[first + part, :]
    count = jnp.sum(jnp.where(lane_iota((1, width)) == 3, small[pl.ds(STATS, 1), :], 0.0))
    masked_rms[...] = jnp.sqrt(small[STATS, pl.ds(0, 128)] / (count * width))[:3]


def finish(block_out, input_grad, sums, mod_sum, small):
    width = small.shape[1]
    vmem = pl.BlockSpec(memory_space=pltpu.VMEM)
    shapes = (
        (width,), (mod_sum.shape[0] // 2, 6 * width // 16), (6 * width,), (144, LANES), (48, LANES), (width,), (192, LANES),
        (4 * width,), (48, 4 * LANES), (width,), (3,),
    )
    block_out, input_grad, *rest = pl.pallas_call(
        finish_kernel,
        out_shape=(
            jax.ShapeDtypeStruct(block_out.shape, block_out.dtype),
            jax.ShapeDtypeStruct(input_grad.shape, input_grad.dtype),
        )
        + tuple(jax.ShapeDtypeStruct(shape, F32) for shape in shapes),
        in_specs=[vmem] * 5,
        out_specs=(vmem,) * (2 + len(shapes)),
    )(block_out, input_grad, sums, mod_sum, small)
    for place in (3, 4, 6, 8):
        rest[place] = rest[place].T
    return (block_out, input_grad, *rest)


def local(
    hidden_in,
    segment_ids,
    piece_lengths,
    time_index,
    first_gain,
    modulation_weight,
    modulation_bias,
    query_key_value_weight,
    attention_output_matrix,
    second_gain,
    widen_weight,
    expand_bias,
    narrow_weight,
    reduce_bias,
    cotangent,
):
    slot_count, own_rows, width = hidden_in.shape
    hidden, cot = hidden_in[0], cotangent[0]
    table = jnp.asarray(angle_table())
    gain_one, gain_two = first_gain, second_gain
    normed, queries, keys, values, attended, query_features, key_features, modulation, condition = forward(
        segment_ids, piece_lengths, time_index, hidden, table, gain_one, modulation_weight,
        modulation_bias, query_key_value_weight,
    )
    block_out, input_grad, block_sum, mod_sum, small_sum = backward(
        segment_ids, piece_lengths, modulation, condition, table, gain_one, gain_two, expand_bias,
        reduce_bias, narrow_weight, widen_weight, attention_output_matrix, attended, cot, queries, keys, values,
        query_features, key_features, normed, hidden, query_key_value_weight,
    )
    dp_size = lax.axis_size("dp")
    if dp_size == 2**GROUP_BITS:
        block_out, input_grad, *rest = finish(block_out, input_grad, block_sum, mod_sum, small_sum)
        return (block_out[None], input_grad[None], *rest)
    expand_block = scatter_rest(block_sum[:192], dp_size).T
    reduce_block = block_sum[192:384].reshape(4, -1, LANES).transpose(1, 0, 2).reshape(-1, 4 * LANES)
    reduce_block = scatter_rest(reduce_block, dp_size).T
    output_block = scatter_rest(block_sum[384:432], dp_size).T
    triple_block = scatter_rest(block_sum[432:576], dp_size).T
    half = mod_sum.shape[0] // 2
    mod_block = lax.dynamic_slice_in_dim(mod_sum, lax.axis_index("seq") * half, half, 0)[:, : 6 * width // 16]
    mod_block = scatter_rest(mod_block.T, dp_size).T
    stats = small_sum[STATS]
    return (
        block_out[None],
        input_grad[None],
        small_sum[FIRST_GAIN],
        mod_block,
        small_sum[MOD_BIAS : MOD_BIAS + 6].reshape(-1),
        triple_block,
        output_block,
        small_sum[SECOND_GAIN],
        expand_block,
        small_sum[EXPAND_BIAS : EXPAND_BIAS + 4].reshape(-1),
        reduce_block,
        small_sum[REDUCE_BIAS],
        jnp.sqrt(stats[:3] / (stats[3] * width)),
    )


def solution(mesh):
    in_specs = (
        P("dp", "seq", None),
        P("dp", None),
        P("dp", None),
        P("dp", None),
        P(),
        P(),
        P(),
        P(),
        P(),
        P(),
        P(),
        P(),
        P(),
        P(),
        P("dp", "seq", None),
    )
    out_specs = (
        P("dp", "seq", None),
        P("dp", "seq", None),
        P(),
        P("seq", "dp"),
        P(),
        P("seq", "dp"),
        P("seq", "dp"),
        P(),
        P("seq", "dp"),
        P(),
        P("seq", "dp"),
        P(),
        P(),
    )
    return jax.shard_map(local, mesh=mesh, in_specs=in_specs, out_specs=out_specs, check_vma=False)
```
